32 devices in a mesh: feat: 4 (over y, x), seq: 4 (over z), dp: 2 (over core).
Axes of the slice: x: 2, y: 2, z: 4, core: 2. Of those that a mesh axis runs over, the one named last changes fastest.
Arguments:
- tokens: bfloat16 [4, 2, 1024, 2048], P('feat', 'dp', 'seq'), may hold values from -6 to 6
- segments: int32 [4, 2, 1024], P(None, 'dp', 'seq'), may hold values from 0 to 3, never falling along the last dimension, each value on 1 to 512 neighbouring positions
- norm1_gain: bfloat16 [2048], P(('feat', 'seq', 'dp')), may hold values from 0.5 to 1.5
- norm2_gain: bfloat16 [2048], P(('feat', 'seq', 'dp')), may hold values from 0.5 to 1.5
- w_query: bfloat16 [2048, 256], P(('feat', 'seq', 'dp')), may hold values from -0.25 to 0.25
- w_key: bfloat16 [2048, 256], P(('feat', 'seq', 'dp')), may hold values from -0.25 to 0.25
- w_value: bfloat16 [2048, 2048], P(('feat', 'seq', 'dp')), may hold values from -0.125 to 0.125
- w_out: bfloat16 [2048, 2048], P(None, ('feat', 'seq', 'dp')), may hold values from -0.375 to 0.375
- w_gate: bfloat16 [2048, 5632], P(('seq', 'dp'), 'feat'), may hold values from -0.125 to 0.125
- w_up: bfloat16 [2048, 5632], P(('seq', 'dp'), 'feat'), may hold values from -0.125 to 0.125
- w_down: bfloat16 [5632, 2048], P('feat', ('seq', 'dp')), may hold values from -0.078125 to 0.078125
- cotangent: bfloat16 [4, 2, 1024, 2048], P('feat', 'dp', 'seq'), may hold values from -6 to 6
Outputs:
- out: bfloat16 [4, 2, 1024, 2048], P('feat', 'dp', 'seq')
- x_grad: float32 [4, 2, 1024, 2048], P('feat', 'dp', 'seq')
- norm1_gain_grad: float32 [2048], P(('feat', 'seq', 'dp'))
- norm2_gain_grad: float32 [2048], P(('feat', 'seq', 'dp'))
- w_query_grad: float32 [2048, 256], P(('feat', 'seq', 'dp'))
- w_key_grad: float32 [2048, 256], P(('feat', 'seq', 'dp'))
- w_value_grad: float32 [2048, 2048], P(('feat', 'seq', 'dp'))
- w_out_grad: float32 [2048, 2048], P(None, ('feat', 'seq', 'dp'))
- w_gate_grad: float32 [2048, 5632], P(('seq', 'dp'), 'feat')
- w_up_grad: float32 [2048, 5632], P(('seq', 'dp'), 'feat')
- w_down_grad: float32 [5632, 2048], P('feat', ('seq', 'dp'))
The draws below stay inside these ranges and needn't reach their ends.
Inputs may be any that keep to these rules, and one draw needn't show every extreme that they name: `segments`: along each sequence the segment numbers never fall; all 4 numbers occur, each on 1 to 512 tokens, and one on exactly 512.
All inputs are finite; a program needn't handle non-finite values.
Results may differ from the reference program's by a relative error of at most 0.019.
Values may be sent and summed in bfloat16 or wider, within the bound.
A program may use at most 256 MiB of HBM per device.

```python
import math
import jax
import jax.numpy as jnp
import numpy as np
from jax import lax

D = 2048
HEADS = 16
FDIM = 16
HV = 128
FF = 5632
SEGS = 4
LENGTH = 1024
FEAT_SEQS = 4
DP_SEQS = 2
QK = 256
VALUE = 2048
DOC_MOST = 512


def strengthened(drawn, rng, source, target, blocks, factor):
    owner, partner = [(jnp.arange(drawn.shape[axis_at]) // (drawn.shape[axis_at] // blocks)).reshape([-1 if axis == axis_at else 1 for axis in range(drawn.ndim)]) for axis_at in (source, target)]
    chosen = jax.random.permutation(rng, blocks)[partner]
    strong = (owner == chosen) | (owner == (partner + blocks // 2) % blocks)
    return jnp.where(strong, factor * drawn, drawn)


def steps_of(rng, extent, shards, low, high):
    def one(dim, parts):
        draws = jax.random.uniform(jax.random.fold_in(jax.random.fold_in(rng, 6), dim), (parts,), jnp.float32, low / len(shards), high / len(shards))
        return jnp.repeat(jnp.exp(draws), extent[dim] // parts).reshape((-1,) + (1,) * (len(extent) - dim - 1))

    loudness = one(*shards[0])
    for cut in shards[1:]:
        loudness = loudness * one(*cut)
    return loudness


def profile(amount, total, limit, skew):
    portions = [(1 << 20) // math.isqrt(standing ** skew) + 1 for standing in range(2, amount + 1)]
    spare, holding = total - limit - (amount - 1), [1] * (amount - 1)
    while spare > 0:
        movable = [i for i in range(amount - 1) if holding[i] < limit]
        whole, remaining = sum([portions[i] for i in movable]), spare
        for i in movable:
            extra = min(limit - holding[i], max(1, remaining * portions[i] // whole), spare)
            holding[i] = holding[i] + extra
            spare = spare - extra
    return np.array([limit] + holding)


def ragged_sizes(key, count, total, limit, lean):
    if count == 2:
        one = jax.random.randint(key, (), max(1, total - limit), min(limit, total - 1) + 1)
        return jnp.stack([one, total - one])
    lengths = jnp.asarray(profile(count, total, limit, lean), jnp.int32)
    pairs = (count - 1) // 2
    donor, sink = lengths[1:1 + 2 * pairs:2], lengths[2:2 + 2 * pairs:2]
    margin = jnp.minimum(donor - 1, limit - sink)
    moved = jax.random.randint(jax.random.fold_in(key, 1), (pairs,), 0, 1 << 20) % (margin + 1)
    lengths = lengths.at[1:1 + 2 * pairs:2].set(donor - moved).at[2:2 + 2 * pairs:2].set(sink + moved)
    return lengths[jax.random.permutation(jax.random.fold_in(key, 2), count)]


def bell_draw(own_key, dims, scale, reach, split=(), held_as=jnp.bfloat16):
    array = scale * jax.random.normal(own_key, dims, jnp.float32)
    if split:
        array = array * steps_of(own_key, dims, split, -0.22, 0.18)
    return jnp.clip(array, -reach, reach).astype(held_as)


def noise_with(own_key, dims, deviation, reach, shards, heavy, dtype=jnp.bfloat16):
    values = deviation * jax.random.normal(own_key, dims, jnp.float32)
    if shards:
        values = values * steps_of(own_key, dims, shards, -0.22, 0.18)
    return jnp.clip(strengthened(values, jax.random.fold_in(own_key, 3), *heavy), -reach, reach).astype(dtype)


def setup_inputs(seed: int = 0) -> dict:
    arg_keys = jax.random.split(jax.random.key(seed), 13)
    return {
        "tokens": bell_draw(arg_keys[0], (FEAT_SEQS, DP_SEQS, LENGTH, D), 1.0, 6.0, ((0, 4), (1, 2), (2, 4))),
        "segments": jax.vmap(lambda own: jnp.searchsorted(jnp.cumsum(ragged_sizes(own, SEGS, LENGTH, DOC_MOST, 1)), jnp.arange(LENGTH), side="right"))(jax.random.split(arg_keys[1], FEAT_SEQS * DP_SEQS)).reshape((FEAT_SEQS, DP_SEQS, LENGTH)).astype(jnp.int32),
        "norm1_gain": jnp.clip(1.0 + 0.1 * jax.random.normal(arg_keys[2], (D,), jnp.float32), 0.5, 1.5).astype(jnp.bfloat16),
        "norm2_gain": jnp.clip(1.0 + 0.1 * jax.random.normal(arg_keys[3], (D,), jnp.float32), 0.5, 1.5).astype(jnp.bfloat16),
        "w_query": bell_draw(arg_keys[4], (D, QK), (D // 4) ** -0.5, 0.25, ((0, 32),)),
        "w_key": bell_draw(arg_keys[5], (D, QK), (D // 4) ** -0.5, 0.25, ((0, 32),)),
        "w_value": bell_draw(arg_keys[6], (D, VALUE), D ** -0.5, 0.125, ((0, 32),)),
        "w_out": bell_draw(arg_keys[7], (VALUE, D), (VALUE // 8) ** -0.5, 0.375, ((1, 32),)),
        "w_gate": bell_draw(arg_keys[8], (D, FF), D ** -0.5, 0.125, ((0, 8), (1, 4))),
        "w_up": bell_draw(arg_keys[9], (D, FF), D ** -0.5, 0.125, ((0, 8), (1, 4))),
        "w_down": bell_draw(arg_keys[10], (FF, D), FF ** -0.5, 0.078125, ((0, 4), (1, 8))),
        "cotangent": noise_with(arg_keys[11], (FEAT_SEQS, DP_SEQS, LENGTH, D), 1.0, 6.0, ((0, 4), (1, 2), (2, 4)), (2, 3, 4, 2.0)),
    }


exact_mode = lax.Precision.HIGHEST
epsilon = 1e-05

@jax.custom_vjp
def low(v):
    return lax.optimization_barrier(v.astype(jnp.bfloat16)).astype(jnp.float32)

@jax.custom_vjp
def low_back(v):
    return v

def low_keep(v):
    return (low(v), None)

def low_pass(kept, grad):
    return (grad,)

def back_keep(v):
    return (v, None)

def back_low(kept, grad):
    return (low(grad),)
low.defvjp(low_keep, low_pass)
low_back.defvjp(back_keep, back_low)

def rms_norm(values, gain):
    inverse = lax.rsqrt(lax.optimization_barrier(jnp.mean(values * values, axis=-1, keepdims=True)) + epsilon)
    return values * inverse * gain

def sequence_attention(element):
    query_in, key_in, value_in, segment = element
    length = query_in.shape[0]
    query_heads = query_in.reshape(length, HEADS, FDIM).transpose(1, 0, 2)
    key_heads = key_in.reshape(length, HEADS, FDIM).transpose(1, 0, 2)
    value_heads = value_in.reshape(length, HEADS, HV).transpose(1, 0, 2)
    scores = jnp.einsum('htf,hsf->hts', query_heads, key_heads, precision=exact_mode)
    positions = jnp.arange(length)
    allowed = (positions[None, :] <= positions[:, None]) & (segment[None, :] == segment[:, None])
    kernel = jnp.where(allowed[None], 1.0 + scores / 4.0 + scores * scores / 32.0, 0.0)
    numerator = low_back(jnp.einsum('hts,hse->hte', kernel, value_heads, precision=exact_mode))
    denominator = low_back(lax.optimization_barrier(jnp.sum(kernel, axis=-1)))
    attended = numerator / denominator[:, :, None]
    return attended.transpose(1, 0, 2).reshape(length, HEADS * HV)

def block_forward(inputs, segment, gain_one, gain_two, query_w, key_w, value_w, out_w, gate_w, up_w, down_w):
    normed_one = low(rms_norm(inputs, gain_one))
    query_in = low_back(low(jnp.einsum('gtd,dq->gtq', normed_one, query_w, precision=exact_mode)))
    key_in = low_back(low(jnp.einsum('gtd,dq->gtq', normed_one, key_w, precision=exact_mode)))
    value_in = low_back(low(jnp.einsum('gtd,de->gte', normed_one, value_w, precision=exact_mode)))
    attended = lax.map(jax.checkpoint(sequence_attention), (query_in, key_in, value_in, segment))
    branch = low_back(jnp.einsum('gte,ed->gtd', low(attended), out_w, precision=exact_mode))
    residual = inputs + branch
    normed_two = low(rms_norm(residual, gain_two))
    gate_out = low_back(jnp.einsum('gtd,df->gtf', normed_two, gate_w, precision=exact_mode))
    up_out = low_back(jnp.einsum('gtd,df->gtf', normed_two, up_w, precision=exact_mode))
    mixed_low = low(jax.nn.silu(gate_out) * up_out)
    return residual + jnp.einsum('gtf,fd->gtd', mixed_low, down_w, precision=exact_mode)

def reference(tokens, segments, norm1_gain, norm2_gain, w_query, w_key, w_value, w_out, w_gate, w_up, w_down, cotangent):
    params = (norm1_gain.astype(jnp.float32), norm2_gain.astype(jnp.float32), w_query.astype(jnp.float32), w_key.astype(jnp.float32), w_value.astype(jnp.float32), w_out.astype(jnp.float32), w_gate.astype(jnp.float32), w_up.astype(jnp.float32), w_down.astype(jnp.float32))

    def group_step(totals, element):
        x_group, seg_group, cot_group = element

        def forward(inputs, gain_one, gain_two, query_w, key_w, value_w, out_w, gate_w, up_w, down_w):
            return block_forward(inputs, seg_group, gain_one, gain_two, query_w, key_w, value_w, out_w, gate_w, up_w, down_w)
        result, pullback = jax.vjp(forward, x_group.astype(jnp.float32), params[0], params[1], params[2], params[3], params[4], params[5], params[6], params[7], params[8])
        gradients = pullback(cot_group.astype(jnp.float32))
        totals = tuple((running + grad_part for running, grad_part in zip(totals, gradients[1:])))
        return (totals, (result.astype(jnp.bfloat16), gradients[0]))
    initial = tuple((jnp.zeros_like(param_item) for param_item in params))
    inputs_all = (jnp.swapaxes(tokens, 0, 1), jnp.swapaxes(segments, 0, 1), jnp.swapaxes(cotangent, 0, 1))
    totals, (outputs, input_grads) = lax.scan(group_step, initial, inputs_all)
    out = jnp.swapaxes(outputs, 0, 1)
    x_grad = jnp.swapaxes(input_grads, 0, 1)
    return (out, x_grad, totals[0], totals[1], totals[2], totals[3], totals[4], totals[5], totals[6], totals[7], totals[8])
```

```python
import functools

import jax
import jax.numpy as jnp
import numpy as np
from jax import lax
from jax.experimental import pallas as pl
from jax.experimental.pallas import tpu as pltpu
from jax.sharding import PartitionSpec as P

HEADS = 16
FDIM = 16
HV = 128
STATE = 160
LANES = 256
epsilon = 1e-05
MESH = pl.DeviceIdType.MESH
ALL = ("feat", "seq", "dp")
f32 = jnp.float32
bf16 = jnp.bfloat16


def dot(a, b):
    return lax.dot_general(a, b, (((1,), (0,)), ((), ())), preferred_element_type=f32)


def dot_nt(a, b):
    return lax.dot_general(a, b, (((1,), (1,)), ((), ())), preferred_element_type=f32)


def dot_tn(a, b):
    return lax.dot_general(a, b, (((0,), (0,)), ((), ())), preferred_element_type=f32)


def feature_tables(heads):
    pairs = [(i, j) for i in range(FDIM) for j in range(i, FDIM)]
    left = np.zeros((heads, heads * FDIM, LANES), np.float32)
    right = np.zeros((heads, heads * FDIM, LANES), np.float32)
    rows = np.zeros((8, LANES), np.float32)
    for h in range(heads):
        for p, (i, j) in enumerate(pairs):
            left[h, h * FDIM + i, p] = 1.0
            right[h, h * FDIM + j, p] = 1.0
            rows[2, p] = 0.25 / 2.0**0.5 if i == j else 0.25
        for i in range(FDIM):
            p = len(pairs) + i
            left[h, h * FDIM + i, p] = 1.0
            rows[1, p] = 1.0
            rows[2, p] = 0.5
        p = len(pairs) + FDIM
        rows[0, p] = rows[1, p] = rows[2, p] = 1.0
    return jnp.asarray(left, bf16), jnp.asarray(right, bf16), jnp.asarray(rows)


def both_sides(entries, h, left_ref, right_ref, rows_ref):
    one = dot(entries, left_ref[h]) + rows_ref[0:1, :]
    two = dot(entries, right_ref[h]) + rows_ref[1:2, :]
    return one, two * rows_ref[2:3, :]


def features(entries, h, left_ref, right_ref, rows_ref):
    one, two = both_sides(entries, h, left_ref, right_ref, rows_ref)
    return one * two


def pull_features(grad, entries, h, left_ref, right_ref, rows_ref):
    one, two = both_sides(entries, h, left_ref, right_ref, rows_ref)
    scaled = rows_ref[2:3, :]
    return dot_nt((grad * two).astype(bf16), left_ref[h]) + dot_nt(
        (grad * one * scaled).astype(bf16), right_ref[h]
    )


def only_head(entries, h):
    lane = lax.broadcasted_iota(jnp.int32, entries.shape, 1)
    keep = (lane >= h * FDIM) & (lane < (h + 1) * FDIM)
    return jnp.where(keep, entries, jnp.zeros_like(entries))


def padded_state(state):
    return jnp.concatenate([state, jnp.zeros((LANES - STATE, state.shape[1]), state.dtype)], 0)


def chain_barrier(place, count):
    barrier = pltpu.get_barrier_semaphore()
    for step in (1, count - 1):
        other = lax.rem(place + step, count)
        pl.semaphore_signal(barrier, inc=1, device_id={"seq": other}, device_id_type=MESH)
    pl.semaphore_wait(barrier, 2)


def allowed_of(segc, segr):
    block = segc.shape[0]
    row = lax.broadcasted_iota(jnp.int32, (block, block), 0)
    col = lax.broadcasted_iota(jnp.int32, (block, block), 1)
    return (row >= col) & (segc == segr)


def forward_kernel(
    count,
    heads,
    qkv_ref,
    segc_ref,
    segr_ref,
    left_ref,
    right_ref,
    rows_ref,
    att_ref,
    rden_ref,
    carry_ref,
    csum_ref,
    send_state,
    send_sum,
    part,
    send_sem,
    recv_sem,
):
    place = lax.axis_index("seq")
    groups, block = qkv_ref.shape[0], qkv_ref.shape[1]
    width = heads * FDIM
    tables = (left_ref, right_ref, rows_ref)

    def hop(g):
        target = {"seq": lax.rem(place + 1, count)}
        return [
            pltpu.make_async_remote_copy(
                src_ref=src.at[g],
                dst_ref=dst.at[g],
                send_sem=send_sem.at[i, g],
                recv_sem=recv_sem.at[i, g],
                device_id=target,
                device_id_type=MESH,
            )
            for i, (src, dst) in enumerate(((send_state, carry_ref), (send_sum, csum_ref)))
        ]

    def send(g):
        for copy in hop(g):
            copy.start()

    chain_barrier(place, count)

    @pl.when(place == 0)
    def _():
        carry_ref[...] = jnp.zeros_like(carry_ref)
        csum_ref[...] = jnp.full_like(csum_ref, -1.0)

    def summarize(g, none):
        segc, segr = segc_ref[g], segr_ref[g]
        tail = segr[:, block - 1 : block]
        at_tail = (segc == tail).astype(f32)
        send_sum[g, heads : heads + 1, :] = jnp.broadcast_to(tail, (1, LANES))
        for h in range(heads):
            key = qkv_ref[g, :, width : 2 * width]
            value = qkv_ref[g, :, 2 * width + h * HV : 2 * width + (h + 1) * HV]
            phi = (features(key, h, *tables) * at_tail).astype(bf16)
            send_state[g, h] = dot_tn(phi, value)[:STATE].astype(bf16)
            ones = jnp.ones((8, block), bf16)
            send_sum[g, h : h + 1, :] = dot(ones, phi)[0:1]

        @pl.when(place == 0)
        def _():
            send(g)

        return none

    lax.fori_loop(0, groups, summarize, 0)

    def attend(g, none):
        segc, segr = segc_ref[g], segr_ref[g]
        allowed = allowed_of(segc, segr)
        for h in range(heads):
            query = only_head(qkv_ref[g, :, 0:width], h)
            key = qkv_ref[g, :, width : 2 * width]
            value = qkv_ref[g, :, 2 * width + h * HV : 2 * width + (h + 1) * HV]
            c = dot_nt(query, key)
            kernel = jnp.where(allowed, 1.0 + c * (0.25 + c * 0.03125), 0.0).astype(bf16)
            wide = jnp.concatenate([value, jnp.ones_like(value)], axis=1)
            part[h] = dot(kernel, wide)

        @pl.when(place > 0)
        def _():
            for copy in hop(g):
                copy.wait_recv()

        mark = csum_ref[g, heads : heads + 1, 0:1]
        head, tail = segr[:, 0:1], segr[:, block - 1 : block]
        whole = ((head == tail) & (head == mark)).astype(f32)

        @pl.when((place > 0) & (place < count - 1))
        def _():
            for h in range(heads):
                send_state[g, h] = (
                    send_state[g, h].astype(f32) + whole * carry_ref[g, h].astype(f32)
                ).astype(bf16)
                send_sum[g, h : h + 1, :] = (
                    send_sum[g, h : h + 1, :] + whole * csum_ref[g, h : h + 1, :]
                )
            send(g)

        carried = (segc == mark).astype(f32)
        for h in range(heads):
            phi = features(qkv_ref[g, :, 0:width], h, *tables) * carried
            state = padded_state(carry_ref[g, h])
            both = part[h]
            numer = both[:, :HV] + dot(phi.astype(bf16), state)
            denom = both[:, HV:] + jnp.sum(
                phi * csum_ref[g, h : h + 1, :], axis=1, keepdims=True
            )
            inverse = 1.0 / denom
            att_ref[g, :, h * HV : (h + 1) * HV] = (numer * inverse).astype(bf16)
            rden_ref[g, :, h * HV : (h + 1) * HV] = inverse
        return none

    lax.fori_loop(0, groups, attend, 0)

    @pl.when(place < count - 1)
    def _():
        def finish(g, none):
            for copy in hop(g):
                copy.wait_send()
            return none

        lax.fori_loop(0, groups, finish, 0)


def backward_kernel(
    count,
    heads,
    qkv_ref,
    segc_ref,
    segr_ref,
    left_ref,
    right_ref,
    rows_ref,
    att_ref,
    rden_ref,
    carry_ref,
    csum_ref,
    ga_ref,
    out_ref,
    gn,
    send_state,
    send_sum,
    recv_state,
    recv_sum,
    dkey,
    dvalue,
    send_sem,
    recv_sem,
):
    place = lax.axis_index("seq")
    groups, block = qkv_ref.shape[0], qkv_ref.shape[1]
    width = heads * FDIM
    tables = (left_ref, right_ref, rows_ref)

    def hop(g):
        target = {"seq": lax.rem(place + count - 1, count)}
        return [
            pltpu.make_async_remote_copy(
                src_ref=src.at[g],
                dst_ref=dst.at[g],
                send_sem=send_sem.at[i, g],
                recv_sem=recv_sem.at[i, g],
                device_id=target,
                device_id_type=MESH,
            )
            for i, (src, dst) in enumerate(((send_state, recv_state), (send_sum, recv_sum)))
        ]

    def send(g):
        for copy in hop(g):
            copy.start()

    chain_barrier(place, count)

    @pl.when(place == count - 1)
    def _():
        recv_state[...] = jnp.zeros_like(recv_state)
        recv_sum[...] = jnp.full_like(recv_sum, -1.0)

    def summarize(g, none):
        segc, segr = segc_ref[g], segr_ref[g]
        head = segr[:, 0:1]
        at_head = (segc == head).astype(f32)
        send_sum[g, heads : heads + 1, :] = jnp.broadcast_to(head, (1, LANES))
        for h in range(heads):
            lanes = slice(h * HV, (h + 1) * HV)
            ga = ga_ref[g, :, lanes]
            inverse = rden_ref[g, :, lanes]
            numer = (ga * inverse).astype(bf16)
            dots = jnp.sum(ga * att_ref[g, :, lanes].astype(f32), axis=1, keepdims=True)
            lane = lax.broadcasted_iota(jnp.int32, (block, HV), 1)
            denom = jnp.where(lane == 0, -dots * inverse, 0.0).astype(bf16)
            gn[g, h, :, :HV] = numer
            gn[g, h, :, HV:] = denom
            phi = (features(qkv_ref[g, :, 0:width], h, *tables) * at_head).astype(bf16)
            send_state[g, h] = dot_tn(phi, numer)[:STATE].astype(bf16)
            send_sum[g, h : h + 1, :] = dot_tn(denom, phi)[0:1]

        @pl.when(place == count - 1)
        def _():
            send(g)

        return none

    lax.fori_loop(0, groups, summarize, 0)

    def pull(g, none):
        segc, segr = segc_ref[g], segr_ref[g]
        allowed = allowed_of(segc, segr)
        query_all = qkv_ref[g, :, 0:width]
        key_all = qkv_ref[g, :, width : 2 * width]
        carried = (segc == csum_ref[g, heads : heads + 1, 0:1]).astype(f32)
        dquery = jnp.zeros((block, width), f32)
        dkey[...] = jnp.zeros_like(dkey)
        for h in range(heads):
            query, key = only_head(query_all, h), only_head(key_all, h)
            value = qkv_ref[g, :, 2 * width + h * HV : 2 * width + (h + 1) * HV]
            wide = jnp.concatenate([value, jnp.ones_like(value)], axis=1)
            both = gn[g, h]
            c = dot_nt(query, key_all)
            kernel = jnp.where(allowed, 1.0 + c * (0.25 + c * 0.03125), 0.0).astype(bf16)
            grad = jnp.where(allowed, dot_nt(both, wide), 0.0)
            grad_c = (grad * (0.25 + c * 0.0625)).astype(bf16)
            dvalue[h] = dot_tn(kernel, both[:, :HV])
            dkey[...] += dot_tn(grad_c, query)
            dquery = dquery + dot(grad_c, key)
            state = padded_state(carry_ref[g, h])
            gphi = dot_nt(both[:, :HV], state) + both[:, HV : HV + 1].astype(f32) * csum_ref[
                g, h : h + 1, :
            ]
            dquery = dquery + pull_features(gphi * carried, query_all, h, *tables)
        out_ref[g, :, 0:width] = dquery.astype(bf16)

        @pl.when(place < count - 1)
        def _():
            for copy in hop(g):
                copy.wait_recv()

        mark = recv_sum[g, heads : heads + 1, 0:1]
        head, tail = segr[:, 0:1], segr[:, block - 1 : block]
        whole = ((head == tail) & (head == mark)).astype(f32)

        @pl.when((place > 0) & (place < count - 1))
        def _():
            for h in range(heads):
                send_state[g, h] = (
                    send_state[g, h].astype(f32) + whole * recv_state[g, h].astype(f32)
                ).astype(bf16)
                send_sum[g, h : h + 1, :] = (
                    send_sum[g, h : h + 1, :] + whole * recv_sum[g, h : h + 1, :]
                )
            send(g)

        later = (segc == mark).astype(f32)
        total = dkey[...]
        for h in range(heads):
            value = qkv_ref[g, :, 2 * width + h * HV : 2 * width + (h + 1) * HV]
            state = padded_state(recv_state[g, h])
            phi = (features(key_all, h, *tables) * later).astype(bf16)
            dv = dvalue[h] + dot(phi, state)
            out_ref[g, :, 2 * width + h * HV : 2 * width + (h + 1) * HV] = dv.astype(bf16)
            gphi = (dot_nt(value, state) + recv_sum[g, h : h + 1, :]) * later
            total = total + pull_features(gphi, key_all, h, *tables)
        out_ref[g, :, width : 2 * width] = total.astype(bf16)
        return none

    lax.fori_loop(0, groups, pull, 0)

    @pl.when(place > 0)
    def _():
        def finish(g, none):
            for copy in hop(g):
                copy.wait_send()
            return none

        lax.fori_loop(0, groups, finish, 0)


def whole_vmem(count):
    return [pl.BlockSpec(memory_space=pltpu.VMEM)] * count


def attention_forward(qkv, segc, segr, tables, heads):
    groups, block, _ = qkv.shape
    count = lax.axis_size("seq")
    states = (groups, heads, STATE, HV)
    sums = (groups, 8, LANES)
    return pl.pallas_call(
        functools.partial(forward_kernel, count, heads),
        out_shape=(
            jax.ShapeDtypeStruct((groups, block, heads * HV), bf16),
            jax.ShapeDtypeStruct((groups, block, heads * HV), f32),
            jax.ShapeDtypeStruct(states, bf16),
            jax.ShapeDtypeStruct(sums, f32),
        ),
        in_specs=whole_vmem(6),
        out_specs=tuple(whole_vmem(4)),
        scratch_shapes=[
            pltpu.VMEM(states, bf16),
            pltpu.VMEM(sums, f32),
            pltpu.VMEM((heads, block, 2 * HV), f32),
            pltpu.SemaphoreType.DMA((2, groups)),
            pltpu.SemaphoreType.DMA((2, groups)),
        ],
        compiler_params=pltpu.CompilerParams(
            collective_id=0, has_side_effects=True, vmem_limit_bytes=40 << 20
        ),
        name="attention_forward",
    )(qkv, segc, segr, *tables)


def attention_backward(qkv, segc, segr, tables, att, rden, carry, csum, ga, heads):
    groups, block, wide = qkv.shape
    count = lax.axis_size("seq")
    states = (groups, heads, STATE, HV)
    sums = (groups, 8, LANES)
    return pl.pallas_call(
        functools.partial(backward_kernel, count, heads),
        out_shape=jax.ShapeDtypeStruct((groups, block, wide), bf16),
        in_specs=whole_vmem(11),
        out_specs=whole_vmem(1)[0],
        scratch_shapes=[
            pltpu.VMEM((groups, heads, block, 2 * HV), bf16),
            pltpu.VMEM(states, bf16),
            pltpu.VMEM(sums, f32),
            pltpu.VMEM(states, bf16),
            pltpu.VMEM(sums, f32),
            pltpu.VMEM((block, heads * FDIM), f32),
            pltpu.VMEM((heads, block, HV), f32),
            pltpu.SemaphoreType.DMA((2, groups)),
            pltpu.SemaphoreType.DMA((2, groups)),
        ],
        compiler_params=pltpu.CompilerParams(
            collective_id=1, has_side_effects=True, vmem_limit_bytes=48 << 20
        ),
        name="attention_backward",
    )(qkv, segc, segr, *tables, att, rden, carry, csum, ga)


def inverse_rms(values):
    return lax.rsqrt(jnp.mean(values * values, axis=-1, keepdims=True) + epsilon)


def norm_back(grad, unit, inverse, gain):
    scaled = grad * gain
    return (scaled - unit * jnp.mean(scaled * unit, axis=-1, keepdims=True)) * inverse


def local(
    tokens,
    segments,
    norm1_gain,
    norm2_gain,
    w_query,
    w_key,
    w_value,
    w_out,
    w_gate,
    w_up,
    w_down,
    cotangent,
):
    parts = lax.axis_size("feat")
    heads = HEADS // parts
    block, width = tokens.shape[2], tokens.shape[3]
    rows_total = parts * block
    rows_each = w_query.shape[0]
    own = tokens.reshape(block, width)
    cot_own = cotangent.reshape(block, width)

    def by_share(w, per):
        return w.reshape(rows_each, parts, heads * per).transpose(1, 0, 2)

    pack = jnp.concatenate(
        [by_share(w_query, FDIM), by_share(w_key, FDIM), by_share(w_value, HV), by_share(w_out.T, HV)],
        axis=2,
    )
    pack_width = pack.shape[2]
    pack = lax.all_to_all(pack, "feat", 0, 0, tiled=True)
    pack = lax.all_gather(pack, ("seq", "dp"), axis=1, tiled=True)
    attn_w = pack.reshape(width, pack_width)
    qkv_width = pack_width - heads * HV
    qkv_w, out_w = attn_w[:, :qkv_width], attn_w[:, qkv_width:]
    gains = lax.all_gather(jnp.stack([norm1_gain, norm2_gain]), ALL, axis=1, tiled=True).astype(f32)
    gain_one, gain_two = gains[0], gains[1]

    x_all = lax.all_gather(own, "feat", axis=0, tiled=True)
    gate_w = lax.all_gather(w_gate, ("seq", "dp"), axis=0, tiled=True)
    up_w = lax.all_gather(w_up, ("seq", "dp"), axis=0, tiled=True)
    down_w = lax.all_gather(w_down.T, ("seq", "dp"), axis=0, tiled=True)
    cot_all = lax.all_gather(cot_own, "feat", axis=0, tiled=True)

    x_wide = x_all.astype(f32)
    normed = (x_wide * inverse_rms(x_wide) * gain_one).astype(bf16)
    qkv = dot(normed, qkv_w).astype(bf16).reshape(parts, block, qkv_width)
    segment = segments.reshape(parts, block).astype(f32)
    segc, segr = segment[:, :, None], segment[:, None, :]
    tables = feature_tables(heads)
    att, rden, carry, csum = attention_forward(qkv, segc, segr, tables, heads)
    att_rows = att.reshape(rows_total, heads * HV)
    branch = lax.psum_scatter(
        dot_nt(att_rows, out_w).astype(bf16), "feat", scatter_dimension=0, tiled=True
    )
    inputs = own.astype(f32)
    residual = inputs + branch.astype(f32)
    inverse_two = inverse_rms(residual)
    unit_two = residual * inverse_two
    rows_all = lax.all_gather((unit_two * gain_two).astype(bf16), "feat", axis=0, tiled=True)

    gate_out = dot(rows_all, gate_w)
    up_out = dot(rows_all, up_w)
    sig = jax.nn.sigmoid(gate_out)
    silu = gate_out * sig
    mixed = (silu * up_out).astype(bf16)
    down_own = lax.psum_scatter(
        dot_nt(mixed, down_w).astype(bf16), "feat", scatter_dimension=0, tiled=True
    )
    output = (residual + down_own.astype(f32)).astype(bf16).reshape(tokens.shape)
    grad_mixed = dot(cot_all, down_w)
    grad_gate = (grad_mixed * up_out * sig * (1.0 + gate_out * (1.0 - sig))).astype(bf16)
    grad_up = (grad_mixed * silu).astype(bf16)
    row_grads = dot_nt(grad_gate, gate_w) + dot_nt(grad_up, up_w)
    grad_normed_two = lax.psum_scatter(
        row_grads.astype(bf16), "feat", scatter_dimension=0, tiled=True
    ).astype(f32)

    def summed(term):
        return lax.psum_scatter(
            term.astype(bf16), ("seq", "dp"), scatter_dimension=0, tiled=True
        ).astype(f32)

    grad_w_down = summed(dot_tn(cot_all, mixed)).T
    grad_w_gate = summed(dot_tn(rows_all, grad_gate))
    grad_w_up = summed(dot_tn(rows_all, grad_up))

    gain_two_part = jnp.sum(grad_normed_two * unit_two, axis=0)
    grad_residual = cot_own.astype(f32) + norm_back(grad_normed_two, unit_two, inverse_two, gain_two)
    branch_all = lax.all_gather(grad_residual.astype(bf16), "feat", axis=0, tiled=True)
    ga = dot(branch_all, out_w).reshape(parts, block, heads * HV)
    dqkv = attention_backward(qkv, segc, segr, tables, att, rden, carry, csum, ga, heads)
    dqkv = dqkv.reshape(rows_total, qkv_width)
    grad_normed_one = lax.psum_scatter(
        dot_nt(dqkv, qkv_w).astype(bf16), "feat", scatter_dimension=0, tiled=True
    ).astype(f32)
    inverse_one = inverse_rms(inputs)
    unit_one = inputs * inverse_one
    x_grad = grad_residual + norm_back(grad_normed_one, unit_one, inverse_one, gain_one)
    gain_one_part = jnp.sum(grad_normed_one * unit_one, axis=0)

    attn_grads = jnp.concatenate([dot_tn(normed, dqkv), dot_tn(branch_all, att_rows)], axis=1)
    attn_grads = attn_grads.astype(bf16).reshape(parts, width // parts, pack_width)
    attn_grads = lax.psum_scatter(attn_grads, ("seq", "dp"), scatter_dimension=1, tiled=True)
    attn_grads = lax.all_to_all(attn_grads, "feat", 0, 0, tiled=True).astype(f32)

    def from_share(first, per):
        piece = attn_grads[:, :, first : first + heads * per]
        return piece.transpose(1, 0, 2).reshape(rows_each, HEADS * per)

    start_value = 2 * heads * FDIM
    query_grad = from_share(0, FDIM)
    key_grad = from_share(heads * FDIM, FDIM)
    value_grad = from_share(start_value, HV)
    out_grad = from_share(start_value + heads * HV, HV).T
    gain_grads = lax.psum_scatter(
        jnp.stack([gain_one_part, gain_two_part]), ALL, scatter_dimension=1, tiled=True
    )
    return (
        output,
        x_grad.reshape(tokens.shape),
        gain_grads[0],
        gain_grads[1],
        query_grad,
        key_grad,
        value_grad,
        out_grad,
        grad_w_gate,
        grad_w_up,
        grad_w_down,
    )


def solution(mesh):
    placed = (
        P("feat", "dp", "seq", None),
        P(None, "dp", "seq"),
        P(ALL),
        P(ALL),
        P(ALL, None),
        P(ALL, None),
        P(ALL, None),
        P(None, ALL),
        P(("seq", "dp"), "feat"),
        P(("seq", "dp"), "feat"),
        P("feat", ("seq", "dp")),
        P("feat", "dp", "seq", None),
    )
    return jax.shard_map(
        local,
        mesh=mesh,
        in_specs=placed,
        out_specs=(
            P("feat", "dp", "seq", None),
            P("feat", "dp", "seq", None),
            P(ALL),
            P(ALL),
            P(ALL, None),
            P(ALL, None),
            P(ALL, None),
            P(None, ALL),
            P(("seq", "dp"), "feat"),
            P(("seq", "dp"), "feat"),
            P("feat", ("seq", "dp")),
        ),
        check_vma=False,
    )
```

```python
import functools

import jax
import jax.numpy as jnp
import numpy as np
from jax import lax
from jax.experimental import pallas as pl
from jax.experimental.pallas import tpu as pltpu
from jax.sharding import PartitionSpec as P

HEADS = 16
FDIM = 16
HV = 128
STATE = 160
LANES = 256
epsilon = 1e-05
MESH = pl.DeviceIdType.MESH
ALL = ("feat", "seq", "dp")
f32 = jnp.float32
bf16 = jnp.bfloat16


def dot(a, b):
    return lax.dot_general(a, b, (((1,), (0,)), ((), ())), preferred_element_type=f32)


def dot_nt(a, b):
    return lax.dot_general(a, b, (((1,), (1,)), ((), ())), preferred_element_type=f32)


def dot_tn(a, b):
    return lax.dot_general(a, b, (((0,), (0,)), ((), ())), preferred_element_type=f32)


def feature_tables(heads):
    pairs = [(i, j) for i in range(FDIM) for j in range(i, FDIM)]
    left = np.zeros((heads, heads * FDIM, LANES), np.float32)
    right = np.zeros((heads, heads * FDIM, LANES), np.float32)
    rows = np.zeros((8, LANES), np.float32)
    for h in range(heads):
        for p, (i, j) in enumerate(pairs):
            left[h, h * FDIM + i, p] = 1.0
            right[h, h * FDIM + j, p] = 1.0
            rows[2, p] = 0.25 / 2.0**0.5 if i == j else 0.25
        for i in range(FDIM):
            p = len(pairs) + i
            left[h, h * FDIM + i, p] = 1.0
            rows[1, p] = 1.0
            rows[2, p] = 0.5
        p = len(pairs) + FDIM
        rows[0, p] = rows[1, p] = rows[2, p] = 1.0
    return jnp.asarray(left, bf16), jnp.asarray(right, bf16), jnp.asarray(rows)


def both_sides(entries, h, left_ref, right_ref, rows_ref):
    one = dot(entries, left_ref[h]) + rows_ref[0:1, :]
    two = dot(entries, right_ref[h]) + rows_ref[1:2, :]
    return one, two * rows_ref[2:3, :]


def features(entries, h, left_ref, right_ref, rows_ref):
    one, two = both_sides(entries, h, left_ref, right_ref, rows_ref)
    return one * two


def pull_features(grad, entries, h, left_ref, right_ref, rows_ref):
    one, two = both_sides(entries, h, left_ref, right_ref, rows_ref)
    scaled = rows_ref[2:3, :]
    return dot_nt((grad * two).astype(bf16), left_ref[h]) + dot_nt(
        (grad * one * scaled).astype(bf16), right_ref[h]
    )


def only_head(entries, h):
    lane = lax.broadcasted_iota(jnp.int32, entries.shape, 1)
    keep = (lane >= h * FDIM) & (lane < (h + 1) * FDIM)
    return jnp.where(keep, entries, jnp.zeros_like(entries))


def padded_state(state):
    return jnp.concatenate([state, jnp.zeros((LANES - STATE, state.shape[1]), state.dtype)], 0)


def allowed_of(segc, segr):
    block = segc.shape[0]
    row = lax.broadcasted_iota(jnp.int32, (block, block), 0)
    col = lax.broadcasted_iota(jnp.int32, (block, block), 1)
    return (row >= col) & (segc == segr)


def forward_kernel(
    count,
    heads,
    qkv_ref,
    segc_ref,
    segr_ref,
    left_ref,
    right_ref,
    rows_ref,
    cot_ref,
    att_ref,
    rden_ref,
    carry_ref,
    csum_ref,
    cots_ref,
    send_state,
    send_sum,
    part,
    send_sem,
    recv_sem,
    f_send,
    f_recv,
    local_sem,
):
    place, f = lax.axis_index("seq"), lax.axis_index("feat")
    groups, block = qkv_ref.shape[0], qkv_ref.shape[1]
    width = heads * FDIM
    tables = (left_ref, right_ref, rows_ref)

    def hop(g):
        target = {"seq": lax.rem(place + 1, count)}
        return [
            pltpu.make_async_remote_copy(
                src_ref=src.at[g],
                dst_ref=dst.at[g],
                send_sem=send_sem.at[i, g],
                recv_sem=recv_sem.at[i, g],
                device_id=target,
                device_id_type=MESH,
            )
            for i, (src, dst) in enumerate(((send_state, carry_ref), (send_sum, csum_ref)))
        ]

    def send(g):
        for copy in hop(g):
            copy.start()

    chain = [lax.rem(place + 1, count), lax.rem(place + count - 1, count)]
    greet([{"seq": c} for c in chain] + square_targets(f))
    stay = pltpu.make_async_copy(cot_ref, cots_ref.at[f], local_sem.at[0])
    stay.start()
    cots = [
        push(cot_ref, cots_ref.at[f], f_send.at[i], f_recv.at[i], {"feat": p})
        for i, p in enumerate(peers(f))
    ]
    for c in cots:
        c.start()

    @pl.when(place == 0)
    def _():
        carry_ref[...] = jnp.zeros_like(carry_ref)
        csum_ref[...] = jnp.full_like(csum_ref, -1.0)

    def summarize(g, none):
        segc, segr = segc_ref[g], segr_ref[g]
        tail = segr[:, block - 1 : block]
        at_tail = (segc == tail).astype(f32)
        send_sum[g, heads : heads + 1, :] = jnp.broadcast_to(tail, (1, LANES))
        for h in range(heads):
            key = qkv_ref[g, :, width : 2 * width]
            value = qkv_ref[g, :, 2 * width + h * HV : 2 * width + (h + 1) * HV]
            phi = (features(key, h, *tables) * at_tail).astype(bf16)
            send_state[g, h] = dot_tn(phi, value)[:STATE].astype(bf16)
            ones = jnp.ones((8, block), bf16)
            send_sum[g, h : h + 1, :] = dot(ones, phi)[0:1]

        @pl.when(place == 0)
        def _():
            send(g)

        return none

    lax.fori_loop(0, groups, summarize, 0)

    def attend(g, none):
        segc, segr = segc_ref[g], segr_ref[g]
        allowed = allowed_of(segc, segr)
        for h in range(heads):
            query = only_head(qkv_ref[g, :, 0:width], h)
            key = qkv_ref[g, :, width : 2 * width]
            value = qkv_ref[g, :, 2 * width + h * HV : 2 * width + (h + 1) * HV]
            c = dot_nt(query, key)
            kernel = jnp.where(allowed, 1.0 + c * (0.25 + c * 0.03125), 0.0).astype(bf16)
            wide = jnp.concatenate([value, jnp.ones_like(value)], axis=1)
            part[h] = dot(kernel, wide)

        @pl.when(place > 0)
        def _():
            for copy in hop(g):
                copy.wait_recv()

        mark = csum_ref[g, heads : heads + 1, 0:1]
        head, tail = segr[:, 0:1], segr[:, block - 1 : block]
        whole = ((head == tail) & (head == mark)).astype(f32)

        @pl.when((place > 0) & (place < count - 1))
        def _():
            for h in range(heads):
                send_state[g, h] = (
                    send_state[g, h].astype(f32) + whole * carry_ref[g, h].astype(f32)
                ).astype(bf16)
                send_sum[g, h : h + 1, :] = (
                    send_sum[g, h : h + 1, :] + whole * csum_ref[g, h : h + 1, :]
                )
            send(g)

        carried = (segc == mark).astype(f32)
        for h in range(heads):
            phi = features(qkv_ref[g, :, 0:width], h, *tables) * carried
            state = padded_state(carry_ref[g, h])
            both = part[h]
            numer = both[:, :HV] + dot(phi.astype(bf16), state)
            denom = both[:, HV:] + jnp.sum(
                phi * csum_ref[g, h : h + 1, :], axis=1, keepdims=True
            )
            inverse = 1.0 / denom
            att_ref[g, :, h * HV : (h + 1) * HV] = (numer * inverse).astype(bf16)
            rden_ref[g, :, h * HV : (h + 1) * HV] = inverse
        return none

    lax.fori_loop(0, groups, attend, 0)

    @pl.when(place < count - 1)
    def _():
        def finish(g, none):
            for copy in hop(g):
                copy.wait_send()
            return none

        lax.fori_loop(0, groups, finish, 0)

    for c in cots:
        c.wait_recv()
    for c in cots:
        c.wait_send()
    stay.wait()


def backward_kernel(
    count,
    heads,
    qkv_ref,
    segc_ref,
    segr_ref,
    left_ref,
    right_ref,
    rows_ref,
    att_ref,
    rden_ref,
    carry_ref,
    csum_ref,
    ga_ref,
    down_ref,
    res_ref,
    out_ref,
    final_ref,
    gn,
    send_state,
    send_sum,
    recv_state,
    recv_sum,
    dkey,
    dvalue,
    downs,
    send_sem,
    recv_sem,
    f_send,
    f_recv,
    local_sem,
):
    place, f = lax.axis_index("seq"), lax.axis_index("feat")
    groups, block = qkv_ref.shape[0], qkv_ref.shape[1]
    width = heads * FDIM
    tables = (left_ref, right_ref, rows_ref)

    def hop(g):
        target = {"seq": lax.rem(place + count - 1, count)}
        return [
            pltpu.make_async_remote_copy(
                src_ref=src.at[g],
                dst_ref=dst.at[g],
                send_sem=send_sem.at[i, g],
                recv_sem=recv_sem.at[i, g],
                device_id=target,
                device_id_type=MESH,
            )
            for i, (src, dst) in enumerate(((send_state, recv_state), (send_sum, recv_sum)))
        ]

    def send(g):
        for copy in hop(g):
            copy.start()

    chain = [lax.rem(place + 1, count), lax.rem(place + count - 1, count)]
    greet([{"seq": c} for c in chain] + square_targets(f))
    stay = pltpu.make_async_copy(down_ref.at[f], downs.at[3], local_sem.at[0])
    stay.start()
    terms = [
        push(down_ref.at[p], downs.at[i], f_send.at[i], f_recv.at[i], {"feat": p})
        for i, p in enumerate(peers(f))
    ]
    for c in terms:
        c.start()

    @pl.when(place == count - 1)
    def _():
        recv_state[...] = jnp.zeros_like(recv_state)
        recv_sum[...] = jnp.full_like(recv_sum, -1.0)

    def summarize(g, none):
        segc, segr = segc_ref[g], segr_ref[g]
        head = segr[:, 0:1]
        at_head = (segc == head).astype(f32)
        send_sum[g, heads : heads + 1, :] = jnp.broadcast_to(head, (1, LANES))
        for h in range(heads):
            lanes = slice(h * HV, (h + 1) * HV)
            ga = ga_ref[g, :, lanes]
            inverse = rden_ref[g, :, lanes]
            numer = (ga * inverse).astype(bf16)
            dots = jnp.sum(ga * att_ref[g, :, lanes].astype(f32), axis=1, keepdims=True)
            lane = lax.broadcasted_iota(jnp.int32, (block, HV), 1)
            denom = jnp.where(lane == 0, -dots * inverse, 0.0).astype(bf16)
            gn[g, h, :, :HV] = numer
            gn[g, h, :, HV:] = denom
            phi = (features(qkv_ref[g, :, 0:width], h, *tables) * at_head).astype(bf16)
            send_state[g, h] = dot_tn(phi, numer)[:STATE].astype(bf16)
            send_sum[g, h : h + 1, :] = dot_tn(denom, phi)[0:1]

        @pl.when(place == count - 1)
        def _():
            send(g)

        return none

    lax.fori_loop(0, groups, summarize, 0)

    def pull(g, none):
        segc, segr = segc_ref[g], segr_ref[g]
        allowed = allowed_of(segc, segr)
        query_all = qkv_ref[g, :, 0:width]
        key_all = qkv_ref[g, :, width : 2 * width]
        carried = (segc == csum_ref[g, heads : heads + 1, 0:1]).astype(f32)
        dquery = jnp.zeros((block, width), f32)
        dkey[...] = jnp.zeros_like(dkey)
        for h in range(heads):
            query, key = only_head(query_all, h), only_head(key_all, h)
            value = qkv_ref[g, :, 2 * width + h * HV : 2 * width + (h + 1) * HV]
            wide = jnp.concatenate([value, jnp.ones_like(value)], axis=1)
            both = gn[g, h]
            c = dot_nt(query, key_all)
            kernel = jnp.where(allowed, 1.0 + c * (0.25 + c * 0.03125), 0.0).astype(bf16)
            grad = jnp.where(allowed, dot_nt(both, wide), 0.0)
            grad_c = (grad * (0.25 + c * 0.0625)).astype(bf16)
            dvalue[h] = dot_tn(kernel, both[:, :HV])
            dkey[...] += dot_tn(grad_c, query)
            dquery = dquery + dot(grad_c, key)
            state = padded_state(carry_ref[g, h])
            gphi = dot_nt(both[:, :HV], state) + both[:, HV : HV + 1].astype(f32) * csum_ref[
                g, h : h + 1, :
            ]
            dquery = dquery + pull_features(gphi * carried, query_all, h, *tables)
        out_ref[g, :, 0:width] = dquery.astype(bf16)

        @pl.when(place < count - 1)
        def _():
            for copy in hop(g):
                copy.wait_recv()

        mark = recv_sum[g, heads : heads + 1, 0:1]
        head, tail = segr[:, 0:1], segr[:, block - 1 : block]
        whole = ((head == tail) & (head == mark)).astype(f32)

        @pl.when((place > 0) & (place < count - 1))
        def _():
            for h in range(heads):
                send_state[g, h] = (
                    send_state[g, h].astype(f32) + whole * recv_state[g, h].astype(f32)
                ).astype(bf16)
                send_sum[g, h : h + 1, :] = (
                    send_sum[g, h : h + 1, :] + whole * recv_sum[g, h : h + 1, :]
                )
            send(g)

        later = (segc == mark).astype(f32)
        total = dkey[...]
        for h in range(heads):
            value = qkv_ref[g, :, 2 * width + h * HV : 2 * width + (h + 1) * HV]
            state = padded_state(recv_state[g, h])
            phi = (features(key_all, h, *tables) * later).astype(bf16)
            dv = dvalue[h] + dot(phi, state)
            out_ref[g, :, 2 * width + h * HV : 2 * width + (h + 1) * HV] = dv.astype(bf16)
            gphi = (dot_nt(value, state) + recv_sum[g, h : h + 1, :]) * later
            total = total + pull_features(gphi, key_all, h, *tables)
        out_ref[g, :, width : 2 * width] = total.astype(bf16)
        return none

    lax.fori_loop(0, groups, pull, 0)

    @pl.when(place > 0)
    def _():
        def finish(g, none):
            for copy in hop(g):
                copy.wait_send()
            return none

        lax.fori_loop(0, groups, finish, 0)

    stay.wait()
    for c in terms:
        c.wait_recv()

    def add_up(i, none):
        rows = pl.ds(pl.multiple_of(i * 16, 16), 16)
        total = res_ref[rows, :]
        for k in range(4):
            total = total + downs[k, rows, :].astype(f32)
        final_ref[rows, :] = total.astype(bf16)
        return none

    lax.fori_loop(0, block // 16, add_up, 0)
    for c in terms:
        c.wait_send()


def whole_vmem(count):
    return [pl.BlockSpec(memory_space=pltpu.VMEM)] * count


def attention_forward(qkv, segc, segr, tables, cot_own, heads):
    groups, block, _ = qkv.shape
    count = lax.axis_size("seq")
    states = (groups, heads, STATE, HV)
    sums = (groups, 8, LANES)
    return pl.pallas_call(
        functools.partial(forward_kernel, count, heads),
        out_shape=(
            jax.ShapeDtypeStruct((groups, block, heads * HV), bf16),
            jax.ShapeDtypeStruct((groups, block, heads * HV), f32),
            jax.ShapeDtypeStruct(states, bf16),
            jax.ShapeDtypeStruct(sums, f32),
            jax.ShapeDtypeStruct((groups,) + cot_own.shape, bf16),
        ),
        in_specs=whole_vmem(6) + in_place(1),
        out_specs=tuple(whole_vmem(4) + in_place(1)),
        scratch_shapes=[
            pltpu.VMEM(states, bf16),
            pltpu.VMEM(sums, f32),
            pltpu.VMEM((heads, block, 2 * HV), f32),
            pltpu.SemaphoreType.DMA((2, groups)),
            pltpu.SemaphoreType.DMA((2, groups)),
            pltpu.SemaphoreType.DMA((3,)),
            pltpu.SemaphoreType.DMA((3,)),
            pltpu.SemaphoreType.DMA((1,)),
        ],
        compiler_params=pltpu.CompilerParams(
            collective_id=0, has_side_effects=True, vmem_limit_bytes=40 << 20
        ),
        cost_estimate=pl.CostEstimate(flops=0, bytes_accessed=1 << 20, transcendentals=0),
        name="attention_forward",
    )(qkv, segc, segr, *tables, cot_own)


def attention_backward(
    qkv, segc, segr, tables, att, rden, carry, csum, ga, down, residual, heads
):
    groups, block, wide = qkv.shape
    count = lax.axis_size("seq")
    states = (groups, heads, STATE, HV)
    sums = (groups, 8, LANES)
    return pl.pallas_call(
        functools.partial(backward_kernel, count, heads),
        out_shape=(
            jax.ShapeDtypeStruct((groups, block, wide), bf16),
            jax.ShapeDtypeStruct(residual.shape, bf16),
        ),
        in_specs=whole_vmem(11) + in_place(1) + whole_vmem(1),
        out_specs=tuple(whole_vmem(2)),
        scratch_shapes=[
            pltpu.VMEM((groups, heads, block, 2 * HV), bf16),
            pltpu.VMEM(states, bf16),
            pltpu.VMEM(sums, f32),
            pltpu.VMEM(states, bf16),
            pltpu.VMEM(sums, f32),
            pltpu.VMEM((block, heads * FDIM), f32),
            pltpu.VMEM((heads, block, HV), f32),
            pltpu.VMEM((groups,) + residual.shape, bf16),
            pltpu.SemaphoreType.DMA((2, groups)),
            pltpu.SemaphoreType.DMA((2, groups)),
            pltpu.SemaphoreType.DMA((3,)),
            pltpu.SemaphoreType.DMA((3,)),
            pltpu.SemaphoreType.DMA((1,)),
        ],
        compiler_params=pltpu.CompilerParams(
            collective_id=1, has_side_effects=True, vmem_limit_bytes=48 << 20
        ),
        cost_estimate=pl.CostEstimate(flops=0, bytes_accessed=1 << 20, transcendentals=0),
        name="attention_backward",
    )(qkv, segc, segr, *tables, att, rden, carry, csum, ga, down, residual)


def peers(f):
    return 2 * (f // 2) + 1 - f % 2, (f + 2) % 4, 3 - f


def greet(targets):
    barrier = pltpu.get_barrier_semaphore()
    for target in targets:
        pl.semaphore_signal(barrier, inc=1, device_id=target, device_id_type=MESH)
    pl.semaphore_wait(barrier, len(targets))


def push(src, dst, send_sem, recv_sem, target):
    return pltpu.make_async_remote_copy(
        src_ref=src,
        dst_ref=dst,
        send_sem=send_sem,
        recv_sem=recv_sem,
        device_id=target,
        device_id_type=MESH,
    )


def square_targets(f):
    return [{"feat": p} for p in peers(f)]


class SquareGather:
    def __init__(self, slots, f, send_sem, recv_sem):
        side, above, across = peers(f)
        half = slots.shape[1] // 2
        first, second = pl.ds(0, half), pl.ds(half, half)

        def copy(i, slot, rows, to):
            ref = slots.at[slot, rows]
            return push(ref, ref, send_sem.at[i], recv_sem.at[i], {"feat": to})

        self.direct = [
            copy(0, f, first, side),
            copy(1, f, second, above),
            copy(2, f, second, side),
            copy(3, f, first, above),
        ]
        self.forward = [copy(4, side, first, above), copy(5, above, second, side)]

    def start(self):
        for c in self.direct:
            c.start()

    def relay(self):
        self.direct[0].wait_recv()
        self.forward[0].start()
        self.direct[1].wait_recv()
        self.forward[1].start()

    def finish(self):
        for c in (self.direct[2], self.direct[3], self.forward[0], self.forward[1]):
            c.wait_recv()
        for c in self.direct + self.forward:
            c.wait_send()


class SquareSum:
    def __init__(self, part, land, f, send_sem, recv_sem):
        self.side, self.above, self.across = peers(f)
        self.f, self.part, self.land = f, part, land
        self.half = part.shape[1] // 2
        first, second = pl.ds(0, self.half), pl.ds(self.half, self.half)

        def copy(i, slot, rows, to):
            return push(
                part.at[slot, rows], land.at[i], send_sem.at[i], recv_sem.at[i], {"feat": to}
            )

        self.cross = [copy(0, self.across, first, self.side), copy(1, self.across, second, self.above)]
        self.near = [copy(2, self.side, first, self.side), copy(3, self.above, second, self.above)]
        self.late = [copy(4, self.above, first, self.above), copy(5, self.side, second, self.side)]

    def start_cross(self):
        for c in self.cross:
            c.start()

    def add_rows(self, slot, base, landed):
        step = 32

        def one(i, none):
            rows = pl.ds(pl.multiple_of(base + i * step, step), step)
            came = self.land[landed, pl.ds(pl.multiple_of(i * step, step), step), :]
            self.part[slot, rows, :] = (
                self.part[slot, rows, :].astype(f32) + came.astype(f32)
            ).astype(bf16)
            return none

        lax.fori_loop(0, self.half // step, one, 0)

    def start_near(self):
        for c in self.near:
            c.start()

    def relay(self):
        self.cross[0].wait_recv()
        self.add_rows(self.above, 0, 0)
        self.late[0].start()
        self.cross[1].wait_recv()
        self.add_rows(self.side, self.half, 1)
        self.late[1].start()

    def arrive(self):
        for c in self.near + self.late:
            c.wait_recv()

    def total(self, half, rows):
        base = half * self.half
        own = self.part[self.f, pl.ds(pl.multiple_of(base + rows.start, 16), rows.size), :]
        near = self.land[2 + half, rows, :]
        late = self.land[4 + half, rows, :]
        return own.astype(f32) + near.astype(f32) + late.astype(f32)

    def finish(self):
        for c in self.cross + self.near + self.late:
            c.wait_send()


def opening_kernel(seqs, dps, tok_ref, pack_ref, gain_ref, x_ref, w_ref, g_ref, *sems):
    x_send, x_recv, a_send, a_recv, z_send, z_recv, d_send, d_recv, local_sem = sems
    f, s, d = lax.axis_index("feat"), lax.axis_index("seq"), lax.axis_index("dp")
    near = peers(f)
    up, down = lax.rem(s + 1, seqs), lax.rem(s + seqs - 1, seqs)
    others = [lax.rem(d + k, dps) for k in range(1, dps)]
    own = [
        pltpu.make_async_copy(tok_ref, x_ref.at[f], local_sem.at[0]),
        pltpu.make_async_copy(pack_ref.at[f], w_ref.at[f, s, d], local_sem.at[1]),
        pltpu.make_async_copy(gain_ref, g_ref.at[f, s, d], local_sem.at[2]),
    ]
    for c in own:
        c.start()
    greet(
        square_targets(f)
        + [{"seq": up}, {"seq": down}]
        + [{"dp": o} for o in others]
    )

    shares = []
    for i, p in enumerate(near):
        shares.append(
            push(pack_ref.at[p], w_ref.at[f, s, d], a_send.at[0, i], a_recv.at[0, i], {"feat": p})
        )
        shares.append(
            push(gain_ref, g_ref.at[f, s, d], a_send.at[1, i], a_recv.at[1, i], {"feat": p})
        )
    for c in shares:
        c.start()
    for c in own:
        c.wait()
    gather = SquareGather(x_ref, f, x_send, x_recv)
    gather.start()
    for c in shares:
        c.wait_recv()

    def column(src, i, direction, to):
        return [
            push(
                ref.at[:, src, d],
                ref.at[:, src, d],
                z_send.at[j, direction, i],
                z_recv.at[j, direction, i],
                {"seq": to},
            )
            for j, ref in enumerate((w_ref, g_ref))
        ]

    def sibling(src, i):
        return [
            push(
                ref.at[:, src, d],
                ref.at[:, src, d],
                d_send.at[j, k, i],
                d_recv.at[j, k, i],
                {"dp": o},
            )
            for j, ref in enumerate((w_ref, g_ref))
            for k, o in enumerate(others)
        ]

    def start_all(copies):
        for c in copies:
            c.start()

    def both_ways(i):
        @pl.when((s >= i) & (s < seqs - 1))
        def _():
            start_all(column(lax.rem(s + seqs - i, seqs), i, 0, up))

        @pl.when((s + i < seqs) & (s > 0))
        def _():
            start_all(column(lax.rem(s + i, seqs), i, 1, down))

    both_ways(0)
    start_all(sibling(s, 0))
    for i in range(1, seqs):
        @pl.when(s >= i)
        def _():
            for c in column(lax.rem(s + seqs - i, seqs), i - 1, 0, up):
                c.wait_recv()
            start_all(sibling(lax.rem(s + seqs - i, seqs), i))

        @pl.when(s + i < seqs)
        def _():
            for c in column(lax.rem(s + i, seqs), i - 1, 1, down):
                c.wait_recv()
            start_all(sibling(lax.rem(s + i, seqs), seqs - 1 + i))

        if i < seqs - 1:
            both_ways(i)
        if i == 1:
            gather.relay()

    def close(copies):
        for c in copies:
            c.wait_recv()
        for c in copies:
            c.wait_send()

    close(sibling(s, 0))
    for i in range(1, seqs):

        @pl.when(s >= i)
        def _():
            close(sibling(lax.rem(s + seqs - i, seqs), i))

        @pl.when(s + i < seqs)
        def _():
            close(sibling(lax.rem(s + i, seqs), seqs - 1 + i))

    for i in range(seqs - 1):

        @pl.when((s >= i) & (s < seqs - 1))
        def _():
            for c in column(lax.rem(s + seqs - i, seqs), i, 0, up):
                c.wait_send()

        @pl.when((s + i < seqs) & (s > 0))
        def _():
            for c in column(lax.rem(s + i, seqs), i, 1, down):
                c.wait_send()

    for c in shares:
        c.wait_send()
    gather.finish()


def in_place(count):
    return [pl.BlockSpec(memory_space=pl.ANY)] * count


def opening(own, pack, gain_tile):
    parts, seqs, dps = (lax.axis_size(a) for a in ALL)
    block, width = own.shape
    _, rows_each, wide = pack.shape
    others = max(dps - 1, 1)
    dma = pltpu.SemaphoreType.DMA
    x_all, w_all, g_all = pl.pallas_call(
        functools.partial(opening_kernel, seqs, dps),
        out_shape=(
            jax.ShapeDtypeStruct((parts, block, width), bf16),
            jax.ShapeDtypeStruct((parts, seqs, dps, rows_each, wide), bf16),
            jax.ShapeDtypeStruct((parts, seqs, dps) + gain_tile.shape, f32),
        ),
        in_specs=in_place(3),
        out_specs=tuple(in_place(3)),
        scratch_shapes=[
            dma((6,)),
            dma((6,)),
            dma((2, 3)),
            dma((2, 3)),
            dma((2, 2, seqs)),
            dma((2, 2, seqs)),
            dma((2, others, 2 * seqs - 1)),
            dma((2, others, 2 * seqs - 1)),
            dma((3,)),
        ],
        compiler_params=pltpu.CompilerParams(collective_id=2, has_side_effects=True),
        cost_estimate=pl.CostEstimate(flops=0, bytes_accessed=1 << 20, transcendentals=0),
        name="opening",
    )(own, pack, gain_tile)
    gains = g_all[..., :2, :rows_each].transpose(3, 0, 1, 2, 4).reshape(2, width)
    return x_all, w_all.reshape(width, wide), gains


def inverse_rms(values):
    return lax.rsqrt(jnp.mean(values * values, axis=-1, keepdims=True) + epsilon)


def norm_back(grad, unit, inverse, gain):
    scaled = grad * gain
    return (scaled - unit * jnp.mean(scaled * unit, axis=-1, keepdims=True)) * inverse


def product_tiles(part, slot, pairs, tile):
    def one(i, none):
        cols = pl.ds(pl.multiple_of(i * tile, tile), tile)
        total = None
        for rows, weights in pairs:
            term = dot_nt(rows[slot], weights[cols, :])
            total = term if total is None else total + term
        part[slot, :, cols] = total.astype(bf16)
        return none

    lax.fori_loop(0, part.shape[2] // tile, one, 0)


def summed_products(part, land, f, pairs, send_sem, recv_sem):
    side, above, across = peers(f)
    ring = SquareSum(part, land, f, send_sem, recv_sem)
    product_tiles(part, across, pairs, 512)
    ring.start_cross()
    product_tiles(part, side, pairs, 512)
    product_tiles(part, above, pairs, 512)
    ring.start_near()
    product_tiles(part, f, pairs, 512)
    ring.relay()
    ring.arrive()
    return ring


def by_rows(ring, body, step=16):
    for half in (0, 1):

        def one(i, none):
            start = pl.multiple_of(i * step, step)
            rows = pl.ds(pl.multiple_of(half * ring.half + i * step, step), step)
            body(rows, ring.total(half, pl.ds(start, step)))
            return none

        lax.fori_loop(0, ring.half // step, one, 0)


def branch_kernel(
    att_ref, w_ref, tok_ref, gain_ref, rows_ref, res_ref, part, land, s_send, s_recv, g_send, g_recv
):
    f = lax.axis_index("feat")
    greet(square_targets(f))
    ring = summed_products(part, land, f, [(att_ref, w_ref)], s_send, s_recv)

    def finish_rows(rows, total):
        residual = tok_ref[rows, :].astype(f32) + total
        res_ref[rows, :] = residual
        rows_ref[f, rows, :] = (residual * inverse_rms(residual) * gain_ref[...]).astype(bf16)

    by_rows(ring, finish_rows)
    gather = SquareGather(rows_ref, f, g_send, g_recv)
    gather.start()
    ring.finish()
    gather.relay()
    gather.finish()


def square_scratch(parts, block, width):
    dma = pltpu.SemaphoreType.DMA
    return [
        pltpu.VMEM((parts, block, width), bf16),
        pltpu.VMEM((6, block // 2, width), bf16),
        dma((6,)),
        dma((6,)),
    ]


def branch_step(att, out_w, own, gain_two):
    parts, block, _ = att.shape
    width = own.shape[1]
    dma = pltpu.SemaphoreType.DMA
    return pl.pallas_call(
        branch_kernel,
        out_shape=(
            jax.ShapeDtypeStruct((parts, block, width), bf16),
            jax.ShapeDtypeStruct((block, width), f32),
        ),
        in_specs=whole_vmem(4),
        out_specs=tuple(whole_vmem(2)),
        scratch_shapes=square_scratch(parts, block, width) + [dma((6,)), dma((6,))],
        compiler_params=pltpu.CompilerParams(
            collective_id=3, has_side_effects=True, vmem_limit_bytes=48 << 20
        ),
        cost_estimate=pl.CostEstimate(flops=0, bytes_accessed=1 << 20, transcendentals=0),
        name="branch_step",
    )(att, out_w, own, gain_two)


def rows_back_kernel(
    gg_ref,
    gu_ref,
    wg_ref,
    wu_ref,
    res_ref,
    cot_ref,
    gain_ref,
    all_ref,
    gres_ref,
    gsum_ref,
    part,
    land,
    s_send,
    s_recv,
    g_send,
    g_recv,
):
    f = lax.axis_index("feat")
    greet(square_targets(f))
    pairs = [(gg_ref, wg_ref), (gu_ref, wu_ref)]
    ring = summed_products(part, land, f, pairs, s_send, s_recv)
    gsum_ref[...] = jnp.zeros_like(gsum_ref)

    def finish_rows(rows, grad):
        residual = res_ref[rows, :]
        inverse = inverse_rms(residual)
        unit = residual * inverse
        gsum_ref[...] += jnp.sum(grad * unit, axis=0, keepdims=True)
        grad_res = cot_ref[rows, :].astype(f32) + norm_back(grad, unit, inverse, gain_ref[...])
        gres_ref[rows, :] = grad_res
        all_ref[f, rows, :] = grad_res.astype(bf16)

    by_rows(ring, finish_rows)
    gather = SquareGather(all_ref, f, g_send, g_recv)
    gather.start()
    ring.finish()
    gather.relay()
    gather.finish()


def rows_back(grad_gate, grad_up, gate_w, up_w, residual, cot_own, gain_two):
    parts, block, _ = grad_gate.shape
    width = residual.shape[1]
    dma = pltpu.SemaphoreType.DMA
    return pl.pallas_call(
        rows_back_kernel,
        out_shape=(
            jax.ShapeDtypeStruct((parts, block, width), bf16),
            jax.ShapeDtypeStruct((block, width), f32),
            jax.ShapeDtypeStruct((1, width), f32),
        ),
        in_specs=whole_vmem(7),
        out_specs=tuple(whole_vmem(3)),
        scratch_shapes=square_scratch(parts, block, width) + [dma((6,)), dma((6,))],
        compiler_params=pltpu.CompilerParams(
            collective_id=4, has_side_effects=True, vmem_limit_bytes=56 << 20
        ),
        cost_estimate=pl.CostEstimate(flops=0, bytes_accessed=1 << 20, transcendentals=0),
        name="rows_back",
    )(grad_gate, grad_up, gate_w, up_w, residual, cot_own, gain_two)


def closing_kernel(
    seqs,
    dps,
    dqkv_ref,
    w_ref,
    tok_ref,
    gres_ref,
    gain_ref,
    gsum_two_ref,
    x_ref,
    tile_ref,
    part,
    land,
    s_send,
    s_recv,
    gsum,
    cut,
    came,
    mid,
    tail,
    c_send,
    c_recv,
    d_send,
    d_recv,
):
    f, s, d = lax.axis_index("feat"), lax.axis_index("seq"), lax.axis_index("dp")
    parts = 4
    others = [lax.rem(d + k, dps) for k in range(1, dps)]
    circle = [
        (lax.rem(f + i, parts), lax.rem(s + j, seqs))
        for i in range(parts)
        for j in range(seqs)
        if i or j
    ]
    greet(
        [{"feat": a, "seq": b} for a, b in circle] + [{"dp": o} for o in others]
    )
    ring = summed_products(part, land, f, [(dqkv_ref, w_ref)], s_send, s_recv)
    gsum[...] = jnp.zeros_like(gsum)

    def finish_rows(rows, grad):
        values = tok_ref[rows, :].astype(f32)
        inverse = inverse_rms(values)
        unit = values * inverse
        gsum[...] += jnp.sum(grad * unit, axis=0, keepdims=True)
        x_ref[rows, :] = gres_ref[rows, :] + norm_back(grad, unit, inverse, gain_ref[...])

    by_rows(ring, finish_rows)
    ring.finish()

    lanes = gsum.shape[1] // (parts * seqs)
    cut[...] = jnp.zeros_like(cut)
    for k in range(parts * seqs):
        cut[k, 0:1, :] = gsum[:, k * lanes : (k + 1) * lanes]
        cut[k, 1:2, :] = gsum_two_ref[:, k * lanes : (k + 1) * lanes]
    place = f * seqs + s
    sends = []
    for i, (a, b) in enumerate(circle):
        sends.append(
            push(
                cut.at[a * seqs + b],
                came.at[i],
                c_send.at[i],
                c_recv.at[i],
                {"feat": a, "seq": b},
            )
        )
    for c in sends:
        c.start()
    total = cut[place]
    for c in sends:
        c.wait_recv()
    for i in range(len(circle)):
        total = total + came[i]
    mid[...] = total
    last = [
        push(mid, tail.at[k], d_send.at[k], d_recv.at[k], {"dp": o})
        for k, o in enumerate(others)
    ]
    for c in last:
        c.start()
    for c in last:
        c.wait_recv()
    for k in range(len(others)):
        total = total + tail[k]
    tile_ref[...] = total
    for c in sends + last:
        c.wait_send()


def closing(dqkv, qkv_w, own, grad_residual, gain_one, gain_two_sum):
    parts, seqs, dps = (lax.axis_size(a) for a in ALL)
    block, width = own.shape
    others = max(dps - 1, 1)
    lanes = width // (parts * seqs)
    circle = parts * seqs - 1
    dma = pltpu.SemaphoreType.DMA
    return pl.pallas_call(
        functools.partial(closing_kernel, seqs, dps),
        out_shape=(
            jax.ShapeDtypeStruct((block, width), f32),
            jax.ShapeDtypeStruct((8, lanes), f32),
        ),
        in_specs=whole_vmem(6),
        out_specs=tuple(whole_vmem(2)),
        scratch_shapes=square_scratch(parts, block, width)
        + [
            pltpu.VMEM((1, width), f32),
            pltpu.VMEM((parts * seqs, 8, lanes), f32),
            pltpu.VMEM((circle, 8, lanes), f32),
            pltpu.VMEM((8, lanes), f32),
            pltpu.VMEM((others, 8, lanes), f32),
            dma((circle,)),
            dma((circle,)),
            dma((others,)),
            dma((others,)),
        ],
        compiler_params=pltpu.CompilerParams(
            collective_id=5, has_side_effects=True, vmem_limit_bytes=48 << 20
        ),
        cost_estimate=pl.CostEstimate(flops=0, bytes_accessed=1 << 20, transcendentals=0),
        name="closing",
    )(dqkv, qkv_w, own, grad_residual, gain_one, gain_two_sum)


def local(
    tokens,
    segments,
    norm1_gain,
    norm2_gain,
    w_query,
    w_key,
    w_value,
    w_out,
    w_gate,
    w_up,
    w_down,
    cotangent,
):
    parts = lax.axis_size("feat")
    heads = HEADS // parts
    block, width = tokens.shape[2], tokens.shape[3]
    rows_total = parts * block
    rows_each = w_query.shape[0]
    own = tokens.reshape(block, width)
    cot_own = cotangent.reshape(block, width)

    def by_share(w, per):
        return w.reshape(rows_each, parts, heads * per).transpose(1, 0, 2)

    pack = jnp.concatenate(
        [by_share(w_query, FDIM), by_share(w_key, FDIM), by_share(w_value, HV), by_share(w_out.T, HV)],
        axis=2,
    )
    pack_width = pack.shape[2]
    gain_tile = jnp.zeros((8, HV), f32)
    gain_tile = gain_tile.at[0, :rows_each].set(norm1_gain.astype(f32))
    gain_tile = gain_tile.at[1, :rows_each].set(norm2_gain.astype(f32))
    gate_w = lax.all_gather(w_gate, ("seq", "dp"), axis=0, tiled=True)
    up_w = lax.all_gather(w_up, ("seq", "dp"), axis=0, tiled=True)
    x_all, attn_w, gains = opening(own, pack, gain_tile)
    qkv_width = pack_width - heads * HV
    qkv_w, out_w = attn_w[:, :qkv_width], attn_w[:, qkv_width:]
    gain_one, gain_two = gains[0:1], gains[1:2]

    x_wide = x_all.astype(f32).reshape(rows_total, width)
    normed = (x_wide * inverse_rms(x_wide) * gain_one).astype(bf16)
    qkv = dot(normed, qkv_w).astype(bf16).reshape(parts, block, qkv_width)
    qkv, w_down = lax.optimization_barrier((qkv, w_down))
    down_w = lax.all_gather(w_down.T, ("seq", "dp"), axis=0, tiled=True)
    segment = segments.reshape(parts, block).astype(f32)
    segc, segr = segment[:, :, None], segment[:, None, :]
    tables = feature_tables(heads)
    att, rden, carry, csum, cot_all = attention_forward(qkv, segc, segr, tables, cot_own, heads)
    cot_all = cot_all.reshape(rows_total, width)
    rows_all, residual = branch_step(att, out_w, own, gain_two)
    rows_all = rows_all.reshape(rows_total, width)

    gate_out = dot(rows_all, gate_w)
    up_out = dot(rows_all, up_w)
    sig = jax.nn.sigmoid(gate_out)
    silu = gate_out * sig
    mixed = (silu * up_out).astype(bf16)
    mixed, cot_late = lax.optimization_barrier((mixed, cot_all))
    down = dot_nt(mixed, down_w).astype(bf16).reshape(parts, block, width)
    grad_mixed = dot(cot_late, down_w)
    grad_gate = (grad_mixed * up_out * sig * (1.0 + gate_out * (1.0 - sig))).astype(bf16)
    grad_up = (grad_mixed * silu).astype(bf16)

    def summed(term):
        return lax.psum_scatter(term, ("seq", "dp"), scatter_dimension=0, tiled=True)

    down_term = dot_tn(cot_all, mixed).astype(bf16)
    gate_term = dot_tn(rows_all, grad_gate).astype(bf16)
    up_term = dot_tn(rows_all, grad_up).astype(bf16)
    grad_gate, grad_up, gate_term, up_term = lax.optimization_barrier(
        (grad_gate, grad_up, gate_term, up_term)
    )
    down_sum, gate_sum, up_sum = summed(down_term), summed(gate_term), summed(up_term)

    by_device = (parts, block, -1)
    branch_all, grad_residual, gain_two_sum = rows_back(
        grad_gate.reshape(by_device),
        grad_up.reshape(by_device),
        gate_w,
        up_w,
        residual,
        cot_own,
        gain_two,
    )
    branch_all = branch_all.reshape(rows_total, width)
    ga = dot(branch_all, out_w).reshape(parts, block, heads * HV)
    dqkv, output = attention_backward(
        qkv, segc, segr, tables, att, rden, carry, csum, ga, down, residual, heads
    )
    x_grad, gain_grads = closing(dqkv, qkv_w, own, grad_residual, gain_one, gain_two_sum)
    dqkv = dqkv.reshape(rows_total, qkv_width)

    def shared(grads):
        grads = grads.astype(bf16).reshape(parts, -1, rows_each, grads.shape[1])
        grads = grads.transpose(1, 0, 2, 3).reshape(width, -1)
        grads = lax.psum_scatter(grads, ("seq", "dp"), scatter_dimension=0, tiled=True)
        grads = grads.reshape(parts, rows_each, -1)
        return lax.all_to_all(grads, "feat", 0, 0, tiled=True).astype(f32)

    def from_share(grads, first, per):
        piece = grads[:, :, first : first + heads * per]
        return piece.transpose(1, 0, 2).reshape(rows_each, HEADS * per)

    out_term = dot_tn(branch_all, att.reshape(rows_total, heads * HV))
    qkv_term = dot_tn(normed, dqkv)
    out_term, qkv_term, down_sum, gate_sum, up_sum = lax.optimization_barrier(
        (out_term, qkv_term, down_sum, gate_sum, up_sum)
    )
    out_grads, qkv_grads = shared(out_term), shared(qkv_term)
    query_grad = from_share(qkv_grads, 0, FDIM)
    key_grad = from_share(qkv_grads, heads * FDIM, FDIM)
    value_grad = from_share(qkv_grads, 2 * heads * FDIM, HV)
    out_grad = from_share(out_grads, 0, HV).T
    gain_each = gain_grads.shape[1] // lax.axis_size("dp")
    gain_grads = lax.dynamic_slice_in_dim(
        gain_grads, lax.axis_index("dp") * gain_each, gain_each, axis=1
    )
    return (
        output.reshape(tokens.shape),
        x_grad.reshape(tokens.shape),
        gain_grads[0],
        gain_grads[1],
        query_grad,
        key_grad,
        value_grad,
        out_grad,
        gate_sum.astype(f32),
        up_sum.astype(f32),
        down_sum.T.astype(f32),
    )


def solution(mesh):
    placed = (
        P("feat", "dp", "seq", None),
        P(None, "dp", "seq"),
        P(ALL),
        P(ALL),
        P(ALL, None),
        P(ALL, None),
        P(ALL, None),
        P(None, ALL),
        P(("seq", "dp"), "feat"),
        P(("seq", "dp"), "feat"),
        P("feat", ("seq", "dp")),
        P("feat", "dp", "seq", None),
    )
    return jax.shard_map(
        local,
        mesh=mesh,
        in_specs=placed,
        out_specs=(
            P("feat", "dp", "seq", None),
            P("feat", "dp", "seq", None),
            P(ALL),
            P(ALL),
            P(ALL, None),
            P(ALL, None),
            P(ALL, None),
            P(None, ALL),
            P(("seq", "dp"), "feat"),
            P(("seq", "dp"), "feat"),
            P("feat", ("seq", "dp")),
        ),
        check_vma=False,
    )
```

```python
import functools

import jax
import jax.numpy as jnp
import numpy as np
from jax import lax
from jax.experimental import pallas as pl
from jax.experimental.pallas import tpu as pltpu
from jax.sharding import PartitionSpec as P

HEADS = 16
FDIM = 16
HV = 128
STATE = 160
LANES = 256
epsilon = 1e-05
MESH = pl.DeviceIdType.MESH
ALL = ("feat", "seq", "dp")
f32 = jnp.float32
bf16 = jnp.bfloat16


def dot(a, b):
    return lax.dot_general(a, b, (((1,), (0,)), ((), ())), preferred_element_type=f32)


def dot_nt(a, b):
    return lax.dot_general(a, b, (((1,), (1,)), ((), ())), preferred_element_type=f32)


def dot_tn(a, b):
    return lax.dot_general(a, b, (((0,), (0,)), ((), ())), preferred_element_type=f32)


def feature_tables(heads):
    pairs = [(i, j) for i in range(FDIM) for j in range(i, FDIM)]
    left = np.zeros((heads, heads * FDIM, LANES), np.float32)
    right = np.zeros((heads, heads * FDIM, LANES), np.float32)
    rows = np.zeros((8, LANES), np.float32)
    for h in range(heads):
        for p, (i, j) in enumerate(pairs):
            left[h, h * FDIM + i, p] = 1.0
            right[h, h * FDIM + j, p] = 1.0
            rows[2, p] = 0.25 / 2.0**0.5 if i == j else 0.25
        for i in range(FDIM):
            p = len(pairs) + i
            left[h, h * FDIM + i, p] = 1.0
            rows[1, p] = 1.0
            rows[2, p] = 0.5
        p = len(pairs) + FDIM
        rows[0, p] = rows[1, p] = rows[2, p] = 1.0
    return jnp.asarray(left, bf16), jnp.asarray(right, bf16), jnp.asarray(rows)


def both_sides(entries, h, left_ref, right_ref, rows_ref):
    one = dot(entries, left_ref[h]) + rows_ref[0:1, :]
    two = dot(entries, right_ref[h]) + rows_ref[1:2, :]
    return one, two * rows_ref[2:3, :]


def features(entries, h, left_ref, right_ref, rows_ref):
    one, two = both_sides(entries, h, left_ref, right_ref, rows_ref)
    return one * two


def pull_features(grad, entries, h, left_ref, right_ref, rows_ref):
    one, two = both_sides(entries, h, left_ref, right_ref, rows_ref)
    scaled = rows_ref[2:3, :]
    return dot_nt((grad * two).astype(bf16), left_ref[h]) + dot_nt(
        (grad * one * scaled).astype(bf16), right_ref[h]
    )


def only_head(entries, h):
    lane = lax.broadcasted_iota(jnp.int32, entries.shape, 1)
    keep = (lane >= h * FDIM) & (lane < (h + 1) * FDIM)
    return jnp.where(keep, entries, jnp.zeros_like(entries))


def padded_state(state):
    return jnp.concatenate([state, jnp.zeros((LANES - STATE, state.shape[1]), state.dtype)], 0)


def allowed_of(segc, segr):
    block = segc.shape[0]
    row = lax.broadcasted_iota(jnp.int32, (block, block), 0)
    col = lax.broadcasted_iota(jnp.int32, (block, block), 1)
    return (row >= col) & (segc == segr)


def forward_kernel(
    count,
    dps,
    heads,
    qkv_ref,
    segc_ref,
    segr_ref,
    left_ref,
    right_ref,
    rows_ref,
    cot_ref,
    share_ref,
    att_ref,
    rden_ref,
    carry_ref,
    csum_ref,
    cots_ref,
    wout_ref,
    send_state,
    send_sum,
    part,
    send_sem,
    recv_sem,
    f_send,
    f_recv,
    a_send,
    a_recv,
    z_send,
    z_recv,
    d_send,
    d_recv,
    local_sem,
):
    place, f, d = lax.axis_index("seq"), lax.axis_index("feat"), lax.axis_index("dp")
    groups, block = qkv_ref.shape[0], qkv_ref.shape[1]
    width = heads * FDIM
    tables = (left_ref, right_ref, rows_ref)

    def hop(g):
        target = {"seq": lax.rem(place + 1, count)}
        return [
            pltpu.make_async_remote_copy(
                src_ref=src.at[g],
                dst_ref=dst.at[g],
                send_sem=send_sem.at[i, g],
                recv_sem=recv_sem.at[i, g],
                device_id=target,
                device_id_type=MESH,
            )
            for i, (src, dst) in enumerate(((send_state, carry_ref), (send_sum, csum_ref)))
        ]

    def send(g):
        for copy in hop(g):
            copy.start()

    columns = [lax.rem(place + k, count) for k in range(1, count)]
    others = [lax.rem(d + k, dps) for k in range(1, dps)]
    stay = [
        pltpu.make_async_copy(cot_ref, cots_ref.at[f], local_sem.at[0]),
        pltpu.make_async_copy(share_ref.at[f], wout_ref.at[f, place, d], local_sem.at[1]),
    ]
    for c in stay:
        c.start()
    greet(
        square_targets(f) + [{"seq": c} for c in columns] + [{"dp": o} for o in others]
    )
    shares = [
        push(share_ref.at[p], wout_ref.at[f, place, d], a_send.at[i], a_recv.at[i], {"feat": p})
        for i, p in enumerate(peers(f))
    ]
    for c in shares:
        c.start()
    gather = SquareGather(cots_ref, f, f_send, f_recv, cot_ref)

    def to_column(k):
        ref = wout_ref.at[:, place, d]
        return push(ref, ref, z_send.at[k - 1], z_recv.at[k - 1], {"seq": columns[k - 1]})

    def to_sibling(k):
        ref = wout_ref.at[:, lax.rem(place + count - k, count), d]
        return [
            push(ref, ref, d_send.at[o, k], d_recv.at[o, k], {"dp": other})
            for o, other in enumerate(others)
        ]

    @pl.when(place == 0)
    def _():
        carry_ref[...] = jnp.zeros_like(carry_ref)
        csum_ref[...] = jnp.full_like(csum_ref, -1.0)

    def summarize(g, none):
        segc, segr = segc_ref[g], segr_ref[g]
        tail = segr[:, block - 1 : block]
        at_tail = (segc == tail).astype(f32)
        send_sum[g, heads : heads + 1, :] = jnp.broadcast_to(tail, (1, LANES))
        for h in range(heads):
            key = qkv_ref[g, :, width : 2 * width]
            value = qkv_ref[g, :, 2 * width + h * HV : 2 * width + (h + 1) * HV]
            phi = (features(key, h, *tables) * at_tail).astype(bf16)
            send_state[g, h] = dot_tn(phi, value)[:STATE].astype(bf16)
            ones = jnp.ones((8, block), bf16)
            send_sum[g, h : h + 1, :] = dot(ones, phi)[0:1]

        @pl.when(place == 0)
        def _():
            send(g)

        return none

    lax.fori_loop(0, groups, summarize, 0)
    gather.start()
    for c in stay:
        c.wait()
    for c in shares:
        c.wait_recv()
    for k in range(1, count):
        to_column(k).start()
    for c in to_sibling(0):
        c.start()

    def join(g, none):
        for copy in hop(g):
            copy.wait_recv()
        segr = segr_ref[g]
        mark = csum_ref[g, heads : heads + 1, 0:1]
        head, tail = segr[:, 0:1], segr[:, block - 1 : block]
        whole = ((head == tail) & (head == mark)).astype(f32)
        for h in range(heads):
            send_state[g, h] = (
                send_state[g, h].astype(f32) + whole * carry_ref[g, h].astype(f32)
            ).astype(bf16)
            send_sum[g, h : h + 1, :] = (
                send_sum[g, h : h + 1, :] + whole * csum_ref[g, h : h + 1, :]
            )
        send(g)
        return none

    def attend(g, none):
        segc, segr = segc_ref[g], segr_ref[g]
        allowed = allowed_of(segc, segr)
        for h in range(heads):
            query = only_head(qkv_ref[g, :, 0:width], h)
            key = qkv_ref[g, :, width : 2 * width]
            value = qkv_ref[g, :, 2 * width + h * HV : 2 * width + (h + 1) * HV]
            c = dot_nt(query, key)
            kernel = jnp.where(allowed, 1.0 + c * (0.25 + c * 0.03125), 0.0).astype(bf16)
            wide = jnp.concatenate([value, jnp.ones_like(value)], axis=1)
            part[g, h] = dot(kernel, wide)

        @pl.when((place > 0) & (place < count - 1) & (g == place - 1))
        def _():
            lax.fori_loop(0, groups, join, 0)

        return none

    lax.fori_loop(0, groups, attend, 0)
    for k in range(1, count):
        to_column(k).wait_recv()
        for c in to_sibling(k):
            c.start()
    gather.relay()

    def carry_on(g, none):
        segc = segc_ref[g]

        @pl.when(place == count - 1)
        def _():
            for copy in hop(g):
                copy.wait_recv()

        mark = csum_ref[g, heads : heads + 1, 0:1]
        carried = (segc == mark).astype(f32)
        for h in range(heads):
            phi = features(qkv_ref[g, :, 0:width], h, *tables) * carried
            state = padded_state(carry_ref[g, h])
            both = part[g, h]
            numer = both[:, :HV] + dot(phi.astype(bf16), state)
            denom = both[:, HV:] + jnp.sum(
                phi * csum_ref[g, h : h + 1, :], axis=1, keepdims=True
            )
            inverse = 1.0 / denom
            att_ref[g, :, h * HV : (h + 1) * HV] = (numer * inverse).astype(bf16)
            rden_ref[g, :, h * HV : (h + 1) * HV] = inverse
        return none

    lax.fori_loop(0, groups, carry_on, 0)

    @pl.when(place < count - 1)
    def _():
        def finish(g, none):
            for copy in hop(g):
                copy.wait_send()
            return none

        lax.fori_loop(0, groups, finish, 0)

    for k in range(count):
        for c in to_sibling(k):
            c.wait_recv()
            c.wait_send()
    for k in range(1, count):
        to_column(k).wait_send()
    for c in shares:
        c.wait_send()
    gather.finish()


def backward_kernel(
    count,
    heads,
    qkv_ref,
    segc_ref,
    segr_ref,
    left_ref,
    right_ref,
    rows_ref,
    att_ref,
    rden_ref,
    carry_ref,
    csum_ref,
    ga_ref,
    down_ref,
    res_ref,
    out_ref,
    final_ref,
    gn,
    send_state,
    send_sum,
    recv_state,
    recv_sum,
    dkey,
    dvalue,
    terms,
    land,
    send_sem,
    recv_sem,
    f_send,
    f_recv,
    local_sem,
):
    place, f = lax.axis_index("seq"), lax.axis_index("feat")
    groups, block = qkv_ref.shape[0], qkv_ref.shape[1]
    width = heads * FDIM
    tables = (left_ref, right_ref, rows_ref)

    def hop(g):
        target = {"seq": lax.rem(place + count - 1, count)}
        return [
            pltpu.make_async_remote_copy(
                src_ref=src.at[g],
                dst_ref=dst.at[g],
                send_sem=send_sem.at[i, g],
                recv_sem=recv_sem.at[i, g],
                device_id=target,
                device_id_type=MESH,
            )
            for i, (src, dst) in enumerate(((send_state, recv_state), (send_sum, recv_sum)))
        ]

    def send(g):
        for copy in hop(g):
            copy.start()

    chain = [lax.rem(place + 1, count), lax.rem(place + count - 1, count)]
    greet([{"seq": c} for c in chain] + square_targets(f))
    fill = pltpu.make_async_copy(down_ref, terms, local_sem.at[0])
    fill.start()
    ring = SquareSum(terms, land, f, f_send, f_recv)

    @pl.when(place == count - 1)
    def _():
        recv_state[...] = jnp.zeros_like(recv_state)
        recv_sum[...] = jnp.full_like(recv_sum, -1.0)

    def summarize(g, none):
        segc, segr = segc_ref[g], segr_ref[g]
        head = segr[:, 0:1]
        at_head = (segc == head).astype(f32)
        send_sum[g, heads : heads + 1, :] = jnp.broadcast_to(head, (1, LANES))
        for h in range(heads):
            lanes = slice(h * HV, (h + 1) * HV)
            ga = ga_ref[g, :, lanes]
            inverse = rden_ref[g, :, lanes]
            numer = (ga * inverse).astype(bf16)
            dots = jnp.sum(ga * att_ref[g, :, lanes].astype(f32), axis=1, keepdims=True)
            lane = lax.broadcasted_iota(jnp.int32, (block, HV), 1)
            denom = jnp.where(lane == 0, -dots * inverse, 0.0).astype(bf16)
            gn[g, h, :, :HV] = numer
            gn[g, h, :, HV:] = denom
            phi = (features(qkv_ref[g, :, 0:width], h, *tables) * at_head).astype(bf16)
            send_state[g, h] = dot_tn(phi, numer)[:STATE].astype(bf16)
            send_sum[g, h : h + 1, :] = dot_tn(denom, phi)[0:1]

        @pl.when(place == count - 1)
        def _():
            send(g)

        return none

    lax.fori_loop(0, groups, summarize, 0)
    fill.wait()
    ring.start_cross()
    ring.start_near()

    def join(g, none):
        for copy in hop(g):
            copy.wait_recv()
        segr = segr_ref[g]
        mark = recv_sum[g, heads : heads + 1, 0:1]
        head, tail = segr[:, 0:1], segr[:, block - 1 : block]
        whole = ((head == tail) & (head == mark)).astype(f32)
        for h in range(heads):
            send_state[g, h] = (
                send_state[g, h].astype(f32) + whole * recv_state[g, h].astype(f32)
            ).astype(bf16)
            send_sum[g, h : h + 1, :] = (
                send_sum[g, h : h + 1, :] + whole * recv_sum[g, h : h + 1, :]
            )
        send(g)
        return none

    def pull(g, none):
        segc, segr = segc_ref[g], segr_ref[g]
        allowed = allowed_of(segc, segr)
        query_all = qkv_ref[g, :, 0:width]
        key_all = qkv_ref[g, :, width : 2 * width]
        carried = (segc == csum_ref[g, heads : heads + 1, 0:1]).astype(f32)
        dquery = jnp.zeros((block, width), f32)
        dkey_sum = jnp.zeros((block, width), f32)
        for h in range(heads):
            query, key = only_head(query_all, h), only_head(key_all, h)
            value = qkv_ref[g, :, 2 * width + h * HV : 2 * width + (h + 1) * HV]
            wide = jnp.concatenate([value, jnp.ones_like(value)], axis=1)
            both = gn[g, h]
            c = dot_nt(query, key_all)
            kernel = jnp.where(allowed, 1.0 + c * (0.25 + c * 0.03125), 0.0).astype(bf16)
            grad = jnp.where(allowed, dot_nt(both, wide), 0.0)
            grad_c = (grad * (0.25 + c * 0.0625)).astype(bf16)
            dvalue[g, h] = dot_tn(kernel, both[:, :HV])
            dkey_sum = dkey_sum + dot_tn(grad_c, query)
            dquery = dquery + dot(grad_c, key)
            state = padded_state(carry_ref[g, h])
            gphi = dot_nt(both[:, :HV], state) + both[:, HV : HV + 1].astype(f32) * csum_ref[
                g, h : h + 1, :
            ]
            dquery = dquery + pull_features(gphi * carried, query_all, h, *tables)
        out_ref[g, :, 0:width] = dquery.astype(bf16)
        dkey[g] = dkey_sum

        @pl.when((place > 0) & (place < count - 1) & (g == count - 2 - place))
        def _():
            lax.fori_loop(0, groups, join, 0)

        return none

    lax.fori_loop(0, groups, pull, 0)
    ring.relay()

    def carry_back(g, none):
        segc = segc_ref[g]
        key_all = qkv_ref[g, :, width : 2 * width]

        @pl.when(place == 0)
        def _():
            for copy in hop(g):
                copy.wait_recv()

        mark = recv_sum[g, heads : heads + 1, 0:1]
        later = (segc == mark).astype(f32)
        total = dkey[g]
        for h in range(heads):
            value = qkv_ref[g, :, 2 * width + h * HV : 2 * width + (h + 1) * HV]
            state = padded_state(recv_state[g, h])
            phi = (features(key_all, h, *tables) * later).astype(bf16)
            dv = dvalue[g, h] + dot(phi, state)
            out_ref[g, :, 2 * width + h * HV : 2 * width + (h + 1) * HV] = dv.astype(bf16)
            gphi = (dot_nt(value, state) + recv_sum[g, h : h + 1, :]) * later
            total = total + pull_features(gphi, key_all, h, *tables)
        out_ref[g, :, width : 2 * width] = total.astype(bf16)
        return none

    lax.fori_loop(0, groups, carry_back, 0)

    @pl.when(place > 0)
    def _():
        def finish(g, none):
            for copy in hop(g):
                copy.wait_send()
            return none

        lax.fori_loop(0, groups, finish, 0)

    ring.arrive()

    def add_up(rows, total):
        final_ref[rows, :] = (res_ref[rows, :] + total).astype(bf16)

    by_rows(ring, add_up)
    ring.finish()


def whole_vmem(count):
    return [pl.BlockSpec(memory_space=pltpu.VMEM)] * count


def attention_forward(qkv, segc, segr, tables, cot_own, out_share, heads):
    groups, block, _ = qkv.shape
    count, dps = lax.axis_size("seq"), lax.axis_size("dp")
    others = max(dps - 1, 1)
    parts, rows_each, wide = out_share.shape
    dma = pltpu.SemaphoreType.DMA
    states = (groups, heads, STATE, HV)
    sums = (groups, 8, LANES)
    return pl.pallas_call(
        functools.partial(forward_kernel, count, dps, heads),
        out_shape=(
            jax.ShapeDtypeStruct((groups, block, heads * HV), bf16),
            jax.ShapeDtypeStruct((groups, block, heads * HV), f32),
            jax.ShapeDtypeStruct(states, bf16),
            jax.ShapeDtypeStruct(sums, f32),
            jax.ShapeDtypeStruct((groups,) + cot_own.shape, bf16),
            jax.ShapeDtypeStruct((parts, count, dps, rows_each, wide), bf16),
        ),
        in_specs=whole_vmem(6) + in_place(2),
        out_specs=tuple(whole_vmem(4) + in_place(2)),
        scratch_shapes=[
            pltpu.VMEM(states, bf16),
            pltpu.VMEM(sums, f32),
            pltpu.VMEM((groups, heads, block, 2 * HV), f32),
            dma((2, groups)),
            dma((2, groups)),
            dma((6,)),
            dma((6,)),
            dma((3,)),
            dma((3,)),
            dma((count - 1,)),
            dma((count - 1,)),
            dma((others, count)),
            dma((others, count)),
            dma((2,)),
        ],
        compiler_params=pltpu.CompilerParams(
            collective_id=0, has_side_effects=True, vmem_limit_bytes=40 << 20
        ),
        cost_estimate=pl.CostEstimate(flops=0, bytes_accessed=1 << 20, transcendentals=0),
        name="attention_forward",
    )(qkv, segc, segr, *tables, cot_own, out_share)


def attention_backward(
    qkv, segc, segr, tables, att, rden, carry, csum, ga, down, residual, heads
):
    groups, block, wide = qkv.shape
    count = lax.axis_size("seq")
    states = (groups, heads, STATE, HV)
    sums = (groups, 8, LANES)
    return pl.pallas_call(
        functools.partial(backward_kernel, count, heads),
        out_shape=(
            jax.ShapeDtypeStruct((groups, block, wide), bf16),
            jax.ShapeDtypeStruct(residual.shape, bf16),
        ),
        in_specs=whole_vmem(11) + in_place(1) + whole_vmem(1),
        out_specs=tuple(whole_vmem(2)),
        scratch_shapes=[
            pltpu.VMEM((groups, heads, block, 2 * HV), bf16),
            pltpu.VMEM(states, bf16),
            pltpu.VMEM(sums, f32),
            pltpu.VMEM(states, bf16),
            pltpu.VMEM(sums, f32),
            pltpu.VMEM((groups, block, heads * FDIM), f32),
            pltpu.VMEM((groups, heads, block, HV), f32),
            pltpu.VMEM((groups,) + residual.shape, bf16),
            pltpu.VMEM((6, block // 2, residual.shape[1]), bf16),
            pltpu.SemaphoreType.DMA((2, groups)),
            pltpu.SemaphoreType.DMA((2, groups)),
            pltpu.SemaphoreType.DMA((6,)),
            pltpu.SemaphoreType.DMA((6,)),
            pltpu.SemaphoreType.DMA((1,)),
        ],
        compiler_params=pltpu.CompilerParams(
            collective_id=1, has_side_effects=True, vmem_limit_bytes=48 << 20
        ),
        cost_estimate=pl.CostEstimate(flops=0, bytes_accessed=1 << 20, transcendentals=0),
        name="attention_backward",
    )(qkv, segc, segr, *tables, att, rden, carry, csum, ga, down, residual)


def peers(f):
    return 2 * (f // 2) + 1 - f % 2, (f + 2) % 4, 3 - f


def greet(targets):
    barrier = pltpu.get_barrier_semaphore()
    for target in targets:
        pl.semaphore_signal(barrier, inc=1, device_id=target, device_id_type=MESH)
    pl.semaphore_wait(barrier, len(targets))


def push(src, dst, send_sem, recv_sem, target):
    return pltpu.make_async_remote_copy(
        src_ref=src,
        dst_ref=dst,
        send_sem=send_sem,
        recv_sem=recv_sem,
        device_id=target,
        device_id_type=MESH,
    )


def square_targets(f):
    return [{"feat": p} for p in peers(f)]


class SquareGather:
    def __init__(self, slots, f, send_sem, recv_sem, own=None):
        side, above, across = peers(f)
        half = slots.shape[1] // 2
        first, second = pl.ds(0, half), pl.ds(half, half)

        def copy(i, slot, rows, to):
            ref = slots.at[slot, rows]
            src = ref if own is None or i > 3 else own.at[rows]
            return push(src, ref, send_sem.at[i], recv_sem.at[i], {"feat": to})

        self.direct = [
            copy(0, f, first, side),
            copy(1, f, second, above),
            copy(2, f, second, side),
            copy(3, f, first, above),
        ]
        self.forward = [copy(4, side, first, above), copy(5, above, second, side)]

    def start(self):
        for c in self.direct:
            c.start()

    def relay(self):
        self.direct[0].wait_recv()
        self.forward[0].start()
        self.direct[1].wait_recv()
        self.forward[1].start()

    def near(self):
        self.direct[2].wait_recv()
        self.direct[3].wait_recv()

    def far(self):
        for c in self.forward:
            c.wait_recv()

    def sent(self):
        for c in self.direct + self.forward:
            c.wait_send()

    def finish(self):
        self.near()
        self.far()
        self.sent()


class SquareSum:
    def __init__(self, part, land, f, send_sem, recv_sem):
        self.side, self.above, self.across = peers(f)
        self.f, self.part, self.land = f, part, land
        self.half = part.shape[1] // 2
        first, second = pl.ds(0, self.half), pl.ds(self.half, self.half)

        def copy(i, slot, rows, to):
            return push(
                part.at[slot, rows], land.at[i], send_sem.at[i], recv_sem.at[i], {"feat": to}
            )

        self.cross = [copy(0, self.across, first, self.side), copy(1, self.across, second, self.above)]
        self.near = [copy(2, self.side, first, self.side), copy(3, self.above, second, self.above)]
        self.late = [copy(4, self.above, first, self.above), copy(5, self.side, second, self.side)]

    def start_cross(self):
        for c in self.cross:
            c.start()

    def add_rows(self, slot, base, landed):
        step = 32

        def one(i, none):
            rows = pl.ds(pl.multiple_of(base + i * step, step), step)
            came = self.land[landed, pl.ds(pl.multiple_of(i * step, step), step), :]
            self.part[slot, rows, :] = (
                self.part[slot, rows, :].astype(f32) + came.astype(f32)
            ).astype(bf16)
            return none

        lax.fori_loop(0, self.half // step, one, 0)

    def start_near(self):
        for c in self.near:
            c.start()

    def relay(self):
        self.cross[0].wait_recv()
        self.add_rows(self.above, 0, 0)
        self.late[0].start()
        self.cross[1].wait_recv()
        self.add_rows(self.side, self.half, 1)
        self.late[1].start()

    def arrive(self):
        for c in self.near + self.late:
            c.wait_recv()

    def total(self, half, rows):
        base = half * self.half
        own = self.part[self.f, pl.ds(pl.multiple_of(base + rows.start, 16), rows.size), :]
        near = self.land[2 + half, rows, :]
        late = self.land[4 + half, rows, :]
        return own.astype(f32) + near.astype(f32) + late.astype(f32)

    def finish(self):
        for c in self.cross + self.near + self.late:
            c.wait_send()


def opening_kernel(
    seqs,
    dps,
    tok_ref,
    query_ref,
    key_ref,
    value_ref,
    one_ref,
    two_ref,
    x_ref,
    w_ref,
    g_ref,
    pack,
    tile,
    x_send,
    x_recv,
    a_send,
    a_recv,
    z_send,
    z_recv,
    d_send,
    d_recv,
    local_sem,
):
    f, s, d = lax.axis_index("feat"), lax.axis_index("seq"), lax.axis_index("dp")
    parts, rows_each = pack.shape[0], pack.shape[1]
    near = peers(f)
    columns = [lax.rem(s + k, seqs) for k in range(1, seqs)]
    others = [lax.rem(d + k, dps) for k in range(1, dps)]
    stay = pltpu.make_async_copy(tok_ref, x_ref.at[f], local_sem.at[0])
    stay.start()
    greet(
        square_targets(f) + [{"seq": c} for c in columns] + [{"dp": o} for o in others]
    )
    gather = SquareGather(x_ref, f, x_send, x_recv, tok_ref)
    gather.start()

    first = 0
    for ref in (query_ref, key_ref, value_ref):
        each = ref.shape[1] // parts
        for p in range(parts):
            pack[p, :, first : first + each] = ref[:, p * each : (p + 1) * each]
        first += each
    tile[...] = jnp.zeros_like(tile)
    tile[0:1, :rows_each] = one_ref[...].astype(f32)
    tile[1:2, :rows_each] = two_ref[...].astype(f32)
    outs = (w_ref, g_ref)
    own = [
        pltpu.make_async_copy(pack.at[f], w_ref.at[f, s, d], local_sem.at[1]),
        pltpu.make_async_copy(tile, g_ref.at[f, s, d], local_sem.at[2]),
    ]
    for c in own:
        c.start()
    shares = [
        [
            push(pack.at[p], w_ref.at[f, s, d], a_send.at[0, i], a_recv.at[0, i], {"feat": p}),
            push(tile, g_ref.at[f, s, d], a_send.at[1, i], a_recv.at[1, i], {"feat": p}),
        ]
        for i, p in enumerate(near)
    ]
    for pair in shares:
        for c in pair:
            c.start()
    for c in own:
        c.wait()

    chunks = (f,) + near

    def to_column(n, k):
        return [
            push(
                ref.at[chunks[n], s, d],
                ref.at[chunks[n], s, d],
                z_send.at[j, k - 1, n],
                z_recv.at[j, k - 1, n],
                {"seq": columns[k - 1]},
            )
            for j, ref in enumerate(outs)
        ]

    def to_sibling(n, k):
        back = lax.rem(s + seqs - k, seqs)
        return [
            push(
                ref.at[chunks[n], back, d],
                ref.at[chunks[n], back, d],
                d_send.at[j, o, k, n],
                d_recv.at[j, o, k, n],
                {"dp": other},
            )
            for j, ref in enumerate(outs)
            for o, other in enumerate(others)
        ]

    def start_all(copies):
        for c in copies:
            c.start()

    for n in range(parts):
        if n:
            for c in shares[n - 1]:
                c.wait_recv()
        for k in range(1, seqs):
            start_all(to_column(n, k))
        start_all(to_sibling(n, 0))
    for n in range(parts):
        for k in range(1, seqs):
            for c in to_column(n, k):
                c.wait_recv()
            start_all(to_sibling(n, k))
    gather.relay()
    for n in range(parts):
        for k in range(seqs):
            for c in to_sibling(n, k):
                c.wait_recv()
    for n in range(parts):
        for k in range(seqs):
            for c in to_sibling(n, k):
                c.wait_send()
        for k in range(1, seqs):
            for c in to_column(n, k):
                c.wait_send()
    for pair in shares:
        for c in pair:
            c.wait_send()
    stay.wait()
    gather.finish()


def in_place(count):
    return [pl.BlockSpec(memory_space=pl.ANY)] * count


def opening(own, w_query, w_key, w_value, gain_one, gain_two):
    parts, seqs, dps = (lax.axis_size(a) for a in ALL)
    block, width = own.shape
    rows_each = w_query.shape[0]
    wide = (w_query.shape[1] + w_key.shape[1] + w_value.shape[1]) // parts
    others = max(dps - 1, 1)
    dma = pltpu.SemaphoreType.DMA
    x_all, w_all, g_all = pl.pallas_call(
        functools.partial(opening_kernel, seqs, dps),
        out_shape=(
            jax.ShapeDtypeStruct((parts, block, width), bf16),
            jax.ShapeDtypeStruct((parts, seqs, dps, rows_each, wide), bf16),
            jax.ShapeDtypeStruct((parts, seqs, dps, 8, HV), f32),
        ),
        in_specs=in_place(1) + whole_vmem(5),
        out_specs=tuple(in_place(3)),
        scratch_shapes=[
            pltpu.VMEM((parts, rows_each, wide), bf16),
            pltpu.VMEM((8, HV), f32),
            dma((6,)),
            dma((6,)),
            dma((2, 3)),
            dma((2, 3)),
            dma((2, seqs - 1, parts)),
            dma((2, seqs - 1, parts)),
            dma((2, others, seqs, parts)),
            dma((2, others, seqs, parts)),
            dma((3,)),
        ],
        compiler_params=pltpu.CompilerParams(collective_id=2, has_side_effects=True),
        cost_estimate=pl.CostEstimate(flops=0, bytes_accessed=1 << 20, transcendentals=0),
        name="opening",
    )(own, w_query, w_key, w_value, gain_one, gain_two)
    gains = g_all[..., :2, :rows_each].transpose(3, 0, 1, 2, 4).reshape(2, width)
    return x_all, w_all.reshape(width, wide), gains


def inverse_rms(values):
    return lax.rsqrt(jnp.mean(values * values, axis=-1, keepdims=True) + epsilon)


def norm_back(grad, unit, inverse, gain):
    scaled = grad * gain
    return (scaled - unit * jnp.mean(scaled * unit, axis=-1, keepdims=True)) * inverse


def product_tiles(part, slot, pairs, tile):
    def one(i, none):
        cols = pl.ds(pl.multiple_of(i * tile, tile), tile)
        total = None
        for rows, weights in pairs:
            term = dot_nt(rows[slot], weights[cols, :])
            total = term if total is None else total + term
        part[slot, :, cols] = total.astype(bf16)
        return none

    lax.fori_loop(0, part.shape[2] // tile, one, 0)


def summed_products(part, land, f, pairs, send_sem, recv_sem, beside=None):
    side, above, across = peers(f)
    ring = SquareSum(part, land, f, send_sem, recv_sem)
    product_tiles(part, across, pairs, 512)
    ring.start_cross()
    product_tiles(part, side, pairs, 512)
    product_tiles(part, above, pairs, 512)
    ring.start_near()
    product_tiles(part, f, pairs, 512)
    if beside is not None:
        beside()
    ring.relay()
    ring.arrive()
    return ring


def by_rows(ring, body, step=16):
    for half in (0, 1):

        def one(i, none):
            start = pl.multiple_of(i * step, step)
            rows = pl.ds(pl.multiple_of(half * ring.half + i * step, step), step)
            body(rows, ring.total(half, pl.ds(start, step)))
            return none

        lax.fori_loop(0, ring.half // step, one, 0)


def branch_kernel(
    att_ref, w_ref, tok_ref, gain_ref, rows_ref, res_ref, part, land, s_send, s_recv, g_send, g_recv
):
    f = lax.axis_index("feat")
    greet(square_targets(f))
    ring = summed_products(part, land, f, [(att_ref, w_ref)], s_send, s_recv)

    def finish_rows(rows, total):
        residual = tok_ref[rows, :].astype(f32) + total
        res_ref[rows, :] = residual
        rows_ref[f, rows, :] = (residual * inverse_rms(residual) * gain_ref[...]).astype(bf16)

    by_rows(ring, finish_rows)
    gather = SquareGather(rows_ref, f, g_send, g_recv)
    gather.start()
    ring.finish()
    gather.relay()
    gather.finish()


def square_scratch(parts, block, width):
    dma = pltpu.SemaphoreType.DMA
    return [
        pltpu.VMEM((parts, block, width), bf16),
        pltpu.VMEM((6, block // 2, width), bf16),
        dma((6,)),
        dma((6,)),
    ]


def branch_step(att, out_w, own, gain_two):
    parts, block, _ = att.shape
    width = own.shape[1]
    dma = pltpu.SemaphoreType.DMA
    return pl.pallas_call(
        branch_kernel,
        out_shape=(
            jax.ShapeDtypeStruct((parts, block, width), bf16),
            jax.ShapeDtypeStruct((block, width), f32),
        ),
        in_specs=whole_vmem(4),
        out_specs=tuple(whole_vmem(2)),
        scratch_shapes=square_scratch(parts, block, width) + [dma((6,)), dma((6,))],
        compiler_params=pltpu.CompilerParams(
            collective_id=3, has_side_effects=True, vmem_limit_bytes=48 << 20
        ),
        cost_estimate=pl.CostEstimate(flops=0, bytes_accessed=1 << 20, transcendentals=0),
        name="branch_step",
    )(att, out_w, own, gain_two)


def rows_back_kernel(
    gg_ref,
    gu_ref,
    wg_ref,
    wu_ref,
    res_ref,
    cot_ref,
    gain_ref,
    mixed_hbm,
    wd_hbm,
    wo_hbm,
    all_ref,
    gres_ref,
    gsum_ref,
    down_ref,
    ga_ref,
    part,
    land,
    mixed,
    wd,
    wo,
    s_send,
    s_recv,
    g_send,
    g_recv,
    local_sem,
):
    f = lax.axis_index("feat")
    fills = [
        pltpu.make_async_copy(src, dst, local_sem.at[i])
        for i, (src, dst) in enumerate(((mixed_hbm, mixed), (wd_hbm, wd), (wo_hbm, wo)))
    ]
    for c in fills:
        c.start()
    greet(square_targets(f))
    pairs = [(gg_ref, wg_ref), (gu_ref, wu_ref)]

    def down_products():
        for c in fills:
            c.wait()
        for p in range(part.shape[0]):
            product_tiles(down_ref, p, [(mixed, wd)], 512)

    ring = summed_products(part, land, f, pairs, s_send, s_recv, down_products)
    gsum_ref[...] = jnp.zeros_like(gsum_ref)

    def finish_rows(rows, grad):
        residual = res_ref[rows, :]
        inverse = inverse_rms(residual)
        unit = residual * inverse
        gsum_ref[...] += jnp.sum(grad * unit, axis=0, keepdims=True)
        grad_res = cot_ref[rows, :].astype(f32) + norm_back(grad, unit, inverse, gain_ref[...])
        gres_ref[rows, :] = grad_res
        all_ref[f, rows, :] = grad_res.astype(bf16)

    by_rows(ring, finish_rows)
    gather = SquareGather(all_ref, f, g_send, g_recv)
    gather.start()
    ring.finish()
    side, above, across = peers(f)

    def attended_grad(slot):
        ga_ref[slot] = dot(all_ref[slot], wo[...])

    attended_grad(f)
    gather.relay()
    gather.near()
    attended_grad(side)
    attended_grad(above)
    gather.far()
    attended_grad(across)
    gather.sent()


def rows_back(
    grad_gate, grad_up, gate_w, up_w, residual, cot_own, gain_two, mixed, down_w, out_w
):
    parts, block, hidden = grad_gate.shape
    width = residual.shape[1]
    dma = pltpu.SemaphoreType.DMA
    return pl.pallas_call(
        rows_back_kernel,
        out_shape=(
            jax.ShapeDtypeStruct((parts, block, width), bf16),
            jax.ShapeDtypeStruct((block, width), f32),
            jax.ShapeDtypeStruct((1, width), f32),
            jax.ShapeDtypeStruct((parts, block, width), bf16),
            jax.ShapeDtypeStruct((parts, block, out_w.shape[1]), f32),
        ),
        in_specs=whole_vmem(7) + in_place(3),
        out_specs=tuple(whole_vmem(5)),
        scratch_shapes=square_scratch(parts, block, width)[:2]
        + [
            pltpu.VMEM((parts, block, hidden), bf16),
            pltpu.VMEM((width, hidden), bf16),
            pltpu.VMEM(out_w.shape, bf16),
        ]
        + [dma((6,))] * 4
        + [dma((3,))],
        compiler_params=pltpu.CompilerParams(
            collective_id=4, has_side_effects=True, vmem_limit_bytes=60 << 20
        ),
        cost_estimate=pl.CostEstimate(flops=0, bytes_accessed=1 << 20, transcendentals=0),
        name="rows_back",
    )(grad_gate, grad_up, gate_w, up_w, residual, cot_own, gain_two, mixed, down_w, out_w)


def closing_kernel(
    seqs,
    dps,
    dqkv_ref,
    w_ref,
    tok_ref,
    gres_ref,
    gain_ref,
    gsum_two_ref,
    x_ref,
    tile_ref,
    part,
    land,
    s_send,
    s_recv,
    gsum,
    cut,
    came,
    mid,
    tail,
    c_send,
    c_recv,
    d_send,
    d_recv,
):
    f, s, d = lax.axis_index("feat"), lax.axis_index("seq"), lax.axis_index("dp")
    parts = 4
    others = [lax.rem(d + k, dps) for k in range(1, dps)]
    circle = [
        (lax.rem(f + i, parts), lax.rem(s + j, seqs))
        for i in range(parts)
        for j in range(seqs)
        if i or j
    ]
    greet(
        [{"feat": a, "seq": b} for a, b in circle] + [{"dp": o} for o in others]
    )
    ring = summed_products(part, land, f, [(dqkv_ref, w_ref)], s_send, s_recv)
    gsum[...] = jnp.zeros_like(gsum)

    def finish_rows(rows, grad):
        values = tok_ref[rows, :].astype(f32)
        inverse = inverse_rms(values)
        unit = values * inverse
        gsum[...] += jnp.sum(grad * unit, axis=0, keepdims=True)
        x_ref[rows, :] = gres_ref[rows, :] + norm_back(grad, unit, inverse, gain_ref[...])

    by_rows(ring, finish_rows)
    ring.finish()

    lanes = gsum.shape[1] // (parts * seqs)
    cut[...] = jnp.zeros_like(cut)
    for k in range(parts * seqs):
        cut[k, 0:1, :] = gsum[:, k * lanes : (k + 1) * lanes]
        cut[k, 1:2, :] = gsum_two_ref[:, k * lanes : (k + 1) * lanes]
    place = f * seqs + s
    sends = []
    for i, (a, b) in enumerate(circle):
        sends.append(
            push(
                cut.at[a * seqs + b],
                came.at[i],
                c_send.at[i],
                c_recv.at[i],
                {"feat": a, "seq": b},
            )
        )
    for c in sends:
        c.start()
    total = cut[place]
    for c in sends:
        c.wait_recv()
    for i in range(len(circle)):
        total = total + came[i]
    mid[...] = total
    last = [
        push(mid, tail.at[k], d_send.at[k], d_recv.at[k], {"dp": o})
        for k, o in enumerate(others)
    ]
    for c in last:
        c.start()
    for c in last:
        c.wait_recv()
    for k in range(len(others)):
        total = total + tail[k]
    tile_ref[...] = total
    for c in sends + last:
        c.wait_send()


def closing(dqkv, qkv_w, own, grad_residual, gain_one, gain_two_sum):
    parts, seqs, dps = (lax.axis_size(a) for a in ALL)
    block, width = own.shape
    others = max(dps - 1, 1)
    lanes = width // (parts * seqs)
    circle = parts * seqs - 1
    dma = pltpu.SemaphoreType.DMA
    return pl.pallas_call(
        functools.partial(closing_kernel, seqs, dps),
        out_shape=(
            jax.ShapeDtypeStruct((block, width), f32),
            jax.ShapeDtypeStruct((8, lanes), f32),
        ),
        in_specs=whole_vmem(6),
        out_specs=tuple(whole_vmem(2)),
        scratch_shapes=square_scratch(parts, block, width)
        + [
            pltpu.VMEM((1, width), f32),
            pltpu.VMEM((parts * seqs, 8, lanes), f32),
            pltpu.VMEM((circle, 8, lanes), f32),
            pltpu.VMEM((8, lanes), f32),
            pltpu.VMEM((others, 8, lanes), f32),
            dma((circle,)),
            dma((circle,)),
            dma((others,)),
            dma((others,)),
        ],
        compiler_params=pltpu.CompilerParams(
            collective_id=5, has_side_effects=True, vmem_limit_bytes=48 << 20
        ),
        cost_estimate=pl.CostEstimate(flops=0, bytes_accessed=1 << 20, transcendentals=0),
        name="closing",
    )(dqkv, qkv_w, own, grad_residual, gain_one, gain_two_sum)


def local(
    tokens,
    segments,
    norm1_gain,
    norm2_gain,
    w_query,
    w_key,
    w_value,
    w_out,
    w_gate,
    w_up,
    w_down,
    cotangent,
):
    parts = lax.axis_size("feat")
    heads = HEADS // parts
    block, width = tokens.shape[2], tokens.shape[3]
    rows_total = parts * block
    rows_each = w_query.shape[0]
    own = tokens.reshape(block, width)
    cot_own = cotangent.reshape(block, width)

    out_share = w_out.T.reshape(rows_each, parts, heads * HV).transpose(1, 0, 2)
    gate_w = lax.all_gather(w_gate, ("seq", "dp"), axis=0, tiled=True)
    up_w = lax.all_gather(w_up, ("seq", "dp"), axis=0, tiled=True)
    x_all, qkv_w, gains = opening(
        own, w_query, w_key, w_value, norm1_gain[None], norm2_gain[None]
    )
    qkv_width = qkv_w.shape[1]
    gain_one, gain_two = gains[0:1], gains[1:2]

    x_wide = x_all.astype(f32).reshape(rows_total, width)
    normed = (x_wide * inverse_rms(x_wide) * gain_one).astype(bf16)
    qkv = dot(normed, qkv_w).astype(bf16).reshape(parts, block, qkv_width)
    qkv, w_down = lax.optimization_barrier((qkv, w_down))
    down_w = lax.all_gather(w_down.T, ("seq", "dp"), axis=0, tiled=True)
    segment = segments.reshape(parts, block).astype(f32)
    segc, segr = segment[:, :, None], segment[:, None, :]
    tables = feature_tables(heads)
    att, rden, carry, csum, cot_all, out_w = attention_forward(
        qkv, segc, segr, tables, cot_own, out_share, heads
    )
    out_w = out_w.reshape(width, heads * HV)
    cot_all = cot_all.reshape(rows_total, width)
    rows_all, residual = branch_step(att, out_w, own, gain_two)
    rows_all = rows_all.reshape(rows_total, width)

    gate_out = dot(rows_all, gate_w)
    up_out = dot(rows_all, up_w)
    sig = jax.nn.sigmoid(gate_out)
    silu = gate_out * sig
    mixed = (silu * up_out).astype(bf16)
    mixed, cot_late = lax.optimization_barrier((mixed, cot_all))
    grad_mixed = dot(cot_late, down_w)
    grad_gate = (grad_mixed * up_out * sig * (1.0 + gate_out * (1.0 - sig))).astype(bf16)
    grad_up = (grad_mixed * silu).astype(bf16)

    def summed(term):
        return lax.psum_scatter(term, ("seq", "dp"), scatter_dimension=0, tiled=True)

    down_term = dot_tn(cot_all, mixed).astype(bf16)
    gate_term = dot_tn(rows_all, grad_gate).astype(bf16)
    up_term = dot_tn(rows_all, grad_up).astype(bf16)
    grad_gate, grad_up, gate_term, up_term = lax.optimization_barrier(
        (grad_gate, grad_up, gate_term, up_term)
    )
    down_sum, gate_sum, up_sum = summed(down_term), summed(gate_term), summed(up_term)

    by_device = (parts, block, -1)
    branch_all, grad_residual, gain_two_sum, down, ga = rows_back(
        grad_gate.reshape(by_device),
        grad_up.reshape(by_device),
        gate_w,
        up_w,
        residual,
        cot_own,
        gain_two,
        mixed.reshape(by_device),
        down_w,
        out_w,
    )
    branch_all = branch_all.reshape(rows_total, width)
    dqkv, output = attention_backward(
        qkv, segc, segr, tables, att, rden, carry, csum, ga, down, residual, heads
    )
    x_grad, gain_grads = closing(dqkv, qkv_w, own, grad_residual, gain_one, gain_two_sum)
    dqkv = dqkv.reshape(rows_total, qkv_width)

    def shared(grads):
        grads = grads.astype(bf16).reshape(parts, -1, rows_each, grads.shape[1])
        grads = grads.transpose(1, 0, 2, 3).reshape(width, -1)
        grads = lax.psum_scatter(grads, ("seq", "dp"), scatter_dimension=0, tiled=True)
        grads = grads.reshape(parts, rows_each, -1)
        return lax.all_to_all(grads, "feat", 0, 0, tiled=True).astype(f32)

    def from_share(grads, first, per):
        piece = grads[:, :, first : first + heads * per]
        return piece.transpose(1, 0, 2).reshape(rows_each, HEADS * per)

    out_term = dot_tn(branch_all, att.reshape(rows_total, heads * HV))
    qkv_term = dot_tn(normed, dqkv)
    out_term, qkv_term, down_sum, gate_sum, up_sum = lax.optimization_barrier(
        (out_term, qkv_term, down_sum, gate_sum, up_sum)
    )
    out_grads, qkv_grads = shared(out_term), shared(qkv_term)
    query_grad = from_share(qkv_grads, 0, FDIM)
    key_grad = from_share(qkv_grads, heads * FDIM, FDIM)
    value_grad = from_share(qkv_grads, 2 * heads * FDIM, HV)
    out_grad = from_share(out_grads, 0, HV).T
    gain_each = gain_grads.shape[1] // lax.axis_size("dp")
    gain_grads = lax.dynamic_slice_in_dim(
        gain_grads, lax.axis_index("dp") * gain_each, gain_each, axis=1
    )
    return (
        output.reshape(tokens.shape),
        x_grad.reshape(tokens.shape),
        gain_grads[0],
        gain_grads[1],
        query_grad,
        key_grad,
        value_grad,
        out_grad,
        gate_sum.astype(f32),
        up_sum.astype(f32),
        down_sum.T.astype(f32),
    )


def solution(mesh):
    placed = (
        P("feat", "dp", "seq", None),
        P(None, "dp", "seq"),
        P(ALL),
        P(ALL),
        P(ALL, None),
        P(ALL, None),
        P(ALL, None),
        P(None, ALL),
        P(("seq", "dp"), "feat"),
        P(("seq", "dp"), "feat"),
        P("feat", ("seq", "dp")),
        P("feat", "dp", "seq", None),
    )
    return jax.shard_map(
        local,
        mesh=mesh,
        in_specs=placed,
        out_specs=(
            P("feat", "dp", "seq", None),
            P("feat", "dp", "seq", None),
            P(ALL),
            P(ALL),
            P(ALL, None),
            P(ALL, None),
            P(ALL, None),
            P(None, ALL),
            P(("seq", "dp"), "feat"),
            P(("seq", "dp"), "feat"),
            P("feat", ("seq", "dp")),
        ),
        check_vma=False,
    )
```

```python
import functools

import jax
import jax.numpy as jnp
import numpy as np
from jax import lax
from jax.experimental import pallas as pl
from jax.experimental.pallas import tpu as pltpu
from jax.sharding import PartitionSpec as P

HEADS = 16
FDIM = 16
HV = 128
STATE = 160
LANES = 256
epsilon = 1e-05
MESH = pl.DeviceIdType.MESH
ALL = ("feat", "seq", "dp")
f32 = jnp.float32
bf16 = jnp.bfloat16


def dot(a, b):
    return lax.dot_general(a, b, (((1,), (0,)), ((), ())), preferred_element_type=f32)


def dot_nt(a, b):
    return lax.dot_general(a, b, (((1,), (1,)), ((), ())), preferred_element_type=f32)


def dot_tn(a, b):
    return lax.dot_general(a, b, (((0,), (0,)), ((), ())), preferred_element_type=f32)


def feature_tables(heads):
    pairs = [(i, j) for i in range(FDIM) for j in range(i, FDIM)]
    left = np.zeros((heads, heads * FDIM, LANES), np.float32)
    right = np.zeros((heads, heads * FDIM, LANES), np.float32)
    rows = np.zeros((8, LANES), np.float32)
    for h in range(heads):
        for p, (i, j) in enumerate(pairs):
            left[h, h * FDIM + i, p] = 1.0
            right[h, h * FDIM + j, p] = 1.0
            rows[2, p] = 0.25 / 2.0**0.5 if i == j else 0.25
        for i in range(FDIM):
            p = len(pairs) + i
            left[h, h * FDIM + i, p] = 1.0
            rows[1, p] = 1.0
            rows[2, p] = 0.5
        p = len(pairs) + FDIM
        rows[0, p] = rows[1, p] = rows[2, p] = 1.0
    return jnp.asarray(left, bf16), jnp.asarray(right, bf16), jnp.asarray(rows)


def both_sides(entries, h, left_ref, right_ref, rows_ref):
    one = dot(entries, left_ref[h]) + rows_ref[0:1, :]
    two = dot(entries, right_ref[h]) + rows_ref[1:2, :]
    return one, two * rows_ref[2:3, :]


def features(entries, h, left_ref, right_ref, rows_ref):
    one, two = both_sides(entries, h, left_ref, right_ref, rows_ref)
    return one * two


def pull_features(grad, entries, h, left_ref, right_ref, rows_ref):
    one, two = both_sides(entries, h, left_ref, right_ref, rows_ref)
    scaled = rows_ref[2:3, :]
    return dot_nt((grad * two).astype(bf16), left_ref[h]) + dot_nt(
        (grad * one * scaled).astype(bf16), right_ref[h]
    )


def only_head(entries, h):
    lane = lax.broadcasted_iota(jnp.int32, entries.shape, 1)
    keep = (lane >= h * FDIM) & (lane < (h + 1) * FDIM)
    return jnp.where(keep, entries, jnp.zeros_like(entries))


def padded_state(state):
    return jnp.concatenate([state, jnp.zeros((LANES - STATE, state.shape[1]), state.dtype)], 0)


def allowed_of(segc, segr):
    block = segc.shape[0]
    row = lax.broadcasted_iota(jnp.int32, (block, block), 0)
    col = lax.broadcasted_iota(jnp.int32, (block, block), 1)
    return (row >= col) & (segc == segr)


def forward_kernel(
    count,
    dps,
    heads,
    qkv_ref,
    segc_ref,
    segr_ref,
    left_ref,
    right_ref,
    rows_ref,
    cot_ref,
    share_ref,
    att_ref,
    rden_ref,
    carry_ref,
    csum_ref,
    cots_ref,
    wout_ref,
    send_state,
    send_sum,
    part,
    send_sem,
    recv_sem,
    f_send,
    f_recv,
    a_send,
    a_recv,
    z_send,
    z_recv,
    d_send,
    d_recv,
    local_sem,
):
    place, f, d = lax.axis_index("seq"), lax.axis_index("feat"), lax.axis_index("dp")
    groups, block = qkv_ref.shape[0], qkv_ref.shape[1]
    width = heads * FDIM
    tables = (left_ref, right_ref, rows_ref)

    def hop(g):
        target = {"seq": lax.rem(place + 1, count)}
        return [
            pltpu.make_async_remote_copy(
                src_ref=src.at[g],
                dst_ref=dst.at[g],
                send_sem=send_sem.at[i, g],
                recv_sem=recv_sem.at[i, g],
                device_id=target,
                device_id_type=MESH,
            )
            for i, (src, dst) in enumerate(((send_state, carry_ref), (send_sum, csum_ref)))
        ]

    def send(g):
        for copy in hop(g):
            copy.start()

    columns = [lax.rem(place + k, count) for k in range(1, count)]
    others = [lax.rem(d + k, dps) for k in range(1, dps)]
    stay = [
        pltpu.make_async_copy(cot_ref, cots_ref.at[f], local_sem.at[0]),
        pltpu.make_async_copy(share_ref.at[f], wout_ref.at[f, place, d], local_sem.at[1]),
    ]
    for c in stay:
        c.start()
    greet(
        square_targets(f) + [{"seq": c} for c in columns] + [{"dp": o} for o in others]
    )
    shares = [
        push(share_ref.at[p], wout_ref.at[f, place, d], a_send.at[i], a_recv.at[i], {"feat": p})
        for i, p in enumerate(peers(f))
    ]
    for c in shares:
        c.start()
    gather = SquareGather(cots_ref, f, f_send, f_recv, cot_ref)

    def to_column(k):
        ref = wout_ref.at[:, place, d]
        return push(ref, ref, z_send.at[k - 1], z_recv.at[k - 1], {"seq": columns[k - 1]})

    def to_sibling(k):
        ref = wout_ref.at[:, lax.rem(place + count - k, count), d]
        return [
            push(ref, ref, d_send.at[o, k], d_recv.at[o, k], {"dp": other})
            for o, other in enumerate(others)
        ]

    @pl.when(place == 0)
    def _():
        carry_ref[...] = jnp.zeros_like(carry_ref)
        csum_ref[...] = jnp.full_like(csum_ref, -1.0)

    def summarize(g, none):
        segc, segr = segc_ref[g], segr_ref[g]
        tail = segr[:, block - 1 : block]
        at_tail = (segc == tail).astype(f32)
        send_sum[g, heads : heads + 1, :] = jnp.broadcast_to(tail, (1, LANES))
        for h in range(heads):
            key = qkv_ref[g, :, width : 2 * width]
            value = qkv_ref[g, :, 2 * width + h * HV : 2 * width + (h + 1) * HV]
            phi = (features(key, h, *tables) * at_tail).astype(bf16)
            send_state[g, h] = dot_tn(phi, value)[:STATE].astype(bf16)
            ones = jnp.ones((8, block), bf16)
            send_sum[g, h : h + 1, :] = dot(ones, phi)[0:1]

        @pl.when(place == 0)
        def _():
            send(g)

        return none

    lax.fori_loop(0, groups, summarize, 0)
    gather.start()
    for c in stay:
        c.wait()
    for c in shares:
        c.wait_recv()
    for k in range(1, count):
        to_column(k).start()
    for c in to_sibling(0):
        c.start()

    def join(g, none):
        for copy in hop(g):
            copy.wait_recv()
        segr = segr_ref[g]
        mark = csum_ref[g, heads : heads + 1, 0:1]
        head, tail = segr[:, 0:1], segr[:, block - 1 : block]
        whole = ((head == tail) & (head == mark)).astype(f32)
        for h in range(heads):
            send_state[g, h] = (
                send_state[g, h].astype(f32) + whole * carry_ref[g, h].astype(f32)
            ).astype(bf16)
            send_sum[g, h : h + 1, :] = (
                send_sum[g, h : h + 1, :] + whole * csum_ref[g, h : h + 1, :]
            )
        send(g)
        return none

    def attend(g, none):
        segc, segr = segc_ref[g], segr_ref[g]
        allowed = allowed_of(segc, segr)
        for h in range(heads):
            query = only_head(qkv_ref[g, :, 0:width], h)
            key = qkv_ref[g, :, width : 2 * width]
            value = qkv_ref[g, :, 2 * width + h * HV : 2 * width + (h + 1) * HV]
            c = dot_nt(query, key)
            kernel = jnp.where(allowed, 1.0 + c * (0.25 + c * 0.03125), 0.0).astype(bf16)
            wide = jnp.concatenate([value, jnp.ones_like(value)], axis=1)
            part[g, h] = dot(kernel, wide)

        @pl.when((place > 0) & (place < count - 1) & (g == place - 1))
        def _():
            lax.fori_loop(0, groups, join, 0)

        return none

    lax.fori_loop(0, groups, attend, 0)
    gather.relay()

    def carry_on(g, none):
        segc = segc_ref[g]

        @pl.when(place == count - 1)
        def _():
            for copy in hop(g):
                copy.wait_recv()

        mark = csum_ref[g, heads : heads + 1, 0:1]
        carried = (segc == mark).astype(f32)
        for h in range(heads):
            phi = features(qkv_ref[g, :, 0:width], h, *tables) * carried
            state = padded_state(carry_ref[g, h])
            both = part[g, h]
            numer = both[:, :HV] + dot(phi.astype(bf16), state)
            denom = both[:, HV:] + jnp.sum(
                phi * csum_ref[g, h : h + 1, :], axis=1, keepdims=True
            )
            inverse = 1.0 / denom
            att_ref[g, :, h * HV : (h + 1) * HV] = (numer * inverse).astype(bf16)
            rden_ref[g, :, h * HV : (h + 1) * HV] = inverse
        return none

    lax.fori_loop(0, groups, carry_on, 0)

    @pl.when(place < count - 1)
    def _():
        def finish(g, none):
            for copy in hop(g):
                copy.wait_send()
            return none

        lax.fori_loop(0, groups, finish, 0)

    for k in range(1, count):
        to_column(k).wait_recv()
        for c in to_sibling(k):
            c.start()
    for k in range(count):
        for c in to_sibling(k):
            c.wait_recv()
            c.wait_send()
    for k in range(1, count):
        to_column(k).wait_send()
    for c in shares:
        c.wait_send()
    gather.finish()


def backward_kernel(
    count,
    dps,
    heads,
    qkv_ref,
    segc_ref,
    segr_ref,
    left_ref,
    right_ref,
    rows_ref,
    att_ref,
    rden_ref,
    carry_ref,
    csum_ref,
    ga_ref,
    down_ref,
    res_ref,
    oterm_ref,
    out_ref,
    final_ref,
    ograd_ref,
    gn,
    send_state,
    send_sum,
    recv_state,
    recv_sum,
    dkey,
    dvalue,
    terms,
    land,
    send_sem,
    recv_sem,
    f_send,
    f_recv,
    local_sem,
    *sum_scratch,
):
    place, f, d = lax.axis_index("seq"), lax.axis_index("feat"), lax.axis_index("dp")
    groups, block = qkv_ref.shape[0], qkv_ref.shape[1]
    width = heads * FDIM
    tables = (left_ref, right_ref, rows_ref)

    def hop(g):
        target = {"seq": lax.rem(place + count - 1, count)}
        return [
            pltpu.make_async_remote_copy(
                src_ref=src.at[g],
                dst_ref=dst.at[g],
                send_sem=send_sem.at[i, g],
                recv_sem=recv_sem.at[i, g],
                device_id=target,
                device_id_type=MESH,
            )
            for i, (src, dst) in enumerate(((send_state, recv_state), (send_sum, recv_sum)))
        ]

    def send(g):
        for copy in hop(g):
            copy.start()

    columns = [lax.rem(place + k, count) for k in range(1, count)]
    others = [lax.rem(d + k, dps) for k in range(1, dps)]
    greet(
        square_targets(f) + [{"seq": c} for c in columns] + [{"dp": o} for o in others]
    )
    rows_sum = row_sum(oterm_ref, sum_scratch, f, place, d, count, dps)
    rows_sum.start()
    fill = pltpu.make_async_copy(down_ref, terms, local_sem.at[0])
    fill.start()
    ring = SquareSum(terms, land, f, f_send, f_recv)

    @pl.when(place == count - 1)
    def _():
        recv_state[...] = jnp.zeros_like(recv_state)
        recv_sum[...] = jnp.full_like(recv_sum, -1.0)

    def summarize(g, none):
        segc, segr = segc_ref[g], segr_ref[g]
        head = segr[:, 0:1]
        at_head = (segc == head).astype(f32)
        send_sum[g, heads : heads + 1, :] = jnp.broadcast_to(head, (1, LANES))
        for h in range(heads):
            lanes = slice(h * HV, (h + 1) * HV)
            ga = ga_ref[g, :, lanes]
            inverse = rden_ref[g, :, lanes]
            numer = (ga * inverse).astype(bf16)
            dots = jnp.sum(ga * att_ref[g, :, lanes].astype(f32), axis=1, keepdims=True)
            lane = lax.broadcasted_iota(jnp.int32, (block, HV), 1)
            denom = jnp.where(lane == 0, -dots * inverse, 0.0).astype(bf16)
            gn[g, h, :, :HV] = numer
            gn[g, h, :, HV:] = denom
            phi = (features(qkv_ref[g, :, 0:width], h, *tables) * at_head).astype(bf16)
            send_state[g, h] = dot_tn(phi, numer)[:STATE].astype(bf16)
            send_sum[g, h : h + 1, :] = dot_tn(denom, phi)[0:1]

        @pl.when(place == count - 1)
        def _():
            send(g)

        return none

    lax.fori_loop(0, groups, summarize, 0)
    fill.wait()
    ring.start_cross()
    ring.start_near()
    rows_sum.over_seq()

    def join(g, none):
        for copy in hop(g):
            copy.wait_recv()
        segr = segr_ref[g]
        mark = recv_sum[g, heads : heads + 1, 0:1]
        head, tail = segr[:, 0:1], segr[:, block - 1 : block]
        whole = ((head == tail) & (head == mark)).astype(f32)
        for h in range(heads):
            send_state[g, h] = (
                send_state[g, h].astype(f32) + whole * recv_state[g, h].astype(f32)
            ).astype(bf16)
            send_sum[g, h : h + 1, :] = (
                send_sum[g, h : h + 1, :] + whole * recv_sum[g, h : h + 1, :]
            )
        send(g)
        return none

    def pull(g, none):
        segc, segr = segc_ref[g], segr_ref[g]
        allowed = allowed_of(segc, segr)
        query_all = qkv_ref[g, :, 0:width]
        key_all = qkv_ref[g, :, width : 2 * width]
        carried = (segc == csum_ref[g, heads : heads + 1, 0:1]).astype(f32)
        dquery = jnp.zeros((block, width), f32)
        dkey_sum = jnp.zeros((block, width), f32)
        for h in range(heads):
            query, key = only_head(query_all, h), only_head(key_all, h)
            value = qkv_ref[g, :, 2 * width + h * HV : 2 * width + (h + 1) * HV]
            wide = jnp.concatenate([value, jnp.ones_like(value)], axis=1)
            both = gn[g, h]
            c = dot_nt(query, key_all)
            kernel = jnp.where(allowed, 1.0 + c * (0.25 + c * 0.03125), 0.0).astype(bf16)
            grad = jnp.where(allowed, dot_nt(both, wide), 0.0)
            grad_c = (grad * (0.25 + c * 0.0625)).astype(bf16)
            dvalue[g, h] = dot_tn(kernel, both[:, :HV])
            dkey_sum = dkey_sum + dot_tn(grad_c, query)
            dquery = dquery + dot(grad_c, key)
            state = padded_state(carry_ref[g, h])
            gphi = dot_nt(both[:, :HV], state) + both[:, HV : HV + 1].astype(f32) * csum_ref[
                g, h : h + 1, :
            ]
            dquery = dquery + pull_features(gphi * carried, query_all, h, *tables)
        out_ref[g, :, 0:width] = dquery.astype(bf16)
        dkey[g] = dkey_sum

        @pl.when((place > 0) & (place < count - 1) & (g == count - 2 - place))
        def _():
            lax.fori_loop(0, groups, join, 0)

        return none

    lax.fori_loop(0, groups, pull, 0)
    ring.relay()
    rows_sum.over_feat()

    def carry_back(g, none):
        segc = segc_ref[g]
        key_all = qkv_ref[g, :, width : 2 * width]

        @pl.when(place == 0)
        def _():
            for copy in hop(g):
                copy.wait_recv()

        mark = recv_sum[g, heads : heads + 1, 0:1]
        later = (segc == mark).astype(f32)
        total = dkey[g]
        for h in range(heads):
            value = qkv_ref[g, :, 2 * width + h * HV : 2 * width + (h + 1) * HV]
            state = padded_state(recv_state[g, h])
            phi = (features(key_all, h, *tables) * later).astype(bf16)
            dv = dvalue[g, h] + dot(phi, state)
            out_ref[g, :, 2 * width + h * HV : 2 * width + (h + 1) * HV] = dv.astype(bf16)
            gphi = (dot_nt(value, state) + recv_sum[g, h : h + 1, :]) * later
            total = total + pull_features(gphi, key_all, h, *tables)
        out_ref[g, :, width : 2 * width] = total.astype(bf16)
        return none

    lax.fori_loop(0, groups, carry_back, 0)

    @pl.when(place > 0)
    def _():
        def finish(g, none):
            for copy in hop(g):
                copy.wait_send()
            return none

        lax.fori_loop(0, groups, finish, 0)

    ring.arrive()

    def add_up(rows, total):
        final_ref[rows, :] = (res_ref[rows, :] + total).astype(bf16)

    by_rows(ring, add_up)
    ring.finish()
    rows_sum.arrive()
    wide = heads * HV
    for p in range(rows_sum.parts):
        ograd_ref[:, p * wide : (p + 1) * wide] = rows_sum.shares[p].astype(f32)
    rows_sum.finish()


def whole_vmem(count):
    return [pl.BlockSpec(memory_space=pltpu.VMEM)] * count


def attention_forward(qkv, segc, segr, tables, cot_own, out_share, heads):
    groups, block, _ = qkv.shape
    count, dps = lax.axis_size("seq"), lax.axis_size("dp")
    others = max(dps - 1, 1)
    parts, rows_each, wide = out_share.shape
    dma = pltpu.SemaphoreType.DMA
    states = (groups, heads, STATE, HV)
    sums = (groups, 8, LANES)
    return pl.pallas_call(
        functools.partial(forward_kernel, count, dps, heads),
        out_shape=(
            jax.ShapeDtypeStruct((groups, block, heads * HV), bf16),
            jax.ShapeDtypeStruct((groups, block, heads * HV), f32),
            jax.ShapeDtypeStruct(states, bf16),
            jax.ShapeDtypeStruct(sums, f32),
            jax.ShapeDtypeStruct((groups,) + cot_own.shape, bf16),
            jax.ShapeDtypeStruct((parts, count, dps, rows_each, wide), bf16),
        ),
        in_specs=whole_vmem(6) + in_place(2),
        out_specs=tuple(whole_vmem(4) + in_place(2)),
        scratch_shapes=[
            pltpu.VMEM(states, bf16),
            pltpu.VMEM(sums, f32),
            pltpu.VMEM((groups, heads, block, 2 * HV), f32),
            dma((2, groups)),
            dma((2, groups)),
            dma((6,)),
            dma((6,)),
            dma((3,)),
            dma((3,)),
            dma((count - 1,)),
            dma((count - 1,)),
            dma((others, count)),
            dma((others, count)),
            dma((2,)),
        ],
        compiler_params=pltpu.CompilerParams(
            collective_id=0, has_side_effects=True, vmem_limit_bytes=40 << 20
        ),
        cost_estimate=pl.CostEstimate(flops=0, bytes_accessed=1 << 20, transcendentals=0),
        name="attention_forward",
    )(qkv, segc, segr, *tables, cot_own, out_share)


def attention_backward(
    qkv, segc, segr, tables, att, rden, carry, csum, ga, down, residual, out_term, heads
):
    groups, block, wide = qkv.shape
    count, dps = lax.axis_size("seq"), lax.axis_size("dp")
    rows_each = out_term.shape[3]
    states = (groups, heads, STATE, HV)
    sums = (groups, 8, LANES)
    return pl.pallas_call(
        functools.partial(backward_kernel, count, dps, heads),
        out_shape=(
            jax.ShapeDtypeStruct((groups, block, wide), bf16),
            jax.ShapeDtypeStruct(residual.shape, bf16),
            jax.ShapeDtypeStruct((rows_each, HEADS * HV), f32),
        ),
        in_specs=whole_vmem(11) + in_place(1) + whole_vmem(2),
        out_specs=tuple(whole_vmem(3)),
        scratch_shapes=[
            pltpu.VMEM((groups, heads, block, 2 * HV), bf16),
            pltpu.VMEM(states, bf16),
            pltpu.VMEM(sums, f32),
            pltpu.VMEM(states, bf16),
            pltpu.VMEM(sums, f32),
            pltpu.VMEM((groups, block, heads * FDIM), f32),
            pltpu.VMEM((groups, heads, block, HV), f32),
            pltpu.VMEM((groups,) + residual.shape, bf16),
            pltpu.VMEM((6, block // 2, residual.shape[1]), bf16),
            pltpu.SemaphoreType.DMA((2, groups)),
            pltpu.SemaphoreType.DMA((2, groups)),
            pltpu.SemaphoreType.DMA((6,)),
            pltpu.SemaphoreType.DMA((6,)),
            pltpu.SemaphoreType.DMA((1,)),
        ]
        + row_sum_scratch(out_term.shape),
        compiler_params=pltpu.CompilerParams(
            collective_id=1, has_side_effects=True, vmem_limit_bytes=48 << 20
        ),
        cost_estimate=pl.CostEstimate(flops=0, bytes_accessed=1 << 20, transcendentals=0),
        name="attention_backward",
    )(qkv, segc, segr, *tables, att, rden, carry, csum, ga, down, residual, out_term)


def peers(f):
    return 2 * (f // 2) + 1 - f % 2, (f + 2) % 4, 3 - f


def greet(targets):
    barrier = pltpu.get_barrier_semaphore()
    for target in targets:
        pl.semaphore_signal(barrier, inc=1, device_id=target, device_id_type=MESH)
    pl.semaphore_wait(barrier, len(targets))


def push(src, dst, send_sem, recv_sem, target):
    return pltpu.make_async_remote_copy(
        src_ref=src,
        dst_ref=dst,
        send_sem=send_sem,
        recv_sem=recv_sem,
        device_id=target,
        device_id_type=MESH,
    )


def square_targets(f):
    return [{"feat": p} for p in peers(f)]


class SquareGather:
    def __init__(self, slots, f, send_sem, recv_sem, own=None):
        side, above, across = peers(f)
        half = slots.shape[1] // 2
        first, second = pl.ds(0, half), pl.ds(half, half)

        def copy(i, slot, rows, to):
            ref = slots.at[slot, rows]
            src = ref if own is None or i > 3 else own.at[rows]
            return push(src, ref, send_sem.at[i], recv_sem.at[i], {"feat": to})

        self.direct = [
            copy(0, f, first, side),
            copy(1, f, second, above),
            copy(2, f, second, side),
            copy(3, f, first, above),
        ]
        self.forward = [copy(4, side, first, above), copy(5, above, second, side)]

    def start(self):
        for c in self.direct:
            c.start()

    def relay(self):
        self.direct[0].wait_recv()
        self.forward[0].start()
        self.direct[1].wait_recv()
        self.forward[1].start()

    def near(self):
        self.direct[2].wait_recv()
        self.direct[3].wait_recv()

    def far(self):
        for c in self.forward:
            c.wait_recv()

    def sent(self):
        for c in self.direct + self.forward:
            c.wait_send()

    def finish(self):
        self.near()
        self.far()
        self.sent()


class SquareSum:
    def __init__(self, part, land, f, send_sem, recv_sem):
        self.side, self.above, self.across = peers(f)
        self.f, self.part, self.land = f, part, land
        self.half = part.shape[1] // 2
        first, second = pl.ds(0, self.half), pl.ds(self.half, self.half)

        def copy(i, slot, rows, to):
            return push(
                part.at[slot, rows], land.at[i], send_sem.at[i], recv_sem.at[i], {"feat": to}
            )

        self.cross = [copy(0, self.across, first, self.side), copy(1, self.across, second, self.above)]
        self.near = [copy(2, self.side, first, self.side), copy(3, self.above, second, self.above)]
        self.late = [copy(4, self.above, first, self.above), copy(5, self.side, second, self.side)]

    def start_cross(self):
        for c in self.cross:
            c.start()

    def add_rows(self, slot, base, landed):
        step = 32

        def one(i, none):
            rows = pl.ds(pl.multiple_of(base + i * step, step), step)
            came = self.land[landed, pl.ds(pl.multiple_of(i * step, step), step), :]
            self.part[slot, rows, :] = (
                self.part[slot, rows, :].astype(f32) + came.astype(f32)
            ).astype(bf16)
            return none

        lax.fori_loop(0, self.half // step, one, 0)

    def start_near(self):
        for c in self.near:
            c.start()

    def relay(self):
        self.cross[0].wait_recv()
        self.add_rows(self.above, 0, 0)
        self.late[0].start()
        self.cross[1].wait_recv()
        self.add_rows(self.side, self.half, 1)
        self.late[1].start()

    def arrive(self):
        for c in self.near + self.late:
            c.wait_recv()

    def total(self, half, rows):
        base = half * self.half
        own = self.part[self.f, pl.ds(pl.multiple_of(base + rows.start, 16), rows.size), :]
        near = self.land[2 + half, rows, :]
        late = self.land[4 + half, rows, :]
        return own.astype(f32) + near.astype(f32) + late.astype(f32)

    def finish(self):
        for c in self.cross + self.near + self.late:
            c.wait_send()


class RowSum:
    def __init__(self, term, acc, shares, lands, sems, f, s, d, seqs, dps):
        self.term, self.acc, self.shares, self.lands = term, acc, shares, lands
        self.f, self.s, self.d = f, s, d
        self.parts, self.seqs = term.shape[0], seqs
        columns = [lax.rem(s + k, seqs) for k in range(1, seqs)]
        others = [lax.rem(d + k, dps) for k in range(1, dps)]
        d_send, d_recv, z_send, z_recv, a_send, a_recv = sems
        self.one = [
            push(term.at[:, :, o], lands[0].at[k], d_send.at[k], d_recv.at[k], {"dp": o})
            for k, o in enumerate(others)
        ]
        self.two = [
            push(acc.at[c], lands[1].at[k], z_send.at[k], z_recv.at[k], {"seq": c})
            for k, c in enumerate(columns)
        ]
        self.three = [
            push(lands[2].at[p], shares.at[f], a_send.at[i], a_recv.at[i], {"feat": p})
            for i, p in enumerate(peers(f))
        ]

    def start(self):
        for c in self.one:
            c.start()

    def over_seq(self):
        for c in self.one:
            c.wait_recv()

        def one(i, none):
            p, c = i // self.seqs, lax.rem(i, self.seqs)
            total = self.term[p, c, self.d].astype(f32)
            for k in range(len(self.one)):
                total = total + self.lands[0][k, p, c].astype(f32)
            self.acc[c, p] = total.astype(bf16)
            return none

        lax.fori_loop(0, self.parts * self.seqs, one, 0)
        for c in self.two:
            c.start()

    def over_feat(self):
        for c in self.two:
            c.wait_recv()

        def one(p, none):
            total = self.acc[self.s, p].astype(f32)
            for k in range(len(self.two)):
                total = total + self.lands[1][k, p].astype(f32)
            self.lands[2][p] = total.astype(bf16)
            return none

        lax.fori_loop(0, self.parts, one, 0)
        self.shares[self.f] = self.lands[2][self.f]
        for c in self.three:
            c.start()

    def arrive(self):
        for c in self.three:
            c.wait_recv()

    def finish(self):
        for c in self.one + self.two + self.three:
            c.wait_send()


def row_sum_scratch(shape):
    parts, seqs, dps, rows, wide = shape
    others = max(dps - 1, 1)
    dma = pltpu.SemaphoreType.DMA
    return [
        pltpu.VMEM((parts, rows, wide), bf16),
        pltpu.VMEM((seqs, parts, rows, wide), bf16),
        pltpu.VMEM((others, parts, seqs, rows, wide), bf16),
        pltpu.VMEM((seqs - 1, parts, rows, wide), bf16),
        pltpu.VMEM((parts, rows, wide), bf16),
        dma((others,)),
        dma((others,)),
        dma((seqs - 1,)),
        dma((seqs - 1,)),
        dma((3,)),
        dma((3,)),
    ]


def row_sum(term, scratch, f, s, d, seqs, dps):
    shares, acc = scratch[:2]
    return RowSum(term, acc, shares, scratch[2:5], scratch[5:], f, s, d, seqs, dps)


def opening_kernel(
    seqs,
    dps,
    tok_ref,
    query_ref,
    key_ref,
    value_ref,
    one_ref,
    two_ref,
    x_ref,
    w_ref,
    g_ref,
    pack,
    tile,
    x_send,
    x_recv,
    a_send,
    a_recv,
    z_send,
    z_recv,
    d_send,
    d_recv,
    local_sem,
):
    f, s, d = lax.axis_index("feat"), lax.axis_index("seq"), lax.axis_index("dp")
    parts, rows_each = pack.shape[0], pack.shape[1]
    near = peers(f)
    columns = [lax.rem(s + k, seqs) for k in range(1, seqs)]
    others = [lax.rem(d + k, dps) for k in range(1, dps)]
    stay = pltpu.make_async_copy(tok_ref, x_ref.at[f], local_sem.at[0])
    stay.start()
    greet(
        square_targets(f) + [{"seq": c} for c in columns] + [{"dp": o} for o in others]
    )
    gather = SquareGather(x_ref, f, x_send, x_recv, tok_ref)
    gather.start()

    first = 0
    for ref in (query_ref, key_ref, value_ref):
        each = ref.shape[1] // parts
        for p in range(parts):
            pack[p, :, first : first + each] = ref[:, p * each : (p + 1) * each]
        first += each
    tile[...] = jnp.zeros_like(tile)
    tile[0:1, :rows_each] = one_ref[...].astype(f32)
    tile[1:2, :rows_each] = two_ref[...].astype(f32)
    outs = (w_ref, g_ref)
    own = [
        pltpu.make_async_copy(pack.at[f], w_ref.at[f, s, d], local_sem.at[1]),
        pltpu.make_async_copy(tile, g_ref.at[f, s, d], local_sem.at[2]),
    ]
    for c in own:
        c.start()
    shares = [
        [
            push(pack.at[p], w_ref.at[f, s, d], a_send.at[0, i], a_recv.at[0, i], {"feat": p}),
            push(tile, g_ref.at[f, s, d], a_send.at[1, i], a_recv.at[1, i], {"feat": p}),
        ]
        for i, p in enumerate(near)
    ]
    for pair in shares:
        for c in pair:
            c.start()
    for c in own:
        c.wait()

    chunks = (f,) + near

    def to_column(n, k):
        return [
            push(
                ref.at[chunks[n], s, d],
                ref.at[chunks[n], s, d],
                z_send.at[j, k - 1, n],
                z_recv.at[j, k - 1, n],
                {"seq": columns[k - 1]},
            )
            for j, ref in enumerate(outs)
        ]

    def to_sibling(n, k):
        back = lax.rem(s + seqs - k, seqs)
        return [
            push(
                ref.at[chunks[n], back, d],
                ref.at[chunks[n], back, d],
                d_send.at[j, o, k, n],
                d_recv.at[j, o, k, n],
                {"dp": other},
            )
            for j, ref in enumerate(outs)
            for o, other in enumerate(others)
        ]

    def start_all(copies):
        for c in copies:
            c.start()

    for n in range(parts):
        if n:
            for c in shares[n - 1]:
                c.wait_recv()
        for k in range(1, seqs):
            start_all(to_column(n, k))
        start_all(to_sibling(n, 0))
    for n in range(parts):
        for k in range(1, seqs):
            for c in to_column(n, k):
                c.wait_recv()
            start_all(to_sibling(n, k))
    gather.relay()
    for n in range(parts):
        for k in range(seqs):
            for c in to_sibling(n, k):
                c.wait_recv()
    for n in range(parts):
        for k in range(seqs):
            for c in to_sibling(n, k):
                c.wait_send()
        for k in range(1, seqs):
            for c in to_column(n, k):
                c.wait_send()
    for pair in shares:
        for c in pair:
            c.wait_send()
    stay.wait()
    gather.finish()


def in_place(count):
    return [pl.BlockSpec(memory_space=pl.ANY)] * count


def opening(own, w_query, w_key, w_value, gain_one, gain_two):
    parts, seqs, dps = (lax.axis_size(a) for a in ALL)
    block, width = own.shape
    rows_each = w_query.shape[0]
    wide = (w_query.shape[1] + w_key.shape[1] + w_value.shape[1]) // parts
    others = max(dps - 1, 1)
    dma = pltpu.SemaphoreType.DMA
    x_all, w_all, g_all = pl.pallas_call(
        functools.partial(opening_kernel, seqs, dps),
        out_shape=(
            jax.ShapeDtypeStruct((parts, block, width), bf16),
            jax.ShapeDtypeStruct((parts, seqs, dps, rows_each, wide), bf16),
            jax.ShapeDtypeStruct((parts, seqs, dps, 8, HV), f32),
        ),
        in_specs=in_place(1) + whole_vmem(5),
        out_specs=tuple(in_place(3)),
        scratch_shapes=[
            pltpu.VMEM((parts, rows_each, wide), bf16),
            pltpu.VMEM((8, HV), f32),
            dma((6,)),
            dma((6,)),
            dma((2, 3)),
            dma((2, 3)),
            dma((2, seqs - 1, parts)),
            dma((2, seqs - 1, parts)),
            dma((2, others, seqs, parts)),
            dma((2, others, seqs, parts)),
            dma((3,)),
        ],
        compiler_params=pltpu.CompilerParams(collective_id=2, has_side_effects=True),
        cost_estimate=pl.CostEstimate(flops=0, bytes_accessed=1 << 20, transcendentals=0),
        name="opening",
    )(own, w_query, w_key, w_value, gain_one, gain_two)
    gains = g_all[..., :2, :rows_each].transpose(3, 0, 1, 2, 4).reshape(2, width)
    return x_all, w_all.reshape(width, wide), gains


def inverse_rms(values):
    return lax.rsqrt(jnp.mean(values * values, axis=-1, keepdims=True) + epsilon)


def norm_back(grad, unit, inverse, gain):
    scaled = grad * gain
    return (scaled - unit * jnp.mean(scaled * unit, axis=-1, keepdims=True)) * inverse


def product_tiles(part, slot, pairs, tile):
    def one(i, none):
        cols = pl.ds(pl.multiple_of(i * tile, tile), tile)
        total = None
        for rows, weights in pairs:
            term = dot_nt(rows[slot], weights[cols, :])
            total = term if total is None else total + term
        part[slot, :, cols] = total.astype(bf16)
        return none

    lax.fori_loop(0, part.shape[2] // tile, one, 0)


def summed_products(part, land, f, pairs, send_sem, recv_sem, beside=None):
    side, above, across = peers(f)
    ring = SquareSum(part, land, f, send_sem, recv_sem)
    product_tiles(part, across, pairs, 512)
    ring.start_cross()
    product_tiles(part, side, pairs, 512)
    product_tiles(part, above, pairs, 512)
    ring.start_near()
    product_tiles(part, f, pairs, 512)
    if beside is not None:
        beside()
    ring.relay()
    ring.arrive()
    return ring


def by_rows(ring, body, step=16):
    for half in (0, 1):

        def one(i, none):
            start = pl.multiple_of(i * step, step)
            rows = pl.ds(pl.multiple_of(half * ring.half + i * step, step), step)
            body(rows, ring.total(half, pl.ds(start, step)))
            return none

        lax.fori_loop(0, ring.half // step, one, 0)


def branch_kernel(
    att_ref, w_ref, tok_ref, gain_ref, rows_ref, res_ref, part, land, s_send, s_recv, g_send, g_recv
):
    f = lax.axis_index("feat")
    greet(square_targets(f))
    ring = summed_products(part, land, f, [(att_ref, w_ref)], s_send, s_recv)

    def finish_rows(rows, total):
        residual = tok_ref[rows, :].astype(f32) + total
        res_ref[rows, :] = residual
        rows_ref[f, rows, :] = (residual * inverse_rms(residual) * gain_ref[...]).astype(bf16)

    by_rows(ring, finish_rows)
    gather = SquareGather(rows_ref, f, g_send, g_recv)
    gather.start()
    ring.finish()
    gather.relay()
    gather.finish()


def square_scratch(parts, block, width):
    dma = pltpu.SemaphoreType.DMA
    return [
        pltpu.VMEM((parts, block, width), bf16),
        pltpu.VMEM((6, block // 2, width), bf16),
        dma((6,)),
        dma((6,)),
    ]


def branch_step(att, out_w, own, gain_two):
    parts, block, _ = att.shape
    width = own.shape[1]
    dma = pltpu.SemaphoreType.DMA
    return pl.pallas_call(
        branch_kernel,
        out_shape=(
            jax.ShapeDtypeStruct((parts, block, width), bf16),
            jax.ShapeDtypeStruct((block, width), f32),
        ),
        in_specs=whole_vmem(4),
        out_specs=tuple(whole_vmem(2)),
        scratch_shapes=square_scratch(parts, block, width) + [dma((6,)), dma((6,))],
        compiler_params=pltpu.CompilerParams(
            collective_id=3, has_side_effects=True, vmem_limit_bytes=48 << 20
        ),
        cost_estimate=pl.CostEstimate(flops=0, bytes_accessed=1 << 20, transcendentals=0),
        name="branch_step",
    )(att, out_w, own, gain_two)


def rows_back_kernel(
    gg_ref,
    gu_ref,
    wg_ref,
    wu_ref,
    res_ref,
    cot_ref,
    gain_ref,
    mixed_hbm,
    wd_hbm,
    wo_hbm,
    all_ref,
    gres_ref,
    gsum_ref,
    down_ref,
    ga_ref,
    part,
    land,
    mixed,
    wd,
    wo,
    s_send,
    s_recv,
    g_send,
    g_recv,
    local_sem,
):
    f = lax.axis_index("feat")
    fills = [
        pltpu.make_async_copy(src, dst, local_sem.at[i])
        for i, (src, dst) in enumerate(((mixed_hbm, mixed), (wd_hbm, wd), (wo_hbm, wo)))
    ]
    for c in fills:
        c.start()
    greet(square_targets(f))
    pairs = [(gg_ref, wg_ref), (gu_ref, wu_ref)]

    def down_products():
        for c in fills:
            c.wait()
        for p in range(part.shape[0]):
            product_tiles(down_ref, p, [(mixed, wd)], 512)

    ring = summed_products(part, land, f, pairs, s_send, s_recv, down_products)
    gsum_ref[...] = jnp.zeros_like(gsum_ref)

    def finish_rows(rows, grad):
        residual = res_ref[rows, :]
        inverse = inverse_rms(residual)
        unit = residual * inverse
        gsum_ref[...] += jnp.sum(grad * unit, axis=0, keepdims=True)
        grad_res = cot_ref[rows, :].astype(f32) + norm_back(grad, unit, inverse, gain_ref[...])
        gres_ref[rows, :] = grad_res
        all_ref[f, rows, :] = grad_res.astype(bf16)

    by_rows(ring, finish_rows)
    gather = SquareGather(all_ref, f, g_send, g_recv)
    gather.start()
    ring.finish()
    side, above, across = peers(f)

    def attended_grad(slot):
        ga_ref[slot] = dot(all_ref[slot], wo[...])

    attended_grad(f)
    gather.relay()
    gather.near()
    attended_grad(side)
    attended_grad(above)
    gather.far()
    attended_grad(across)
    gather.sent()


def rows_back(
    grad_gate, grad_up, gate_w, up_w, residual, cot_own, gain_two, mixed, down_w, out_w
):
    parts, block, hidden = grad_gate.shape
    width = residual.shape[1]
    dma = pltpu.SemaphoreType.DMA
    return pl.pallas_call(
        rows_back_kernel,
        out_shape=(
            jax.ShapeDtypeStruct((parts, block, width), bf16),
            jax.ShapeDtypeStruct((block, width), f32),
            jax.ShapeDtypeStruct((1, width), f32),
            jax.ShapeDtypeStruct((parts, block, width), bf16),
            jax.ShapeDtypeStruct((parts, block, out_w.shape[1]), f32),
        ),
        in_specs=whole_vmem(7) + in_place(3),
        out_specs=tuple(whole_vmem(5)),
        scratch_shapes=square_scratch(parts, block, width)[:2]
        + [
            pltpu.VMEM((parts, block, hidden), bf16),
            pltpu.VMEM((width, hidden), bf16),
            pltpu.VMEM(out_w.shape, bf16),
        ]
        + [dma((6,))] * 4
        + [dma((3,))],
        compiler_params=pltpu.CompilerParams(
            collective_id=4, has_side_effects=True, vmem_limit_bytes=60 << 20
        ),
        cost_estimate=pl.CostEstimate(flops=0, bytes_accessed=1 << 20, transcendentals=0),
        name="rows_back",
    )(grad_gate, grad_up, gate_w, up_w, residual, cot_own, gain_two, mixed, down_w, out_w)


def closing_kernel(
    seqs,
    dps,
    dqkv_ref,
    w_ref,
    tok_ref,
    gres_ref,
    gain_ref,
    gsum_two_ref,
    term_ref,
    x_ref,
    tile_ref,
    query_ref,
    key_ref,
    value_ref,
    part,
    land,
    s_send,
    s_recv,
    gsum,
    cut,
    came,
    mid,
    tail,
    c_send,
    c_recv,
    d_send,
    d_recv,
    *sum_scratch,
):
    f, s, d = lax.axis_index("feat"), lax.axis_index("seq"), lax.axis_index("dp")
    parts = 4
    others = [lax.rem(d + k, dps) for k in range(1, dps)]
    circle = [
        (lax.rem(f + i, parts), lax.rem(s + j, seqs))
        for i in range(parts)
        for j in range(seqs)
        if i or j
    ]
    greet(
        [{"feat": a, "seq": b} for a, b in circle] + [{"dp": o} for o in others]
    )
    rows_sum = row_sum(term_ref, sum_scratch, f, s, d, seqs, dps)
    rows_sum.start()
    ring = summed_products(
        part, land, f, [(dqkv_ref, w_ref)], s_send, s_recv, rows_sum.over_seq
    )
    gsum[...] = jnp.zeros_like(gsum)

    def finish_rows(rows, grad):
        values = tok_ref[rows, :].astype(f32)
        inverse = inverse_rms(values)
        unit = values * inverse
        gsum[...] += jnp.sum(grad * unit, axis=0, keepdims=True)
        x_ref[rows, :] = gres_ref[rows, :] + norm_back(grad, unit, inverse, gain_ref[...])

    by_rows(ring, finish_rows)
    rows_sum.over_feat()
    ring.finish()

    lanes = gsum.shape[1] // (parts * seqs)
    cut[...] = jnp.zeros_like(cut)
    for k in range(parts * seqs):
        cut[k, 0:1, :] = gsum[:, k * lanes : (k + 1) * lanes]
        cut[k, 1:2, :] = gsum_two_ref[:, k * lanes : (k + 1) * lanes]
    place = f * seqs + s
    sends = []
    for i, (a, b) in enumerate(circle):
        sends.append(
            push(
                cut.at[a * seqs + b],
                came.at[i],
                c_send.at[i],
                c_recv.at[i],
                {"feat": a, "seq": b},
            )
        )
    for c in sends:
        c.start()
    total = cut[place]
    for c in sends:
        c.wait_recv()
    for i in range(len(circle)):
        total = total + came[i]
    mid[...] = total
    last = [
        push(mid, tail.at[k], d_send.at[k], d_recv.at[k], {"dp": o})
        for k, o in enumerate(others)
    ]
    for c in last:
        c.start()
    for c in last:
        c.wait_recv()
    for k in range(len(others)):
        total = total + tail[k]
    tile_ref[...] = total
    rows_sum.arrive()
    first = 0
    for ref in (query_ref, key_ref, value_ref):
        each = ref.shape[1] // parts
        for p in range(parts):
            piece = rows_sum.shares[p, :, first : first + each]
            ref[:, p * each : (p + 1) * each] = piece.astype(f32)
        first += each
    rows_sum.finish()
    for c in sends + last:
        c.wait_send()


def closing(dqkv, qkv_w, own, grad_residual, gain_one, gain_two_sum, qkv_term):
    parts, seqs, dps = (lax.axis_size(a) for a in ALL)
    block, width = own.shape
    others = max(dps - 1, 1)
    lanes = width // (parts * seqs)
    circle = parts * seqs - 1
    rows_each = qkv_term.shape[3]
    dma = pltpu.SemaphoreType.DMA
    return pl.pallas_call(
        functools.partial(closing_kernel, seqs, dps),
        out_shape=(
            jax.ShapeDtypeStruct((block, width), f32),
            jax.ShapeDtypeStruct((8, lanes), f32),
            jax.ShapeDtypeStruct((rows_each, HEADS * FDIM), f32),
            jax.ShapeDtypeStruct((rows_each, HEADS * FDIM), f32),
            jax.ShapeDtypeStruct((rows_each, HEADS * HV), f32),
        ),
        in_specs=whole_vmem(7),
        out_specs=tuple(whole_vmem(5)),
        scratch_shapes=square_scratch(parts, block, width)
        + [
            pltpu.VMEM((1, width), f32),
            pltpu.VMEM((parts * seqs, 8, lanes), f32),
            pltpu.VMEM((circle, 8, lanes), f32),
            pltpu.VMEM((8, lanes), f32),
            pltpu.VMEM((others, 8, lanes), f32),
            dma((circle,)),
            dma((circle,)),
            dma((others,)),
            dma((others,)),
        ]
        + row_sum_scratch(qkv_term.shape),
        compiler_params=pltpu.CompilerParams(
            collective_id=5, has_side_effects=True, vmem_limit_bytes=48 << 20
        ),
        cost_estimate=pl.CostEstimate(flops=0, bytes_accessed=1 << 20, transcendentals=0),
        name="closing",
    )(dqkv, qkv_w, own, grad_residual, gain_one, gain_two_sum, qkv_term)


def local(
    tokens,
    segments,
    norm1_gain,
    norm2_gain,
    w_query,
    w_key,
    w_value,
    w_out,
    w_gate,
    w_up,
    w_down,
    cotangent,
):
    parts = lax.axis_size("feat")
    heads = HEADS // parts
    block, width = tokens.shape[2], tokens.shape[3]
    rows_total = parts * block
    rows_each = w_query.shape[0]
    own = tokens.reshape(block, width)
    cot_own = cotangent.reshape(block, width)

    out_share = w_out.T.reshape(rows_each, parts, heads * HV).transpose(1, 0, 2)
    x_all, qkv_w, gains = opening(
        own, w_query, w_key, w_value, norm1_gain[None], norm2_gain[None]
    )
    qkv_width = qkv_w.shape[1]
    x_all, w_gate, w_up = lax.optimization_barrier((x_all, w_gate, w_up))
    gate_w = lax.all_gather(w_gate, ("seq", "dp"), axis=0, tiled=True)
    up_w = lax.all_gather(w_up, ("seq", "dp"), axis=0, tiled=True)
    gain_one, gain_two = gains[0:1], gains[1:2]

    x_wide = x_all.astype(f32).reshape(rows_total, width)
    normed = (x_wide * inverse_rms(x_wide) * gain_one).astype(bf16)
    qkv = dot(normed, qkv_w).astype(bf16).reshape(parts, block, qkv_width)
    qkv, w_down = lax.optimization_barrier((qkv, w_down))
    down_w = lax.all_gather(w_down.T, ("seq", "dp"), axis=0, tiled=True)
    segment = segments.reshape(parts, block).astype(f32)
    segc, segr = segment[:, :, None], segment[:, None, :]
    tables = feature_tables(heads)
    att, rden, carry, csum, cot_all, out_w = attention_forward(
        qkv, segc, segr, tables, cot_own, out_share, heads
    )
    out_w = out_w.reshape(width, heads * HV)
    cot_all = cot_all.reshape(rows_total, width)
    rows_all, residual = branch_step(att, out_w, own, gain_two)
    rows_all = rows_all.reshape(rows_total, width)

    gate_out = dot(rows_all, gate_w)
    up_out = dot(rows_all, up_w)
    sig = jax.nn.sigmoid(gate_out)
    silu = gate_out * sig
    mixed = (silu * up_out).astype(bf16)
    down_term = dot_tn(cot_all, mixed).astype(bf16)
    mixed, cot_late, down_term = lax.optimization_barrier((mixed, cot_all, down_term))
    grad_mixed = dot(cot_late, down_w)
    grad_gate = (grad_mixed * up_out * sig * (1.0 + gate_out * (1.0 - sig))).astype(bf16)
    grad_up = (grad_mixed * silu).astype(bf16)

    def summed(term):
        return lax.psum_scatter(term, ("seq", "dp"), scatter_dimension=0, tiled=True)

    gate_term = dot_tn(rows_all, grad_gate).astype(bf16)
    up_term = dot_tn(rows_all, grad_up).astype(bf16)
    grad_gate, grad_up, gate_term, up_term = lax.optimization_barrier(
        (grad_gate, grad_up, gate_term, up_term)
    )
    down_sum, gate_sum, up_sum = summed(down_term), summed(gate_term), summed(up_term)

    by_device = (parts, block, -1)
    branch_all, grad_residual, gain_two_sum, down, ga = rows_back(
        grad_gate.reshape(by_device),
        grad_up.reshape(by_device),
        gate_w,
        up_w,
        residual,
        cot_own,
        gain_two,
        mixed.reshape(by_device),
        down_w,
        out_w,
    )
    branch_all = branch_all.reshape(rows_total, width)
    by_row = (parts, lax.axis_size("seq"), lax.axis_size("dp"), rows_each, -1)
    out_term = dot_tn(branch_all, att.reshape(rows_total, heads * HV)).astype(bf16)
    dqkv, output, out_grad = attention_backward(
        qkv,
        segc,
        segr,
        tables,
        att,
        rden,
        carry,
        csum,
        ga,
        down,
        residual,
        out_term.reshape(by_row),
        heads,
    )
    qkv_term = dot_tn(normed, dqkv.reshape(rows_total, qkv_width)).astype(bf16)
    x_grad, gain_grads, query_grad, key_grad, value_grad = closing(
        dqkv, qkv_w, own, grad_residual, gain_one, gain_two_sum, qkv_term.reshape(by_row)
    )
    gain_each = gain_grads.shape[1] // lax.axis_size("dp")
    gain_grads = lax.dynamic_slice_in_dim(
        gain_grads, lax.axis_index("dp") * gain_each, gain_each, axis=1
    )
    return (
        output.reshape(tokens.shape),
        x_grad.reshape(tokens.shape),
        gain_grads[0],
        gain_grads[1],
        query_grad,
        key_grad,
        value_grad,
        out_grad.T,
        gate_sum.astype(f32),
        up_sum.astype(f32),
        down_sum.T.astype(f32),
    )


def solution(mesh):
    placed = (
        P("feat", "dp", "seq", None),
        P(None, "dp", "seq"),
        P(ALL),
        P(ALL),
        P(ALL, None),
        P(ALL, None),
        P(ALL, None),
        P(None, ALL),
        P(("seq", "dp"), "feat"),
        P(("seq", "dp"), "feat"),
        P("feat", ("seq", "dp")),
        P("feat", "dp", "seq", None),
    )
    return jax.shard_map(
        local,
        mesh=mesh,
        in_specs=placed,
        out_specs=(
            P("feat", "dp", "seq", None),
            P("feat", "dp", "seq", None),
            P(ALL),
            P(ALL),
            P(ALL, None),
            P(ALL, None),
            P(ALL, None),
            P(None, ALL),
            P(("seq", "dp"), "feat"),
            P(("seq", "dp"), "feat"),
            P("feat", ("seq", "dp")),
        ),
        check_vma=False,
    )
```

```python
import functools

import jax
import jax.numpy as jnp
import numpy as np
from jax import lax
from jax.experimental import pallas as pl
from jax.experimental.pallas import tpu as pltpu
from jax.sharding import PartitionSpec as P

HEADS = 16
FDIM = 16
HV = 128
STATE = 160
LANES = 256
epsilon = 1e-05
MESH = pl.DeviceIdType.MESH
ALL = ("feat", "seq", "dp")
f32 = jnp.float32
bf16 = jnp.bfloat16


def dot(a, b):
    return lax.dot_general(a, b, (((1,), (0,)), ((), ())), preferred_element_type=f32)


def dot_nt(a, b):
    return lax.dot_general(a, b, (((1,), (1,)), ((), ())), preferred_element_type=f32)


def dot_tn(a, b):
    return lax.dot_general(a, b, (((0,), (0,)), ((), ())), preferred_element_type=f32)


def feature_tables(heads):
    pairs = [(i, j) for i in range(FDIM) for j in range(i, FDIM)]
    left = np.zeros((heads, heads * FDIM, LANES), np.float32)
    right = np.zeros((heads, heads * FDIM, LANES), np.float32)
    rows = np.zeros((8, LANES), np.float32)
    for h in range(heads):
        for p, (i, j) in enumerate(pairs):
            left[h, h * FDIM + i, p] = 1.0
            right[h, h * FDIM + j, p] = 1.0
            rows[2, p] = 0.25 / 2.0**0.5 if i == j else 0.25
        for i in range(FDIM):
            p = len(pairs) + i
            left[h, h * FDIM + i, p] = 1.0
            rows[1, p] = 1.0
            rows[2, p] = 0.5
        p = len(pairs) + FDIM
        rows[0, p] = rows[1, p] = rows[2, p] = 1.0
    return jnp.asarray(left, bf16), jnp.asarray(right, bf16), jnp.asarray(rows)


def both_sides(entries, h, left_ref, right_ref, rows_ref):
    one = dot(entries, left_ref[h]) + rows_ref[0:1, :]
    two = dot(entries, right_ref[h]) + rows_ref[1:2, :]
    return one, two * rows_ref[2:3, :]


def features(entries, h, left_ref, right_ref, rows_ref):
    one, two = both_sides(entries, h, left_ref, right_ref, rows_ref)
    return one * two


def pull_features(grad, entries, h, left_ref, right_ref, rows_ref):
    one, two = both_sides(entries, h, left_ref, right_ref, rows_ref)
    scaled = rows_ref[2:3, :]
    return dot_nt((grad * two).astype(bf16), left_ref[h]) + dot_nt(
        (grad * one * scaled).astype(bf16), right_ref[h]
    )


def only_head(entries, h):
    lane = lax.broadcasted_iota(jnp.int32, entries.shape, 1)
    keep = (lane >= h * FDIM) & (lane < (h + 1) * FDIM)
    return jnp.where(keep, entries, jnp.zeros_like(entries))


def padded_state(state):
    return jnp.concatenate([state, jnp.zeros((LANES - STATE, state.shape[1]), state.dtype)], 0)


def allowed_of(segc, segr):
    block = segc.shape[0]
    row = lax.broadcasted_iota(jnp.int32, (block, block), 0)
    col = lax.broadcasted_iota(jnp.int32, (block, block), 1)
    return (row >= col) & (segc == segr)


def forward_kernel(
    count,
    heads,
    qkv_ref,
    segc_ref,
    segr_ref,
    left_ref,
    right_ref,
    rows_ref,
    cot_ref,
    att_ref,
    rden_ref,
    carry_ref,
    csum_ref,
    cots_ref,
    send_state,
    send_sum,
    part,
    send_sem,
    recv_sem,
    f_send,
    f_recv,
    local_sem,
):
    place, f = lax.axis_index("seq"), lax.axis_index("feat")
    groups, block = qkv_ref.shape[0], qkv_ref.shape[1]
    width = heads * FDIM
    tables = (left_ref, right_ref, rows_ref)

    def hop(g):
        target = {"seq": lax.rem(place + 1, count)}
        return [
            pltpu.make_async_remote_copy(
                src_ref=src.at[g],
                dst_ref=dst.at[g],
                send_sem=send_sem.at[i, g],
                recv_sem=recv_sem.at[i, g],
                device_id=target,
                device_id_type=MESH,
            )
            for i, (src, dst) in enumerate(((send_state, carry_ref), (send_sum, csum_ref)))
        ]

    def send(g):
        for copy in hop(g):
            copy.start()

    chain = [lax.rem(place + 1, count), lax.rem(place + count - 1, count)]
    stay = pltpu.make_async_copy(cot_ref, cots_ref.at[f], local_sem.at[0])
    stay.start()
    greet(square_targets(f) + [{"seq": c} for c in chain])
    gather = SquareGather(cots_ref, f, f_send, f_recv, cot_ref)
    gather.start()

    @pl.when(place == 0)
    def _():
        carry_ref[...] = jnp.zeros_like(carry_ref)
        csum_ref[...] = jnp.full_like(csum_ref, -1.0)

    def summarize(g, none):
        segc, segr = segc_ref[g], segr_ref[g]
        tail = segr[:, block - 1 : block]
        at_tail = (segc == tail).astype(f32)
        send_sum[g, heads : heads + 1, :] = jnp.broadcast_to(tail, (1, LANES))
        for h in range(heads):
            key = qkv_ref[g, :, width : 2 * width]
            value = qkv_ref[g, :, 2 * width + h * HV : 2 * width + (h + 1) * HV]
            phi = (features(key, h, *tables) * at_tail).astype(bf16)
            send_state[g, h] = dot_tn(phi, value)[:STATE].astype(bf16)
            ones = jnp.ones((8, block), bf16)
            send_sum[g, h : h + 1, :] = dot(ones, phi)[0:1]

        @pl.when(place == 0)
        def _():
            send(g)

        return none

    lax.fori_loop(0, groups, summarize, 0)
    def join(g, none):
        for copy in hop(g):
            copy.wait_recv()
        segr = segr_ref[g]
        mark = csum_ref[g, heads : heads + 1, 0:1]
        head, tail = segr[:, 0:1], segr[:, block - 1 : block]
        whole = ((head == tail) & (head == mark)).astype(f32)
        for h in range(heads):
            send_state[g, h] = (
                send_state[g, h].astype(f32) + whole * carry_ref[g, h].astype(f32)
            ).astype(bf16)
            send_sum[g, h : h + 1, :] = (
                send_sum[g, h : h + 1, :] + whole * csum_ref[g, h : h + 1, :]
            )
        send(g)
        return none

    def attend(g, none):
        segc, segr = segc_ref[g], segr_ref[g]
        allowed = allowed_of(segc, segr)
        for h in range(heads):
            query = only_head(qkv_ref[g, :, 0:width], h)
            key = qkv_ref[g, :, width : 2 * width]
            value = qkv_ref[g, :, 2 * width + h * HV : 2 * width + (h + 1) * HV]
            c = dot_nt(query, key)
            kernel = jnp.where(allowed, 1.0 + c * (0.25 + c * 0.03125), 0.0).astype(bf16)
            wide = jnp.concatenate([value, jnp.ones_like(value)], axis=1)
            part[g, h] = dot(kernel, wide)

        @pl.when((place > 0) & (place < count - 1) & (g == place - 1))
        def _():
            lax.fori_loop(0, groups, join, 0)

        return none

    lax.fori_loop(0, groups, attend, 0)
    gather.relay()

    def carry_on(g, none):
        segc = segc_ref[g]

        @pl.when(place == count - 1)
        def _():
            for copy in hop(g):
                copy.wait_recv()

        mark = csum_ref[g, heads : heads + 1, 0:1]
        carried = (segc == mark).astype(f32)
        for h in range(heads):
            phi = features(qkv_ref[g, :, 0:width], h, *tables) * carried
            state = padded_state(carry_ref[g, h])
            both = part[g, h]
            numer = both[:, :HV] + dot(phi.astype(bf16), state)
            denom = both[:, HV:] + jnp.sum(
                phi * csum_ref[g, h : h + 1, :], axis=1, keepdims=True
            )
            inverse = 1.0 / denom
            att_ref[g, :, h * HV : (h + 1) * HV] = (numer * inverse).astype(bf16)
            rden_ref[g, :, h * HV : (h + 1) * HV] = inverse
        return none

    lax.fori_loop(0, groups, carry_on, 0)

    @pl.when(place < count - 1)
    def _():
        def finish(g, none):
            for copy in hop(g):
                copy.wait_send()
            return none

        lax.fori_loop(0, groups, finish, 0)

    stay.wait()
    gather.finish()


def backward_kernel(
    count,
    heads,
    qkv_ref,
    segc_ref,
    segr_ref,
    left_ref,
    right_ref,
    rows_ref,
    att_ref,
    rden_ref,
    carry_ref,
    csum_ref,
    ga_ref,
    down_ref,
    res_ref,
    out_ref,
    final_ref,
    gn,
    send_state,
    send_sum,
    recv_state,
    recv_sum,
    dkey,
    dvalue,
    terms,
    land,
    send_sem,
    recv_sem,
    f_send,
    f_recv,
    local_sem,
):
    place, f = lax.axis_index("seq"), lax.axis_index("feat")
    groups, block = qkv_ref.shape[0], qkv_ref.shape[1]
    width = heads * FDIM
    tables = (left_ref, right_ref, rows_ref)

    def hop(g):
        target = {"seq": lax.rem(place + count - 1, count)}
        return [
            pltpu.make_async_remote_copy(
                src_ref=src.at[g],
                dst_ref=dst.at[g],
                send_sem=send_sem.at[i, g],
                recv_sem=recv_sem.at[i, g],
                device_id=target,
                device_id_type=MESH,
            )
            for i, (src, dst) in enumerate(((send_state, recv_state), (send_sum, recv_sum)))
        ]

    def send(g):
        for copy in hop(g):
            copy.start()

    chain = [lax.rem(place + 1, count), lax.rem(place + count - 1, count)]
    greet(square_targets(f) + [{"seq": c} for c in chain])
    fill = pltpu.make_async_copy(down_ref, terms, local_sem.at[0])
    fill.start()
    ring = SquareSum(terms, land, f, f_send, f_recv)

    @pl.when(place == count - 1)
    def _():
        recv_state[...] = jnp.zeros_like(recv_state)
        recv_sum[...] = jnp.full_like(recv_sum, -1.0)

    def summarize(g, none):
        segc, segr = segc_ref[g], segr_ref[g]
        head = segr[:, 0:1]
        at_head = (segc == head).astype(f32)
        send_sum[g, heads : heads + 1, :] = jnp.broadcast_to(head, (1, LANES))
        for h in range(heads):
            lanes = slice(h * HV, (h + 1) * HV)
            ga = ga_ref[g, :, lanes]
            inverse = rden_ref[g, :, lanes]
            numer = (ga * inverse).astype(bf16)
            dots = jnp.sum(ga * att_ref[g, :, lanes].astype(f32), axis=1, keepdims=True)
            lane = lax.broadcasted_iota(jnp.int32, (block, HV), 1)
            denom = jnp.where(lane == 0, -dots * inverse, 0.0).astype(bf16)
            gn[g, h, :, :HV] = numer
            gn[g, h, :, HV:] = denom
            phi = (features(qkv_ref[g, :, 0:width], h, *tables) * at_head).astype(bf16)
            send_state[g, h] = dot_tn(phi, numer)[:STATE].astype(bf16)
            send_sum[g, h : h + 1, :] = dot_tn(denom, phi)[0:1]

        @pl.when(place == count - 1)
        def _():
            send(g)

        return none

    lax.fori_loop(0, groups, summarize, 0)
    fill.wait()
    ring.start_cross()
    ring.start_near()

    def join(g, none):
        for copy in hop(g):
            copy.wait_recv()
        segr = segr_ref[g]
        mark = recv_sum[g, heads : heads + 1, 0:1]
        head, tail = segr[:, 0:1], segr[:, block - 1 : block]
        whole = ((head == tail) & (head == mark)).astype(f32)
        for h in range(heads):
            send_state[g, h] = (
                send_state[g, h].astype(f32) + whole * recv_state[g, h].astype(f32)
            ).astype(bf16)
            send_sum[g, h : h + 1, :] = (
                send_sum[g, h : h + 1, :] + whole * recv_sum[g, h : h + 1, :]
            )
        send(g)
        return none

    def pull(g, none):
        segc, segr = segc_ref[g], segr_ref[g]
        allowed = allowed_of(segc, segr)
        query_all = qkv_ref[g, :, 0:width]
        key_all = qkv_ref[g, :, width : 2 * width]
        carried = (segc == csum_ref[g, heads : heads + 1, 0:1]).astype(f32)
        dquery = jnp.zeros((block, width), f32)
        dkey_sum = jnp.zeros((block, width), f32)
        for h in range(heads):
            query, key = only_head(query_all, h), only_head(key_all, h)
            value = qkv_ref[g, :, 2 * width + h * HV : 2 * width + (h + 1) * HV]
            wide = jnp.concatenate([value, jnp.ones_like(value)], axis=1)
            both = gn[g, h]
            c = dot_nt(query, key_all)
            kernel = jnp.where(allowed, 1.0 + c * (0.25 + c * 0.03125), 0.0).astype(bf16)
            grad = jnp.where(allowed, dot_nt(both, wide), 0.0)
            grad_c = (grad * (0.25 + c * 0.0625)).astype(bf16)
            dvalue[g, h] = dot_tn(kernel, both[:, :HV])
            dkey_sum = dkey_sum + dot_tn(grad_c, query)
            dquery = dquery + dot(grad_c, key)
            state = padded_state(carry_ref[g, h])
            gphi = dot_nt(both[:, :HV], state) + both[:, HV : HV + 1].astype(f32) * csum_ref[
                g, h : h + 1, :
            ]
            dquery = dquery + pull_features(gphi * carried, query_all, h, *tables)
        out_ref[g, :, 0:width] = dquery.astype(bf16)
        dkey[g] = dkey_sum

        @pl.when((place > 0) & (place < count - 1) & (g == count - 2 - place))
        def _():
            lax.fori_loop(0, groups, join, 0)

        return none

    lax.fori_loop(0, groups, pull, 0)
    ring.relay()

    def carry_back(g, none):
        segc = segc_ref[g]
        key_all = qkv_ref[g, :, width : 2 * width]

        @pl.when(place == 0)
        def _():
            for copy in hop(g):
                copy.wait_recv()

        mark = recv_sum[g, heads : heads + 1, 0:1]
        later = (segc == mark).astype(f32)
        total = dkey[g]
        for h in range(heads):
            value = qkv_ref[g, :, 2 * width + h * HV : 2 * width + (h + 1) * HV]
            state = padded_state(recv_state[g, h])
            phi = (features(key_all, h, *tables) * later).astype(bf16)
            dv = dvalue[g, h] + dot(phi, state)
            out_ref[g, :, 2 * width + h * HV : 2 * width + (h + 1) * HV] = dv.astype(bf16)
            gphi = (dot_nt(value, state) + recv_sum[g, h : h + 1, :]) * later
            total = total + pull_features(gphi, key_all, h, *tables)
        out_ref[g, :, width : 2 * width] = total.astype(bf16)
        return none

    lax.fori_loop(0, groups, carry_back, 0)

    @pl.when(place > 0)
    def _():
        def finish(g, none):
            for copy in hop(g):
                copy.wait_send()
            return none

        lax.fori_loop(0, groups, finish, 0)

    ring.arrive()

    def add_up(rows, total):
        final_ref[rows, :] = (res_ref[rows, :] + total).astype(bf16)

    by_rows(ring, add_up)
    ring.finish()


def whole_vmem(count):
    return [pl.BlockSpec(memory_space=pltpu.VMEM)] * count


def attention_forward(qkv, segc, segr, tables, cot_own, heads):
    groups, block, _ = qkv.shape
    count = lax.axis_size("seq")
    dma = pltpu.SemaphoreType.DMA
    states = (groups, heads, STATE, HV)
    sums = (groups, 8, LANES)
    return pl.pallas_call(
        functools.partial(forward_kernel, count, heads),
        out_shape=(
            jax.ShapeDtypeStruct((groups, block, heads * HV), bf16),
            jax.ShapeDtypeStruct((groups, block, heads * HV), f32),
            jax.ShapeDtypeStruct(states, bf16),
            jax.ShapeDtypeStruct(sums, f32),
            jax.ShapeDtypeStruct((groups,) + cot_own.shape, bf16),
        ),
        in_specs=whole_vmem(6) + in_place(1),
        out_specs=tuple(whole_vmem(4) + in_place(1)),
        scratch_shapes=[
            pltpu.VMEM(states, bf16),
            pltpu.VMEM(sums, f32),
            pltpu.VMEM((groups, heads, block, 2 * HV), f32),
            dma((2, groups)),
            dma((2, groups)),
            dma((6,)),
            dma((6,)),
            dma((1,)),
        ],
        compiler_params=pltpu.CompilerParams(
            collective_id=0, has_side_effects=True, vmem_limit_bytes=40 << 20
        ),
        cost_estimate=pl.CostEstimate(flops=0, bytes_accessed=1 << 20, transcendentals=0),
        name="attention_forward",
    )(qkv, segc, segr, *tables, cot_own)


def attention_backward(
    qkv, segc, segr, tables, att, rden, carry, csum, ga, down, residual, heads
):
    groups, block, wide = qkv.shape
    count = lax.axis_size("seq")
    states = (groups, heads, STATE, HV)
    sums = (groups, 8, LANES)
    return pl.pallas_call(
        functools.partial(backward_kernel, count, heads),
        out_shape=(
            jax.ShapeDtypeStruct((groups, block, wide), bf16),
            jax.ShapeDtypeStruct(residual.shape, bf16),
        ),
        in_specs=whole_vmem(11) + in_place(1) + whole_vmem(1),
        out_specs=tuple(whole_vmem(2)),
        scratch_shapes=[
            pltpu.VMEM((groups, heads, block, 2 * HV), bf16),
            pltpu.VMEM(states, bf16),
            pltpu.VMEM(sums, f32),
            pltpu.VMEM(states, bf16),
            pltpu.VMEM(sums, f32),
            pltpu.VMEM((groups, block, heads * FDIM), f32),
            pltpu.VMEM((groups, heads, block, HV), f32),
            pltpu.VMEM((groups,) + residual.shape, bf16),
            pltpu.VMEM((6, block // 2, residual.shape[1]), bf16),
            pltpu.SemaphoreType.DMA((2, groups)),
            pltpu.SemaphoreType.DMA((2, groups)),
            pltpu.SemaphoreType.DMA((6,)),
            pltpu.SemaphoreType.DMA((6,)),
            pltpu.SemaphoreType.DMA((1,)),
        ],
        compiler_params=pltpu.CompilerParams(
            collective_id=1, has_side_effects=True, vmem_limit_bytes=48 << 20
        ),
        cost_estimate=pl.CostEstimate(flops=0, bytes_accessed=1 << 20, transcendentals=0),
        name="attention_backward",
    )(qkv, segc, segr, *tables, att, rden, carry, csum, ga, down, residual)


def peers(f):
    return 2 * (f // 2) + 1 - f % 2, (f + 2) % 4, 3 - f


def greet(targets):
    barrier = pltpu.get_barrier_semaphore()
    for target in targets:
        pl.semaphore_signal(barrier, inc=1, device_id=target, device_id_type=MESH)
    pl.semaphore_wait(barrier, len(targets))


def push(src, dst, send_sem, recv_sem, target):
    return pltpu.make_async_remote_copy(
        src_ref=src,
        dst_ref=dst,
        send_sem=send_sem,
        recv_sem=recv_sem,
        device_id=target,
        device_id_type=MESH,
    )


def square_targets(f):
    return [{"feat": p} for p in peers(f)]


class SquareGather:
    def __init__(self, slots, f, send_sem, recv_sem, own=None):
        side, above, across = peers(f)
        half = slots.shape[1] // 2
        first, second = pl.ds(0, half), pl.ds(half, half)

        def copy(i, slot, rows, to):
            ref = slots.at[slot, rows]
            src = ref if own is None or i > 3 else own.at[rows]
            return push(src, ref, send_sem.at[i], recv_sem.at[i], {"feat": to})

        self.direct = [
            copy(0, f, first, side),
            copy(1, f, second, above),
            copy(2, f, second, side),
            copy(3, f, first, above),
        ]
        self.forward = [copy(4, side, first, above), copy(5, above, second, side)]

    def start(self):
        for c in self.direct:
            c.start()

    def relay(self):
        self.direct[0].wait_recv()
        self.forward[0].start()
        self.direct[1].wait_recv()
        self.forward[1].start()

    def near(self):
        self.direct[2].wait_recv()
        self.direct[3].wait_recv()

    def far(self):
        for c in self.forward:
            c.wait_recv()

    def sent(self):
        for c in self.direct + self.forward:
            c.wait_send()

    def finish(self):
        self.near()
        self.far()
        self.sent()


class SquareSum:
    def __init__(self, part, land, f, send_sem, recv_sem):
        self.side, self.above, self.across = peers(f)
        self.f, self.part, self.land = f, part, land
        self.half = part.shape[1] // 2
        first, second = pl.ds(0, self.half), pl.ds(self.half, self.half)

        def copy(i, slot, rows, to):
            return push(
                part.at[slot, rows], land.at[i], send_sem.at[i], recv_sem.at[i], {"feat": to}
            )

        self.cross = [copy(0, self.across, first, self.side), copy(1, self.across, second, self.above)]
        self.near = [copy(2, self.side, first, self.side), copy(3, self.above, second, self.above)]
        self.late = [copy(4, self.above, first, self.above), copy(5, self.side, second, self.side)]

    def start_cross(self):
        for c in self.cross:
            c.start()

    def add_rows(self, slot, base, landed):
        step = 32

        def one(i, none):
            rows = pl.ds(pl.multiple_of(base + i * step, step), step)
            came = self.land[landed, pl.ds(pl.multiple_of(i * step, step), step), :]
            self.part[slot, rows, :] = (
                self.part[slot, rows, :].astype(f32) + came.astype(f32)
            ).astype(bf16)
            return none

        lax.fori_loop(0, self.half // step, one, 0)

    def start_near(self):
        for c in self.near:
            c.start()

    def relay(self):
        self.cross[0].wait_recv()
        self.add_rows(self.above, 0, 0)
        self.late[0].start()
        self.cross[1].wait_recv()
        self.add_rows(self.side, self.half, 1)
        self.late[1].start()

    def arrive(self):
        for c in self.near + self.late:
            c.wait_recv()

    def total(self, half, rows):
        base = half * self.half
        own = self.part[self.f, pl.ds(pl.multiple_of(base + rows.start, 16), rows.size), :]
        near = self.land[2 + half, rows, :]
        late = self.land[4 + half, rows, :]
        return own.astype(f32) + near.astype(f32) + late.astype(f32)

    def finish(self):
        for c in self.cross + self.near + self.late:
            c.wait_send()


class RowSum:
    def __init__(self, term, acc, shares, lands, sems, f, s, d, seqs, dps):
        self.term, self.acc, self.shares, self.lands = term, acc, shares, lands
        self.f, self.s, self.d = f, s, d
        self.parts, self.seqs = term.shape[0], seqs
        columns = [lax.rem(s + k, seqs) for k in range(1, seqs)]
        others = [lax.rem(d + k, dps) for k in range(1, dps)]
        d_send, d_recv, z_send, z_recv, a_send, a_recv = sems
        self.one = [
            push(term.at[:, :, o], lands[0].at[k], d_send.at[k], d_recv.at[k], {"dp": o})
            for k, o in enumerate(others)
        ]
        self.two = [
            push(acc.at[c], lands[1].at[k], z_send.at[k], z_recv.at[k], {"seq": c})
            for k, c in enumerate(columns)
        ]
        self.three = [
            push(lands[2].at[p], shares.at[f], a_send.at[i], a_recv.at[i], {"feat": p})
            for i, p in enumerate(peers(f))
        ]

    def start(self):
        for c in self.one:
            c.start()

    def over_seq(self):
        for c in self.one:
            c.wait_recv()

        def one(i, none):
            p, c = i // self.seqs, lax.rem(i, self.seqs)
            total = self.term[p, c, self.d].astype(f32)
            for k in range(len(self.one)):
                total = total + self.lands[0][k, p, c].astype(f32)
            self.acc[c, p] = total.astype(bf16)
            return none

        lax.fori_loop(0, self.parts * self.seqs, one, 0)
        for c in self.two:
            c.start()

    def over_feat(self):
        for c in self.two:
            c.wait_recv()

        def one(p, none):
            total = self.acc[self.s, p].astype(f32)
            for k in range(len(self.two)):
                total = total + self.lands[1][k, p].astype(f32)
            self.lands[2][p] = total.astype(bf16)
            return none

        lax.fori_loop(0, self.parts, one, 0)
        self.shares[self.f] = self.lands[2][self.f]
        for c in self.three:
            c.start()

    def arrive(self):
        for c in self.three:
            c.wait_recv()

    def finish(self):
        for c in self.one + self.two + self.three:
            c.wait_send()


def row_sum_scratch(shape):
    parts, seqs, dps, rows, wide = shape
    others = max(dps - 1, 1)
    dma = pltpu.SemaphoreType.DMA
    return [
        pltpu.VMEM((parts, rows, wide), bf16),
        pltpu.VMEM((seqs, parts, rows, wide), bf16),
        pltpu.VMEM((others, parts, seqs, rows, wide), bf16),
        pltpu.VMEM((seqs - 1, parts, rows, wide), bf16),
        pltpu.VMEM((parts, rows, wide), bf16),
        dma((others,)),
        dma((others,)),
        dma((seqs - 1,)),
        dma((seqs - 1,)),
        dma((3,)),
        dma((3,)),
    ]


def row_sum(term, scratch, f, s, d, seqs, dps):
    shares, acc = scratch[:2]
    return RowSum(term, acc, shares, scratch[2:5], scratch[5:], f, s, d, seqs, dps)


def opening_kernel(
    seqs,
    dps,
    tok_ref,
    query_ref,
    key_ref,
    value_ref,
    out_ref,
    one_ref,
    two_ref,
    x_ref,
    w_ref,
    g_ref,
    o_ref,
    pack,
    opack,
    tile,
    x_send,
    x_recv,
    a_send,
    a_recv,
    z_send,
    z_recv,
    d_send,
    d_recv,
    local_sem,
):
    f, s, d = lax.axis_index("feat"), lax.axis_index("seq"), lax.axis_index("dp")
    parts, rows_each = pack.shape[0], pack.shape[1]
    near = peers(f)
    columns = [lax.rem(s + k, seqs) for k in range(1, seqs)]
    others = [lax.rem(d + k, dps) for k in range(1, dps)]
    stay = pltpu.make_async_copy(tok_ref, x_ref.at[f], local_sem.at[0])
    stay.start()
    first = 0
    for ref in (query_ref, key_ref, value_ref):
        each = ref.shape[1] // parts
        for p in range(parts):
            pack[p, :, first : first + each] = ref[:, p * each : (p + 1) * each]
        first += each
    tile[...] = jnp.zeros_like(tile)
    tile[0:1, :rows_each] = one_ref[...].astype(f32)
    tile[1:2, :rows_each] = two_ref[...].astype(f32)
    outs = (w_ref, g_ref)
    own = [
        pltpu.make_async_copy(pack.at[f], w_ref.at[f, s, d], local_sem.at[1]),
        pltpu.make_async_copy(tile, g_ref.at[f, s, d], local_sem.at[2]),
    ]
    for c in own:
        c.start()
    greet(
        square_targets(f) + [{"seq": c} for c in columns] + [{"dp": o} for o in others]
    )
    shares = [
        [
            push(pack.at[p], w_ref.at[f, s, d], a_send.at[0, i], a_recv.at[0, i], {"feat": p}),
            push(tile, g_ref.at[f, s, d], a_send.at[1, i], a_recv.at[1, i], {"feat": p}),
        ]
        for i, p in enumerate(near)
    ]
    for pair in shares:
        for c in pair:
            c.start()
    gather = SquareGather(x_ref, f, x_send, x_recv, tok_ref)
    gather.start()
    each = out_ref.shape[1] // parts
    for p in range(parts):
        opack[p] = out_ref[:, p * each : (p + 1) * each]
    own_out = pltpu.make_async_copy(opack.at[f], o_ref.at[f], local_sem.at[3])
    own_out.start()
    out_shares = [
        push(opack.at[p], o_ref.at[f], a_send.at[2, i], a_recv.at[2, i], {"feat": p})
        for i, p in enumerate(near)
    ]
    for c in out_shares:
        c.start()
    for c in own:
        c.wait()

    chunks = (f,) + near

    def to_column(n, k):
        return [
            push(
                ref.at[chunks[n], s, d],
                ref.at[chunks[n], s, d],
                z_send.at[j, k - 1, n],
                z_recv.at[j, k - 1, n],
                {"seq": columns[k - 1]},
            )
            for j, ref in enumerate(outs)
        ]

    def to_sibling(n, k):
        back = lax.rem(s + seqs - k, seqs)
        return [
            push(
                ref.at[chunks[n], back, d],
                ref.at[chunks[n], back, d],
                d_send.at[j, o, k, n],
                d_recv.at[j, o, k, n],
                {"dp": other},
            )
            for j, ref in enumerate(outs)
            for o, other in enumerate(others)
        ]

    def start_all(copies):
        for c in copies:
            c.start()

    for n in range(parts):
        if n:
            for c in shares[n - 1]:
                c.wait_recv()
        for k in range(1, seqs):
            start_all(to_column(n, k))
        start_all(to_sibling(n, 0))
    for n in range(parts):
        for k in range(1, seqs):
            for c in to_column(n, k):
                c.wait_recv()
            start_all(to_sibling(n, k))
    gather.relay()
    for n in range(parts):
        for k in range(seqs):
            for c in to_sibling(n, k):
                c.wait_recv()
    for n in range(parts):
        for k in range(seqs):
            for c in to_sibling(n, k):
                c.wait_send()
        for k in range(1, seqs):
            for c in to_column(n, k):
                c.wait_send()
    for pair in shares:
        for c in pair:
            c.wait_send()
    stay.wait()
    own_out.wait()
    for c in out_shares:
        c.wait_recv()
    for c in out_shares:
        c.wait_send()
    gather.finish()


def in_place(count):
    return [pl.BlockSpec(memory_space=pl.ANY)] * count


def opening(own, w_query, w_key, w_value, w_out, gain_one, gain_two):
    parts, seqs, dps = (lax.axis_size(a) for a in ALL)
    block, width = own.shape
    rows_each = w_query.shape[0]
    wide = (w_query.shape[1] + w_key.shape[1] + w_value.shape[1]) // parts
    others = max(dps - 1, 1)
    dma = pltpu.SemaphoreType.DMA
    out_wide = w_out.shape[1] // parts
    x_all, w_all, g_all, o_own = pl.pallas_call(
        functools.partial(opening_kernel, seqs, dps),
        out_shape=(
            jax.ShapeDtypeStruct((parts, block, width), bf16),
            jax.ShapeDtypeStruct((parts, seqs, dps, rows_each, wide), bf16),
            jax.ShapeDtypeStruct((parts, seqs, dps, 8, HV), f32),
            jax.ShapeDtypeStruct((parts, rows_each, out_wide), bf16),
        ),
        in_specs=in_place(1) + whole_vmem(6),
        out_specs=tuple(in_place(4)),
        scratch_shapes=[
            pltpu.VMEM((parts, rows_each, wide), bf16),
            pltpu.VMEM((parts, rows_each, out_wide), bf16),
            pltpu.VMEM((8, HV), f32),
            dma((6,)),
            dma((6,)),
            dma((3, 3)),
            dma((3, 3)),
            dma((2, seqs - 1, parts)),
            dma((2, seqs - 1, parts)),
            dma((2, others, seqs, parts)),
            dma((2, others, seqs, parts)),
            dma((4,)),
        ],
        compiler_params=pltpu.CompilerParams(collective_id=2, has_side_effects=True),
        cost_estimate=pl.CostEstimate(flops=0, bytes_accessed=1 << 20, transcendentals=0),
        name="opening",
    )(own, w_query, w_key, w_value, w_out, gain_one, gain_two)
    gains = g_all[..., :2, :rows_each].transpose(3, 0, 1, 2, 4).reshape(2, width)
    return x_all, w_all.reshape(width, wide), gains, o_own


def inverse_rms(values):
    return lax.rsqrt(jnp.mean(values * values, axis=-1, keepdims=True) + epsilon)


def norm_back(grad, unit, inverse, gain):
    scaled = grad * gain
    return (scaled - unit * jnp.mean(scaled * unit, axis=-1, keepdims=True)) * inverse


class ByShare:
    def __init__(self, ref):
        self.ref = ref

    def tile(self, i, size):
        block = self.ref[:, i]
        return block.reshape(size, block.shape[2])


class ByTiles:
    def __init__(self, src, ref, sem, tile):
        self.ref = ref
        self.fills = [
            pltpu.make_async_copy(
                src.at[pl.ds(i * tile, tile)], ref.at[pl.ds(i * tile, tile)], sem.at[i]
            )
            for i in range(ref.shape[0] // tile)
        ]

    def tile(self, i, size):
        return self.ref[pl.ds(pl.multiple_of(i * size, size), size), :]


def product_tiles(part, slot, pairs, tile, first=False):
    def one(i, none):
        cols = pl.ds(pl.multiple_of(i * tile, tile), tile)
        total = None
        for rows, weights in pairs:
            if hasattr(weights, "tile"):
                block = weights.tile(i, tile)
            else:
                block = weights[cols, :]
            term = dot_nt(rows[slot], block)
            total = term if total is None else total + term
        part[slot, :, cols] = total.astype(bf16)
        return none

    if first:
        for i in range(part.shape[2] // tile):
            for _, weights in pairs:
                weights.fills[i].wait()
            one(i, 0)
    else:
        lax.fori_loop(0, part.shape[2] // tile, one, 0)


def summed_products(part, land, f, pairs, send_sem, recv_sem, beside=None, first=False):
    side, above, across = peers(f)
    ring = SquareSum(part, land, f, send_sem, recv_sem)
    product_tiles(part, across, pairs, 512, first)
    ring.start_cross()
    product_tiles(part, side, pairs, 512)
    product_tiles(part, above, pairs, 512)
    ring.start_near()
    product_tiles(part, f, pairs, 512)
    ring.relay()
    if beside is not None:
        beside()
    ring.arrive()
    return ring


def by_rows(ring, body, step=16):
    for half in (0, 1):

        def one(i, none):
            start = pl.multiple_of(i * step, step)
            rows = pl.ds(pl.multiple_of(half * ring.half + i * step, step), step)
            body(rows, ring.total(half, pl.ds(start, step)))
            return none

        lax.fori_loop(0, ring.half // step, one, 0)


def branch_kernel(
    att_ref, w_ref, tok_ref, gain_ref, rows_ref, res_ref, part, land, s_send, s_recv, g_send, g_recv
):
    f = lax.axis_index("feat")
    greet(square_targets(f))
    ring = summed_products(part, land, f, [(att_ref, ByShare(w_ref))], s_send, s_recv)

    def finish_rows(rows, total):
        residual = tok_ref[rows, :].astype(f32) + total
        res_ref[rows, :] = residual
        rows_ref[f, rows, :] = (residual * inverse_rms(residual) * gain_ref[...]).astype(bf16)

    by_rows(ring, finish_rows)
    gather = SquareGather(rows_ref, f, g_send, g_recv)
    gather.start()
    ring.finish()
    gather.relay()
    gather.finish()


def square_scratch(parts, block, width):
    dma = pltpu.SemaphoreType.DMA
    return [
        pltpu.VMEM((parts, block, width), bf16),
        pltpu.VMEM((6, block // 2, width), bf16),
        dma((6,)),
        dma((6,)),
    ]


def branch_step(att, out_w, own, gain_two):
    parts, block, _ = att.shape
    width = own.shape[1]
    dma = pltpu.SemaphoreType.DMA
    return pl.pallas_call(
        branch_kernel,
        out_shape=(
            jax.ShapeDtypeStruct((parts, block, width), bf16),
            jax.ShapeDtypeStruct((block, width), f32),
        ),
        in_specs=whole_vmem(4),
        out_specs=tuple(whole_vmem(2)),
        scratch_shapes=square_scratch(parts, block, width) + [dma((6,)), dma((6,))],
        compiler_params=pltpu.CompilerParams(
            collective_id=3, has_side_effects=True, vmem_limit_bytes=48 << 20
        ),
        cost_estimate=pl.CostEstimate(flops=0, bytes_accessed=1 << 20, transcendentals=0),
        name="branch_step",
    )(att, out_w, own, gain_two)


def rows_back_kernel(
    gg_ref,
    gu_ref,
    wg_hbm,
    wu_hbm,
    res_ref,
    cot_ref,
    gain_ref,
    mixed_hbm,
    wd_hbm,
    wo_hbm,
    all_ref,
    gres_ref,
    gsum_ref,
    down_ref,
    ga_ref,
    part,
    land,
    wg,
    wu,
    mixed,
    wd,
    wo,
    s_send,
    s_recv,
    g_send,
    g_recv,
    local_sem,
    tile_sem,
):
    f = lax.axis_index("feat")
    weights = [
        ByTiles(src, dst, tile_sem.at[i], 512)
        for i, (src, dst) in enumerate(((wg_hbm, wg), (wu_hbm, wu)))
    ]
    for pair in zip(*(w.fills for w in weights)):
        for c in pair:
            c.start()
    fills = [
        pltpu.make_async_copy(src, dst, local_sem.at[i])
        for i, (src, dst) in enumerate(((mixed_hbm, mixed), (wd_hbm, wd), (wo_hbm, wo)))
    ]
    for c in fills:
        c.start()
    greet(square_targets(f))
    pairs = [(gg_ref, weights[0]), (gu_ref, weights[1])]

    def down_products():
        for c in fills:
            c.wait()
        for p in range(part.shape[0]):
            product_tiles(down_ref, p, [(mixed, wd)], 512)

    ring = summed_products(part, land, f, pairs, s_send, s_recv, down_products, True)
    gsum_ref[...] = jnp.zeros_like(gsum_ref)

    def finish_rows(rows, grad):
        residual = res_ref[rows, :]
        inverse = inverse_rms(residual)
        unit = residual * inverse
        gsum_ref[...] += jnp.sum(grad * unit, axis=0, keepdims=True)
        grad_res = cot_ref[rows, :].astype(f32) + norm_back(grad, unit, inverse, gain_ref[...])
        gres_ref[rows, :] = grad_res
        all_ref[f, rows, :] = grad_res.astype(bf16)

    by_rows(ring, finish_rows)
    gather = SquareGather(all_ref, f, g_send, g_recv)
    gather.start()
    ring.finish()
    side, above, across = peers(f)

    def attended_grad(slot):
        blocks = ByShare(wo)
        size = all_ref.shape[2] // wo.shape[1]
        total = None
        for i in range(wo.shape[1]):
            term = dot(all_ref[slot, :, i * size : (i + 1) * size], blocks.tile(i, size))
            total = term if total is None else total + term
        ga_ref[slot] = total

    attended_grad(f)
    gather.relay()
    gather.near()
    attended_grad(side)
    attended_grad(above)
    gather.far()
    attended_grad(across)
    gather.sent()


def rows_back(
    grad_gate, grad_up, gate_w, up_w, residual, cot_own, gain_two, mixed, down_w, out_w
):
    parts, block, hidden = grad_gate.shape
    width = residual.shape[1]
    dma = pltpu.SemaphoreType.DMA
    return pl.pallas_call(
        rows_back_kernel,
        out_shape=(
            jax.ShapeDtypeStruct((parts, block, width), bf16),
            jax.ShapeDtypeStruct((block, width), f32),
            jax.ShapeDtypeStruct((1, width), f32),
            jax.ShapeDtypeStruct((parts, block, width), bf16),
            jax.ShapeDtypeStruct((parts, block, out_w.shape[3]), f32),
        ),
        in_specs=whole_vmem(2) + in_place(2) + whole_vmem(3) + in_place(3),
        out_specs=tuple(whole_vmem(5)),
        scratch_shapes=square_scratch(parts, block, width)[:2]
        + [
            pltpu.VMEM((width, hidden), bf16),
            pltpu.VMEM((width, hidden), bf16),
            pltpu.VMEM((parts, block, hidden), bf16),
            pltpu.VMEM((width, hidden), bf16),
            pltpu.VMEM(out_w.shape, bf16),
        ]
        + [dma((6,))] * 4
        + [dma((3,)), dma((2, width // 512))],
        compiler_params=pltpu.CompilerParams(
            collective_id=4, has_side_effects=True, vmem_limit_bytes=60 << 20
        ),
        cost_estimate=pl.CostEstimate(flops=0, bytes_accessed=1 << 20, transcendentals=0),
        name="rows_back",
    )(grad_gate, grad_up, gate_w, up_w, residual, cot_own, gain_two, mixed, down_w, out_w)


def closing_kernel(
    seqs,
    dps,
    dqkv_ref,
    w_ref,
    tok_ref,
    gres_ref,
    gain_ref,
    gsum_two_ref,
    term_ref,
    osum_ref,
    x_ref,
    tile_ref,
    query_ref,
    key_ref,
    value_ref,
    ograd_ref,
    part,
    land,
    s_send,
    s_recv,
    gsum,
    cut,
    came,
    mid,
    tail,
    c_send,
    c_recv,
    d_send,
    d_recv,
    oland,
    o_send,
    o_recv,
    *sum_scratch,
):
    f, s, d = lax.axis_index("feat"), lax.axis_index("seq"), lax.axis_index("dp")
    parts = 4
    others = [lax.rem(d + k, dps) for k in range(1, dps)]
    circle = [
        (lax.rem(f + i, parts), lax.rem(s + j, seqs))
        for i in range(parts)
        for j in range(seqs)
        if i or j
    ]
    greet(
        [{"feat": a, "seq": b} for a, b in circle] + [{"dp": o} for o in others]
    )
    rows_sum = row_sum(term_ref, sum_scratch, f, s, d, seqs, dps)
    rows_sum.start()
    outs = [
        push(osum_ref.at[p], oland.at[f], o_send.at[i], o_recv.at[i], {"feat": p})
        for i, p in enumerate(peers(f))
    ]
    for c in outs:
        c.start()
    ring = summed_products(
        part, land, f, [(dqkv_ref, w_ref)], s_send, s_recv, rows_sum.over_seq
    )
    gsum[...] = jnp.zeros_like(gsum)

    def finish_rows(rows, grad):
        values = tok_ref[rows, :].astype(f32)
        inverse = inverse_rms(values)
        unit = values * inverse
        gsum[...] += jnp.sum(grad * unit, axis=0, keepdims=True)
        x_ref[rows, :] = gres_ref[rows, :] + norm_back(grad, unit, inverse, gain_ref[...])

    by_rows(ring, finish_rows)
    rows_sum.over_feat()
    ring.finish()

    lanes = gsum.shape[1] // (parts * seqs)
    cut[...] = jnp.zeros_like(cut)
    for k in range(parts * seqs):
        cut[k, 0:1, :] = gsum[:, k * lanes : (k + 1) * lanes]
        cut[k, 1:2, :] = gsum_two_ref[:, k * lanes : (k + 1) * lanes]
    place = f * seqs + s
    sends = []
    for i, (a, b) in enumerate(circle):
        sends.append(
            push(
                cut.at[a * seqs + b],
                came.at[i],
                c_send.at[i],
                c_recv.at[i],
                {"feat": a, "seq": b},
            )
        )
    for c in sends:
        c.start()
    total = cut[place]
    for c in sends:
        c.wait_recv()
    for i in range(len(circle)):
        total = total + came[i]
    mid[...] = total
    last = [
        push(mid, tail.at[k], d_send.at[k], d_recv.at[k], {"dp": o})
        for k, o in enumerate(others)
    ]
    for c in last:
        c.start()
    for c in last:
        c.wait_recv()
    for k in range(len(others)):
        total = total + tail[k]
    tile_ref[...] = total
    rows_sum.arrive()
    first = 0
    for ref in (query_ref, key_ref, value_ref):
        each = ref.shape[1] // parts
        for p in range(parts):
            piece = rows_sum.shares[p, :, first : first + each]
            ref[:, p * each : (p + 1) * each] = piece.astype(f32)
        first += each
    rows_sum.finish()
    oland[f] = osum_ref[f]
    for c in outs:
        c.wait_recv()
    each = ograd_ref.shape[1] // parts
    for p in range(parts):
        ograd_ref[:, p * each : (p + 1) * each] = oland[p].astype(f32)
    for c in outs + sends + last:
        c.wait_send()


def closing(dqkv, qkv_w, own, grad_residual, gain_one, gain_two_sum, qkv_term, out_sum):
    parts, seqs, dps = (lax.axis_size(a) for a in ALL)
    block, width = own.shape
    others = max(dps - 1, 1)
    lanes = width // (parts * seqs)
    circle = parts * seqs - 1
    rows_each = qkv_term.shape[3]
    dma = pltpu.SemaphoreType.DMA
    return pl.pallas_call(
        functools.partial(closing_kernel, seqs, dps),
        out_shape=(
            jax.ShapeDtypeStruct((block, width), f32),
            jax.ShapeDtypeStruct((8, lanes), f32),
            jax.ShapeDtypeStruct((rows_each, HEADS * FDIM), f32),
            jax.ShapeDtypeStruct((rows_each, HEADS * FDIM), f32),
            jax.ShapeDtypeStruct((rows_each, HEADS * HV), f32),
            jax.ShapeDtypeStruct((rows_each, HEADS * HV), f32),
        ),
        in_specs=whole_vmem(8),
        out_specs=tuple(whole_vmem(6)),
        scratch_shapes=square_scratch(parts, block, width)
        + [
            pltpu.VMEM((1, width), f32),
            pltpu.VMEM((parts * seqs, 8, lanes), f32),
            pltpu.VMEM((circle, 8, lanes), f32),
            pltpu.VMEM((8, lanes), f32),
            pltpu.VMEM((others, 8, lanes), f32),
            dma((circle,)),
            dma((circle,)),
            dma((others,)),
            dma((others,)),
            pltpu.VMEM(out_sum.shape, bf16),
            dma((3,)),
            dma((3,)),
        ]
        + row_sum_scratch(qkv_term.shape),
        compiler_params=pltpu.CompilerParams(
            collective_id=5, has_side_effects=True, vmem_limit_bytes=48 << 20
        ),
        cost_estimate=pl.CostEstimate(flops=0, bytes_accessed=1 << 20, transcendentals=0),
        name="closing",
    )(dqkv, qkv_w, own, grad_residual, gain_one, gain_two_sum, qkv_term, out_sum)


def local(
    tokens,
    segments,
    norm1_gain,
    norm2_gain,
    w_query,
    w_key,
    w_value,
    w_out,
    w_gate,
    w_up,
    w_down,
    cotangent,
):
    parts = lax.axis_size("feat")
    heads = HEADS // parts
    block, width = tokens.shape[2], tokens.shape[3]
    rows_total = parts * block
    rows_each = w_query.shape[0]
    own = tokens.reshape(block, width)
    cot_own = cotangent.reshape(block, width)

    x_all, qkv_w, gains, out_share = opening(
        own, w_query, w_key, w_value, w_out.T, norm1_gain[None], norm2_gain[None]
    )
    qkv_width = qkv_w.shape[1]
    x_all, w_gate, w_up = lax.optimization_barrier((x_all, w_gate, w_up))
    out_w = lax.all_gather(out_share[None], ("seq", "dp"), axis=0, tiled=True)
    gate_w = lax.all_gather(w_gate, ("seq", "dp"), axis=0, tiled=True)
    up_w = lax.all_gather(w_up, ("seq", "dp"), axis=0, tiled=True)
    gain_one, gain_two = gains[0:1], gains[1:2]

    x_wide = x_all.astype(f32).reshape(rows_total, width)
    normed = (x_wide * inverse_rms(x_wide) * gain_one).astype(bf16)
    qkv = dot(normed, qkv_w).astype(bf16).reshape(parts, block, qkv_width)
    qkv, w_down = lax.optimization_barrier((qkv, w_down))
    down_w = lax.all_gather(w_down.T, ("seq", "dp"), axis=0, tiled=True)
    segment = segments.reshape(parts, block).astype(f32)
    segc, segr = segment[:, :, None], segment[:, None, :]
    tables = feature_tables(heads)
    att, rden, carry, csum, cot_all = attention_forward(qkv, segc, segr, tables, cot_own, heads)
    cot_all = cot_all.reshape(rows_total, width)
    rows_all, residual = branch_step(att, out_w, own, gain_two)
    rows_all = rows_all.reshape(rows_total, width)

    gate_out = dot(rows_all, gate_w)
    up_out = dot(rows_all, up_w)
    sig = jax.nn.sigmoid(gate_out)
    silu = gate_out * sig
    mixed = (silu * up_out).astype(bf16)
    down_term = dot_tn(cot_all, mixed).astype(bf16)
    mixed, cot_late, down_term = lax.optimization_barrier((mixed, cot_all, down_term))
    grad_mixed = dot(cot_late, down_w)
    grad_gate = (grad_mixed * up_out * sig * (1.0 + gate_out * (1.0 - sig))).astype(bf16)
    grad_up = (grad_mixed * silu).astype(bf16)

    def summed(term):
        return lax.psum_scatter(term, ("seq", "dp"), scatter_dimension=0, tiled=True)

    gate_term = dot_tn(rows_all, grad_gate).astype(bf16)
    up_term = dot_tn(rows_all, grad_up).astype(bf16)
    grad_gate, grad_up, gate_term, up_term = lax.optimization_barrier(
        (grad_gate, grad_up, gate_term, up_term)
    )
    down_sum, gate_sum, up_sum = summed(down_term), summed(gate_term), summed(up_term)

    by_device = (parts, block, -1)
    branch_all, grad_residual, gain_two_sum, down, ga = rows_back(
        grad_gate.reshape(by_device),
        grad_up.reshape(by_device),
        gate_w,
        up_w,
        residual,
        cot_own,
        gain_two,
        mixed.reshape(by_device),
        down_w,
        out_w,
    )
    branch_all = branch_all.reshape(rows_total, width)
    by_row = (parts, lax.axis_size("seq"), lax.axis_size("dp"), rows_each, -1)
    out_term = dot_tn(branch_all, att.reshape(rows_total, heads * HV)).astype(bf16)
    out_term = out_term.reshape(parts, -1, rows_each, heads * HV).transpose(1, 0, 2, 3)
    out_sum = summed(out_term.reshape(width, -1)).reshape(parts, rows_each, -1)
    dqkv, output = attention_backward(
        qkv, segc, segr, tables, att, rden, carry, csum, ga, down, residual, heads
    )
    dqkv_late, down_sum, gate_sum, up_sum = lax.optimization_barrier(
        (dqkv, down_sum, gate_sum, up_sum)
    )
    qkv_term = dot_tn(normed, dqkv_late.reshape(rows_total, qkv_width)).astype(bf16)
    x_grad, gain_grads, query_grad, key_grad, value_grad, out_grad = closing(
        dqkv, qkv_w, own, grad_residual, gain_one, gain_two_sum, qkv_term.reshape(by_row), out_sum
    )
    gain_each = gain_grads.shape[1] // lax.axis_size("dp")
    gain_grads = lax.dynamic_slice_in_dim(
        gain_grads, lax.axis_index("dp") * gain_each, gain_each, axis=1
    )
    return (
        output.reshape(tokens.shape),
        x_grad.reshape(tokens.shape),
        gain_grads[0],
        gain_grads[1],
        query_grad,
        key_grad,
        value_grad,
        out_grad.T,
        gate_sum.astype(f32),
        up_sum.astype(f32),
        down_sum.T.astype(f32),
    )


def solution(mesh):
    placed = (
        P("feat", "dp", "seq", None),
        P(None, "dp", "seq"),
        P(ALL),
        P(ALL),
        P(ALL, None),
        P(ALL, None),
        P(ALL, None),
        P(None, ALL),
        P(("seq", "dp"), "feat"),
        P(("seq", "dp"), "feat"),
        P("feat", ("seq", "dp")),
        P("feat", "dp", "seq", None),
    )
    return jax.shard_map(
        local,
        mesh=mesh,
        in_specs=placed,
        out_specs=(
            P("feat", "dp", "seq", None),
            P("feat", "dp", "seq", None),
            P(ALL),
            P(ALL),
            P(ALL, None),
            P(ALL, None),
            P(ALL, None),
            P(None, ALL),
            P(("seq", "dp"), "feat"),
            P(("seq", "dp"), "feat"),
            P("feat", ("seq", "dp")),
        ),
        check_vma=False,
    )
```

```python
import functools

import jax
import jax.numpy as jnp
import numpy as np
from jax import lax
from jax.experimental import pallas as pl
from jax.experimental.pallas import tpu as pltpu
from jax.sharding import PartitionSpec as P

HEADS = 16
FDIM = 16
HV = 128
STATE = 160
LANES = 256
epsilon = 1e-05
MESH = pl.DeviceIdType.MESH
ALL = ("feat", "seq", "dp")
f32 = jnp.float32
bf16 = jnp.bfloat16


def dot(a, b):
    return lax.dot_general(a, b, (((1,), (0,)), ((), ())), preferred_element_type=f32)


def dot_nt(a, b):
    return lax.dot_general(a, b, (((1,), (1,)), ((), ())), preferred_element_type=f32)


def dot_tn(a, b):
    return lax.dot_general(a, b, (((0,), (0,)), ((), ())), preferred_element_type=f32)


def feature_tables(heads):
    pairs = [(i, j) for i in range(FDIM) for j in range(i, FDIM)]
    left = np.zeros((heads, heads * FDIM, LANES), np.float32)
    right = np.zeros((heads, heads * FDIM, LANES), np.float32)
    rows = np.zeros((8, LANES), np.float32)
    for h in range(heads):
        for p, (i, j) in enumerate(pairs):
            left[h, h * FDIM + i, p] = 1.0
            right[h, h * FDIM + j, p] = 1.0
            rows[2, p] = 0.25 / 2.0**0.5 if i == j else 0.25
        for i in range(FDIM):
            p = len(pairs) + i
            left[h, h * FDIM + i, p] = 1.0
            rows[1, p] = 1.0
            rows[2, p] = 0.5
        p = len(pairs) + FDIM
        rows[0, p] = rows[1, p] = rows[2, p] = 1.0
    return jnp.asarray(left, bf16), jnp.asarray(right, bf16), jnp.asarray(rows)


def both_sides(entries, h, left_ref, right_ref, rows_ref):
    one = dot(entries, left_ref[h]) + rows_ref[0:1, :]
    two = dot(entries, right_ref[h]) + rows_ref[1:2, :]
    return one, two * rows_ref[2:3, :]


def features(entries, h, left_ref, right_ref, rows_ref):
    one, two = both_sides(entries, h, left_ref, right_ref, rows_ref)
    return one * two


def pull_features(grad, entries, h, left_ref, right_ref, rows_ref):
    one, two = both_sides(entries, h, left_ref, right_ref, rows_ref)
    scaled = rows_ref[2:3, :]
    return dot_nt((grad * two).astype(bf16), left_ref[h]) + dot_nt(
        (grad * one * scaled).astype(bf16), right_ref[h]
    )


def only_head(entries, h):
    lane = lax.broadcasted_iota(jnp.int32, entries.shape, 1)
    keep = (lane >= h * FDIM) & (lane < (h + 1) * FDIM)
    return jnp.where(keep, entries, jnp.zeros_like(entries))


def padded_state(state):
    return jnp.concatenate([state, jnp.zeros((LANES - STATE, state.shape[1]), state.dtype)], 0)


def allowed_of(segc, segr):
    block = segc.shape[0]
    row = lax.broadcasted_iota(jnp.int32, (block, block), 0)
    col = lax.broadcasted_iota(jnp.int32, (block, block), 1)
    return (row >= col) & (segc == segr)


def forward_kernel(
    count,
    heads,
    qkv_ref,
    segc_ref,
    segr_ref,
    left_ref,
    right_ref,
    rows_ref,
    cot_ref,
    att_ref,
    rden_ref,
    carry_ref,
    csum_ref,
    cots_ref,
    send_state,
    send_sum,
    part,
    send_sem,
    recv_sem,
    f_send,
    f_recv,
    local_sem,
):
    place, f = lax.axis_index("seq"), lax.axis_index("feat")
    groups, block = qkv_ref.shape[0], qkv_ref.shape[1]
    width = heads * FDIM
    tables = (left_ref, right_ref, rows_ref)

    def hop(g):
        target = {"seq": lax.rem(place + 1, count)}
        return [
            pltpu.make_async_remote_copy(
                src_ref=src.at[g],
                dst_ref=dst.at[g],
                send_sem=send_sem.at[i, g],
                recv_sem=recv_sem.at[i, g],
                device_id=target,
                device_id_type=MESH,
            )
            for i, (src, dst) in enumerate(((send_state, carry_ref), (send_sum, csum_ref)))
        ]

    def send(g):
        for copy in hop(g):
            copy.start()

    chain = [lax.rem(place + 1, count), lax.rem(place + count - 1, count)]
    stay = pltpu.make_async_copy(cot_ref, cots_ref.at[f], local_sem.at[0])
    stay.start()
    greet(square_targets(f) + [{"seq": c} for c in chain])
    gather = SquareGather(cots_ref, f, f_send, f_recv, cot_ref)
    gather.start()

    @pl.when(place == 0)
    def _():
        carry_ref[...] = jnp.zeros_like(carry_ref)
        csum_ref[...] = jnp.full_like(csum_ref, -1.0)

    def summarize(g, none):
        segc, segr = segc_ref[g], segr_ref[g]
        tail = segr[:, block - 1 : block]
        at_tail = (segc == tail).astype(f32)
        send_sum[g, heads : heads + 1, :] = jnp.broadcast_to(tail, (1, LANES))
        for h in range(heads):
            key = qkv_ref[g, :, width : 2 * width]
            value = qkv_ref[g, :, 2 * width + h * HV : 2 * width + (h + 1) * HV]
            phi = (features(key, h, *tables) * at_tail).astype(bf16)
            send_state[g, h] = dot_tn(phi, value)[:STATE].astype(bf16)
            ones = jnp.ones((8, block), bf16)
            send_sum[g, h : h + 1, :] = dot(ones, phi)[0:1]

        @pl.when(place == 0)
        def _():
            send(g)

        return none

    lax.fori_loop(0, groups, summarize, 0)
    def join(g, none):
        for copy in hop(g):
            copy.wait_recv()
        segr = segr_ref[g]
        mark = csum_ref[g, heads : heads + 1, 0:1]
        head, tail = segr[:, 0:1], segr[:, block - 1 : block]
        whole = ((head == tail) & (head == mark)).astype(f32)
        for h in range(heads):
            send_state[g, h] = (
                send_state[g, h].astype(f32) + whole * carry_ref[g, h].astype(f32)
            ).astype(bf16)
            send_sum[g, h : h + 1, :] = (
                send_sum[g, h : h + 1, :] + whole * csum_ref[g, h : h + 1, :]
            )
        send(g)
        return none

    def attend(g, none):
        segc, segr = segc_ref[g], segr_ref[g]
        allowed = allowed_of(segc, segr)
        for h in range(heads):
            query = only_head(qkv_ref[g, :, 0:width], h)
            key = qkv_ref[g, :, width : 2 * width]
            value = qkv_ref[g, :, 2 * width + h * HV : 2 * width + (h + 1) * HV]
            c = dot_nt(query, key)
            kernel = jnp.where(allowed, 1.0 + c * (0.25 + c * 0.03125), 0.0).astype(bf16)
            wide = jnp.concatenate([value, jnp.ones_like(value)], axis=1)
            part[g, h] = dot(kernel, wide)

        @pl.when((place > 0) & (place < count - 1) & (g == place - 1))
        def _():
            lax.fori_loop(0, groups, join, 0)

        return none

    lax.fori_loop(0, groups, attend, 0)
    gather.relay()

    def carry_on(g, none):
        segc = segc_ref[g]

        @pl.when(place == count - 1)
        def _():
            for copy in hop(g):
                copy.wait_recv()

        mark = csum_ref[g, heads : heads + 1, 0:1]
        carried = (segc == mark).astype(f32)
        for h in range(heads):
            phi = features(qkv_ref[g, :, 0:width], h, *tables) * carried
            state = padded_state(carry_ref[g, h])
            both = part[g, h]
            numer = both[:, :HV] + dot(phi.astype(bf16), state)
            denom = both[:, HV:] + jnp.sum(
                phi * csum_ref[g, h : h + 1, :], axis=1, keepdims=True
            )
            inverse = 1.0 / denom
            att_ref[g, :, h * HV : (h + 1) * HV] = (numer * inverse).astype(bf16)
            rden_ref[g, :, h * HV : (h + 1) * HV] = inverse
        return none

    lax.fori_loop(0, groups, carry_on, 0)

    @pl.when(place < count - 1)
    def _():
        def finish(g, none):
            for copy in hop(g):
                copy.wait_send()
            return none

        lax.fori_loop(0, groups, finish, 0)

    stay.wait()
    gather.finish()


def backward_kernel(
    count,
    heads,
    qkv_ref,
    segc_ref,
    segr_ref,
    left_ref,
    right_ref,
    rows_ref,
    att_ref,
    rden_ref,
    carry_ref,
    csum_ref,
    ga_ref,
    down_ref,
    res_ref,
    out_ref,
    final_ref,
    gn,
    send_state,
    send_sum,
    recv_state,
    recv_sum,
    dkey,
    dvalue,
    terms,
    land,
    send_sem,
    recv_sem,
    f_send,
    f_recv,
    local_sem,
):
    place, f = lax.axis_index("seq"), lax.axis_index("feat")
    groups, block = qkv_ref.shape[0], qkv_ref.shape[1]
    width = heads * FDIM
    tables = (left_ref, right_ref, rows_ref)

    def hop(g):
        target = {"seq": lax.rem(place + count - 1, count)}
        return [
            pltpu.make_async_remote_copy(
                src_ref=src.at[g],
                dst_ref=dst.at[g],
                send_sem=send_sem.at[i, g],
                recv_sem=recv_sem.at[i, g],
                device_id=target,
                device_id_type=MESH,
            )
            for i, (src, dst) in enumerate(((send_state, recv_state), (send_sum, recv_sum)))
        ]

    def send(g):
        for copy in hop(g):
            copy.start()

    chain = [lax.rem(place + 1, count), lax.rem(place + count - 1, count)]
    greet(square_targets(f) + [{"seq": c} for c in chain])
    fill = pltpu.make_async_copy(down_ref, terms, local_sem.at[0])
    fill.start()
    ring = SquareSum(terms, land, f, f_send, f_recv)

    @pl.when(place == count - 1)
    def _():
        recv_state[...] = jnp.zeros_like(recv_state)
        recv_sum[...] = jnp.full_like(recv_sum, -1.0)

    def summarize(g, none):
        segc, segr = segc_ref[g], segr_ref[g]
        head = segr[:, 0:1]
        at_head = (segc == head).astype(f32)
        send_sum[g, heads : heads + 1, :] = jnp.broadcast_to(head, (1, LANES))
        for h in range(heads):
            lanes = slice(h * HV, (h + 1) * HV)
            ga = ga_ref[g, :, lanes]
            inverse = rden_ref[g, :, lanes]
            numer = (ga * inverse).astype(bf16)
            dots = jnp.sum(ga * att_ref[g, :, lanes].astype(f32), axis=1, keepdims=True)
            lane = lax.broadcasted_iota(jnp.int32, (block, HV), 1)
            denom = jnp.where(lane == 0, -dots * inverse, 0.0).astype(bf16)
            gn[g, h, :, :HV] = numer
            gn[g, h, :, HV:] = denom
            phi = (features(qkv_ref[g, :, 0:width], h, *tables) * at_head).astype(bf16)
            send_state[g, h] = dot_tn(phi, numer)[:STATE].astype(bf16)
            send_sum[g, h : h + 1, :] = dot_tn(denom, phi)[0:1]

        @pl.when(place == count - 1)
        def _():
            send(g)

        return none

    lax.fori_loop(0, groups, summarize, 0)
    fill.wait()
    ring.start_cross()
    ring.start_near()

    def join(g, none):
        for copy in hop(g):
            copy.wait_recv()
        segr = segr_ref[g]
        mark = recv_sum[g, heads : heads + 1, 0:1]
        head, tail = segr[:, 0:1], segr[:, block - 1 : block]
        whole = ((head == tail) & (head == mark)).astype(f32)
        for h in range(heads):
            send_state[g, h] = (
                send_state[g, h].astype(f32) + whole * recv_state[g, h].astype(f32)
            ).astype(bf16)
            send_sum[g, h : h + 1, :] = (
                send_sum[g, h : h + 1, :] + whole * recv_sum[g, h : h + 1, :]
            )
        send(g)
        return none

    def pull(g, none):
        segc, segr = segc_ref[g], segr_ref[g]
        allowed = allowed_of(segc, segr)
        query_all = qkv_ref[g, :, 0:width]
        key_all = qkv_ref[g, :, width : 2 * width]
        carried = (segc == csum_ref[g, heads : heads + 1, 0:1]).astype(f32)
        dquery = jnp.zeros((block, width), f32)
        dkey_sum = jnp.zeros((block, width), f32)
        for h in range(heads):
            query, key = only_head(query_all, h), only_head(key_all, h)
            value = qkv_ref[g, :, 2 * width + h * HV : 2 * width + (h + 1) * HV]
            wide = jnp.concatenate([value, jnp.ones_like(value)], axis=1)
            both = gn[g, h]
            c = dot_nt(query, key_all)
            kernel = jnp.where(allowed, 1.0 + c * (0.25 + c * 0.03125), 0.0).astype(bf16)
            grad = jnp.where(allowed, dot_nt(both, wide), 0.0)
            grad_c = (grad * (0.25 + c * 0.0625)).astype(bf16)
            dvalue[g, h] = dot_tn(kernel, both[:, :HV])
            dkey_sum = dkey_sum + dot_tn(grad_c, query)
            dquery = dquery + dot(grad_c, key)
            state = padded_state(carry_ref[g, h])
            gphi = dot_nt(both[:, :HV], state) + both[:, HV : HV + 1].astype(f32) * csum_ref[
                g, h : h + 1, :
            ]
            dquery = dquery + pull_features(gphi * carried, query_all, h, *tables)
        out_ref[g, :, 0:width] = dquery.astype(bf16)
        dkey[g] = dkey_sum

        @pl.when((place > 0) & (place < count - 1) & (g == count - 2 - place))
        def _():
            lax.fori_loop(0, groups, join, 0)

        return none

    lax.fori_loop(0, groups, pull, 0)
    ring.relay()

    def carry_back(g, none):
        segc = segc_ref[g]
        key_all = qkv_ref[g, :, width : 2 * width]

        @pl.when(place == 0)
        def _():
            for copy in hop(g):
                copy.wait_recv()

        mark = recv_sum[g, heads : heads + 1, 0:1]
        later = (segc == mark).astype(f32)
        total = dkey[g]
        for h in range(heads):
            value = qkv_ref[g, :, 2 * width + h * HV : 2 * width + (h + 1) * HV]
            state = padded_state(recv_state[g, h])
            phi = (features(key_all, h, *tables) * later).astype(bf16)
            dv = dvalue[g, h] + dot(phi, state)
            out_ref[g, :, 2 * width + h * HV : 2 * width + (h + 1) * HV] = dv.astype(bf16)
            gphi = (dot_nt(value, state) + recv_sum[g, h : h + 1, :]) * later
            total = total + pull_features(gphi, key_all, h, *tables)
        out_ref[g, :, width : 2 * width] = total.astype(bf16)
        return none

    lax.fori_loop(0, groups, carry_back, 0)

    @pl.when(place > 0)
    def _():
        def finish(g, none):
            for copy in hop(g):
                copy.wait_send()
            return none

        lax.fori_loop(0, groups, finish, 0)

    ring.arrive()

    def add_up(rows, total):
        final_ref[rows, :] = (res_ref[rows, :] + total).astype(bf16)

    by_rows(ring, add_up)
    ring.finish()


def whole_vmem(count):
    return [pl.BlockSpec(memory_space=pltpu.VMEM)] * count


def attention_forward(qkv, segc, segr, tables, cot_own, heads):
    groups, block, _ = qkv.shape
    count = lax.axis_size("seq")
    dma = pltpu.SemaphoreType.DMA
    states = (groups, heads, STATE, HV)
    sums = (groups, 8, LANES)
    return pl.pallas_call(
        functools.partial(forward_kernel, count, heads),
        out_shape=(
            jax.ShapeDtypeStruct((groups, block, heads * HV), bf16),
            jax.ShapeDtypeStruct((groups, block, heads * HV), f32),
            jax.ShapeDtypeStruct(states, bf16),
            jax.ShapeDtypeStruct(sums, f32),
            jax.ShapeDtypeStruct((groups,) + cot_own.shape, bf16),
        ),
        in_specs=whole_vmem(6) + in_place(1),
        out_specs=tuple(whole_vmem(4) + in_place(1)),
        scratch_shapes=[
            pltpu.VMEM(states, bf16),
            pltpu.VMEM(sums, f32),
            pltpu.VMEM((groups, heads, block, 2 * HV), f32),
            dma((2, groups)),
            dma((2, groups)),
            dma((6,)),
            dma((6,)),
            dma((1,)),
        ],
        compiler_params=pltpu.CompilerParams(
            collective_id=0, has_side_effects=True, vmem_limit_bytes=40 << 20
        ),
        cost_estimate=pl.CostEstimate(flops=0, bytes_accessed=1 << 20, transcendentals=0),
        name="attention_forward",
    )(qkv, segc, segr, *tables, cot_own)


def attention_backward(
    qkv, segc, segr, tables, att, rden, carry, csum, ga, down, residual, heads
):
    groups, block, wide = qkv.shape
    count = lax.axis_size("seq")
    states = (groups, heads, STATE, HV)
    sums = (groups, 8, LANES)
    return pl.pallas_call(
        functools.partial(backward_kernel, count, heads),
        out_shape=(
            jax.ShapeDtypeStruct((groups, block, wide), bf16),
            jax.ShapeDtypeStruct(residual.shape, bf16),
        ),
        in_specs=whole_vmem(11) + in_place(1) + whole_vmem(1),
        out_specs=tuple(whole_vmem(2)),
        scratch_shapes=[
            pltpu.VMEM((groups, heads, block, 2 * HV), bf16),
            pltpu.VMEM(states, bf16),
            pltpu.VMEM(sums, f32),
            pltpu.VMEM(states, bf16),
            pltpu.VMEM(sums, f32),
            pltpu.VMEM((groups, block, heads * FDIM), f32),
            pltpu.VMEM((groups, heads, block, HV), f32),
            pltpu.VMEM((groups,) + residual.shape, bf16),
            pltpu.VMEM((6, block // 2, residual.shape[1]), bf16),
            pltpu.SemaphoreType.DMA((2, groups)),
            pltpu.SemaphoreType.DMA((2, groups)),
            pltpu.SemaphoreType.DMA((6,)),
            pltpu.SemaphoreType.DMA((6,)),
            pltpu.SemaphoreType.DMA((1,)),
        ],
        compiler_params=pltpu.CompilerParams(
            collective_id=1, has_side_effects=True, vmem_limit_bytes=48 << 20
        ),
        cost_estimate=pl.CostEstimate(flops=0, bytes_accessed=1 << 20, transcendentals=0),
        name="attention_backward",
    )(qkv, segc, segr, *tables, att, rden, carry, csum, ga, down, residual)


def peers(f):
    return 2 * (f // 2) + 1 - f % 2, (f + 2) % 4, 3 - f


def greet(targets):
    barrier = pltpu.get_barrier_semaphore()
    for target in targets:
        pl.semaphore_signal(barrier, inc=1, device_id=target, device_id_type=MESH)
    pl.semaphore_wait(barrier, len(targets))


def push(src, dst, send_sem, recv_sem, target):
    return pltpu.make_async_remote_copy(
        src_ref=src,
        dst_ref=dst,
        send_sem=send_sem,
        recv_sem=recv_sem,
        device_id=target,
        device_id_type=MESH,
    )


def square_targets(f):
    return [{"feat": p} for p in peers(f)]


class SquareGather:
    def __init__(self, slots, f, send_sem, recv_sem, own=None):
        side, above, across = peers(f)
        half = slots.shape[1] // 2
        first, second = pl.ds(0, half), pl.ds(half, half)

        def copy(i, slot, rows, to):
            ref = slots.at[slot, rows]
            src = ref if own is None or i > 3 else own.at[rows]
            return push(src, ref, send_sem.at[i], recv_sem.at[i], {"feat": to})

        self.direct = [
            copy(0, f, first, side),
            copy(1, f, second, above),
            copy(2, f, second, side),
            copy(3, f, first, above),
        ]
        self.forward = [copy(4, side, first, above), copy(5, above, second, side)]

    def start(self):
        for c in self.direct:
            c.start()

    def relay(self):
        self.direct[0].wait_recv()
        self.forward[0].start()
        self.direct[1].wait_recv()
        self.forward[1].start()

    def near(self):
        self.direct[2].wait_recv()
        self.direct[3].wait_recv()

    def far(self):
        for c in self.forward:
            c.wait_recv()

    def sent(self):
        for c in self.direct + self.forward:
            c.wait_send()

    def finish(self):
        self.near()
        self.far()
        self.sent()


class SquareSum:
    def __init__(self, part, land, f, send_sem, recv_sem):
        self.side, self.above, self.across = peers(f)
        self.f, self.part, self.land = f, part, land
        self.half = part.shape[1] // 2
        first, second = pl.ds(0, self.half), pl.ds(self.half, self.half)

        def copy(i, slot, rows, to):
            return push(
                part.at[slot, rows], land.at[i], send_sem.at[i], recv_sem.at[i], {"feat": to}
            )

        self.cross = [copy(0, self.across, first, self.side), copy(1, self.across, second, self.above)]
        self.near = [copy(2, self.side, first, self.side), copy(3, self.above, second, self.above)]
        self.late = [copy(4, self.above, first, self.above), copy(5, self.side, second, self.side)]

    def start_cross(self):
        for c in self.cross:
            c.start()

    def add_rows(self, slot, base, landed):
        step = 32

        def one(i, none):
            rows = pl.ds(pl.multiple_of(base + i * step, step), step)
            came = self.land[landed, pl.ds(pl.multiple_of(i * step, step), step), :]
            self.part[slot, rows, :] = (
                self.part[slot, rows, :].astype(f32) + came.astype(f32)
            ).astype(bf16)
            return none

        lax.fori_loop(0, self.half // step, one, 0)

    def start_near(self):
        for c in self.near:
            c.start()

    def relay(self):
        self.cross[0].wait_recv()
        self.add_rows(self.above, 0, 0)
        self.late[0].start()
        self.cross[1].wait_recv()
        self.add_rows(self.side, self.half, 1)
        self.late[1].start()

    def arrive(self):
        for c in self.near + self.late:
            c.wait_recv()

    def total(self, half, rows):
        base = half * self.half
        own = self.part[self.f, pl.ds(pl.multiple_of(base + rows.start, 16), rows.size), :]
        near = self.land[2 + half, rows, :]
        late = self.land[4 + half, rows, :]
        return own.astype(f32) + near.astype(f32) + late.astype(f32)

    def finish(self):
        for c in self.cross + self.near + self.late:
            c.wait_send()


class RowSum:
    def __init__(self, term, acc, shares, lands, sems, f, s, d, seqs, dps):
        self.term, self.acc, self.shares, self.lands = term, acc, shares, lands
        self.f, self.s, self.d = f, s, d
        self.parts, self.seqs = term.shape[0], seqs
        columns = [lax.rem(s + k, seqs) for k in range(1, seqs)]
        others = [lax.rem(d + k, dps) for k in range(1, dps)]
        d_send, d_recv, z_send, z_recv, a_send, a_recv = sems
        self.one = [
            push(term.at[:, :, o], lands[0].at[k], d_send.at[k], d_recv.at[k], {"dp": o})
            for k, o in enumerate(others)
        ]
        self.two = [
            push(acc.at[c], lands[1].at[k], z_send.at[k], z_recv.at[k], {"seq": c})
            for k, c in enumerate(columns)
        ]
        self.three = [
            push(lands[2].at[p], shares.at[f], a_send.at[i], a_recv.at[i], {"feat": p})
            for i, p in enumerate(peers(f))
        ]

    def start(self):
        for c in self.one:
            c.start()

    def over_seq(self):
        for c in self.one:
            c.wait_recv()

        def one(i, none):
            p, c = i // self.seqs, lax.rem(i, self.seqs)
            total = self.term[p, c, self.d].astype(f32)
            for k in range(len(self.one)):
                total = total + self.lands[0][k, p, c].astype(f32)
            self.acc[c, p] = total.astype(bf16)
            return none

        lax.fori_loop(0, self.parts * self.seqs, one, 0)
        for c in self.two:
            c.start()

    def over_feat(self):
        for c in self.two:
            c.wait_recv()

        def one(p, none):
            total = self.acc[self.s, p].astype(f32)
            for k in range(len(self.two)):
                total = total + self.lands[1][k, p].astype(f32)
            self.lands[2][p] = total.astype(bf16)
            return none

        lax.fori_loop(0, self.parts, one, 0)
        self.shares[self.f] = self.lands[2][self.f]
        for c in self.three:
            c.start()

    def arrive(self):
        for c in self.three:
            c.wait_recv()

    def finish(self):
        for c in self.one + self.two + self.three:
            c.wait_send()


def row_sum_scratch(shape):
    parts, seqs, dps, rows, wide = shape
    others = max(dps - 1, 1)
    dma = pltpu.SemaphoreType.DMA
    return [
        pltpu.VMEM((parts, rows, wide), bf16),
        pltpu.VMEM((seqs, parts, rows, wide), bf16),
        pltpu.VMEM((others, parts, seqs, rows, wide), bf16),
        pltpu.VMEM((seqs - 1, parts, rows, wide), bf16),
        pltpu.VMEM((parts, rows, wide), bf16),
        dma((others,)),
        dma((others,)),
        dma((seqs - 1,)),
        dma((seqs - 1,)),
        dma((3,)),
        dma((3,)),
    ]


def row_sum(term, scratch, f, s, d, seqs, dps):
    shares, acc = scratch[:2]
    return RowSum(term, acc, shares, scratch[2:5], scratch[5:], f, s, d, seqs, dps)


def opening_kernel(
    seqs,
    dps,
    tok_ref,
    query_ref,
    key_ref,
    value_ref,
    out_ref,
    one_ref,
    two_ref,
    x_ref,
    w_ref,
    g_ref,
    o_ref,
    pack,
    opack,
    tile,
    x_send,
    x_recv,
    a_send,
    a_recv,
    z_send,
    z_recv,
    d_send,
    d_recv,
    local_sem,
):
    f, s, d = lax.axis_index("feat"), lax.axis_index("seq"), lax.axis_index("dp")
    parts, rows_each = pack.shape[0], pack.shape[1]
    near = peers(f)
    columns = [lax.rem(s + k, seqs) for k in range(1, seqs)]
    others = [lax.rem(d + k, dps) for k in range(1, dps)]
    stay = pltpu.make_async_copy(tok_ref, x_ref.at[f], local_sem.at[0])
    stay.start()
    first = 0
    for ref in (query_ref, key_ref, value_ref):
        each = ref.shape[1] // parts
        for p in range(parts):
            pack[p, :, first : first + each] = ref[:, p * each : (p + 1) * each]
        first += each
    tile[...] = jnp.zeros_like(tile)
    tile[0:1, :rows_each] = one_ref[...].astype(f32)
    tile[1:2, :rows_each] = two_ref[...].astype(f32)
    outs = (w_ref, g_ref)
    own = [
        pltpu.make_async_copy(pack.at[f], w_ref.at[f, s, d], local_sem.at[1]),
        pltpu.make_async_copy(tile, g_ref.at[f, s, d], local_sem.at[2]),
    ]
    for c in own:
        c.start()
    greet(
        square_targets(f) + [{"seq": c} for c in columns] + [{"dp": o} for o in others]
    )
    shares = [
        [
            push(pack.at[p], w_ref.at[f, s, d], a_send.at[0, i], a_recv.at[0, i], {"feat": p}),
            push(tile, g_ref.at[f, s, d], a_send.at[1, i], a_recv.at[1, i], {"feat": p}),
        ]
        for i, p in enumerate(near)
    ]
    for pair in shares:
        for c in pair:
            c.start()
    gather = SquareGather(x_ref, f, x_send, x_recv, tok_ref)
    gather.start()
    each = out_ref.shape[1] // parts
    for p in range(parts):
        opack[p] = out_ref[:, p * each : (p + 1) * each]
    own_out = pltpu.make_async_copy(opack.at[f], o_ref.at[f], local_sem.at[3])
    own_out.start()
    out_shares = [
        push(opack.at[p], o_ref.at[f], a_send.at[2, i], a_recv.at[2, i], {"feat": p})
        for i, p in enumerate(near)
    ]
    for c in out_shares:
        c.start()
    for c in own:
        c.wait()

    chunks = (f,) + near

    def to_column(n, k):
        return [
            push(
                ref.at[chunks[n], s, d],
                ref.at[chunks[n], s, d],
                z_send.at[j, k - 1, n],
                z_recv.at[j, k - 1, n],
                {"seq": columns[k - 1]},
            )
            for j, ref in enumerate(outs)
        ]

    def to_sibling(n, k):
        back = lax.rem(s + seqs - k, seqs)
        return [
            push(
                ref.at[chunks[n], back, d],
                ref.at[chunks[n], back, d],
                d_send.at[j, o, k, n],
                d_recv.at[j, o, k, n],
                {"dp": other},
            )
            for j, ref in enumerate(outs)
            for o, other in enumerate(others)
        ]

    def start_all(copies):
        for c in copies:
            c.start()

    for n in range(parts):
        if n:
            for c in shares[n - 1]:
                c.wait_recv()
        for k in range(1, seqs):
            start_all(to_column(n, k))
        start_all(to_sibling(n, 0))
    for n in range(parts):
        for k in range(1, seqs):
            for c in to_column(n, k):
                c.wait_recv()
            start_all(to_sibling(n, k))
    gather.relay()
    for n in range(parts):
        for k in range(seqs):
            for c in to_sibling(n, k):
                c.wait_recv()
    for n in range(parts):
        for k in range(seqs):
            for c in to_sibling(n, k):
                c.wait_send()
        for k in range(1, seqs):
            for c in to_column(n, k):
                c.wait_send()
    for pair in shares:
        for c in pair:
            c.wait_send()
    stay.wait()
    own_out.wait()
    for c in out_shares:
        c.wait_recv()
    for c in out_shares:
        c.wait_send()
    gather.finish()


def in_place(count):
    return [pl.BlockSpec(memory_space=pl.ANY)] * count


def opening(own, w_query, w_key, w_value, w_out, gain_one, gain_two):
    parts, seqs, dps = (lax.axis_size(a) for a in ALL)
    block, width = own.shape
    rows_each = w_query.shape[0]
    wide = (w_query.shape[1] + w_key.shape[1] + w_value.shape[1]) // parts
    others = max(dps - 1, 1)
    dma = pltpu.SemaphoreType.DMA
    out_wide = w_out.shape[1] // parts
    x_all, w_all, g_all, o_own = pl.pallas_call(
        functools.partial(opening_kernel, seqs, dps),
        out_shape=(
            jax.ShapeDtypeStruct((parts, block, width), bf16),
            jax.ShapeDtypeStruct((parts, seqs, dps, rows_each, wide), bf16),
            jax.ShapeDtypeStruct((parts, seqs, dps, 8, HV), f32),
            jax.ShapeDtypeStruct((parts, rows_each, out_wide), bf16),
        ),
        in_specs=in_place(1) + whole_vmem(6),
        out_specs=tuple(in_place(4)),
        scratch_shapes=[
            pltpu.VMEM((parts, rows_each, wide), bf16),
            pltpu.VMEM((parts, rows_each, out_wide), bf16),
            pltpu.VMEM((8, HV), f32),
            dma((6,)),
            dma((6,)),
            dma((3, 3)),
            dma((3, 3)),
            dma((2, seqs - 1, parts)),
            dma((2, seqs - 1, parts)),
            dma((2, others, seqs, parts)),
            dma((2, others, seqs, parts)),
            dma((4,)),
        ],
        compiler_params=pltpu.CompilerParams(collective_id=2, has_side_effects=True),
        cost_estimate=pl.CostEstimate(flops=0, bytes_accessed=1 << 20, transcendentals=0),
        name="opening",
    )(own, w_query, w_key, w_value, w_out, gain_one, gain_two)
    gains = g_all[..., :2, :rows_each].transpose(3, 0, 1, 2, 4).reshape(2, width)
    return x_all, w_all.reshape(width, wide), gains, o_own


def inverse_rms(values):
    return lax.rsqrt(jnp.mean(values * values, axis=-1, keepdims=True) + epsilon)


def norm_back(grad, unit, inverse, gain):
    scaled = grad * gain
    return (scaled - unit * jnp.mean(scaled * unit, axis=-1, keepdims=True)) * inverse


class ByShare:
    def __init__(self, ref):
        self.ref = ref

    def tile(self, i, size):
        block = self.ref[:, i]
        return block.reshape(size, block.shape[2])


class ByTiles:
    def __init__(self, src, ref, sem, tile):
        self.ref = ref
        self.fills = [
            pltpu.make_async_copy(
                src.at[pl.ds(i * tile, tile)], ref.at[pl.ds(i * tile, tile)], sem.at[i]
            )
            for i in range(ref.shape[0] // tile)
        ]

    def tile(self, i, size):
        return self.ref[pl.ds(pl.multiple_of(i * size, size), size), :]


def product_tiles(part, slot, pairs, tile, first=False):
    def one(i, none):
        cols = pl.ds(pl.multiple_of(i * tile, tile), tile)
        total = None
        for rows, weights in pairs:
            if hasattr(weights, "tile"):
                block = weights.tile(i, tile)
            else:
                block = weights[cols, :]
            term = dot_nt(rows[slot], block)
            total = term if total is None else total + term
        part[slot, :, cols] = total.astype(bf16)
        return none

    if first:
        for i in range(part.shape[2] // tile):
            for _, weights in pairs:
                weights.fills[i].wait()
            one(i, 0)
    else:
        lax.fori_loop(0, part.shape[2] // tile, one, 0)


def summed_products(part, land, f, pairs, send_sem, recv_sem, beside=None, first=False):
    side, above, across = peers(f)
    ring = SquareSum(part, land, f, send_sem, recv_sem)
    product_tiles(part, across, pairs, 512, first)
    ring.start_cross()
    product_tiles(part, side, pairs, 512)
    ring.near[0].start()
    product_tiles(part, above, pairs, 512)
    ring.near[1].start()
    ring.relay()
    product_tiles(part, f, pairs, 512)
    if beside is not None:
        beside()
    ring.arrive()
    return ring


def by_rows(ring, body, step=16):
    for half in (0, 1):

        def one(i, none):
            start = pl.multiple_of(i * step, step)
            rows = pl.ds(pl.multiple_of(half * ring.half + i * step, step), step)
            body(rows, ring.total(half, pl.ds(start, step)))
            return none

        lax.fori_loop(0, ring.half // step, one, 0)


def branch_kernel(
    att_ref, w_ref, tok_ref, gain_ref, rows_ref, res_ref, part, land, s_send, s_recv, g_send, g_recv
):
    f = lax.axis_index("feat")
    greet(square_targets(f))
    ring = summed_products(part, land, f, [(att_ref, ByShare(w_ref))], s_send, s_recv)

    def finish_rows(rows, total):
        residual = tok_ref[rows, :].astype(f32) + total
        res_ref[rows, :] = residual
        rows_ref[f, rows, :] = (residual * inverse_rms(residual) * gain_ref[...]).astype(bf16)

    by_rows(ring, finish_rows)
    gather = SquareGather(rows_ref, f, g_send, g_recv)
    gather.start()
    ring.finish()
    gather.relay()
    gather.finish()


def square_scratch(parts, block, width):
    dma = pltpu.SemaphoreType.DMA
    return [
        pltpu.VMEM((parts, block, width), bf16),
        pltpu.VMEM((6, block // 2, width), bf16),
        dma((6,)),
        dma((6,)),
    ]


def branch_step(att, out_w, own, gain_two):
    parts, block, _ = att.shape
    width = own.shape[1]
    dma = pltpu.SemaphoreType.DMA
    return pl.pallas_call(
        branch_kernel,
        out_shape=(
            jax.ShapeDtypeStruct((parts, block, width), bf16),
            jax.ShapeDtypeStruct((block, width), f32),
        ),
        in_specs=whole_vmem(4),
        out_specs=tuple(whole_vmem(2)),
        scratch_shapes=square_scratch(parts, block, width) + [dma((6,)), dma((6,))],
        compiler_params=pltpu.CompilerParams(
            collective_id=3, has_side_effects=True, vmem_limit_bytes=48 << 20
        ),
        cost_estimate=pl.CostEstimate(flops=0, bytes_accessed=1 << 20, transcendentals=0),
        name="branch_step",
    )(att, out_w, own, gain_two)


def rows_back_kernel(
    gg_ref,
    gu_ref,
    wg_hbm,
    wu_hbm,
    res_ref,
    cot_ref,
    gain_ref,
    mixed_hbm,
    wd_hbm,
    wo_hbm,
    all_ref,
    gres_ref,
    gsum_ref,
    down_ref,
    ga_ref,
    part,
    land,
    wg,
    wu,
    mixed,
    wd,
    wo,
    s_send,
    s_recv,
    g_send,
    g_recv,
    local_sem,
    tile_sem,
):
    f = lax.axis_index("feat")
    weights = [
        ByTiles(src, dst, tile_sem.at[i], 512)
        for i, (src, dst) in enumerate(((wg_hbm, wg), (wu_hbm, wu)))
    ]
    for pair in zip(*(w.fills for w in weights)):
        for c in pair:
            c.start()
    fills = [
        pltpu.make_async_copy(src, dst, local_sem.at[i])
        for i, (src, dst) in enumerate(((mixed_hbm, mixed), (wd_hbm, wd), (wo_hbm, wo)))
    ]
    for c in fills:
        c.start()
    greet(square_targets(f))
    pairs = [(gg_ref, weights[0]), (gu_ref, weights[1])]

    def down_products():
        for p in range(part.shape[0]):
            product_tiles(down_ref, p, [(mixed, wd)], 512)

    ring = summed_products(part, land, f, pairs, s_send, s_recv, first=True)
    gsum_ref[...] = jnp.zeros_like(gsum_ref)

    def finish_rows(rows, grad):
        residual = res_ref[rows, :]
        inverse = inverse_rms(residual)
        unit = residual * inverse
        gsum_ref[...] += jnp.sum(grad * unit, axis=0, keepdims=True)
        grad_res = cot_ref[rows, :].astype(f32) + norm_back(grad, unit, inverse, gain_ref[...])
        gres_ref[rows, :] = grad_res
        all_ref[f, rows, :] = grad_res.astype(bf16)

    by_rows(ring, finish_rows)
    gather = SquareGather(all_ref, f, g_send, g_recv)
    gather.start()
    ring.finish()
    side, above, across = peers(f)

    def attended_grad(slot):
        blocks = ByShare(wo)
        size = all_ref.shape[2] // wo.shape[1]
        total = None
        for i in range(wo.shape[1]):
            term = dot(all_ref[slot, :, i * size : (i + 1) * size], blocks.tile(i, size))
            total = term if total is None else total + term
        ga_ref[slot] = total

    for c in fills:
        c.wait()
    attended_grad(f)
    down_products()
    gather.relay()
    gather.near()
    attended_grad(side)
    attended_grad(above)
    gather.far()
    attended_grad(across)
    gather.sent()


def rows_back(
    grad_gate, grad_up, gate_w, up_w, residual, cot_own, gain_two, mixed, down_w, out_w
):
    parts, block, hidden = grad_gate.shape
    width = residual.shape[1]
    dma = pltpu.SemaphoreType.DMA
    return pl.pallas_call(
        rows_back_kernel,
        out_shape=(
            jax.ShapeDtypeStruct((parts, block, width), bf16),
            jax.ShapeDtypeStruct((block, width), f32),
            jax.ShapeDtypeStruct((1, width), f32),
            jax.ShapeDtypeStruct((parts, block, width), bf16),
            jax.ShapeDtypeStruct((parts, block, out_w.shape[3]), f32),
        ),
        in_specs=whole_vmem(2) + in_place(2) + whole_vmem(3) + in_place(3),
        out_specs=tuple(whole_vmem(5)),
        scratch_shapes=square_scratch(parts, block, width)[:2]
        + [
            pltpu.VMEM((width, hidden), bf16),
            pltpu.VMEM((width, hidden), bf16),
            pltpu.VMEM((parts, block, hidden), bf16),
            pltpu.VMEM((width, hidden), bf16),
            pltpu.VMEM(out_w.shape, bf16),
        ]
        + [dma((6,))] * 4
        + [dma((3,)), dma((2, width // 512))],
        compiler_params=pltpu.CompilerParams(
            collective_id=4, has_side_effects=True, vmem_limit_bytes=60 << 20
        ),
        cost_estimate=pl.CostEstimate(flops=0, bytes_accessed=1 << 20, transcendentals=0),
        name="rows_back",
    )(grad_gate, grad_up, gate_w, up_w, residual, cot_own, gain_two, mixed, down_w, out_w)


def closing_kernel(
    seqs,
    dps,
    dqkv_ref,
    w_ref,
    tok_ref,
    gres_ref,
    gain_ref,
    gsum_two_ref,
    term_ref,
    osum_ref,
    x_ref,
    tile_ref,
    query_ref,
    key_ref,
    value_ref,
    ograd_ref,
    part,
    land,
    s_send,
    s_recv,
    gsum,
    cut,
    came,
    mid,
    tail,
    c_send,
    c_recv,
    d_send,
    d_recv,
    oland,
    o_send,
    o_recv,
    *sum_scratch,
):
    f, s, d = lax.axis_index("feat"), lax.axis_index("seq"), lax.axis_index("dp")
    parts = 4
    others = [lax.rem(d + k, dps) for k in range(1, dps)]
    circle = [
        (lax.rem(f + i, parts), lax.rem(s + j, seqs))
        for i in range(parts)
        for j in range(seqs)
        if i or j
    ]
    greet(
        [{"feat": a, "seq": b} for a, b in circle] + [{"dp": o} for o in others]
    )
    rows_sum = row_sum(term_ref, sum_scratch, f, s, d, seqs, dps)
    rows_sum.start()
    outs = [
        push(osum_ref.at[p], oland.at[f], o_send.at[i], o_recv.at[i], {"feat": p})
        for i, p in enumerate(peers(f))
    ]
    for c in outs:
        c.start()
    ring = summed_products(
        part, land, f, [(dqkv_ref, w_ref)], s_send, s_recv, rows_sum.over_seq
    )
    gsum[...] = jnp.zeros_like(gsum)

    def finish_rows(rows, grad):
        values = tok_ref[rows, :].astype(f32)
        inverse = inverse_rms(values)
        unit = values * inverse
        gsum[...] += jnp.sum(grad * unit, axis=0, keepdims=True)
        x_ref[rows, :] = gres_ref[rows, :] + norm_back(grad, unit, inverse, gain_ref[...])

    by_rows(ring, finish_rows)
    rows_sum.over_feat()
    ring.finish()

    lanes = gsum.shape[1] // (parts * seqs)
    cut[...] = jnp.zeros_like(cut)
    for k in range(parts * seqs):
        cut[k, 0:1, :] = gsum[:, k * lanes : (k + 1) * lanes]
        cut[k, 1:2, :] = gsum_two_ref[:, k * lanes : (k + 1) * lanes]
    place = f * seqs + s
    sends = []
    for i, (a, b) in enumerate(circle):
        sends.append(
            push(
                cut.at[a * seqs + b],
                came.at[i],
                c_send.at[i],
                c_recv.at[i],
                {"feat": a, "seq": b},
            )
        )
    for c in sends:
        c.start()
    total = cut[place]
    for c in sends:
        c.wait_recv()
    for i in range(len(circle)):
        total = total + came[i]
    mid[...] = total
    last = [
        push(mid, tail.at[k], d_send.at[k], d_recv.at[k], {"dp": o})
        for k, o in enumerate(others)
    ]
    for c in last:
        c.start()
    for c in last:
        c.wait_recv()
    for k in range(len(others)):
        total = total + tail[k]
    tile_ref[...] = total
    rows_sum.arrive()
    first = 0
    for ref in (query_ref, key_ref, value_ref):
        each = ref.shape[1] // parts
        for p in range(parts):
            piece = rows_sum.shares[p, :, first : first + each]
            ref[:, p * each : (p + 1) * each] = piece.astype(f32)
        first += each
    rows_sum.finish()
    oland[f] = osum_ref[f]
    for c in outs:
        c.wait_recv()
    each = ograd_ref.shape[1] // parts
    for p in range(parts):
        ograd_ref[:, p * each : (p + 1) * each] = oland[p].astype(f32)
    for c in outs + sends + last:
        c.wait_send()


def closing(dqkv, qkv_w, own, grad_residual, gain_one, gain_two_sum, qkv_term, out_sum):
    parts, seqs, dps = (lax.axis_size(a) for a in ALL)
    block, width = own.shape
    others = max(dps - 1, 1)
    lanes = width // (parts * seqs)
    circle = parts * seqs - 1
    rows_each = qkv_term.shape[3]
    dma = pltpu.SemaphoreType.DMA
    return pl.pallas_call(
        functools.partial(closing_kernel, seqs, dps),
        out_shape=(
            jax.ShapeDtypeStruct((block, width), f32),
            jax.ShapeDtypeStruct((8, lanes), f32),
            jax.ShapeDtypeStruct((rows_each, HEADS * FDIM), f32),
            jax.ShapeDtypeStruct((rows_each, HEADS * FDIM), f32),
            jax.ShapeDtypeStruct((rows_each, HEADS * HV), f32),
            jax.ShapeDtypeStruct((rows_each, HEADS * HV), f32),
        ),
        in_specs=whole_vmem(8),
        out_specs=tuple(whole_vmem(6)),
        scratch_shapes=square_scratch(parts, block, width)
        + [
            pltpu.VMEM((1, width), f32),
            pltpu.VMEM((parts * seqs, 8, lanes), f32),
            pltpu.VMEM((circle, 8, lanes), f32),
            pltpu.VMEM((8, lanes), f32),
            pltpu.VMEM((others, 8, lanes), f32),
            dma((circle,)),
            dma((circle,)),
            dma((others,)),
            dma((others,)),
            pltpu.VMEM(out_sum.shape, bf16),
            dma((3,)),
            dma((3,)),
        ]
        + row_sum_scratch(qkv_term.shape),
        compiler_params=pltpu.CompilerParams(
            collective_id=5, has_side_effects=True, vmem_limit_bytes=48 << 20
        ),
        cost_estimate=pl.CostEstimate(flops=0, bytes_accessed=1 << 20, transcendentals=0),
        name="closing",
    )(dqkv, qkv_w, own, grad_residual, gain_one, gain_two_sum, qkv_term, out_sum)


def local(
    tokens,
    segments,
    norm1_gain,
    norm2_gain,
    w_query,
    w_key,
    w_value,
    w_out,
    w_gate,
    w_up,
    w_down,
    cotangent,
):
    parts = lax.axis_size("feat")
    heads = HEADS // parts
    block, width = tokens.shape[2], tokens.shape[3]
    rows_total = parts * block
    rows_each = w_query.shape[0]
    own = tokens.reshape(block, width)
    cot_own = cotangent.reshape(block, width)

    x_all, qkv_w, gains, out_share = opening(
        own, w_query, w_key, w_value, w_out.T, norm1_gain[None], norm2_gain[None]
    )
    qkv_width = qkv_w.shape[1]
    gate_w = lax.all_gather(w_gate, ("seq", "dp"), axis=0, tiled=True)
    gate_w, out_share, w_up = lax.optimization_barrier((gate_w, out_share, w_up))
    out_w = lax.all_gather(out_share[None], ("seq", "dp"), axis=0, tiled=True)
    up_w = lax.all_gather(w_up, ("seq", "dp"), axis=0, tiled=True)
    gain_one, gain_two = gains[0:1], gains[1:2]

    x_wide = x_all.astype(f32).reshape(rows_total, width)
    normed = (x_wide * inverse_rms(x_wide) * gain_one).astype(bf16)
    qkv = dot(normed, qkv_w).astype(bf16).reshape(parts, block, qkv_width)
    qkv, w_down = lax.optimization_barrier((qkv, w_down))
    down_w = lax.all_gather(w_down.T, ("seq", "dp"), axis=0, tiled=True)
    segment = segments.reshape(parts, block).astype(f32)
    segc, segr = segment[:, :, None], segment[:, None, :]
    tables = feature_tables(heads)
    att, rden, carry, csum, cot_all = attention_forward(qkv, segc, segr, tables, cot_own, heads)
    cot_all = cot_all.reshape(rows_total, width)
    rows_all, residual = branch_step(att, out_w, own, gain_two)
    rows_all = rows_all.reshape(rows_total, width)

    gate_out = dot(rows_all, gate_w)
    up_out = dot(rows_all, up_w)
    sig = jax.nn.sigmoid(gate_out)
    silu = gate_out * sig
    mixed = (silu * up_out).astype(bf16)
    down_term = dot_tn(cot_all, mixed).astype(bf16)
    mixed, cot_late, down_term = lax.optimization_barrier((mixed, cot_all, down_term))
    grad_mixed = dot(cot_late, down_w)
    grad_gate = (grad_mixed * up_out * sig * (1.0 + gate_out * (1.0 - sig))).astype(bf16)
    grad_up = (grad_mixed * silu).astype(bf16)

    def summed(term):
        return lax.psum_scatter(term, ("seq", "dp"), scatter_dimension=0, tiled=True)

    gate_term = dot_tn(rows_all, grad_gate).astype(bf16)
    up_term = dot_tn(rows_all, grad_up).astype(bf16)
    grad_gate, grad_up, gate_term, up_term = lax.optimization_barrier(
        (grad_gate, grad_up, gate_term, up_term)
    )
    down_sum, gate_sum, up_sum = summed(down_term), summed(gate_term), summed(up_term)

    by_device = (parts, block, -1)
    branch_all, grad_residual, gain_two_sum, down, ga = rows_back(
        grad_gate.reshape(by_device),
        grad_up.reshape(by_device),
        gate_w,
        up_w,
        residual,
        cot_own,
        gain_two,
        mixed.reshape(by_device),
        down_w,
        out_w,
    )
    branch_all = branch_all.reshape(rows_total, width)
    by_row = (parts, lax.axis_size("seq"), lax.axis_size("dp"), rows_each, -1)
    out_term = dot_tn(branch_all, att.reshape(rows_total, heads * HV)).astype(bf16)
    out_term = out_term.reshape(parts, -1, rows_each, heads * HV).transpose(1, 0, 2, 3)
    out_sum = summed(out_term.reshape(width, -1)).reshape(parts, rows_each, -1)
    dqkv, output = attention_backward(
        qkv, segc, segr, tables, att, rden, carry, csum, ga, down, residual, heads
    )
    dqkv_late, down_sum, gate_sum = lax.optimization_barrier((dqkv, down_sum, gate_sum))
    qkv_term = dot_tn(normed, dqkv_late.reshape(rows_total, qkv_width)).astype(bf16)
    x_grad, gain_grads, query_grad, key_grad, value_grad, out_grad = closing(
        dqkv, qkv_w, own, grad_residual, gain_one, gain_two_sum, qkv_term.reshape(by_row), out_sum
    )
    gain_each = gain_grads.shape[1] // lax.axis_size("dp")
    gain_grads = lax.dynamic_slice_in_dim(
        gain_grads, lax.axis_index("dp") * gain_each, gain_each, axis=1
    )
    return (
        output.reshape(tokens.shape),
        x_grad.reshape(tokens.shape),
        gain_grads[0],
        gain_grads[1],
        query_grad,
        key_grad,
        value_grad,
        out_grad.T,
        gate_sum.astype(f32),
        up_sum.astype(f32),
        down_sum.T.astype(f32),
    )


def solution(mesh):
    placed = (
        P("feat", "dp", "seq", None),
        P(None, "dp", "seq"),
        P(ALL),
        P(ALL),
        P(ALL, None),
        P(ALL, None),
        P(ALL, None),
        P(None, ALL),
        P(("seq", "dp"), "feat"),
        P(("seq", "dp"), "feat"),
        P("feat", ("seq", "dp")),
        P("feat", "dp", "seq", None),
    )
    return jax.shard_map(
        local,
        mesh=mesh,
        in_specs=placed,
        out_specs=(
            P("feat", "dp", "seq", None),
            P("feat", "dp", "seq", None),
            P(ALL),
            P(ALL),
            P(ALL, None),
            P(ALL, None),
            P(ALL, None),
            P(None, ALL),
            P(("seq", "dp"), "feat"),
            P(("seq", "dp"), "feat"),
            P("feat", ("seq", "dp")),
        ),
        check_vma=False,
    )
```

```python
import functools

import jax
import jax.numpy as jnp
import numpy as np
from jax import lax
from jax.experimental import pallas as pl
from jax.experimental.pallas import tpu as pltpu
from jax.sharding import PartitionSpec as P

HEADS = 16
FDIM = 16
HV = 128
STATE = 160
LANES = 256
epsilon = 1e-05
MESH = pl.DeviceIdType.MESH
ALL = ("feat", "seq", "dp")
f32 = jnp.float32
bf16 = jnp.bfloat16


def dot(a, b):
    return lax.dot_general(a, b, (((1,), (0,)), ((), ())), preferred_element_type=f32)


def dot_nt(a, b):
    return lax.dot_general(a, b, (((1,), (1,)), ((), ())), preferred_element_type=f32)


def dot_tn(a, b):
    return lax.dot_general(a, b, (((0,), (0,)), ((), ())), preferred_element_type=f32)


def feature_tables(heads):
    pairs = [(i, j) for i in range(FDIM) for j in range(i, FDIM)]
    left = np.zeros((heads, heads * FDIM, LANES), np.float32)
    right = np.zeros((heads, heads * FDIM, LANES), np.float32)
    rows = np.zeros((8, LANES), np.float32)
    for h in range(heads):
        for p, (i, j) in enumerate(pairs):
            left[h, h * FDIM + i, p] = 1.0
            right[h, h * FDIM + j, p] = 1.0
            rows[2, p] = 0.25 / 2.0**0.5 if i == j else 0.25
        for i in range(FDIM):
            p = len(pairs) + i
            left[h, h * FDIM + i, p] = 1.0
            rows[1, p] = 1.0
            rows[2, p] = 0.5
        p = len(pairs) + FDIM
        rows[0, p] = rows[1, p] = rows[2, p] = 1.0
    return jnp.asarray(left, bf16), jnp.asarray(right, bf16), jnp.asarray(rows)


def both_sides(entries, h, left_ref, right_ref, rows_ref):
    one = dot(entries, left_ref[h]) + rows_ref[0:1, :]
    two = dot(entries, right_ref[h]) + rows_ref[1:2, :]
    return one, two * rows_ref[2:3, :]


def features(entries, h, left_ref, right_ref, rows_ref):
    one, two = both_sides(entries, h, left_ref, right_ref, rows_ref)
    return one * two


def pull_features(grad, entries, h, left_ref, right_ref, rows_ref):
    one, two = both_sides(entries, h, left_ref, right_ref, rows_ref)
    scaled = rows_ref[2:3, :]
    return dot_nt((grad * two).astype(bf16), left_ref[h]) + dot_nt(
        (grad * one * scaled).astype(bf16), right_ref[h]
    )


def only_head(entries, h):
    lane = lax.broadcasted_iota(jnp.int32, entries.shape, 1)
    keep = (lane >= h * FDIM) & (lane < (h + 1) * FDIM)
    return jnp.where(keep, entries, jnp.zeros_like(entries))


def padded_state(state):
    return jnp.concatenate([state, jnp.zeros((LANES - STATE, state.shape[1]), state.dtype)], 0)


def allowed_of(segc, segr):
    block = segc.shape[0]
    row = lax.broadcasted_iota(jnp.int32, (block, block), 0)
    col = lax.broadcasted_iota(jnp.int32, (block, block), 1)
    return (row >= col) & (segc == segr)


def forward_kernel(
    count,
    dps,
    heads,
    qkv_ref,
    segc_ref,
    segr_ref,
    left_ref,
    right_ref,
    rows_ref,
    cot_ref,
    old_ref,
    att_ref,
    rden_ref,
    carry_ref,
    csum_ref,
    cots_ref,
    downs_ref,
    send_state,
    send_sum,
    part,
    send_sem,
    recv_sem,
    f_send,
    f_recv,
    local_sem,
    h_send,
    h_recv,
    b_send,
    b_recv,
):
    place, f, d = lax.axis_index("seq"), lax.axis_index("feat"), lax.axis_index("dp")
    groups, block = qkv_ref.shape[0], qkv_ref.shape[1]
    width = heads * FDIM
    tables = (left_ref, right_ref, rows_ref)

    def hop(g):
        target = {"seq": lax.rem(place + 1, count)}
        return [
            pltpu.make_async_remote_copy(
                src_ref=src.at[g],
                dst_ref=dst.at[g],
                send_sem=send_sem.at[i, g],
                recv_sem=recv_sem.at[i, g],
                device_id=target,
                device_id_type=MESH,
            )
            for i, (src, dst) in enumerate(((send_state, carry_ref), (send_sum, csum_ref)))
        ]

    def send(g):
        for copy in hop(g):
            copy.start()

    chain = [lax.rem(place + 1, count), lax.rem(place + count - 1, count)]
    stay = pltpu.make_async_copy(cot_ref, cots_ref.at[f], local_sem.at[0])
    stay.start()
    greet(
        square_targets(f)
        + [{"seq": c} for c in chain]
        + [{"dp": lax.rem(d + o, dps)} for o in range(1, dps)]
    )
    gather = SquareGather(cots_ref, f, f_send, f_recv, cot_ref)
    gather.start()
    line = LineHop(downs_ref, 2, place, d, count, h_send, h_recv)
    beside = SiblingHop(downs_ref, 1, place, d, count, dps, b_send, b_recv)
    beside.start()

    @pl.when(place == 0)
    def _():
        carry_ref[...] = jnp.zeros_like(carry_ref)
        csum_ref[...] = jnp.full_like(csum_ref, -1.0)

    def summarize(g, none):
        segc, segr = segc_ref[g], segr_ref[g]
        tail = segr[:, block - 1 : block]
        at_tail = (segc == tail).astype(f32)
        send_sum[g, heads : heads + 1, :] = jnp.broadcast_to(tail, (1, LANES))
        for h in range(heads):
            key = qkv_ref[g, :, width : 2 * width]
            value = qkv_ref[g, :, 2 * width + h * HV : 2 * width + (h + 1) * HV]
            phi = (features(key, h, *tables) * at_tail).astype(bf16)
            send_state[g, h] = dot_tn(phi, value)[:STATE].astype(bf16)
            ones = jnp.ones((8, block), bf16)
            send_sum[g, h : h + 1, :] = dot(ones, phi)[0:1]

        @pl.when(place == 0)
        def _():
            send(g)

        return none

    lax.fori_loop(0, groups, summarize, 0)
    def join(g, none):
        for copy in hop(g):
            copy.wait_recv()
        segr = segr_ref[g]
        mark = csum_ref[g, heads : heads + 1, 0:1]
        head, tail = segr[:, 0:1], segr[:, block - 1 : block]
        whole = ((head == tail) & (head == mark)).astype(f32)
        for h in range(heads):
            send_state[g, h] = (
                send_state[g, h].astype(f32) + whole * carry_ref[g, h].astype(f32)
            ).astype(bf16)
            send_sum[g, h : h + 1, :] = (
                send_sum[g, h : h + 1, :] + whole * csum_ref[g, h : h + 1, :]
            )
        send(g)
        return none

    def attend(g, none):
        segc, segr = segc_ref[g], segr_ref[g]
        allowed = allowed_of(segc, segr)
        for h in range(heads):
            query = only_head(qkv_ref[g, :, 0:width], h)
            key = qkv_ref[g, :, width : 2 * width]
            value = qkv_ref[g, :, 2 * width + h * HV : 2 * width + (h + 1) * HV]
            c = dot_nt(query, key)
            kernel = jnp.where(allowed, 1.0 + c * (0.25 + c * 0.03125), 0.0).astype(bf16)
            wide = jnp.concatenate([value, jnp.ones_like(value)], axis=1)
            part[g, h] = dot(kernel, wide)

        @pl.when((place > 0) & (place < count - 1) & (g == place - 1))
        def _():
            lax.fori_loop(0, groups, join, 0)

        return none

    lax.fori_loop(0, groups, attend, 0)
    line.start()
    gather.relay()

    def carry_on(g, none):
        segc = segc_ref[g]

        @pl.when(place == count - 1)
        def _():
            for copy in hop(g):
                copy.wait_recv()

        mark = csum_ref[g, heads : heads + 1, 0:1]
        carried = (segc == mark).astype(f32)
        for h in range(heads):
            phi = features(qkv_ref[g, :, 0:width], h, *tables) * carried
            state = padded_state(carry_ref[g, h])
            both = part[g, h]
            numer = both[:, :HV] + dot(phi.astype(bf16), state)
            denom = both[:, HV:] + jnp.sum(
                phi * csum_ref[g, h : h + 1, :], axis=1, keepdims=True
            )
            inverse = 1.0 / denom
            att_ref[g, :, h * HV : (h + 1) * HV] = (numer * inverse).astype(bf16)
            rden_ref[g, :, h * HV : (h + 1) * HV] = inverse
        return none

    lax.fori_loop(0, groups, carry_on, 0)

    @pl.when(place < count - 1)
    def _():
        def finish(g, none):
            for copy in hop(g):
                copy.wait_send()
            return none

        lax.fori_loop(0, groups, finish, 0)

    stay.wait()
    gather.finish()
    beside.finish()
    line.arrive()
    line.finish()


def backward_kernel(
    count,
    heads,
    qkv_ref,
    segc_ref,
    segr_ref,
    left_ref,
    right_ref,
    rows_ref,
    att_ref,
    rden_ref,
    carry_ref,
    csum_ref,
    ga_ref,
    down_ref,
    res_ref,
    acc_ref,
    came_ref,
    out_ref,
    final_ref,
    next_ref,
    gn,
    send_state,
    send_sum,
    recv_state,
    recv_sum,
    dkey,
    dvalue,
    terms,
    land,
    send_sem,
    recv_sem,
    f_send,
    f_recv,
    local_sem,
    *line_refs,
):
    place, f = lax.axis_index("seq"), lax.axis_index("feat")
    groups, block = qkv_ref.shape[0], qkv_ref.shape[1]
    width = heads * FDIM
    tables = (left_ref, right_ref, rows_ref)

    def hop(g):
        target = {"seq": lax.rem(place + count - 1, count)}
        return [
            pltpu.make_async_remote_copy(
                src_ref=src.at[g],
                dst_ref=dst.at[g],
                send_sem=send_sem.at[i, g],
                recv_sem=recv_sem.at[i, g],
                device_id=target,
                device_id_type=MESH,
            )
            for i, (src, dst) in enumerate(((send_state, recv_state), (send_sum, recv_sum)))
        ]

    def send(g):
        for copy in hop(g):
            copy.start()

    chain = [lax.rem(place + 1, count), lax.rem(place + count - 1, count)]
    greet(square_targets(f) + [{"seq": c} for c in chain])
    fill = pltpu.make_async_copy(down_ref, terms, local_sem.at[0])
    fill.start()
    ring = SquareSum(terms, land, f, f_send, f_recv)
    line = LineSum(acc_ref, came_ref, next_ref, line_refs[0], line_refs[1], 2, place, count, *line_refs[2:])
    line.load()

    @pl.when(place == count - 1)
    def _():
        recv_state[...] = jnp.zeros_like(recv_state)
        recv_sum[...] = jnp.full_like(recv_sum, -1.0)

    def summarize(g, none):
        segc, segr = segc_ref[g], segr_ref[g]
        head = segr[:, 0:1]
        at_head = (segc == head).astype(f32)
        send_sum[g, heads : heads + 1, :] = jnp.broadcast_to(head, (1, LANES))
        for h in range(heads):
            lanes = slice(h * HV, (h + 1) * HV)
            ga = ga_ref[g, :, lanes]
            inverse = rden_ref[g, :, lanes]
            numer = (ga * inverse).astype(bf16)
            dots = jnp.sum(ga * att_ref[g, :, lanes].astype(f32), axis=1, keepdims=True)
            lane = lax.broadcasted_iota(jnp.int32, (block, HV), 1)
            denom = jnp.where(lane == 0, -dots * inverse, 0.0).astype(bf16)
            gn[g, h, :, :HV] = numer
            gn[g, h, :, HV:] = denom
            phi = (features(qkv_ref[g, :, 0:width], h, *tables) * at_head).astype(bf16)
            send_state[g, h] = dot_tn(phi, numer)[:STATE].astype(bf16)
            send_sum[g, h : h + 1, :] = dot_tn(denom, phi)[0:1]

        @pl.when(place == count - 1)
        def _():
            send(g)

        return none

    lax.fori_loop(0, groups, summarize, 0)
    fill.wait()
    ring.start_cross()
    ring.start_near()

    def join(g, none):
        for copy in hop(g):
            copy.wait_recv()
        segr = segr_ref[g]
        mark = recv_sum[g, heads : heads + 1, 0:1]
        head, tail = segr[:, 0:1], segr[:, block - 1 : block]
        whole = ((head == tail) & (head == mark)).astype(f32)
        for h in range(heads):
            send_state[g, h] = (
                send_state[g, h].astype(f32) + whole * recv_state[g, h].astype(f32)
            ).astype(bf16)
            send_sum[g, h : h + 1, :] = (
                send_sum[g, h : h + 1, :] + whole * recv_sum[g, h : h + 1, :]
            )
        send(g)
        return none

    def pull(g, none):
        segc, segr = segc_ref[g], segr_ref[g]
        allowed = allowed_of(segc, segr)
        query_all = qkv_ref[g, :, 0:width]
        key_all = qkv_ref[g, :, width : 2 * width]
        carried = (segc == csum_ref[g, heads : heads + 1, 0:1]).astype(f32)
        dquery = jnp.zeros((block, width), f32)
        dkey_sum = jnp.zeros((block, width), f32)
        for h in range(heads):
            query, key = only_head(query_all, h), only_head(key_all, h)
            value = qkv_ref[g, :, 2 * width + h * HV : 2 * width + (h + 1) * HV]
            wide = jnp.concatenate([value, jnp.ones_like(value)], axis=1)
            both = gn[g, h]
            c = dot_nt(query, key_all)
            kernel = jnp.where(allowed, 1.0 + c * (0.25 + c * 0.03125), 0.0).astype(bf16)
            grad = jnp.where(allowed, dot_nt(both, wide), 0.0)
            grad_c = (grad * (0.25 + c * 0.0625)).astype(bf16)
            dvalue[g, h] = dot_tn(kernel, both[:, :HV])
            dkey_sum = dkey_sum + dot_tn(grad_c, query)
            dquery = dquery + dot(grad_c, key)
            state = padded_state(carry_ref[g, h])
            gphi = dot_nt(both[:, :HV], state) + both[:, HV : HV + 1].astype(f32) * csum_ref[
                g, h : h + 1, :
            ]
            dquery = dquery + pull_features(gphi * carried, query_all, h, *tables)
        out_ref[g, :, 0:width] = dquery.astype(bf16)
        dkey[g] = dkey_sum

        @pl.when((place > 0) & (place < count - 1) & (g == count - 2 - place))
        def _():
            lax.fori_loop(0, groups, join, 0)

        return none

    lax.fori_loop(0, groups, pull, 0)
    line.start()
    ring.relay()

    def carry_back(g, none):
        segc = segc_ref[g]
        key_all = qkv_ref[g, :, width : 2 * width]

        @pl.when(place == 0)
        def _():
            for copy in hop(g):
                copy.wait_recv()

        mark = recv_sum[g, heads : heads + 1, 0:1]
        later = (segc == mark).astype(f32)
        total = dkey[g]
        for h in range(heads):
            value = qkv_ref[g, :, 2 * width + h * HV : 2 * width + (h + 1) * HV]
            state = padded_state(recv_state[g, h])
            phi = (features(key_all, h, *tables) * later).astype(bf16)
            dv = dvalue[g, h] + dot(phi, state)
            out_ref[g, :, 2 * width + h * HV : 2 * width + (h + 1) * HV] = dv.astype(bf16)
            gphi = (dot_nt(value, state) + recv_sum[g, h : h + 1, :]) * later
            total = total + pull_features(gphi, key_all, h, *tables)
        out_ref[g, :, width : 2 * width] = total.astype(bf16)
        return none

    lax.fori_loop(0, groups, carry_back, 0)

    @pl.when(place > 0)
    def _():
        def finish(g, none):
            for copy in hop(g):
                copy.wait_send()
            return none

        lax.fori_loop(0, groups, finish, 0)

    ring.arrive()

    def add_up(rows, total):
        final_ref[rows, :] = (res_ref[rows, :] + total).astype(bf16)

    by_rows(ring, add_up)
    ring.finish()
    line.arrive()
    line.finish()


def whole_vmem(count):
    return [pl.BlockSpec(memory_space=pltpu.VMEM)] * count


def attention_forward(qkv, segc, segr, tables, cot_own, downs, heads):
    groups, block, _ = qkv.shape
    count, dps = downs.shape[:2]
    others = max(dps - 1, 1)
    dma = pltpu.SemaphoreType.DMA
    states = (groups, heads, STATE, HV)
    sums = (groups, 8, LANES)
    return pl.pallas_call(
        functools.partial(forward_kernel, count, dps, heads),
        out_shape=(
            jax.ShapeDtypeStruct((groups, block, heads * HV), bf16),
            jax.ShapeDtypeStruct((groups, block, heads * HV), f32),
            jax.ShapeDtypeStruct(states, bf16),
            jax.ShapeDtypeStruct(sums, f32),
            jax.ShapeDtypeStruct((groups,) + cot_own.shape, bf16),
            jax.ShapeDtypeStruct(downs.shape, bf16),
        ),
        in_specs=whole_vmem(6) + in_place(2),
        out_specs=tuple(whole_vmem(4) + in_place(2)),
        input_output_aliases={7: 5},
        scratch_shapes=[
            pltpu.VMEM(states, bf16),
            pltpu.VMEM(sums, f32),
            pltpu.VMEM((groups, heads, block, 2 * HV), f32),
            dma((2, groups)),
            dma((2, groups)),
            dma((6,)),
            dma((6,)),
            dma((1,)),
            dma((2,)),
            dma((2,)),
            dma((2, others)),
            dma((2, others)),
        ],
        compiler_params=pltpu.CompilerParams(
            collective_id=0, has_side_effects=True, vmem_limit_bytes=40 << 20
        ),
        cost_estimate=pl.CostEstimate(flops=0, bytes_accessed=1 << 20, transcendentals=0),
        name="attention_forward",
    )(qkv, segc, segr, *tables, cot_own, downs)


def attention_backward(
    qkv, segc, segr, tables, att, rden, carry, csum, ga, down, residual, acc, came, heads
):
    groups, block, wide = qkv.shape
    count = lax.axis_size("seq")
    states = (groups, heads, STATE, HV)
    sums = (groups, 8, LANES)
    return pl.pallas_call(
        functools.partial(backward_kernel, count, heads),
        out_shape=(
            jax.ShapeDtypeStruct((groups, block, wide), bf16),
            jax.ShapeDtypeStruct(residual.shape, bf16),
            jax.ShapeDtypeStruct(came.shape, bf16),
        ),
        in_specs=whole_vmem(11) + in_place(1) + whole_vmem(1) + in_place(2),
        out_specs=tuple(whole_vmem(2) + in_place(1)),
        scratch_shapes=[
            pltpu.VMEM((groups, heads, block, 2 * HV), bf16),
            pltpu.VMEM(states, bf16),
            pltpu.VMEM(sums, f32),
            pltpu.VMEM(states, bf16),
            pltpu.VMEM(sums, f32),
            pltpu.VMEM((groups, block, heads * FDIM), f32),
            pltpu.VMEM((groups, heads, block, HV), f32),
            pltpu.VMEM((groups,) + residual.shape, bf16),
            pltpu.VMEM((6, block // 2, residual.shape[1]), bf16),
            pltpu.SemaphoreType.DMA((2, groups)),
            pltpu.SemaphoreType.DMA((2, groups)),
            pltpu.SemaphoreType.DMA((6,)),
            pltpu.SemaphoreType.DMA((6,)),
            pltpu.SemaphoreType.DMA((1,)),
        ]
        + line_scratch(acc.shape[1:]),
        compiler_params=pltpu.CompilerParams(
            collective_id=1, has_side_effects=True, vmem_limit_bytes=48 << 20
        ),
        cost_estimate=pl.CostEstimate(flops=0, bytes_accessed=1 << 20, transcendentals=0),
        name="attention_backward",
    )(qkv, segc, segr, *tables, att, rden, carry, csum, ga, down, residual, acc, came)


def peers(f):
    return 2 * (f // 2) + 1 - f % 2, (f + 2) % 4, 3 - f


def greet(targets):
    barrier = pltpu.get_barrier_semaphore()
    for target in targets:
        pl.semaphore_signal(barrier, inc=1, device_id=target, device_id_type=MESH)
    pl.semaphore_wait(barrier, len(targets))


def push(src, dst, send_sem, recv_sem, target):
    return pltpu.make_async_remote_copy(
        src_ref=src,
        dst_ref=dst,
        send_sem=send_sem,
        recv_sem=recv_sem,
        device_id=target,
        device_id_type=MESH,
    )


def square_targets(f):
    return [{"feat": p} for p in peers(f)]


class SquareGather:
    def __init__(self, slots, f, send_sem, recv_sem, own=None):
        side, above, across = peers(f)
        half = slots.shape[1] // 2
        first, second = pl.ds(0, half), pl.ds(half, half)

        def copy(i, slot, rows, to):
            ref = slots.at[slot, rows]
            src = ref if own is None or i > 3 else own.at[rows]
            return push(src, ref, send_sem.at[i], recv_sem.at[i], {"feat": to})

        self.direct = [
            copy(0, f, first, side),
            copy(1, f, second, above),
            copy(2, f, second, side),
            copy(3, f, first, above),
        ]
        self.forward = [copy(4, side, first, above), copy(5, above, second, side)]

    def start(self):
        for c in self.direct:
            c.start()

    def relay(self):
        self.direct[0].wait_recv()
        self.forward[0].start()
        self.direct[1].wait_recv()
        self.forward[1].start()

    def near(self):
        self.direct[2].wait_recv()
        self.direct[3].wait_recv()

    def far(self):
        for c in self.forward:
            c.wait_recv()

    def sent(self):
        for c in self.direct + self.forward:
            c.wait_send()

    def finish(self):
        self.near()
        self.far()
        self.sent()


class SquareSum:
    def __init__(self, part, land, f, send_sem, recv_sem):
        self.side, self.above, self.across = peers(f)
        self.f, self.part, self.land = f, part, land
        self.half = part.shape[1] // 2
        first, second = pl.ds(0, self.half), pl.ds(self.half, self.half)

        def copy(i, slot, rows, to):
            return push(
                part.at[slot, rows], land.at[i], send_sem.at[i], recv_sem.at[i], {"feat": to}
            )

        self.cross = [copy(0, self.across, first, self.side), copy(1, self.across, second, self.above)]
        self.near = [copy(2, self.side, first, self.side), copy(3, self.above, second, self.above)]
        self.late = [copy(4, self.above, first, self.above), copy(5, self.side, second, self.side)]

    def start_cross(self):
        for c in self.cross:
            c.start()

    def add_rows(self, slot, base, landed):
        step = 32

        def one(i, none):
            rows = pl.ds(pl.multiple_of(base + i * step, step), step)
            came = self.land[landed, pl.ds(pl.multiple_of(i * step, step), step), :]
            self.part[slot, rows, :] = (
                self.part[slot, rows, :].astype(f32) + came.astype(f32)
            ).astype(bf16)
            return none

        lax.fori_loop(0, self.half // step, one, 0)

    def start_near(self):
        for c in self.near:
            c.start()

    def relay(self):
        self.cross[0].wait_recv()
        self.add_rows(self.above, 0, 0)
        self.late[0].start()
        self.cross[1].wait_recv()
        self.add_rows(self.side, self.half, 1)
        self.late[1].start()

    def arrive(self):
        for c in self.near + self.late:
            c.wait_recv()

    def total(self, half, rows):
        base = half * self.half
        own = self.part[self.f, pl.ds(pl.multiple_of(base + rows.start, 16), rows.size), :]
        near = self.land[2 + half, rows, :]
        late = self.land[4 + half, rows, :]
        return own.astype(f32) + near.astype(f32) + late.astype(f32)

    def finish(self):
        for c in self.cross + self.near + self.late:
            c.wait_send()


class LineHop:
    def __init__(self, ref, k, s, d, seqs, send_sem, recv_sem, own=None):
        back, ahead = lax.rem(s + seqs - (k - 1), seqs), lax.rem(s + k - 1, seqs)
        up, down = lax.rem(s + 1, seqs), lax.rem(s + seqs - 1, seqs)

        def copy(i, block, to):
            src = ref.at[block, d] if own is None else own
            return push(src, ref.at[block, d], send_sem.at[i], recv_sem.at[i], {"seq": to})

        self.copies = (copy(0, back, up), copy(1, ahead, down))
        self.sends = ((s >= k - 1) & (s < seqs - 1), (s + k - 1 < seqs) & (s > 0))
        self.comes = (s >= k, s + k < seqs)

    def start(self):
        for c, sends in zip(self.copies, self.sends):
            pl.when(sends)(c.start)

    def arrive(self):
        for c, comes in zip(self.copies, self.comes):
            pl.when(comes)(c.wait_recv)

    def finish(self):
        for c, sends in zip(self.copies, self.sends):
            pl.when(sends)(c.wait_send)


class SiblingHop:
    def __init__(self, ref, k, s, d, seqs, dps, send_sem, recv_sem, own=None):
        back, ahead = lax.rem(s + seqs - k, seqs), lax.rem(s + k, seqs)
        blocks = ((back, s >= k), (ahead, s + k < seqs)) if k else ((s, s >= 0),)
        self.groups = []
        for i, (block, there) in enumerate(blocks):
            copies = []
            for o in range(1, dps):
                src = ref.at[block, d] if own is None else own
                copies.append(
                    push(
                        src,
                        ref.at[block, d],
                        send_sem.at[i, o - 1],
                        recv_sem.at[i, o - 1],
                        {"dp": lax.rem(d + o, dps)},
                    )
                )
            self.groups.append((there, copies))

    def each(self, act):
        for there, copies in self.groups:

            @pl.when(there)
            def _():
                for c in copies:
                    act(c)

    def start(self):
        self.each(lambda c: c.start())

    def finish(self):
        self.each(lambda c: c.wait_recv())
        self.each(lambda c: c.wait_send())


def add_block(into, more):
    def one(i, none):
        rows = pl.ds(pl.multiple_of(i * 32, 32), 32)
        into[rows, :] = (into[rows, :].astype(f32) + more[rows, :].astype(f32)).astype(into.dtype)
        return none

    lax.fori_loop(0, into.shape[0] // 32, one, 0)


class LineSum:
    def __init__(self, acc, came, to, room, more, t, s, seqs, send_sem, recv_sem, local_sem):
        self.room, self.more, self.t, self.s, self.seqs = room, more, t, s, seqs
        up, down = lax.rem(s + 1, seqs), lax.rem(s + seqs - 1, seqs)
        blocks = (lax.rem(s + seqs - t, seqs), lax.rem(s + t, seqs))
        self.sends = (s < t, s > seqs - 1 - t)
        self.added = tuple(
            sends & here
            for sends, here in zip(self.sends, (s > 0, s < seqs - 1))
        )
        self.loads = [
            pltpu.make_async_copy(acc.at[b], room.at[i], local_sem.at[i])
            for i, b in enumerate(blocks)
        ]
        if t > 1:
            self.extra = [
                pltpu.make_async_copy(came.at[i], more.at[i], local_sem.at[2 + i])
                for i in range(2)
            ]
        self.copies = [
            push(room.at[i], to.at[i], send_sem.at[i], recv_sem.at[i], {"seq": p})
            for i, p in enumerate((up, down))
        ]
        self.comes = ((s > 0) & (s - 1 < t), (s < seqs - 1) & (s + 1 > seqs - 1 - t))

    def load(self):
        for i in range(2):
            pl.when(self.sends[i])(self.loads[i].start)
            if self.t > 1:
                pl.when(self.added[i])(self.extra[i].start)

    def start(self):
        for i in range(2):
            pl.when(self.sends[i])(self.loads[i].wait)
            if self.t > 1:

                @pl.when(self.added[i])
                def _():
                    self.extra[i].wait()
                    add_block(self.room.at[i], self.more.at[i])

            pl.when(self.sends[i])(self.copies[i].start)

    def arrive(self):
        for i in range(2):
            pl.when(self.comes[i])(self.copies[i].wait_recv)

    def finish(self):
        for i in range(2):
            pl.when(self.sends[i])(self.copies[i].wait_send)


def line_scratch(shape):
    dma = pltpu.SemaphoreType.DMA
    return [
        pltpu.VMEM((2,) + shape, bf16),
        pltpu.VMEM((2,) + shape, bf16),
        dma((2,)),
        dma((2,)),
        dma((4,)),
    ]


class RowSum:
    def __init__(self, term, acc, shares, lands, sems, f, s, d, seqs, dps):
        self.term, self.acc, self.shares, self.lands = term, acc, shares, lands
        self.f, self.s, self.d = f, s, d
        self.parts, self.seqs = term.shape[0], seqs
        columns = [lax.rem(s + k, seqs) for k in range(1, seqs)]
        others = [lax.rem(d + k, dps) for k in range(1, dps)]
        d_send, d_recv, z_send, z_recv, a_send, a_recv = sems
        self.one = [
            push(term.at[:, :, o], lands[0].at[k], d_send.at[k], d_recv.at[k], {"dp": o})
            for k, o in enumerate(others)
        ]
        self.two = [
            push(acc.at[c], lands[1].at[k], z_send.at[k], z_recv.at[k], {"seq": c})
            for k, c in enumerate(columns)
        ]
        self.three = [
            push(lands[2].at[p], shares.at[f], a_send.at[i], a_recv.at[i], {"feat": p})
            for i, p in enumerate(peers(f))
        ]

    def start(self):
        for c in self.one:
            c.start()

    def over_seq(self):
        for c in self.one:
            c.wait_recv()

        def one(i, none):
            p, c = i // self.seqs, lax.rem(i, self.seqs)
            total = self.term[p, c, self.d].astype(f32)
            for k in range(len(self.one)):
                total = total + self.lands[0][k, p, c].astype(f32)
            self.acc[c, p] = total.astype(bf16)
            return none

        lax.fori_loop(0, self.parts * self.seqs, one, 0)
        for c in self.two:
            c.start()

    def over_feat(self):
        for c in self.two:
            c.wait_recv()

        def one(p, none):
            total = self.acc[self.s, p].astype(f32)
            for k in range(len(self.two)):
                total = total + self.lands[1][k, p].astype(f32)
            self.lands[2][p] = total.astype(bf16)
            return none

        lax.fori_loop(0, self.parts, one, 0)
        self.shares[self.f] = self.lands[2][self.f]
        for c in self.three:
            c.start()

    def arrive(self):
        for c in self.three:
            c.wait_recv()

    def finish(self):
        for c in self.one + self.two + self.three:
            c.wait_send()


def row_sum_scratch(shape):
    parts, seqs, dps, rows, wide = shape
    others = max(dps - 1, 1)
    dma = pltpu.SemaphoreType.DMA
    return [
        pltpu.VMEM((parts, rows, wide), bf16),
        pltpu.VMEM((seqs, parts, rows, wide), bf16),
        pltpu.VMEM((others, parts, seqs, rows, wide), bf16),
        pltpu.VMEM((seqs - 1, parts, rows, wide), bf16),
        pltpu.VMEM((parts, rows, wide), bf16),
        dma((others,)),
        dma((others,)),
        dma((seqs - 1,)),
        dma((seqs - 1,)),
        dma((3,)),
        dma((3,)),
    ]


def row_sum(term, scratch, f, s, d, seqs, dps):
    shares, acc = scratch[:2]
    return RowSum(term, acc, shares, scratch[2:5], scratch[5:], f, s, d, seqs, dps)


def opening_kernel(
    seqs,
    dps,
    tok_ref,
    query_ref,
    key_ref,
    value_ref,
    out_ref,
    one_ref,
    two_ref,
    down_ref,
    x_ref,
    w_ref,
    g_ref,
    o_ref,
    downs_ref,
    pack,
    opack,
    tile,
    x_send,
    x_recv,
    a_send,
    a_recv,
    z_send,
    z_recv,
    d_send,
    d_recv,
    local_sem,
    h_send,
    h_recv,
    b_send,
    b_recv,
):
    f, s, d = lax.axis_index("feat"), lax.axis_index("seq"), lax.axis_index("dp")
    parts, rows_each = pack.shape[0], pack.shape[1]
    near = peers(f)
    columns = [lax.rem(s + k, seqs) for k in range(1, seqs)]
    others = [lax.rem(d + k, dps) for k in range(1, dps)]
    stay = pltpu.make_async_copy(tok_ref, x_ref.at[f], local_sem.at[0])
    stay.start()
    first = 0
    for ref in (query_ref, key_ref, value_ref):
        each = ref.shape[1] // parts
        for p in range(parts):
            pack[p, :, first : first + each] = ref[:, p * each : (p + 1) * each]
        first += each
    tile[...] = jnp.zeros_like(tile)
    tile[0:1, :rows_each] = one_ref[...].astype(f32)
    tile[1:2, :rows_each] = two_ref[...].astype(f32)
    outs = (w_ref, g_ref)
    own = [
        pltpu.make_async_copy(pack.at[f], w_ref.at[f, s, d], local_sem.at[1]),
        pltpu.make_async_copy(tile, g_ref.at[f, s, d], local_sem.at[2]),
    ]
    for c in own:
        c.start()
    greet(
        square_targets(f) + [{"seq": c} for c in columns] + [{"dp": o} for o in others]
    )
    shares = [
        [
            push(pack.at[p], w_ref.at[f, s, d], a_send.at[0, i], a_recv.at[0, i], {"feat": p}),
            push(tile, g_ref.at[f, s, d], a_send.at[1, i], a_recv.at[1, i], {"feat": p}),
        ]
        for i, p in enumerate(near)
    ]
    for pair in shares:
        for c in pair:
            c.start()
    gather = SquareGather(x_ref, f, x_send, x_recv, tok_ref)
    gather.start()
    each = out_ref.shape[1] // parts
    for p in range(parts):
        opack[p] = out_ref[:, p * each : (p + 1) * each]
    own_out = pltpu.make_async_copy(opack.at[f], o_ref.at[f], local_sem.at[3])
    own_out.start()
    out_shares = [
        push(opack.at[p], o_ref.at[f], a_send.at[2, i], a_recv.at[2, i], {"feat": p})
        for i, p in enumerate(near)
    ]
    for c in out_shares:
        c.start()
    for c in own:
        c.wait()

    chunks = (f,) + near

    def to_column(n, k):
        return [
            push(
                ref.at[chunks[n], s, d],
                ref.at[chunks[n], s, d],
                z_send.at[j, k - 1, n],
                z_recv.at[j, k - 1, n],
                {"seq": columns[k - 1]},
            )
            for j, ref in enumerate(outs)
        ]

    def to_sibling(n, k):
        back = lax.rem(s + seqs - k, seqs)
        return [
            push(
                ref.at[chunks[n], back, d],
                ref.at[chunks[n], back, d],
                d_send.at[j, o, k, n],
                d_recv.at[j, o, k, n],
                {"dp": other},
            )
            for j, ref in enumerate(outs)
            for o, other in enumerate(others)
        ]

    def start_all(copies):
        for c in copies:
            c.start()

    for n in range(parts):
        if n:
            for c in shares[n - 1]:
                c.wait_recv()
        for k in range(1, seqs):
            start_all(to_column(n, k))
        start_all(to_sibling(n, 0))
    hop = LineHop(downs_ref, 1, s, d, seqs, h_send, h_recv, down_ref)
    beside = SiblingHop(downs_ref, 0, s, d, seqs, dps, b_send, b_recv, down_ref)
    own_down = pltpu.make_async_copy(down_ref, downs_ref.at[s, d], local_sem.at[4])
    own_down.start()
    hop.start()
    beside.start()
    for n in range(parts):
        for k in range(1, seqs):
            for c in to_column(n, k):
                c.wait_recv()
            start_all(to_sibling(n, k))
    gather.relay()
    for n in range(parts):
        for k in range(seqs):
            for c in to_sibling(n, k):
                c.wait_recv()
    for n in range(parts):
        for k in range(seqs):
            for c in to_sibling(n, k):
                c.wait_send()
        for k in range(1, seqs):
            for c in to_column(n, k):
                c.wait_send()
    for pair in shares:
        for c in pair:
            c.wait_send()
    stay.wait()
    own_down.wait()
    hop.arrive()
    hop.finish()
    beside.finish()
    own_out.wait()
    for c in out_shares:
        c.wait_recv()
    for c in out_shares:
        c.wait_send()
    gather.finish()


def in_place(count):
    return [pl.BlockSpec(memory_space=pl.ANY)] * count


def opening(own, w_query, w_key, w_value, w_out, gain_one, gain_two, w_down):
    parts, seqs, dps = (lax.axis_size(a) for a in ALL)
    block, width = own.shape
    rows_each = w_query.shape[0]
    wide = (w_query.shape[1] + w_key.shape[1] + w_value.shape[1]) // parts
    others = max(dps - 1, 1)
    dma = pltpu.SemaphoreType.DMA
    out_wide = w_out.shape[1] // parts
    x_all, w_all, g_all, o_own, downs = pl.pallas_call(
        functools.partial(opening_kernel, seqs, dps),
        out_shape=(
            jax.ShapeDtypeStruct((parts, block, width), bf16),
            jax.ShapeDtypeStruct((parts, seqs, dps, rows_each, wide), bf16),
            jax.ShapeDtypeStruct((parts, seqs, dps, 8, HV), f32),
            jax.ShapeDtypeStruct((parts, rows_each, out_wide), bf16),
            jax.ShapeDtypeStruct((seqs, dps) + w_down.shape, bf16),
        ),
        in_specs=in_place(1) + whole_vmem(6) + in_place(1),
        out_specs=tuple(in_place(5)),
        scratch_shapes=[
            pltpu.VMEM((parts, rows_each, wide), bf16),
            pltpu.VMEM((parts, rows_each, out_wide), bf16),
            pltpu.VMEM((8, HV), f32),
            dma((6,)),
            dma((6,)),
            dma((3, 3)),
            dma((3, 3)),
            dma((2, seqs - 1, parts)),
            dma((2, seqs - 1, parts)),
            dma((2, others, seqs, parts)),
            dma((2, others, seqs, parts)),
            dma((5,)),
            dma((2,)),
            dma((2,)),
            dma((1, others)),
            dma((1, others)),
        ],
        compiler_params=pltpu.CompilerParams(collective_id=2, has_side_effects=True),
        cost_estimate=pl.CostEstimate(flops=0, bytes_accessed=1 << 20, transcendentals=0),
        name="opening",
    )(own, w_query, w_key, w_value, w_out, gain_one, gain_two, w_down)
    gains = g_all[..., :2, :rows_each].transpose(3, 0, 1, 2, 4).reshape(2, width)
    return x_all, w_all.reshape(width, wide), gains, o_own, downs


def inverse_rms(values):
    return lax.rsqrt(jnp.mean(values * values, axis=-1, keepdims=True) + epsilon)


def norm_back(grad, unit, inverse, gain):
    scaled = grad * gain
    return (scaled - unit * jnp.mean(scaled * unit, axis=-1, keepdims=True)) * inverse


class ByShare:
    def __init__(self, ref):
        self.ref = ref

    def tile(self, i, size):
        block = self.ref[:, i]
        return block.reshape(size, block.shape[2])


class ByTiles:
    def __init__(self, src, ref, sem, tile):
        self.ref = ref
        self.fills = [
            pltpu.make_async_copy(
                src.at[pl.ds(i * tile, tile)], ref.at[pl.ds(i * tile, tile)], sem.at[i]
            )
            for i in range(ref.shape[0] // tile)
        ]

    def tile(self, i, size):
        return self.ref[pl.ds(pl.multiple_of(i * size, size), size), :]


def product_tiles(part, slot, pairs, tile, first=False):
    def one(i, none):
        cols = pl.ds(pl.multiple_of(i * tile, tile), tile)
        total = None
        for rows, weights in pairs:
            if hasattr(weights, "tile"):
                block = weights.tile(i, tile)
            else:
                block = weights[cols, :]
            term = dot_nt(rows[slot], block)
            total = term if total is None else total + term
        part[slot, :, cols] = total.astype(bf16)
        return none

    if first:
        for i in range(part.shape[2] // tile):
            for _, weights in pairs:
                weights.fills[i].wait()
            one(i, 0)
    else:
        lax.fori_loop(0, part.shape[2] // tile, one, 0)


def summed_products(part, land, f, pairs, send_sem, recv_sem, beside=None, first=False):
    side, above, across = peers(f)
    ring = SquareSum(part, land, f, send_sem, recv_sem)
    product_tiles(part, across, pairs, 512, first)
    ring.start_cross()
    product_tiles(part, side, pairs, 512)
    ring.near[0].start()
    product_tiles(part, above, pairs, 512)
    ring.near[1].start()
    ring.relay()
    product_tiles(part, f, pairs, 512)
    if beside is not None:
        beside()
    ring.arrive()
    return ring


def by_rows(ring, body, step=16):
    for half in (0, 1):

        def one(i, none):
            start = pl.multiple_of(i * step, step)
            rows = pl.ds(pl.multiple_of(half * ring.half + i * step, step), step)
            body(rows, ring.total(half, pl.ds(start, step)))
            return none

        lax.fori_loop(0, ring.half // step, one, 0)


def branch_kernel(
    att_ref,
    w_ref,
    tok_ref,
    gain_ref,
    old_ref,
    rows_ref,
    res_ref,
    downs_ref,
    part,
    land,
    s_send,
    s_recv,
    g_send,
    g_recv,
    h_send,
    h_recv,
    b_send,
    b_recv,
    e_send,
    e_recv,
):
    f, s, d = lax.axis_index("feat"), lax.axis_index("seq"), lax.axis_index("dp")
    seqs, dps = downs_ref.shape[:2]
    greet(
        square_targets(f)
        + [{"seq": lax.rem(s + 1, seqs)}, {"seq": lax.rem(s + seqs - 1, seqs)}]
        + [{"dp": lax.rem(d + o, dps)} for o in range(1, dps)]
    )
    line = LineHop(downs_ref, 3, s, d, seqs, h_send, h_recv)
    beside = SiblingHop(downs_ref, 2, s, d, seqs, dps, b_send, b_recv)
    after = SiblingHop(downs_ref, 3, s, d, seqs, dps, e_send, e_recv)
    line.start()
    beside.start()
    ring = summed_products(part, land, f, [(att_ref, ByShare(w_ref))], s_send, s_recv)

    def finish_rows(rows, total):
        residual = tok_ref[rows, :].astype(f32) + total
        res_ref[rows, :] = residual
        rows_ref[f, rows, :] = (residual * inverse_rms(residual) * gain_ref[...]).astype(bf16)

    by_rows(ring, finish_rows)
    gather = SquareGather(rows_ref, f, g_send, g_recv)
    gather.start()
    ring.finish()
    line.arrive()
    after.start()
    gather.relay()
    gather.finish()
    beside.finish()
    after.finish()
    line.finish()


def square_scratch(parts, block, width):
    dma = pltpu.SemaphoreType.DMA
    return [
        pltpu.VMEM((parts, block, width), bf16),
        pltpu.VMEM((6, block // 2, width), bf16),
        dma((6,)),
        dma((6,)),
    ]


def branch_step(att, out_w, own, gain_two, downs):
    parts, block, _ = att.shape
    others = max(downs.shape[1] - 1, 1)
    width = own.shape[1]
    dma = pltpu.SemaphoreType.DMA
    return pl.pallas_call(
        branch_kernel,
        out_shape=(
            jax.ShapeDtypeStruct((parts, block, width), bf16),
            jax.ShapeDtypeStruct((block, width), f32),
            jax.ShapeDtypeStruct(downs.shape, bf16),
        ),
        in_specs=whole_vmem(4) + in_place(1),
        out_specs=tuple(whole_vmem(2) + in_place(1)),
        input_output_aliases={4: 2},
        scratch_shapes=square_scratch(parts, block, width)
        + [dma((6,)), dma((6,)), dma((2,)), dma((2,))]
        + [dma((2, others))] * 4,
        compiler_params=pltpu.CompilerParams(
            collective_id=3, has_side_effects=True, vmem_limit_bytes=48 << 20
        ),
        cost_estimate=pl.CostEstimate(flops=0, bytes_accessed=1 << 20, transcendentals=0),
        name="branch_step",
    )(att, out_w, own, gain_two, downs)


def rows_back_kernel(
    gg_ref,
    gu_ref,
    wg_hbm,
    wu_hbm,
    res_ref,
    cot_ref,
    gain_ref,
    mixed_hbm,
    wd_hbm,
    wo_hbm,
    acc_ref,
    all_ref,
    gres_ref,
    gsum_ref,
    down_ref,
    ga_ref,
    next_ref,
    part,
    land,
    wg,
    wu,
    mixed,
    wd,
    wo,
    s_send,
    s_recv,
    g_send,
    g_recv,
    local_sem,
    tile_sem,
    *line_refs,
):
    f, s = lax.axis_index("feat"), lax.axis_index("seq")
    seqs = acc_ref.shape[0]
    weights = [
        ByTiles(src, dst, tile_sem.at[i], 512)
        for i, (src, dst) in enumerate(((wg_hbm, wg), (wu_hbm, wu)))
    ]
    for pair in zip(*(w.fills for w in weights)):
        for c in pair:
            c.start()
    fills = [
        pltpu.make_async_copy(src, dst, local_sem.at[i])
        for i, (src, dst) in enumerate(((mixed_hbm, mixed), (wd_hbm, wd), (wo_hbm, wo)))
    ]
    for c in fills:
        c.start()
    line = LineSum(acc_ref, None, next_ref, line_refs[0], None, 1, s, seqs, *line_refs[1:])
    line.load()
    greet(
        square_targets(f)
        + [{"seq": lax.rem(s + 1, seqs)}, {"seq": lax.rem(s + seqs - 1, seqs)}]
    )
    line.start()
    pairs = [(gg_ref, weights[0]), (gu_ref, weights[1])]

    def down_products():
        for p in range(part.shape[0]):
            product_tiles(down_ref, p, [(mixed, wd)], 512)

    ring = summed_products(part, land, f, pairs, s_send, s_recv, first=True)
    gsum_ref[...] = jnp.zeros_like(gsum_ref)

    def finish_rows(rows, grad):
        residual = res_ref[rows, :]
        inverse = inverse_rms(residual)
        unit = residual * inverse
        gsum_ref[...] += jnp.sum(grad * unit, axis=0, keepdims=True)
        grad_res = cot_ref[rows, :].astype(f32) + norm_back(grad, unit, inverse, gain_ref[...])
        gres_ref[rows, :] = grad_res
        all_ref[f, rows, :] = grad_res.astype(bf16)

    by_rows(ring, finish_rows)
    gather = SquareGather(all_ref, f, g_send, g_recv)
    gather.start()
    ring.finish()
    side, above, across = peers(f)

    def attended_grad(slot):
        blocks = ByShare(wo)
        size = all_ref.shape[2] // wo.shape[1]
        total = None
        for i in range(wo.shape[1]):
            term = dot(all_ref[slot, :, i * size : (i + 1) * size], blocks.tile(i, size))
            total = term if total is None else total + term
        ga_ref[slot] = total

    for c in fills:
        c.wait()
    attended_grad(f)
    down_products()
    gather.relay()
    gather.near()
    attended_grad(side)
    attended_grad(above)
    gather.far()
    attended_grad(across)
    gather.sent()
    line.arrive()
    line.finish()


def rows_back(
    grad_gate, grad_up, gate_w, up_w, residual, cot_own, gain_two, mixed, down_w, out_w, acc
):
    parts, block, hidden = grad_gate.shape
    width = residual.shape[1]
    dma = pltpu.SemaphoreType.DMA
    return pl.pallas_call(
        rows_back_kernel,
        out_shape=(
            jax.ShapeDtypeStruct((parts, block, width), bf16),
            jax.ShapeDtypeStruct((block, width), f32),
            jax.ShapeDtypeStruct((1, width), f32),
            jax.ShapeDtypeStruct((parts, block, width), bf16),
            jax.ShapeDtypeStruct((parts, block, out_w.shape[3]), f32),
            jax.ShapeDtypeStruct((2,) + acc.shape[1:], bf16),
        ),
        in_specs=whole_vmem(2) + in_place(2) + whole_vmem(3) + in_place(4),
        out_specs=tuple(whole_vmem(5) + in_place(1)),
        scratch_shapes=square_scratch(parts, block, width)[:2]
        + [
            pltpu.VMEM((width, hidden), bf16),
            pltpu.VMEM((width, hidden), bf16),
            pltpu.VMEM((parts, block, hidden), bf16),
            pltpu.VMEM((width, hidden), bf16),
            pltpu.VMEM(out_w.shape, bf16),
        ]
        + [dma((6,))] * 4
        + [dma((3,)), dma((2, width // 512))]
        + line_scratch(acc.shape[1:])[1:],
        compiler_params=pltpu.CompilerParams(
            collective_id=4, has_side_effects=True, vmem_limit_bytes=60 << 20
        ),
        cost_estimate=pl.CostEstimate(flops=0, bytes_accessed=1 << 20, transcendentals=0),
        name="rows_back",
    )(grad_gate, grad_up, gate_w, up_w, residual, cot_own, gain_two, mixed, down_w, out_w, acc)


def closing_kernel(
    seqs,
    dps,
    dqkv_ref,
    w_ref,
    tok_ref,
    gres_ref,
    gain_ref,
    gsum_two_ref,
    term_ref,
    osum_ref,
    acc_ref,
    came_ref,
    x_ref,
    tile_ref,
    query_ref,
    key_ref,
    value_ref,
    ograd_ref,
    dgrad_ref,
    part,
    land,
    s_send,
    s_recv,
    gsum,
    cut,
    came,
    mid,
    tail,
    c_send,
    c_recv,
    d_send,
    d_recv,
    oland,
    o_send,
    o_recv,
    last_ref,
    mine,
    mine_sem,
    *more_refs,
):
    line_refs, sum_scratch = more_refs[:5], more_refs[5:]
    f, s, d = lax.axis_index("feat"), lax.axis_index("seq"), lax.axis_index("dp")
    parts = 4
    others = [lax.rem(d + k, dps) for k in range(1, dps)]
    circle = [
        (lax.rem(f + i, parts), lax.rem(s + j, seqs))
        for i in range(parts)
        for j in range(seqs)
        if i or j
    ]
    greet(
        [{"feat": a, "seq": b} for a, b in circle] + [{"dp": o} for o in others]
    )
    line = LineSum(acc_ref, came_ref, last_ref, line_refs[0], line_refs[1], 3, s, seqs, *line_refs[2:])
    line.load()
    own_block = pltpu.make_async_copy(acc_ref.at[s], mine, mine_sem.at[0])
    own_block.start()
    rows_sum = row_sum(term_ref, sum_scratch, f, s, d, seqs, dps)
    rows_sum.start()
    outs = [
        push(osum_ref.at[p], oland.at[f], o_send.at[i], o_recv.at[i], {"feat": p})
        for i, p in enumerate(peers(f))
    ]
    for c in outs:
        c.start()
    ring = summed_products(
        part, land, f, [(dqkv_ref, w_ref)], s_send, s_recv, rows_sum.over_seq
    )
    line.start()
    gsum[...] = jnp.zeros_like(gsum)

    def finish_rows(rows, grad):
        values = tok_ref[rows, :].astype(f32)
        inverse = inverse_rms(values)
        unit = values * inverse
        gsum[...] += jnp.sum(grad * unit, axis=0, keepdims=True)
        x_ref[rows, :] = gres_ref[rows, :] + norm_back(grad, unit, inverse, gain_ref[...])

    by_rows(ring, finish_rows)
    rows_sum.over_feat()
    ring.finish()

    lanes = gsum.shape[1] // (parts * seqs)
    cut[...] = jnp.zeros_like(cut)
    for k in range(parts * seqs):
        cut[k, 0:1, :] = gsum[:, k * lanes : (k + 1) * lanes]
        cut[k, 1:2, :] = gsum_two_ref[:, k * lanes : (k + 1) * lanes]
    place = f * seqs + s
    sends = []
    for i, (a, b) in enumerate(circle):
        sends.append(
            push(
                cut.at[a * seqs + b],
                came.at[i],
                c_send.at[i],
                c_recv.at[i],
                {"feat": a, "seq": b},
            )
        )
    for c in sends:
        c.start()
    total = cut[place]
    for c in sends:
        c.wait_recv()
    for i in range(len(circle)):
        total = total + came[i]
    mid[...] = total
    last = [
        push(mid, tail.at[k], d_send.at[k], d_recv.at[k], {"dp": o})
        for k, o in enumerate(others)
    ]
    for c in last:
        c.start()
    for c in last:
        c.wait_recv()
    for k in range(len(others)):
        total = total + tail[k]
    tile_ref[...] = total
    rows_sum.arrive()
    first = 0
    for ref in (query_ref, key_ref, value_ref):
        each = ref.shape[1] // parts
        for p in range(parts):
            piece = rows_sum.shares[p, :, first : first + each]
            ref[:, p * each : (p + 1) * each] = piece.astype(f32)
        first += each
    rows_sum.finish()
    oland[f] = osum_ref[f]
    for c in outs:
        c.wait_recv()
    each = ograd_ref.shape[1] // parts
    for p in range(parts):
        ograd_ref[:, p * each : (p + 1) * each] = oland[p].astype(f32)
    own_block.wait()
    line.arrive()

    def widen(i, none):
        rows = pl.ds(pl.multiple_of(i * 32, 32), 32)
        dgrad_ref[rows, :] = mine[rows, :].astype(f32)
        return none

    lax.fori_loop(0, mine.shape[0] // 32, widen, 0)
    for i in range(2):

        @pl.when(line.comes[i])
        def _():
            add_block(dgrad_ref, last_ref.at[i])

    line.finish()
    for c in outs + sends + last:
        c.wait_send()


def closing(dqkv, qkv_w, own, grad_residual, gain_one, gain_two_sum, qkv_term, out_sum, acc, came):
    parts, seqs, dps = (lax.axis_size(a) for a in ALL)
    block, width = own.shape
    others = max(dps - 1, 1)
    lanes = width // (parts * seqs)
    circle = parts * seqs - 1
    rows_each = qkv_term.shape[3]
    dma = pltpu.SemaphoreType.DMA
    return pl.pallas_call(
        functools.partial(closing_kernel, seqs, dps),
        out_shape=(
            jax.ShapeDtypeStruct((block, width), f32),
            jax.ShapeDtypeStruct((8, lanes), f32),
            jax.ShapeDtypeStruct((rows_each, HEADS * FDIM), f32),
            jax.ShapeDtypeStruct((rows_each, HEADS * FDIM), f32),
            jax.ShapeDtypeStruct((rows_each, HEADS * HV), f32),
            jax.ShapeDtypeStruct((rows_each, HEADS * HV), f32),
            jax.ShapeDtypeStruct(acc.shape[1:], f32),
        ),
        in_specs=whole_vmem(8) + in_place(2),
        out_specs=tuple(whole_vmem(7)),
        scratch_shapes=square_scratch(parts, block, width)
        + [
            pltpu.VMEM((1, width), f32),
            pltpu.VMEM((parts * seqs, 8, lanes), f32),
            pltpu.VMEM((circle, 8, lanes), f32),
            pltpu.VMEM((8, lanes), f32),
            pltpu.VMEM((others, 8, lanes), f32),
            dma((circle,)),
            dma((circle,)),
            dma((others,)),
            dma((others,)),
            pltpu.VMEM(out_sum.shape, bf16),
            dma((3,)),
            dma((3,)),
            pltpu.VMEM(came.shape, bf16),
            pltpu.VMEM(acc.shape[1:], bf16),
            dma((1,)),
        ]
        + line_scratch(acc.shape[1:])
        + row_sum_scratch(qkv_term.shape),
        compiler_params=pltpu.CompilerParams(
            collective_id=5, has_side_effects=True, vmem_limit_bytes=48 << 20
        ),
        cost_estimate=pl.CostEstimate(flops=0, bytes_accessed=1 << 20, transcendentals=0),
        name="closing",
    )(dqkv, qkv_w, own, grad_residual, gain_one, gain_two_sum, qkv_term, out_sum, acc, came)


def local(
    tokens,
    segments,
    norm1_gain,
    norm2_gain,
    w_query,
    w_key,
    w_value,
    w_out,
    w_gate,
    w_up,
    w_down,
    cotangent,
):
    parts = lax.axis_size("feat")
    heads = HEADS // parts
    block, width = tokens.shape[2], tokens.shape[3]
    rows_total = parts * block
    rows_each = w_query.shape[0]
    own = tokens.reshape(block, width)
    cot_own = cotangent.reshape(block, width)

    x_all, qkv_w, gains, out_share, downs = opening(
        own, w_query, w_key, w_value, w_out.T, norm1_gain[None], norm2_gain[None], w_down.T
    )
    qkv_width = qkv_w.shape[1]
    x_all, w_gate, w_up = lax.optimization_barrier((x_all, w_gate, w_up))
    out_w = lax.all_gather(out_share[None], ("seq", "dp"), axis=0, tiled=True)
    gate_w = lax.all_gather(w_gate, ("seq", "dp"), axis=0, tiled=True)
    up_w = lax.all_gather(w_up, ("seq", "dp"), axis=0, tiled=True)
    gain_one, gain_two = gains[0:1], gains[1:2]

    x_wide = x_all.astype(f32).reshape(rows_total, width)
    normed = (x_wide * inverse_rms(x_wide) * gain_one).astype(bf16)
    qkv = dot(normed, qkv_w).astype(bf16).reshape(parts, block, qkv_width)
    segment = segments.reshape(parts, block).astype(f32)
    segc, segr = segment[:, :, None], segment[:, None, :]
    tables = feature_tables(heads)
    att, rden, carry, csum, cot_all, downs = attention_forward(
        qkv, segc, segr, tables, cot_own, downs, heads
    )
    cot_all = cot_all.reshape(rows_total, width)
    rows_all, residual, downs = branch_step(att, out_w, own, gain_two, downs)
    down_w = downs.reshape(width, -1)
    rows_all = rows_all.reshape(rows_total, width)

    gate_out = dot(rows_all, gate_w)
    up_out = dot(rows_all, up_w)
    sig = jax.nn.sigmoid(gate_out)
    silu = gate_out * sig
    mixed = (silu * up_out).astype(bf16)
    down_term = dot_tn(cot_all, mixed).astype(bf16)
    mixed, cot_late, down_term = lax.optimization_barrier((mixed, cot_all, down_term))
    grad_mixed = dot(cot_late, down_w)
    grad_gate = (grad_mixed * up_out * sig * (1.0 + gate_out * (1.0 - sig))).astype(bf16)
    grad_up = (grad_mixed * silu).astype(bf16)

    def summed(term):
        return lax.psum_scatter(term, ("seq", "dp"), scatter_dimension=0, tiled=True)

    gate_term = dot_tn(rows_all, grad_gate).astype(bf16)
    up_term = dot_tn(rows_all, grad_up).astype(bf16)
    grad_gate, grad_up, gate_term, up_term = lax.optimization_barrier(
        (grad_gate, grad_up, gate_term, up_term)
    )
    seqs = lax.axis_size("seq")
    down_acc = lax.psum_scatter(
        down_term.reshape(seqs, width // seqs, -1), "dp", scatter_dimension=1, tiled=True
    )
    gate_sum, up_sum = summed(gate_term), summed(up_term)

    by_device = (parts, block, -1)
    branch_all, grad_residual, gain_two_sum, down, ga, came = rows_back(
        grad_gate.reshape(by_device),
        grad_up.reshape(by_device),
        gate_w,
        up_w,
        residual,
        cot_own,
        gain_two,
        mixed.reshape(by_device),
        down_w,
        out_w,
        down_acc,
    )
    branch_all = branch_all.reshape(rows_total, width)
    by_row = (parts, lax.axis_size("seq"), lax.axis_size("dp"), rows_each, -1)
    out_term = dot_tn(branch_all, att.reshape(rows_total, heads * HV)).astype(bf16)
    out_term = out_term.reshape(parts, -1, rows_each, heads * HV).transpose(1, 0, 2, 3)
    out_sum = summed(out_term.reshape(width, -1)).reshape(parts, rows_each, -1)
    dqkv, output, came = attention_backward(
        qkv,
        segc,
        segr,
        tables,
        att,
        rden,
        carry,
        csum,
        ga,
        down,
        residual,
        down_acc,
        came,
        heads,
    )
    dqkv_late, gate_sum, up_sum = lax.optimization_barrier((dqkv, gate_sum, up_sum))
    qkv_term = dot_tn(normed, dqkv_late.reshape(rows_total, qkv_width)).astype(bf16)
    x_grad, gain_grads, query_grad, key_grad, value_grad, out_grad, down_grad = closing(
        dqkv,
        qkv_w,
        own,
        grad_residual,
        gain_one,
        gain_two_sum,
        qkv_term.reshape(by_row),
        out_sum,
        down_acc,
        came,
    )
    gain_each = gain_grads.shape[1] // lax.axis_size("dp")
    gain_grads = lax.dynamic_slice_in_dim(
        gain_grads, lax.axis_index("dp") * gain_each, gain_each, axis=1
    )
    return (
        output.reshape(tokens.shape),
        x_grad.reshape(tokens.shape),
        gain_grads[0],
        gain_grads[1],
        query_grad,
        key_grad,
        value_grad,
        out_grad.T,
        gate_sum.astype(f32),
        up_sum.astype(f32),
        down_grad.T,
    )


def solution(mesh):
    placed = (
        P("feat", "dp", "seq", None),
        P(None, "dp", "seq"),
        P(ALL),
        P(ALL),
        P(ALL, None),
        P(ALL, None),
        P(ALL, None),
        P(None, ALL),
        P(("seq", "dp"), "feat"),
        P(("seq", "dp"), "feat"),
        P("feat", ("seq", "dp")),
        P("feat", "dp", "seq", None),
    )
    return jax.shard_map(
        local,
        mesh=mesh,
        in_specs=placed,
        out_specs=(
            P("feat", "dp", "seq", None),
            P("feat", "dp", "seq", None),
            P(ALL),
            P(ALL),
            P(ALL, None),
            P(ALL, None),
            P(ALL, None),
            P(None, ALL),
            P(("seq", "dp"), "feat"),
            P(("seq", "dp"), "feat"),
            P("feat", ("seq", "dp")),
        ),
        check_vma=False,
    )
```

```python
import functools

import jax
import jax.numpy as jnp
import numpy as np
from jax import lax
from jax.experimental import pallas as pl
from jax.experimental.pallas import tpu as pltpu
from jax.sharding import PartitionSpec as P

HEADS = 16
FDIM = 16
HV = 128
STATE = 160
LANES = 256
epsilon = 1e-05
MESH = pl.DeviceIdType.MESH
ALL = ("feat", "seq", "dp")
f32 = jnp.float32
bf16 = jnp.bfloat16


def dot(a, b):
    return lax.dot_general(a, b, (((1,), (0,)), ((), ())), preferred_element_type=f32)


def dot_nt(a, b):
    return lax.dot_general(a, b, (((1,), (1,)), ((), ())), preferred_element_type=f32)


def dot_tn(a, b):
    return lax.dot_general(a, b, (((0,), (0,)), ((), ())), preferred_element_type=f32)


def feature_tables(heads):
    pairs = [(i, j) for i in range(FDIM) for j in range(i, FDIM)]
    left = np.zeros((heads, heads * FDIM, LANES), np.float32)
    right = np.zeros((heads, heads * FDIM, LANES), np.float32)
    rows = np.zeros((8, LANES), np.float32)
    for h in range(heads):
        for p, (i, j) in enumerate(pairs):
            left[h, h * FDIM + i, p] = 1.0
            right[h, h * FDIM + j, p] = 1.0
            rows[2, p] = 0.25 / 2.0**0.5 if i == j else 0.25
        for i in range(FDIM):
            p = len(pairs) + i
            left[h, h * FDIM + i, p] = 1.0
            rows[1, p] = 1.0
            rows[2, p] = 0.5
        p = len(pairs) + FDIM
        rows[0, p] = rows[1, p] = rows[2, p] = 1.0
    return jnp.asarray(left, bf16), jnp.asarray(right, bf16), jnp.asarray(rows)


def both_sides(entries, h, left_ref, right_ref, rows_ref):
    one = dot(entries, left_ref[h]) + rows_ref[0:1, :]
    two = dot(entries, right_ref[h]) + rows_ref[1:2, :]
    return one, two * rows_ref[2:3, :]


def features(entries, h, left_ref, right_ref, rows_ref):
    one, two = both_sides(entries, h, left_ref, right_ref, rows_ref)
    return one * two


def pull_features(grad, entries, h, left_ref, right_ref, rows_ref):
    one, two = both_sides(entries, h, left_ref, right_ref, rows_ref)
    scaled = rows_ref[2:3, :]
    return dot_nt((grad * two).astype(bf16), left_ref[h]) + dot_nt(
        (grad * one * scaled).astype(bf16), right_ref[h]
    )


def only_head(entries, h):
    lane = lax.broadcasted_iota(jnp.int32, entries.shape, 1)
    keep = (lane >= h * FDIM) & (lane < (h + 1) * FDIM)
    return jnp.where(keep, entries, jnp.zeros_like(entries))


def padded_state(state):
    return jnp.concatenate([state, jnp.zeros((LANES - STATE, state.shape[1]), state.dtype)], 0)


def allowed_of(segc, segr):
    block = segc.shape[0]
    row = lax.broadcasted_iota(jnp.int32, (block, block), 0)
    col = lax.broadcasted_iota(jnp.int32, (block, block), 1)
    return (row >= col) & (segc == segr)


def forward_kernel(
    count,
    heads,
    qkv_ref,
    segc_ref,
    segr_ref,
    left_ref,
    right_ref,
    rows_ref,
    cot_ref,
    att_hbm,
    rden_hbm,
    carry_hbm,
    csum_hbm,
    cots_ref,
    att_ref,
    rden_ref,
    carry_ref,
    csum_ref,
    send_state,
    send_sum,
    part,
    send_sem,
    recv_sem,
    f_send,
    f_recv,
    local_sem,
    store_sem,
):
    place, f = lax.axis_index("seq"), lax.axis_index("feat")
    groups, block = qkv_ref.shape[0], qkv_ref.shape[1]
    width = heads * FDIM
    tables = (left_ref, right_ref, rows_ref)

    def stores(g):
        pairs = (
            (att_ref, att_hbm),
            (rden_ref, rden_hbm),
            (carry_ref, carry_hbm),
            (csum_ref, csum_hbm),
        )
        return Loads([(a.at[g], b.at[g]) for a, b in pairs], store_sem.at[g])

    def hop(g):
        target = {"seq": lax.rem(place + 1, count)}
        return [
            pltpu.make_async_remote_copy(
                src_ref=src.at[g],
                dst_ref=dst.at[g],
                send_sem=send_sem.at[i, g],
                recv_sem=recv_sem.at[i, g],
                device_id=target,
                device_id_type=MESH,
            )
            for i, (src, dst) in enumerate(((send_state, carry_ref), (send_sum, csum_ref)))
        ]

    def send(g):
        for copy in hop(g):
            copy.start()

    chain = [lax.rem(place + 1, count), lax.rem(place + count - 1, count)]
    stay = pltpu.make_async_copy(cot_ref, cots_ref.at[f], local_sem.at[0])
    stay.start()
    greet(square_targets(f) + [{"seq": c} for c in chain])
    gather = SquareGather(cots_ref, f, f_send, f_recv, cot_ref)
    gather.start()

    @pl.when(place == 0)
    def _():
        carry_ref[...] = jnp.zeros_like(carry_ref)
        csum_ref[...] = jnp.full_like(csum_ref, -1.0)

    def summarize(g, none):
        segc, segr = segc_ref[g], segr_ref[g]
        tail = segr[:, block - 1 : block]
        at_tail = (segc == tail).astype(f32)
        send_sum[g, heads : heads + 1, :] = jnp.broadcast_to(tail, (1, LANES))
        for h in range(heads):
            key = qkv_ref[g, :, width : 2 * width]
            value = qkv_ref[g, :, 2 * width + h * HV : 2 * width + (h + 1) * HV]
            phi = (features(key, h, *tables) * at_tail).astype(bf16)
            send_state[g, h] = dot_tn(phi, value)[:STATE].astype(bf16)
            ones = jnp.ones((8, block), bf16)
            send_sum[g, h : h + 1, :] = dot(ones, phi)[0:1]

        @pl.when(place == 0)
        def _():
            send(g)

        return none

    lax.fori_loop(0, groups, summarize, 0)
    def join(g, none):
        for copy in hop(g):
            copy.wait_recv()
        segr = segr_ref[g]
        mark = csum_ref[g, heads : heads + 1, 0:1]
        head, tail = segr[:, 0:1], segr[:, block - 1 : block]
        whole = ((head == tail) & (head == mark)).astype(f32)
        for h in range(heads):
            send_state[g, h] = (
                send_state[g, h].astype(f32) + whole * carry_ref[g, h].astype(f32)
            ).astype(bf16)
            send_sum[g, h : h + 1, :] = (
                send_sum[g, h : h + 1, :] + whole * csum_ref[g, h : h + 1, :]
            )
        send(g)
        return none

    def attend(g, none):
        segc, segr = segc_ref[g], segr_ref[g]
        allowed = allowed_of(segc, segr)
        for h in range(heads):
            query = only_head(qkv_ref[g, :, 0:width], h)
            key = qkv_ref[g, :, width : 2 * width]
            value = qkv_ref[g, :, 2 * width + h * HV : 2 * width + (h + 1) * HV]
            c = dot_nt(query, key)
            kernel = jnp.where(allowed, 1.0 + c * (0.25 + c * 0.03125), 0.0).astype(bf16)
            wide = jnp.concatenate([value, jnp.ones_like(value)], axis=1)
            part[g, h] = dot(kernel, wide)

        @pl.when((place > 0) & (place < count - 1) & (g == place - 1))
        def _():
            lax.fori_loop(0, groups, join, 0)

        return none

    lax.fori_loop(0, groups, attend, 0)
    gather.relay()

    def carry_on(g, none):
        segc = segc_ref[g]

        @pl.when(place == count - 1)
        def _():
            for copy in hop(g):
                copy.wait_recv()

        mark = csum_ref[g, heads : heads + 1, 0:1]
        carried = (segc == mark).astype(f32)
        for h in range(heads):
            phi = features(qkv_ref[g, :, 0:width], h, *tables) * carried
            state = padded_state(carry_ref[g, h])
            both = part[g, h]
            numer = both[:, :HV] + dot(phi.astype(bf16), state)
            denom = both[:, HV:] + jnp.sum(
                phi * csum_ref[g, h : h + 1, :], axis=1, keepdims=True
            )
            inverse = 1.0 / denom
            att_ref[g, :, h * HV : (h + 1) * HV] = (numer * inverse).astype(bf16)
            rden_ref[g, :, h * HV : (h + 1) * HV] = inverse
        stores(g).start()
        return none

    lax.fori_loop(0, groups, carry_on, 0)

    @pl.when(place < count - 1)
    def _():
        def finish(g, none):
            for copy in hop(g):
                copy.wait_send()
            return none

        lax.fori_loop(0, groups, finish, 0)

    stay.wait()
    gather.finish()

    def stored(g, none):
        stores(g).wait()
        return none

    lax.fori_loop(0, groups, stored, 0)


def backward_kernel(
    count,
    heads,
    qkv_hbm,
    segc_ref,
    segr_ref,
    left_ref,
    right_ref,
    rows_ref,
    att_hbm,
    rden_hbm,
    carry_hbm,
    csum_ref,
    ga_hbm,
    down_ref,
    res_hbm,
    out_hbm,
    final_ref,
    qkv_ref,
    att_ref,
    rden_ref,
    carry_ref,
    ga_ref,
    res_ref,
    out_ref,
    gn,
    send_state,
    send_sum,
    recv_state,
    recv_sum,
    dkey,
    dvalue,
    terms,
    land,
    send_sem,
    recv_sem,
    f_send,
    f_recv,
    local_sem,
    load_sem,
    store_sem,
):
    place, f = lax.axis_index("seq"), lax.axis_index("feat")
    loads = Loads(
        (
            (qkv_hbm, qkv_ref),
            (ga_hbm, ga_ref),
            (rden_hbm, rden_ref),
            (att_hbm, att_ref),
            (carry_hbm, carry_ref),
            (res_hbm, res_ref),
        ),
        load_sem,
    ).start()
    groups, block = qkv_ref.shape[0], qkv_ref.shape[1]
    width = heads * FDIM
    tables = (left_ref, right_ref, rows_ref)

    def hop(g):
        target = {"seq": lax.rem(place + count - 1, count)}
        return [
            pltpu.make_async_remote_copy(
                src_ref=src.at[g],
                dst_ref=dst.at[g],
                send_sem=send_sem.at[i, g],
                recv_sem=recv_sem.at[i, g],
                device_id=target,
                device_id_type=MESH,
            )
            for i, (src, dst) in enumerate(((send_state, recv_state), (send_sum, recv_sum)))
        ]

    def send(g):
        for copy in hop(g):
            copy.start()

    chain = [lax.rem(place + 1, count), lax.rem(place + count - 1, count)]
    greet(square_targets(f) + [{"seq": c} for c in chain])
    fill = pltpu.make_async_copy(down_ref, terms, local_sem.at[0])
    fill.start()
    ring = SquareSum(terms, land, f, f_send, f_recv)
    loads.wait()

    def store(g):
        return pltpu.make_async_copy(out_ref.at[g], out_hbm.at[g], store_sem.at[g])


    @pl.when(place == count - 1)
    def _():
        recv_state[...] = jnp.zeros_like(recv_state)
        recv_sum[...] = jnp.full_like(recv_sum, -1.0)

    def summarize(g, none):
        segc, segr = segc_ref[g], segr_ref[g]
        head = segr[:, 0:1]
        at_head = (segc == head).astype(f32)
        send_sum[g, heads : heads + 1, :] = jnp.broadcast_to(head, (1, LANES))
        for h in range(heads):
            lanes = slice(h * HV, (h + 1) * HV)
            ga = ga_ref[g, :, lanes]
            inverse = rden_ref[g, :, lanes]
            numer = (ga * inverse).astype(bf16)
            dots = jnp.sum(ga * att_ref[g, :, lanes].astype(f32), axis=1, keepdims=True)
            lane = lax.broadcasted_iota(jnp.int32, (block, HV), 1)
            denom = jnp.where(lane == 0, -dots * inverse, 0.0).astype(bf16)
            gn[g, h, :, :HV] = numer
            gn[g, h, :, HV:] = denom
            phi = (features(qkv_ref[g, :, 0:width], h, *tables) * at_head).astype(bf16)
            send_state[g, h] = dot_tn(phi, numer)[:STATE].astype(bf16)
            send_sum[g, h : h + 1, :] = dot_tn(denom, phi)[0:1]

        @pl.when(place == count - 1)
        def _():
            send(g)

        return none

    lax.fori_loop(0, groups, summarize, 0)
    fill.wait()
    ring.start_cross()
    ring.start_near()

    def join(g, none):
        for copy in hop(g):
            copy.wait_recv()
        segr = segr_ref[g]
        mark = recv_sum[g, heads : heads + 1, 0:1]
        head, tail = segr[:, 0:1], segr[:, block - 1 : block]
        whole = ((head == tail) & (head == mark)).astype(f32)
        for h in range(heads):
            send_state[g, h] = (
                send_state[g, h].astype(f32) + whole * recv_state[g, h].astype(f32)
            ).astype(bf16)
            send_sum[g, h : h + 1, :] = (
                send_sum[g, h : h + 1, :] + whole * recv_sum[g, h : h + 1, :]
            )
        send(g)
        return none

    def pull(g, none):
        segc, segr = segc_ref[g], segr_ref[g]
        allowed = allowed_of(segc, segr)
        query_all = qkv_ref[g, :, 0:width]
        key_all = qkv_ref[g, :, width : 2 * width]
        carried = (segc == csum_ref[g, heads : heads + 1, 0:1]).astype(f32)
        dquery = jnp.zeros((block, width), f32)
        dkey_sum = jnp.zeros((block, width), f32)
        for h in range(heads):
            query, key = only_head(query_all, h), only_head(key_all, h)
            value = qkv_ref[g, :, 2 * width + h * HV : 2 * width + (h + 1) * HV]
            wide = jnp.concatenate([value, jnp.ones_like(value)], axis=1)
            both = gn[g, h]
            c = dot_nt(query, key_all)
            kernel = jnp.where(allowed, 1.0 + c * (0.25 + c * 0.03125), 0.0).astype(bf16)
            grad = jnp.where(allowed, dot_nt(both, wide), 0.0)
            grad_c = (grad * (0.25 + c * 0.0625)).astype(bf16)
            dvalue[g, h] = dot_tn(kernel, both[:, :HV])
            dkey_sum = dkey_sum + dot_tn(grad_c, query)
            dquery = dquery + dot(grad_c, key)
            state = padded_state(carry_ref[g, h])
            gphi = dot_nt(both[:, :HV], state) + both[:, HV : HV + 1].astype(f32) * csum_ref[
                g, h : h + 1, :
            ]
            dquery = dquery + pull_features(gphi * carried, query_all, h, *tables)
        out_ref[g, :, 0:width] = dquery.astype(bf16)
        dkey[g] = dkey_sum

        @pl.when((place > 0) & (place < count - 1) & (g == count - 2 - place))
        def _():
            lax.fori_loop(0, groups, join, 0)

        return none

    lax.fori_loop(0, groups, pull, 0)
    ring.relay()

    def carry_back(g, none):
        segc = segc_ref[g]
        key_all = qkv_ref[g, :, width : 2 * width]

        @pl.when(place == 0)
        def _():
            for copy in hop(g):
                copy.wait_recv()

        mark = recv_sum[g, heads : heads + 1, 0:1]
        later = (segc == mark).astype(f32)
        total = dkey[g]
        for h in range(heads):
            value = qkv_ref[g, :, 2 * width + h * HV : 2 * width + (h + 1) * HV]
            state = padded_state(recv_state[g, h])
            phi = (features(key_all, h, *tables) * later).astype(bf16)
            dv = dvalue[g, h] + dot(phi, state)
            out_ref[g, :, 2 * width + h * HV : 2 * width + (h + 1) * HV] = dv.astype(bf16)
            gphi = (dot_nt(value, state) + recv_sum[g, h : h + 1, :]) * later
            total = total + pull_features(gphi, key_all, h, *tables)
        out_ref[g, :, width : 2 * width] = total.astype(bf16)
        store(g).start()
        return none

    lax.fori_loop(0, groups, carry_back, 0)

    @pl.when(place > 0)
    def _():
        def finish(g, none):
            for copy in hop(g):
                copy.wait_send()
            return none

        lax.fori_loop(0, groups, finish, 0)

    ring.arrive()

    def add_up(rows, total):
        final_ref[rows, :] = (res_ref[rows, :] + total).astype(bf16)

    by_rows(ring, add_up)
    ring.finish()

    def stored(g, none):
        store(g).wait()
        return none

    lax.fori_loop(0, groups, stored, 0)


def whole_vmem(count):
    return [pl.BlockSpec(memory_space=pltpu.VMEM)] * count


def attention_forward(qkv, segc, segr, tables, cot_own, heads):
    groups, block, _ = qkv.shape
    count = lax.axis_size("seq")
    dma = pltpu.SemaphoreType.DMA
    states = (groups, heads, STATE, HV)
    sums = (groups, 8, LANES)
    return pl.pallas_call(
        functools.partial(forward_kernel, count, heads),
        out_shape=(
            jax.ShapeDtypeStruct((groups, block, heads * HV), bf16),
            jax.ShapeDtypeStruct((groups, block, heads * HV), f32),
            jax.ShapeDtypeStruct(states, bf16),
            jax.ShapeDtypeStruct(sums, f32),
            jax.ShapeDtypeStruct((groups,) + cot_own.shape, bf16),
        ),
        in_specs=whole_vmem(6) + in_place(1),
        out_specs=tuple(in_place(5)),
        scratch_shapes=[
            pltpu.VMEM((groups, block, heads * HV), bf16),
            pltpu.VMEM((groups, block, heads * HV), f32),
            pltpu.VMEM(states, bf16),
            pltpu.VMEM(sums, f32),
            pltpu.VMEM(states, bf16),
            pltpu.VMEM(sums, f32),
            pltpu.VMEM((groups, heads, block, 2 * HV), f32),
            dma((2, groups)),
            dma((2, groups)),
            dma((6,)),
            dma((6,)),
            dma((1,)),
            dma((groups, 4)),
        ],
        compiler_params=pltpu.CompilerParams(
            collective_id=0, has_side_effects=True, vmem_limit_bytes=60 << 20
        ),
        cost_estimate=pl.CostEstimate(flops=0, bytes_accessed=1 << 20, transcendentals=0),
        name="attention_forward",
    )(qkv, segc, segr, *tables, cot_own)


def attention_backward(
    qkv, segc, segr, tables, att, rden, carry, csum, ga, down, residual, heads
):
    groups, block, wide = qkv.shape
    count = lax.axis_size("seq")
    states = (groups, heads, STATE, HV)
    sums = (groups, 8, LANES)
    return pl.pallas_call(
        functools.partial(backward_kernel, count, heads),
        out_shape=(
            jax.ShapeDtypeStruct((groups, block, wide), bf16),
            jax.ShapeDtypeStruct(residual.shape, bf16),
        ),
        in_specs=in_place(1)
        + whole_vmem(5)
        + in_place(3)
        + whole_vmem(1)
        + in_place(3),
        out_specs=tuple(in_place(1) + whole_vmem(1)),
        scratch_shapes=vmem_like(qkv, att, rden, carry, ga, residual)
        + [
            pltpu.VMEM((groups, block, wide), bf16),
            pltpu.VMEM((groups, heads, block, 2 * HV), bf16),
            pltpu.VMEM(states, bf16),
            pltpu.VMEM(sums, f32),
            pltpu.VMEM(states, bf16),
            pltpu.VMEM(sums, f32),
            pltpu.VMEM((groups, block, heads * FDIM), f32),
            pltpu.VMEM((groups, heads, block, HV), f32),
            pltpu.VMEM((groups,) + residual.shape, bf16),
            pltpu.VMEM((6, block // 2, residual.shape[1]), bf16),
            pltpu.SemaphoreType.DMA((2, groups)),
            pltpu.SemaphoreType.DMA((2, groups)),
            pltpu.SemaphoreType.DMA((6,)),
            pltpu.SemaphoreType.DMA((6,)),
            pltpu.SemaphoreType.DMA((1,)),
            pltpu.SemaphoreType.DMA((6,)),
            pltpu.SemaphoreType.DMA((groups,)),
        ],
        compiler_params=pltpu.CompilerParams(
            collective_id=1, has_side_effects=True, vmem_limit_bytes=60 << 20
        ),
        cost_estimate=pl.CostEstimate(flops=0, bytes_accessed=1 << 20, transcendentals=0),
        name="attention_backward",
    )(qkv, segc, segr, *tables, att, rden, carry, csum, ga, down, residual)


def peers(f):
    return 2 * (f // 2) + 1 - f % 2, (f + 2) % 4, 3 - f


def greet(targets):
    barrier = pltpu.get_barrier_semaphore()
    for target in targets:
        pl.semaphore_signal(barrier, inc=1, device_id=target, device_id_type=MESH)
    pl.semaphore_wait(barrier, len(targets))


def push(src, dst, send_sem, recv_sem, target):
    return pltpu.make_async_remote_copy(
        src_ref=src,
        dst_ref=dst,
        send_sem=send_sem,
        recv_sem=recv_sem,
        device_id=target,
        device_id_type=MESH,
    )


def square_targets(f):
    return [{"feat": p} for p in peers(f)]


class Loads:
    def __init__(self, pairs, sem):
        self.copies = [pltpu.make_async_copy(a, b, sem.at[i]) for i, (a, b) in enumerate(pairs)]

    def start(self):
        for c in self.copies:
            c.start()
        return self

    def wait(self):
        for c in self.copies:
            c.wait()


def vmem_like(*arrays):
    return [pltpu.VMEM(a.shape, a.dtype) for a in arrays]


class SquareGather:
    def __init__(self, slots, f, send_sem, recv_sem, own=None, base=0, rows=None):
        side, above, across = peers(f)
        half = (slots.shape[1] if rows is None else rows) // 2
        first, second = pl.ds(base, half), pl.ds(base + half, half)

        def copy(i, slot, rows, to):
            ref = slots.at[slot, rows]
            src = ref if own is None or i > 3 else own.at[rows]
            return push(src, ref, send_sem.at[i], recv_sem.at[i], {"feat": to})

        self.direct = [
            copy(0, f, first, side),
            copy(1, f, second, above),
            copy(2, f, second, side),
            copy(3, f, first, above),
        ]
        self.forward = [copy(4, side, first, above), copy(5, above, second, side)]

    def start(self):
        for c in self.direct:
            c.start()

    def relay(self):
        self.direct[0].wait_recv()
        self.forward[0].start()
        self.direct[1].wait_recv()
        self.forward[1].start()

    def near(self):
        self.direct[2].wait_recv()
        self.direct[3].wait_recv()

    def far(self):
        for c in self.forward:
            c.wait_recv()

    def sent(self):
        for c in self.direct + self.forward:
            c.wait_send()

    def finish(self):
        self.near()
        self.far()
        self.sent()


class SquareSum:
    def __init__(self, part, land, f, send_sem, recv_sem, base=0, rows=None):
        self.side, self.above, self.across = peers(f)
        self.f, self.part, self.land, self.base = f, part, land, base
        self.half = (part.shape[1] if rows is None else rows) // 2
        first, second = pl.ds(base, self.half), pl.ds(base + self.half, self.half)

        def copy(i, slot, rows, to):
            return push(
                part.at[slot, rows], land.at[i], send_sem.at[i], recv_sem.at[i], {"feat": to}
            )

        self.cross = [copy(0, self.across, first, self.side), copy(1, self.across, second, self.above)]
        self.near = [copy(2, self.side, first, self.side), copy(3, self.above, second, self.above)]
        self.late = [copy(4, self.above, first, self.above), copy(5, self.side, second, self.side)]

    def start_cross(self):
        for c in self.cross:
            c.start()

    def add_rows(self, slot, base, landed):
        step = 16

        def one(i, none):
            rows = pl.ds(pl.multiple_of(base + i * step, step), step)
            came = self.land[landed, pl.ds(pl.multiple_of(i * step, step), step), :]
            self.part[slot, rows, :] = (
                self.part[slot, rows, :].astype(f32) + came.astype(f32)
            ).astype(bf16)
            return none

        lax.fori_loop(0, self.half // step, one, 0)

    def start_near(self):
        for c in self.near:
            c.start()

    def relay(self):
        self.cross[0].wait_recv()
        self.add_rows(self.above, self.base, 0)
        self.late[0].start()
        self.cross[1].wait_recv()
        self.add_rows(self.side, self.base + self.half, 1)
        self.late[1].start()

    def arrive(self):
        for c in self.near + self.late:
            c.wait_recv()

    def total(self, half, rows):
        base = self.base + half * self.half
        own = self.part[self.f, pl.ds(pl.multiple_of(base + rows.start, 16), rows.size), :]
        near = self.land[2 + half, rows, :]
        late = self.land[4 + half, rows, :]
        return own.astype(f32) + near.astype(f32) + late.astype(f32)

    def finish(self):
        for c in self.cross + self.near + self.late:
            c.wait_send()


class RowSum:
    def __init__(self, term, acc, shares, lands, sems, f, s, d, seqs, dps):
        self.term, self.acc, self.shares, self.lands = term, acc, shares, lands
        self.f, self.s, self.d = f, s, d
        self.parts, self.seqs = term.shape[0], seqs
        columns = [lax.rem(s + k, seqs) for k in range(1, seqs)]
        others = [lax.rem(d + k, dps) for k in range(1, dps)]
        d_send, d_recv, z_send, z_recv, a_send, a_recv = sems
        self.one = [
            push(term.at[:, :, o], lands[0].at[k], d_send.at[k], d_recv.at[k], {"dp": o})
            for k, o in enumerate(others)
        ]
        self.two = [
            push(acc.at[c], lands[1].at[k], z_send.at[k], z_recv.at[k], {"seq": c})
            for k, c in enumerate(columns)
        ]
        self.three = [
            push(lands[2].at[p], shares.at[f], a_send.at[i], a_recv.at[i], {"feat": p})
            for i, p in enumerate(peers(f))
        ]

    def start(self):
        for c in self.one:
            c.start()

    def over_seq(self):
        for c in self.one:
            c.wait_recv()

        def one(i, none):
            p, c = i // self.seqs, lax.rem(i, self.seqs)
            total = self.term[p, c, self.d].astype(f32)
            for k in range(len(self.one)):
                total = total + self.lands[0][k, p, c].astype(f32)
            self.acc[c, p] = total.astype(bf16)
            return none

        lax.fori_loop(0, self.parts * self.seqs, one, 0)
        for c in self.two:
            c.start()

    def over_feat(self):
        for c in self.two:
            c.wait_recv()

        def one(p, none):
            total = self.acc[self.s, p].astype(f32)
            for k in range(len(self.two)):
                total = total + self.lands[1][k, p].astype(f32)
            self.lands[2][p] = total.astype(bf16)
            return none

        lax.fori_loop(0, self.parts, one, 0)
        self.shares[self.f] = self.lands[2][self.f]
        for c in self.three:
            c.start()

    def arrive(self):
        for c in self.three:
            c.wait_recv()

    def finish(self):
        for c in self.one + self.two + self.three:
            c.wait_send()


def row_sum_scratch(shape):
    parts, seqs, dps, rows, wide = shape
    others = max(dps - 1, 1)
    dma = pltpu.SemaphoreType.DMA
    return [
        pltpu.VMEM((parts, rows, wide), bf16),
        pltpu.VMEM((seqs, parts, rows, wide), bf16),
        pltpu.VMEM((others, parts, seqs, rows, wide), bf16),
        pltpu.VMEM((seqs - 1, parts, rows, wide), bf16),
        pltpu.VMEM((parts, rows, wide), bf16),
        dma((others,)),
        dma((others,)),
        dma((seqs - 1,)),
        dma((seqs - 1,)),
        dma((3,)),
        dma((3,)),
    ]


def row_sum(term, scratch, f, s, d, seqs, dps):
    shares, acc = scratch[:2]
    return RowSum(term, acc, shares, scratch[2:5], scratch[5:], f, s, d, seqs, dps)


def opening_kernel(
    seqs,
    dps,
    tok_ref,
    query_ref,
    key_ref,
    value_ref,
    out_ref,
    one_ref,
    two_ref,
    x_ref,
    w_ref,
    g_ref,
    o_ref,
    pack,
    opack,
    tile,
    x_send,
    x_recv,
    a_send,
    a_recv,
    z_send,
    z_recv,
    d_send,
    d_recv,
    local_sem,
):
    f, s, d = lax.axis_index("feat"), lax.axis_index("seq"), lax.axis_index("dp")
    parts, rows_each = pack.shape[0], pack.shape[1]
    near = peers(f)
    columns = [lax.rem(s + k, seqs) for k in range(1, seqs)]
    others = [lax.rem(d + k, dps) for k in range(1, dps)]
    stay = pltpu.make_async_copy(tok_ref, x_ref.at[f], local_sem.at[0])
    stay.start()
    first = 0
    for ref in (query_ref, key_ref, value_ref):
        each = ref.shape[1] // parts
        for p in range(parts):
            pack[p, :, first : first + each] = ref[:, p * each : (p + 1) * each]
        first += each
    tile[...] = jnp.zeros_like(tile)
    tile[0:1, :rows_each] = one_ref[...].astype(f32)
    tile[1:2, :rows_each] = two_ref[...].astype(f32)
    outs = (w_ref, g_ref)
    own = [
        pltpu.make_async_copy(pack.at[f], w_ref.at[f, s, d], local_sem.at[1]),
        pltpu.make_async_copy(tile, g_ref.at[f, s, d], local_sem.at[2]),
    ]
    for c in own:
        c.start()
    greet(
        square_targets(f) + [{"seq": c} for c in columns] + [{"dp": o} for o in others]
    )
    shares = [
        [
            push(pack.at[p], w_ref.at[f, s, d], a_send.at[0, i], a_recv.at[0, i], {"feat": p}),
            push(tile, g_ref.at[f, s, d], a_send.at[1, i], a_recv.at[1, i], {"feat": p}),
        ]
        for i, p in enumerate(near)
    ]
    for pair in shares:
        for c in pair:
            c.start()
    gather = SquareGather(x_ref, f, x_send, x_recv, tok_ref)
    gather.start()
    each = out_ref.shape[1] // parts
    for p in range(parts):
        opack[p] = out_ref[:, p * each : (p + 1) * each]
    own_out = pltpu.make_async_copy(opack.at[f], o_ref.at[f], local_sem.at[3])
    own_out.start()
    out_shares = [
        push(opack.at[p], o_ref.at[f], a_send.at[2, i], a_recv.at[2, i], {"feat": p})
        for i, p in enumerate(near)
    ]
    for c in out_shares:
        c.start()
    for c in own:
        c.wait()

    chunks = (f,) + near

    def to_column(n, k):
        return [
            push(
                ref.at[chunks[n], s, d],
                ref.at[chunks[n], s, d],
                z_send.at[j, k - 1, n],
                z_recv.at[j, k - 1, n],
                {"seq": columns[k - 1]},
            )
            for j, ref in enumerate(outs)
        ]

    def to_sibling(n, k):
        back = lax.rem(s + seqs - k, seqs)
        return [
            push(
                ref.at[chunks[n], back, d],
                ref.at[chunks[n], back, d],
                d_send.at[j, o, k, n],
                d_recv.at[j, o, k, n],
                {"dp": other},
            )
            for j, ref in enumerate(outs)
            for o, other in enumerate(others)
        ]

    def start_all(copies):
        for c in copies:
            c.start()

    for n in range(parts):
        if n:
            for c in shares[n - 1]:
                c.wait_recv()
        for k in range(1, seqs):
            start_all(to_column(n, k))
        start_all(to_sibling(n, 0))
    for n in range(parts):
        for k in range(1, seqs):
            for c in to_column(n, k):
                c.wait_recv()
            start_all(to_sibling(n, k))
    gather.relay()
    for n in range(parts):
        for k in range(seqs):
            for c in to_sibling(n, k):
                c.wait_recv()
    for n in range(parts):
        for k in range(seqs):
            for c in to_sibling(n, k):
                c.wait_send()
        for k in range(1, seqs):
            for c in to_column(n, k):
                c.wait_send()
    for pair in shares:
        for c in pair:
            c.wait_send()
    stay.wait()
    own_out.wait()
    for c in out_shares:
        c.wait_recv()
    for c in out_shares:
        c.wait_send()
    gather.finish()


def in_place(count):
    return [pl.BlockSpec(memory_space=pltpu.HBM)] * count


def opening(own, w_query, w_key, w_value, w_out, gain_one, gain_two):
    parts, seqs, dps = (lax.axis_size(a) for a in ALL)
    block, width = own.shape
    rows_each = w_query.shape[0]
    wide = (w_query.shape[1] + w_key.shape[1] + w_value.shape[1]) // parts
    others = max(dps - 1, 1)
    dma = pltpu.SemaphoreType.DMA
    out_wide = w_out.shape[1] // parts
    x_all, w_all, g_all, o_own = pl.pallas_call(
        functools.partial(opening_kernel, seqs, dps),
        out_shape=(
            jax.ShapeDtypeStruct((parts, block, width), bf16),
            jax.ShapeDtypeStruct((parts, seqs, dps, rows_each, wide), bf16),
            jax.ShapeDtypeStruct((parts, seqs, dps, 8, HV), f32),
            jax.ShapeDtypeStruct((parts, rows_each, out_wide), bf16),
        ),
        in_specs=in_place(1) + whole_vmem(6),
        out_specs=tuple(in_place(4)),
        scratch_shapes=[
            pltpu.VMEM((parts, rows_each, wide), bf16),
            pltpu.VMEM((parts, rows_each, out_wide), bf16),
            pltpu.VMEM((8, HV), f32),
            dma((6,)),
            dma((6,)),
            dma((3, 3)),
            dma((3, 3)),
            dma((2, seqs - 1, parts)),
            dma((2, seqs - 1, parts)),
            dma((2, others, seqs, parts)),
            dma((2, others, seqs, parts)),
            dma((4,)),
        ],
        compiler_params=pltpu.CompilerParams(collective_id=2, has_side_effects=True, vmem_limit_bytes=60 << 20),
        cost_estimate=pl.CostEstimate(flops=0, bytes_accessed=1 << 20, transcendentals=0),
        name="opening",
    )(own, w_query, w_key, w_value, w_out, gain_one, gain_two)
    gains = g_all[..., :2, :rows_each].transpose(3, 0, 1, 2, 4).reshape(2, width)
    return x_all, w_all.reshape(width, wide), gains, o_own


def inverse_rms(values):
    return lax.rsqrt(jnp.mean(values * values, axis=-1, keepdims=True) + epsilon)


def norm_back(grad, unit, inverse, gain):
    scaled = grad * gain
    return (scaled - unit * jnp.mean(scaled * unit, axis=-1, keepdims=True)) * inverse


class ByShare:
    def __init__(self, ref):
        self.ref = ref

    def tile(self, i, size):
        block = self.ref[:, i]
        return block.reshape(size, block.shape[2])


class ByTiles:
    def __init__(self, src, ref, sem, tile):
        self.ref = ref
        self.fills = [
            pltpu.make_async_copy(
                src.at[pl.ds(i * tile, tile)], ref.at[pl.ds(i * tile, tile)], sem.at[i]
            )
            for i in range(ref.shape[0] // tile)
        ]

    def tile(self, i, size):
        return self.ref[pl.ds(pl.multiple_of(i * size, size), size), :]


def product_tiles(part, slot, pairs, tile, first=False):
    def one(i, none):
        cols = pl.ds(pl.multiple_of(i * tile, tile), tile)
        total = None
        for rows, weights in pairs:
            if hasattr(weights, "tile"):
                block = weights.tile(i, tile)
            else:
                block = weights[cols, :]
            term = dot_nt(rows[slot], block)
            total = term if total is None else total + term
        part[slot, :, cols] = total.astype(bf16)
        return none

    if first:
        for i in range(part.shape[2] // tile):
            for _, weights in pairs:
                weights.fills[i].wait()
            one(i, 0)
    else:
        lax.fori_loop(0, part.shape[2] // tile, one, 0)


def summed_products(part, land, f, pairs, send_sem, recv_sem, chunks=1, beside=None, first=False):
    side, above, across = peers(f)
    rows = part.shape[1] // chunks
    rings = [
        SquareSum(
            part, land.at[c], f, send_sem.at[c], recv_sem.at[c], base=c * rows, rows=rows
        )
        for c in range(chunks)
    ]
    product_tiles(part, across, pairs, 512, first)
    for ring in rings:
        ring.start_cross()
    if beside is not None:
        beside()
    product_tiles(part, side, pairs, 512)
    for ring in rings:
        ring.near[0].start()
    product_tiles(part, above, pairs, 512)
    for ring in rings:
        ring.near[1].start()
    rings[0].relay()
    product_tiles(part, f, pairs, 512)
    for ring in rings[1:]:
        ring.relay()
    return rings


def sum_then_gather(rings, finish_rows, slots, f, send_sem, recv_sem):
    gathers = []
    for c, ring in enumerate(rings):
        ring.arrive()
        by_rows(ring, finish_rows)
        gather = SquareGather(
            slots, f, send_sem.at[c], recv_sem.at[c], base=ring.base, rows=2 * ring.half
        )
        gather.start()
        gathers.append(gather)
    for ring in rings:
        ring.finish()
    return gathers


def by_rows(ring, body, step=16):
    for half in (0, 1):

        def one(i, none):
            start = pl.multiple_of(i * step, step)
            rows = pl.ds(
                pl.multiple_of(ring.base + half * ring.half + i * step, step), step
            )
            body(rows, ring.total(half, pl.ds(start, step)))
            return none

        lax.fori_loop(0, ring.half // step, one, 0)


def branch_kernel(
    att_hbm,
    w_hbm,
    tok_hbm,
    gain_ref,
    rows_hbm,
    res_hbm,
    rows_ref,
    res_ref,
    att_ref,
    w_ref,
    tok_ref,
    part,
    land,
    s_send,
    s_recv,
    g_send,
    g_recv,
    load_sem,
    store_sem,
):
    f = lax.axis_index("feat")
    loads = Loads(((att_hbm, att_ref), (w_hbm, w_ref), (tok_hbm, tok_ref)), load_sem).start()
    greet(square_targets(f))
    loads.wait()
    rings = summed_products(
        part, land, f, [(att_ref, ByShare(w_ref))], s_send, s_recv, land.shape[0]
    )

    def finish_rows(rows, total):
        residual = tok_ref[rows, :].astype(f32) + total
        res_ref[rows, :] = residual
        rows_ref[f, rows, :] = (residual * inverse_rms(residual) * gain_ref[...]).astype(bf16)

    gathers = sum_then_gather(rings, finish_rows, rows_ref, f, g_send, g_recv)
    stores = [pltpu.make_async_copy(res_ref, res_hbm, store_sem.at[0])]
    stores[0].start()

    def store(slot):
        c = pltpu.make_async_copy(rows_ref.at[slot], rows_hbm.at[slot], store_sem.at[len(stores)])
        c.start()
        stores.append(c)

    side, above, across = peers(f)
    store(f)
    for gather in gathers:
        gather.relay()
    for gather in gathers:
        gather.near()
    store(side)
    store(above)
    for gather in gathers:
        gather.far()
    store(across)
    for gather in gathers:
        gather.sent()
    for c in stores:
        c.wait()


CHUNKS = 2


def square_scratch(parts, block, width, chunks=CHUNKS):
    dma = pltpu.SemaphoreType.DMA
    return [
        pltpu.VMEM((parts, block, width), bf16),
        pltpu.VMEM((chunks, 6, block // 2 // chunks, width), bf16),
        dma((chunks, 6)),
        dma((chunks, 6)),
    ]


def branch_step(att, out_w, own, gain_two):
    parts, block, _ = att.shape
    width = own.shape[1]
    dma = pltpu.SemaphoreType.DMA
    return pl.pallas_call(
        branch_kernel,
        out_shape=(
            jax.ShapeDtypeStruct((parts, block, width), bf16),
            jax.ShapeDtypeStruct((block, width), f32),
        ),
        in_specs=in_place(3) + whole_vmem(1),
        out_specs=tuple(in_place(2)),
        scratch_shapes=[pltpu.VMEM((parts, block, width), bf16), pltpu.VMEM((block, width), f32)]
        + vmem_like(att, out_w, own)
        + square_scratch(parts, block, width)
        + [dma((CHUNKS, 6)), dma((CHUNKS, 6)), dma((3,)), dma((1 + parts,))],
        compiler_params=pltpu.CompilerParams(
            collective_id=3, has_side_effects=True, vmem_limit_bytes=60 << 20
        ),
        cost_estimate=pl.CostEstimate(flops=0, bytes_accessed=1 << 20, transcendentals=0),
        name="branch_step",
    )(att, out_w, own, gain_two)


def rows_back_kernel(
    gg_hbm,
    gu_hbm,
    wg_hbm,
    wu_hbm,
    res_hbm,
    cot_hbm,
    gain_ref,
    mixed_hbm,
    wd_hbm,
    wo_hbm,
    all_hbm,
    gres_hbm,
    gsum_ref,
    down_hbm,
    ga_hbm,
    all_ref,
    gres_ref,
    down_ref,
    ga_ref,
    gg_ref,
    gu_ref,
    res_ref,
    cot_ref,
    part,
    land,
    wg,
    wu,
    mixed,
    wd,
    wo,
    s_send,
    s_recv,
    g_send,
    g_recv,
    local_sem,
    tile_sem,
    load_sem,
    store_sem,
):
    f = lax.axis_index("feat")
    rows_in = Loads(((gg_hbm, gg_ref), (gu_hbm, gu_ref)), load_sem).start()
    weights = [
        ByTiles(src, dst, tile_sem.at[i], 512)
        for i, (src, dst) in enumerate(((wg_hbm, wg), (wu_hbm, wu)))
    ]
    for pair in zip(*(w.fills for w in weights)):
        for c in pair:
            c.start()
    fills = [
        pltpu.make_async_copy(src, dst, local_sem.at[i])
        for i, (src, dst) in enumerate(((mixed_hbm, mixed), (wd_hbm, wd), (wo_hbm, wo)))
    ]
    late_in = Loads(((res_hbm, res_ref), (cot_hbm, cot_ref)), load_sem.at[pl.ds(2, 2)]).start()
    for c in fills:
        c.start()
    greet(square_targets(f))
    rows_in.wait()
    pairs = [(gg_ref, weights[0]), (gu_ref, weights[1])]

    def down_products(slots):
        for p in slots:
            product_tiles(down_ref, p, [(mixed, wd)], 512)

    rings = summed_products(part, land, f, pairs, s_send, s_recv, land.shape[0], first=True)
    gsum_ref[...] = jnp.zeros_like(gsum_ref)
    late_in.wait()

    def finish_rows(rows, grad):
        residual = res_ref[rows, :]
        inverse = inverse_rms(residual)
        unit = residual * inverse
        gsum_ref[...] += jnp.sum(grad * unit, axis=0, keepdims=True)
        grad_res = cot_ref[rows, :].astype(f32) + norm_back(grad, unit, inverse, gain_ref[...])
        gres_ref[rows, :] = grad_res
        all_ref[f, rows, :] = grad_res.astype(bf16)

    gathers = sum_then_gather(rings, finish_rows, all_ref, f, g_send, g_recv)
    side, above, across = peers(f)

    def attended_grad(slot):
        blocks = ByShare(wo)
        size = all_ref.shape[2] // wo.shape[1]
        total = None
        for i in range(wo.shape[1]):
            term = dot(all_ref[slot, :, i * size : (i + 1) * size], blocks.tile(i, size))
            total = term if total is None else total + term
        ga_ref[slot] = total
        store(ga_ref.at[slot], ga_hbm.at[slot])
        store(all_ref.at[slot], all_hbm.at[slot])

    stores = []

    def store(src, dst):
        c = pltpu.make_async_copy(src, dst, store_sem.at[len(stores)])
        c.start()
        stores.append(c)

    store(gres_ref, gres_hbm)
    for c in fills:
        c.wait()
    attended_grad(f)
    down_products(range(2))
    for gather in gathers:
        gather.relay()
    down_products(range(2, part.shape[0]))
    store(down_ref, down_hbm)
    for gather in gathers:
        gather.near()
    attended_grad(side)
    attended_grad(above)
    for gather in gathers:
        gather.far()
    attended_grad(across)
    for gather in gathers:
        gather.sent()
    for c in stores:
        c.wait()


def rows_back(
    grad_gate, grad_up, gate_w, up_w, residual, cot_own, gain_two, mixed, down_w, out_w
):
    parts, block, hidden = grad_gate.shape
    width = residual.shape[1]
    dma = pltpu.SemaphoreType.DMA
    return pl.pallas_call(
        rows_back_kernel,
        out_shape=(
            jax.ShapeDtypeStruct((parts, block, width), bf16),
            jax.ShapeDtypeStruct((block, width), f32),
            jax.ShapeDtypeStruct((1, width), f32),
            jax.ShapeDtypeStruct((parts, block, width), bf16),
            jax.ShapeDtypeStruct((parts, block, out_w.shape[3]), f32),
        ),
        in_specs=in_place(6) + whole_vmem(1) + in_place(3),
        out_specs=tuple(in_place(2) + whole_vmem(1) + in_place(2)),
        scratch_shapes=[
            pltpu.VMEM((parts, block, width), bf16),
            pltpu.VMEM((block, width), f32),
            pltpu.VMEM((parts, block, width), bf16),
            pltpu.VMEM((parts, block, out_w.shape[3]), f32),
        ]
        + vmem_like(grad_gate, grad_up, residual, cot_own)
        + square_scratch(parts, block, width)[:2]
        + [
            pltpu.VMEM((width, hidden), bf16),
            pltpu.VMEM((width, hidden), bf16),
            pltpu.VMEM((parts, block, hidden), bf16),
            pltpu.VMEM((width, hidden), bf16),
            pltpu.VMEM(out_w.shape, bf16),
        ]
        + [dma((CHUNKS, 6))] * 4
        + [dma((3,)), dma((2, width // 512)), dma((4,)), dma((2 * parts + 2,))],
        compiler_params=pltpu.CompilerParams(
            collective_id=4, has_side_effects=True, vmem_limit_bytes=60 << 20
        ),
        cost_estimate=pl.CostEstimate(flops=0, bytes_accessed=1 << 20, transcendentals=0),
        name="rows_back",
    )(grad_gate, grad_up, gate_w, up_w, residual, cot_own, gain_two, mixed, down_w, out_w)


def closing_kernel(
    seqs,
    dps,
    dqkv_hbm,
    w_hbm,
    tok_hbm,
    gres_hbm,
    gain_ref,
    gsum_two_ref,
    term_hbm,
    oterm_hbm,
    x_ref,
    tile_ref,
    query_ref,
    key_ref,
    value_ref,
    ograd_ref,
    part,
    land,
    s_send,
    s_recv,
    gsum,
    cut,
    came,
    mid,
    tail,
    c_send,
    c_recv,
    d_send,
    d_recv,
    dqkv_ref,
    w_ref,
    tok_ref,
    gres_ref,
    term_ref,
    oterm_ref,
    load_sem,
    *sum_scratch,
):
    loads = Loads(
        (
            (oterm_hbm, oterm_ref),
            (term_hbm, term_ref),
            (dqkv_hbm, dqkv_ref),
            (w_hbm, w_ref),
            (tok_hbm, tok_ref),
            (gres_hbm, gres_ref),
        ),
        load_sem,
    ).start()
    half = len(sum_scratch) // 2
    f, s, d = lax.axis_index("feat"), lax.axis_index("seq"), lax.axis_index("dp")
    parts = 4
    others = [lax.rem(d + k, dps) for k in range(1, dps)]
    circle = [
        (lax.rem(f + i, parts), lax.rem(s + j, seqs))
        for i in range(parts)
        for j in range(seqs)
        if i or j
    ]
    greet(
        [{"feat": a, "seq": b} for a, b in circle] + [{"dp": o} for o in others]
    )
    loads.wait()
    rows_sum = row_sum(term_ref, sum_scratch[:half], f, s, d, seqs, dps)
    out_sum = row_sum(oterm_ref, sum_scratch[half:], f, s, d, seqs, dps)
    out_sum.start()
    rows_sum.start()

    def over_seq():
        out_sum.over_seq()
        rows_sum.over_seq()

    rings = summed_products(
        part, land, f, [(dqkv_ref, w_ref)], s_send, s_recv, land.shape[0], over_seq
    )
    gsum[...] = jnp.zeros_like(gsum)

    def finish_rows(rows, grad):
        values = tok_ref[rows, :].astype(f32)
        inverse = inverse_rms(values)
        unit = values * inverse
        gsum[...] += jnp.sum(grad * unit, axis=0, keepdims=True)
        x_ref[rows, :] = gres_ref[rows, :] + norm_back(grad, unit, inverse, gain_ref[...])

    for ring in rings:
        ring.arrive()
        by_rows(ring, finish_rows)
    out_sum.over_feat()
    rows_sum.over_feat()
    for ring in rings:
        ring.finish()

    lanes = gsum.shape[1] // (parts * seqs)
    cut[...] = jnp.zeros_like(cut)
    for k in range(parts * seqs):
        cut[k, 0:1, :] = gsum[:, k * lanes : (k + 1) * lanes]
        cut[k, 1:2, :] = gsum_two_ref[:, k * lanes : (k + 1) * lanes]
    place = f * seqs + s
    sends = []
    for i, (a, b) in enumerate(circle):
        sends.append(
            push(
                cut.at[a * seqs + b],
                came.at[i],
                c_send.at[i],
                c_recv.at[i],
                {"feat": a, "seq": b},
            )
        )
    for c in sends:
        c.start()
    total = cut[place]
    for c in sends:
        c.wait_recv()
    for i in range(len(circle)):
        total = total + came[i]
    mid[...] = total
    last = [
        push(mid, tail.at[k], d_send.at[k], d_recv.at[k], {"dp": o})
        for k, o in enumerate(others)
    ]
    for c in last:
        c.start()
    for c in last:
        c.wait_recv()
    for k in range(len(others)):
        total = total + tail[k]
    tile_ref[...] = total
    rows_sum.arrive()
    first = 0
    for ref in (query_ref, key_ref, value_ref):
        each = ref.shape[1] // parts
        for p in range(parts):
            piece = rows_sum.shares[p, :, first : first + each]
            ref[:, p * each : (p + 1) * each] = piece.astype(f32)
        first += each
    rows_sum.finish()
    out_sum.arrive()
    each = ograd_ref.shape[1] // parts
    for p in range(parts):
        ograd_ref[:, p * each : (p + 1) * each] = out_sum.shares[p].astype(f32)
    out_sum.finish()
    for c in sends + last:
        c.wait_send()


def closing(dqkv, qkv_w, own, grad_residual, gain_one, gain_two_sum, qkv_term, out_term):
    parts, seqs, dps = (lax.axis_size(a) for a in ALL)
    block, width = own.shape
    others = max(dps - 1, 1)
    lanes = width // (parts * seqs)
    circle = parts * seqs - 1
    rows_each = qkv_term.shape[3]
    dma = pltpu.SemaphoreType.DMA
    return pl.pallas_call(
        functools.partial(closing_kernel, seqs, dps),
        out_shape=(
            jax.ShapeDtypeStruct((block, width), f32),
            jax.ShapeDtypeStruct((8, lanes), f32),
            jax.ShapeDtypeStruct((rows_each, HEADS * FDIM), f32),
            jax.ShapeDtypeStruct((rows_each, HEADS * FDIM), f32),
            jax.ShapeDtypeStruct((rows_each, HEADS * HV), f32),
            jax.ShapeDtypeStruct((rows_each, HEADS * HV), f32),
        ),
        in_specs=in_place(4) + whole_vmem(2) + in_place(2),
        out_specs=tuple(whole_vmem(6)),
        scratch_shapes=square_scratch(parts, block, width)
        + [
            pltpu.VMEM((1, width), f32),
            pltpu.VMEM((parts * seqs, 8, lanes), f32),
            pltpu.VMEM((circle, 8, lanes), f32),
            pltpu.VMEM((8, lanes), f32),
            pltpu.VMEM((others, 8, lanes), f32),
            dma((circle,)),
            dma((circle,)),
            dma((others,)),
            dma((others,)),
        ]
        + vmem_like(dqkv, qkv_w, own, grad_residual, qkv_term, out_term)
        + [dma((6,))]
        + row_sum_scratch(qkv_term.shape)
        + row_sum_scratch(out_term.shape),
        compiler_params=pltpu.CompilerParams(
            collective_id=5, has_side_effects=True, vmem_limit_bytes=60 << 20
        ),
        cost_estimate=pl.CostEstimate(flops=0, bytes_accessed=1 << 20, transcendentals=0),
        name="closing",
    )(dqkv, qkv_w, own, grad_residual, gain_one, gain_two_sum, qkv_term, out_term)


def local(
    tokens,
    segments,
    norm1_gain,
    norm2_gain,
    w_query,
    w_key,
    w_value,
    w_out,
    w_gate,
    w_up,
    w_down,
    cotangent,
):
    parts = lax.axis_size("feat")
    heads = HEADS // parts
    block, width = tokens.shape[2], tokens.shape[3]
    rows_total = parts * block
    rows_each = w_query.shape[0]
    own = tokens.reshape(block, width)
    cot_own = cotangent.reshape(block, width)

    x_all, qkv_w, gains, out_share = opening(
        own, w_query, w_key, w_value, w_out.T, norm1_gain[None], norm2_gain[None]
    )
    qkv_width = qkv_w.shape[1]
    gate_w = lax.all_gather(w_gate, ("seq", "dp"), axis=0, tiled=True)
    gain_one, gain_two = gains[0:1], gains[1:2]

    x_wide = x_all.astype(f32).reshape(rows_total, width)
    normed = (x_wide * inverse_rms(x_wide) * gain_one).astype(bf16)
    qkv = dot(normed, qkv_w).astype(bf16).reshape(parts, block, qkv_width)
    qkv, gate_w, out_share, w_up, w_down = lax.optimization_barrier(
        (qkv, gate_w, out_share, w_up, w_down)
    )
    out_w = lax.all_gather(out_share[None], ("seq", "dp"), axis=0, tiled=True)
    up_w = lax.all_gather(w_up, ("seq", "dp"), axis=0, tiled=True)
    down_w = lax.all_gather(w_down.T, ("seq", "dp"), axis=0, tiled=True)
    segment = segments.reshape(parts, block).astype(f32)
    segc, segr = segment[:, :, None], segment[:, None, :]
    tables = feature_tables(heads)
    att, rden, carry, csum, cot_all = attention_forward(qkv, segc, segr, tables, cot_own, heads)
    cot_all = cot_all.reshape(rows_total, width)
    rows_all, residual = branch_step(att, out_w, own, gain_two)
    rows_all = rows_all.reshape(rows_total, width)

    gate_out = dot(rows_all, gate_w)
    up_out = dot(rows_all, up_w)
    sig = jax.nn.sigmoid(gate_out)
    silu = gate_out * sig
    mixed = (silu * up_out).astype(bf16)
    down_term = dot_tn(cot_all, mixed).astype(bf16)
    mixed, cot_late, down_term = lax.optimization_barrier((mixed, cot_all, down_term))
    grad_mixed = dot(cot_late, down_w)
    grad_gate = (grad_mixed * up_out * sig * (1.0 + gate_out * (1.0 - sig))).astype(bf16)
    grad_up = (grad_mixed * silu).astype(bf16)

    def summed(term):
        return lax.psum_scatter(term, ("seq", "dp"), scatter_dimension=0, tiled=True)

    gate_term = dot_tn(rows_all, grad_gate).astype(bf16)
    up_term = dot_tn(rows_all, grad_up).astype(bf16)
    grad_gate, grad_up, gate_term, up_term = lax.optimization_barrier(
        (grad_gate, grad_up, gate_term, up_term)
    )
    down_sum, gate_sum, up_sum = summed(down_term), summed(gate_term), summed(up_term)

    by_device = (parts, block, -1)
    branch_all, grad_residual, gain_two_sum, down, ga = rows_back(
        grad_gate.reshape(by_device),
        grad_up.reshape(by_device),
        gate_w,
        up_w,
        residual,
        cot_own,
        gain_two,
        mixed.reshape(by_device),
        down_w,
        out_w,
    )
    branch_all = branch_all.reshape(rows_total, width)
    by_row = (parts, lax.axis_size("seq"), lax.axis_size("dp"), rows_each, -1)
    out_term = dot_tn(branch_all, att.reshape(rows_total, heads * HV)).astype(bf16)
    dqkv, output = attention_backward(
        qkv, segc, segr, tables, att, rden, carry, csum, ga, down, residual, heads
    )
    dqkv_late, down_sum = lax.optimization_barrier((dqkv, down_sum))
    qkv_term = dot_tn(normed, dqkv_late.reshape(rows_total, qkv_width)).astype(bf16)
    x_grad, gain_grads, query_grad, key_grad, value_grad, out_grad = closing(
        dqkv, qkv_w, own, grad_residual, gain_one, gain_two_sum, qkv_term.reshape(by_row), out_term.reshape(by_row)
    )
    gain_each = gain_grads.shape[1] // lax.axis_size("dp")
    gain_grads = lax.dynamic_slice_in_dim(
        gain_grads, lax.axis_index("dp") * gain_each, gain_each, axis=1
    )
    return (
        output.reshape(tokens.shape),
        x_grad.reshape(tokens.shape),
        gain_grads[0],
        gain_grads[1],
        query_grad,
        key_grad,
        value_grad,
        out_grad.T,
        gate_sum.astype(f32),
        up_sum.astype(f32),
        down_sum.T.astype(f32),
    )


def solution(mesh):
    placed = (
        P("feat", "dp", "seq", None),
        P(None, "dp", "seq"),
        P(ALL),
        P(ALL),
        P(ALL, None),
        P(ALL, None),
        P(ALL, None),
        P(None, ALL),
        P(("seq", "dp"), "feat"),
        P(("seq", "dp"), "feat"),
        P("feat", ("seq", "dp")),
        P("feat", "dp", "seq", None),
    )
    return jax.shard_map(
        local,
        mesh=mesh,
        in_specs=placed,
        out_specs=(
            P("feat", "dp", "seq", None),
            P("feat", "dp", "seq", None),
            P(ALL),
            P(ALL),
            P(ALL, None),
            P(ALL, None),
            P(ALL, None),
            P(None, ALL),
            P(("seq", "dp"), "feat"),
            P(("seq", "dp"), "feat"),
            P("feat", ("seq", "dp")),
        ),
        check_vma=False,
    )
```

```python
import functools

import jax
import jax.numpy as jnp
import numpy as np
from jax import lax
from jax.experimental import pallas as pl
from jax.experimental.pallas import tpu as pltpu
from jax.sharding import PartitionSpec as P

HEADS = 16
FDIM = 16
HV = 128
STATE = 160
LANES = 256
epsilon = 1e-05
MESH = pl.DeviceIdType.MESH
ALL = ("feat", "seq", "dp")
f32 = jnp.float32
bf16 = jnp.bfloat16


def dot(a, b):
    return lax.dot_general(a, b, (((1,), (0,)), ((), ())), preferred_element_type=f32)


def dot_nt(a, b):
    return lax.dot_general(a, b, (((1,), (1,)), ((), ())), preferred_element_type=f32)


def dot_tn(a, b):
    return lax.dot_general(a, b, (((0,), (0,)), ((), ())), preferred_element_type=f32)


def feature_tables(heads):
    pairs = [(i, j) for i in range(FDIM) for j in range(i, FDIM)]
    left = np.zeros((heads, heads * FDIM, LANES), np.float32)
    right = np.zeros((heads, heads * FDIM, LANES), np.float32)
    rows = np.zeros((8, LANES), np.float32)
    for h in range(heads):
        for p, (i, j) in enumerate(pairs):
            left[h, h * FDIM + i, p] = 1.0
            right[h, h * FDIM + j, p] = 1.0
            rows[2, p] = 0.25 / 2.0**0.5 if i == j else 0.25
        for i in range(FDIM):
            p = len(pairs) + i
            left[h, h * FDIM + i, p] = 1.0
            rows[1, p] = 1.0
            rows[2, p] = 0.5
        p = len(pairs) + FDIM
        rows[0, p] = rows[1, p] = rows[2, p] = 1.0
    return jnp.asarray(left, bf16), jnp.asarray(right, bf16), jnp.asarray(rows)


def both_sides(entries, h, left_ref, right_ref, rows_ref):
    one = dot(entries, left_ref[h]) + rows_ref[0:1, :]
    two = dot(entries, right_ref[h]) + rows_ref[1:2, :]
    return one, two * rows_ref[2:3, :]


def features(entries, h, left_ref, right_ref, rows_ref):
    one, two = both_sides(entries, h, left_ref, right_ref, rows_ref)
    return one * two


def pull_features(grad, entries, h, left_ref, right_ref, rows_ref):
    one, two = both_sides(entries, h, left_ref, right_ref, rows_ref)
    scaled = rows_ref[2:3, :]
    return dot_nt((grad * two).astype(bf16), left_ref[h]) + dot_nt(
        (grad * one * scaled).astype(bf16), right_ref[h]
    )


def only_head(entries, h):
    lane = lax.broadcasted_iota(jnp.int32, entries.shape, 1)
    keep = (lane >= h * FDIM) & (lane < (h + 1) * FDIM)
    return jnp.where(keep, entries, jnp.zeros_like(entries))


def padded_state(state):
    return jnp.concatenate([state, jnp.zeros((LANES - STATE, state.shape[1]), state.dtype)], 0)


def allowed_of(segc, segr):
    block = segc.shape[0]
    row = lax.broadcasted_iota(jnp.int32, (block, block), 0)
    col = lax.broadcasted_iota(jnp.int32, (block, block), 1)
    return (row >= col) & (segc == segr)


def forward_kernel(
    count,
    heads,
    qkv_ref,
    segc_ref,
    segr_ref,
    left_ref,
    right_ref,
    rows_ref,
    cot_ref,
    att_hbm,
    rden_hbm,
    carry_hbm,
    csum_hbm,
    cots_ref,
    att_ref,
    rden_ref,
    carry_ref,
    csum_ref,
    send_state,
    send_sum,
    part,
    send_sem,
    recv_sem,
    f_send,
    f_recv,
    local_sem,
    store_sem,
):
    place, f = lax.axis_index("seq"), lax.axis_index("feat")
    groups, block = qkv_ref.shape[0], qkv_ref.shape[1]
    width = heads * FDIM
    tables = (left_ref, right_ref, rows_ref)

    def stores(g):
        pairs = (
            (att_ref, att_hbm),
            (rden_ref, rden_hbm),
            (carry_ref, carry_hbm),
            (csum_ref, csum_hbm),
        )
        return Loads([(a.at[g], b.at[g]) for a, b in pairs], store_sem.at[g])

    def hop(g):
        target = {"seq": lax.rem(place + 1, count)}
        return [
            pltpu.make_async_remote_copy(
                src_ref=src.at[g],
                dst_ref=dst.at[g],
                send_sem=send_sem.at[i, g],
                recv_sem=recv_sem.at[i, g],
                device_id=target,
                device_id_type=MESH,
            )
            for i, (src, dst) in enumerate(((send_state, carry_ref), (send_sum, csum_ref)))
        ]

    def send(g):
        for copy in hop(g):
            copy.start()

    chain = [lax.rem(place + 1, count), lax.rem(place + count - 1, count)]
    stay = pltpu.make_async_copy(cot_ref, cots_ref.at[f], local_sem.at[0])
    stay.start()
    greet(square_targets(f) + [{"seq": c} for c in chain])
    gather = SquareGather(cots_ref, f, f_send, f_recv, cot_ref)
    gather.start()

    @pl.when(place == 0)
    def _():
        carry_ref[...] = jnp.zeros_like(carry_ref)
        csum_ref[...] = jnp.full_like(csum_ref, -1.0)

    def summarize(g, none):
        segc, segr = segc_ref[g], segr_ref[g]
        tail = segr[:, block - 1 : block]
        at_tail = (segc == tail).astype(f32)
        send_sum[g, heads : heads + 1, :] = jnp.broadcast_to(tail, (1, LANES))
        for h in range(heads):
            key = qkv_ref[g, :, width : 2 * width]
            value = qkv_ref[g, :, 2 * width + h * HV : 2 * width + (h + 1) * HV]
            phi = (features(key, h, *tables) * at_tail).astype(bf16)
            send_state[g, h] = dot_tn(phi, value)[:STATE].astype(bf16)
            ones = jnp.ones((8, block), bf16)
            send_sum[g, h : h + 1, :] = dot(ones, phi)[0:1]

        @pl.when(place == 0)
        def _():
            send(g)

        return none

    lax.fori_loop(0, groups, summarize, 0)
    def join(g, none):
        for copy in hop(g):
            copy.wait_recv()
        segr = segr_ref[g]
        mark = csum_ref[g, heads : heads + 1, 0:1]
        head, tail = segr[:, 0:1], segr[:, block - 1 : block]
        whole = ((head == tail) & (head == mark)).astype(f32)
        for h in range(heads):
            send_state[g, h] = (
                send_state[g, h].astype(f32) + whole * carry_ref[g, h].astype(f32)
            ).astype(bf16)
            send_sum[g, h : h + 1, :] = (
                send_sum[g, h : h + 1, :] + whole * csum_ref[g, h : h + 1, :]
            )
        send(g)
        return none

    def attend(g, none):
        segc, segr = segc_ref[g], segr_ref[g]
        allowed = allowed_of(segc, segr)
        for h in range(heads):
            query = only_head(qkv_ref[g, :, 0:width], h)
            key = qkv_ref[g, :, width : 2 * width]
            value = qkv_ref[g, :, 2 * width + h * HV : 2 * width + (h + 1) * HV]
            c = dot_nt(query, key)
            kernel = jnp.where(allowed, 1.0 + c * (0.25 + c * 0.03125), 0.0).astype(bf16)
            wide = jnp.concatenate([value, jnp.ones_like(value)], axis=1)
            part[g, h] = dot(kernel, wide)

        @pl.when((place > 0) & (place < count - 1) & (g == place - 1))
        def _():
            lax.fori_loop(0, groups, join, 0)

        return none

    lax.fori_loop(0, groups, attend, 0)
    gather.relay()

    def carry_on(g, none):
        segc = segc_ref[g]

        @pl.when(place == count - 1)
        def _():
            for copy in hop(g):
                copy.wait_recv()

        mark = csum_ref[g, heads : heads + 1, 0:1]
        carried = (segc == mark).astype(f32)
        for h in range(heads):
            phi = features(qkv_ref[g, :, 0:width], h, *tables) * carried
            state = padded_state(carry_ref[g, h])
            both = part[g, h]
            numer = both[:, :HV] + dot(phi.astype(bf16), state)
            denom = both[:, HV:] + jnp.sum(
                phi * csum_ref[g, h : h + 1, :], axis=1, keepdims=True
            )
            inverse = 1.0 / denom
            att_ref[g, :, h * HV : (h + 1) * HV] = (numer * inverse).astype(bf16)
            rden_ref[g, :, h * HV : (h + 1) * HV] = inverse
        stores(g).start()
        return none

    lax.fori_loop(0, groups, carry_on, 0)

    @pl.when(place < count - 1)
    def _():
        def finish(g, none):
            for copy in hop(g):
                copy.wait_send()
            return none

        lax.fori_loop(0, groups, finish, 0)

    stay.wait()
    gather.finish()

    def stored(g, none):
        stores(g).wait()
        return none

    lax.fori_loop(0, groups, stored, 0)


def backward_kernel(
    count,
    heads,
    qkv_hbm,
    segc_ref,
    segr_ref,
    left_ref,
    right_ref,
    rows_ref,
    att_hbm,
    rden_hbm,
    carry_hbm,
    csum_ref,
    ga_hbm,
    down_ref,
    res_hbm,
    branch_hbm,
    out_hbm,
    final_ref,
    acc_hbm,
    qkv_ref,
    att_ref,
    rden_ref,
    carry_ref,
    ga_ref,
    res_ref,
    branch_ref,
    out_ref,
    gn,
    send_state,
    send_sum,
    recv_state,
    recv_sum,
    dkey,
    dvalue,
    terms,
    land,
    send_sem,
    recv_sem,
    f_send,
    f_recv,
    local_sem,
    load_sem,
    store_sem,
    term_ref,
    acc_ref,
    sib_land,
    sib_send,
    sib_recv,
):
    place, f, d = lax.axis_index("seq"), lax.axis_index("feat"), lax.axis_index("dp")
    dps = term_ref.shape[2]
    loads = Loads(
        (
            (qkv_hbm, qkv_ref),
            (ga_hbm, ga_ref),
            (rden_hbm, rden_ref),
            (att_hbm, att_ref),
            (carry_hbm, carry_ref),
            (res_hbm, res_ref),
        ),
        load_sem,
    ).start()
    late = Loads(((branch_hbm, branch_ref),), load_sem.at[pl.ds(6, 1)]).start()
    groups, block = qkv_ref.shape[0], qkv_ref.shape[1]
    width = heads * FDIM
    tables = (left_ref, right_ref, rows_ref)

    def hop(g):
        target = {"seq": lax.rem(place + count - 1, count)}
        return [
            pltpu.make_async_remote_copy(
                src_ref=src.at[g],
                dst_ref=dst.at[g],
                send_sem=send_sem.at[i, g],
                recv_sem=recv_sem.at[i, g],
                device_id=target,
                device_id_type=MESH,
            )
            for i, (src, dst) in enumerate(((send_state, recv_state), (send_sum, recv_sum)))
        ]

    def send(g):
        for copy in hop(g):
            copy.start()

    chain = [lax.rem(place + 1, count), lax.rem(place + count - 1, count)]
    greet(
        square_targets(f)
        + [{"seq": c} for c in chain]
        + [{"dp": lax.rem(d + o, dps)} for o in range(1, dps)]
    )
    fill = pltpu.make_async_copy(down_ref, terms, local_sem.at[0])
    fill.start()
    ring = SquareSum(terms, land, f, f_send, f_recv)
    loads.wait()

    def store(g):
        return pltpu.make_async_copy(out_ref.at[g], out_hbm.at[g], store_sem.at[g])


    @pl.when(place == count - 1)
    def _():
        recv_state[...] = jnp.zeros_like(recv_state)
        recv_sum[...] = jnp.full_like(recv_sum, -1.0)

    def summarize(g, none):
        segc, segr = segc_ref[g], segr_ref[g]
        head = segr[:, 0:1]
        at_head = (segc == head).astype(f32)
        send_sum[g, heads : heads + 1, :] = jnp.broadcast_to(head, (1, LANES))
        for h in range(heads):
            lanes = slice(h * HV, (h + 1) * HV)
            ga = ga_ref[g, :, lanes]
            inverse = rden_ref[g, :, lanes]
            numer = (ga * inverse).astype(bf16)
            dots = jnp.sum(ga * att_ref[g, :, lanes].astype(f32), axis=1, keepdims=True)
            lane = lax.broadcasted_iota(jnp.int32, (block, HV), 1)
            denom = jnp.where(lane == 0, -dots * inverse, 0.0).astype(bf16)
            gn[g, h, :, :HV] = numer
            gn[g, h, :, HV:] = denom
            phi = (features(qkv_ref[g, :, 0:width], h, *tables) * at_head).astype(bf16)
            send_state[g, h] = dot_tn(phi, numer)[:STATE].astype(bf16)
            send_sum[g, h : h + 1, :] = dot_tn(denom, phi)[0:1]

        @pl.when(place == count - 1)
        def _():
            send(g)

        return none

    lax.fori_loop(0, groups, summarize, 0)
    fill.wait()
    ring.start_cross()
    ring.start_near()

    def join(g, none):
        for copy in hop(g):
            copy.wait_recv()
        segr = segr_ref[g]
        mark = recv_sum[g, heads : heads + 1, 0:1]
        head, tail = segr[:, 0:1], segr[:, block - 1 : block]
        whole = ((head == tail) & (head == mark)).astype(f32)
        for h in range(heads):
            send_state[g, h] = (
                send_state[g, h].astype(f32) + whole * recv_state[g, h].astype(f32)
            ).astype(bf16)
            send_sum[g, h : h + 1, :] = (
                send_sum[g, h : h + 1, :] + whole * recv_sum[g, h : h + 1, :]
            )
        send(g)
        return none

    def pull(g, none):
        segc, segr = segc_ref[g], segr_ref[g]
        allowed = allowed_of(segc, segr)
        query_all = qkv_ref[g, :, 0:width]
        key_all = qkv_ref[g, :, width : 2 * width]
        carried = (segc == csum_ref[g, heads : heads + 1, 0:1]).astype(f32)
        dquery = jnp.zeros((block, width), f32)
        dkey_sum = jnp.zeros((block, width), f32)
        for h in range(heads):
            query, key = only_head(query_all, h), only_head(key_all, h)
            value = qkv_ref[g, :, 2 * width + h * HV : 2 * width + (h + 1) * HV]
            wide = jnp.concatenate([value, jnp.ones_like(value)], axis=1)
            both = gn[g, h]
            c = dot_nt(query, key_all)
            kernel = jnp.where(allowed, 1.0 + c * (0.25 + c * 0.03125), 0.0).astype(bf16)
            grad = jnp.where(allowed, dot_nt(both, wide), 0.0)
            grad_c = (grad * (0.25 + c * 0.0625)).astype(bf16)
            dvalue[g, h] = dot_tn(kernel, both[:, :HV])
            dkey_sum = dkey_sum + dot_tn(grad_c, query)
            dquery = dquery + dot(grad_c, key)
            state = padded_state(carry_ref[g, h])
            gphi = dot_nt(both[:, :HV], state) + both[:, HV : HV + 1].astype(f32) * csum_ref[
                g, h : h + 1, :
            ]
            dquery = dquery + pull_features(gphi * carried, query_all, h, *tables)
        out_ref[g, :, 0:width] = dquery.astype(bf16)
        dkey[g] = dkey_sum

        @pl.when((place > 0) & (place < count - 1) & (g == count - 2 - place))
        def _():
            lax.fori_loop(0, groups, join, 0)

        return none

    lax.fori_loop(0, groups, pull, 0)
    ring.relay()
    late.wait()
    term_tiles(term_ref, branch_ref, att_ref)
    sibling = SiblingSum(term_ref, acc_ref, sib_land, (sib_send, sib_recv), d, dps)
    sibling.start()

    def carry_back(g, none):
        segc = segc_ref[g]
        key_all = qkv_ref[g, :, width : 2 * width]

        @pl.when(place == 0)
        def _():
            for copy in hop(g):
                copy.wait_recv()

        mark = recv_sum[g, heads : heads + 1, 0:1]
        later = (segc == mark).astype(f32)
        total = dkey[g]
        for h in range(heads):
            value = qkv_ref[g, :, 2 * width + h * HV : 2 * width + (h + 1) * HV]
            state = padded_state(recv_state[g, h])
            phi = (features(key_all, h, *tables) * later).astype(bf16)
            dv = dvalue[g, h] + dot(phi, state)
            out_ref[g, :, 2 * width + h * HV : 2 * width + (h + 1) * HV] = dv.astype(bf16)
            gphi = (dot_nt(value, state) + recv_sum[g, h : h + 1, :]) * later
            total = total + pull_features(gphi, key_all, h, *tables)
        out_ref[g, :, width : 2 * width] = total.astype(bf16)
        store(g).start()
        return none

    lax.fori_loop(0, groups, carry_back, 0)

    @pl.when(place > 0)
    def _():
        def finish(g, none):
            for copy in hop(g):
                copy.wait_send()
            return none

        lax.fori_loop(0, groups, finish, 0)

    ring.arrive()

    def add_up(rows, total):
        final_ref[rows, :] = (res_ref[rows, :] + total).astype(bf16)

    by_rows(ring, add_up)
    ring.finish()
    sibling.add()
    keep = pltpu.make_async_copy(acc_ref, acc_hbm, store_sem.at[groups])
    keep.start()

    def stored(g, none):
        store(g).wait()
        return none

    lax.fori_loop(0, groups, stored, 0)
    sibling.finish()
    keep.wait()


def term_tiles(term, left, right):
    parts, *shape = term.shape
    tile = left.shape[2] // parts

    def one(i, none):
        cols = pl.ds(pl.multiple_of(i * tile, tile), tile)
        total = dot_tn(left[0, :, cols], right[0])
        for g in range(1, left.shape[0]):
            total = total + dot_tn(left[g, :, cols], right[g])
        term[i] = total.astype(bf16).reshape(shape)
        return none

    lax.fori_loop(0, parts, one, 0)


def whole_vmem(count):
    return [pl.BlockSpec(memory_space=pltpu.VMEM)] * count


def attention_forward(qkv, segc, segr, tables, cot_own, heads):
    groups, block, _ = qkv.shape
    count = lax.axis_size("seq")
    dma = pltpu.SemaphoreType.DMA
    states = (groups, heads, STATE, HV)
    sums = (groups, 8, LANES)
    return pl.pallas_call(
        functools.partial(forward_kernel, count, heads),
        out_shape=(
            jax.ShapeDtypeStruct((groups, block, heads * HV), bf16),
            jax.ShapeDtypeStruct((groups, block, heads * HV), f32),
            jax.ShapeDtypeStruct(states, bf16),
            jax.ShapeDtypeStruct(sums, f32),
            jax.ShapeDtypeStruct((groups,) + cot_own.shape, bf16),
        ),
        in_specs=whole_vmem(6) + in_place(1),
        out_specs=tuple(in_place(5)),
        scratch_shapes=[
            pltpu.VMEM((groups, block, heads * HV), bf16),
            pltpu.VMEM((groups, block, heads * HV), f32),
            pltpu.VMEM(states, bf16),
            pltpu.VMEM(sums, f32),
            pltpu.VMEM(states, bf16),
            pltpu.VMEM(sums, f32),
            pltpu.VMEM((groups, heads, block, 2 * HV), f32),
            dma((2, groups)),
            dma((2, groups)),
            dma((6,)),
            dma((6,)),
            dma((1,)),
            dma((groups, 4)),
        ],
        compiler_params=pltpu.CompilerParams(
            collective_id=0, has_side_effects=True, vmem_limit_bytes=60 << 20
        ),
        cost_estimate=pl.CostEstimate(flops=0, bytes_accessed=1 << 20, transcendentals=0),
        name="attention_forward",
    )(qkv, segc, segr, *tables, cot_own)


def attention_backward(
    qkv, segc, segr, tables, att, rden, carry, csum, ga, down, residual, branch, heads
):
    groups, block, wide = qkv.shape
    count = lax.axis_size("seq")
    parts, dps = lax.axis_size("feat"), lax.axis_size("dp")
    rows_each = branch.shape[2] // (parts * count * dps)
    by_row = (parts, count, dps, rows_each, heads * HV)
    states = (groups, heads, STATE, HV)
    sums = (groups, 8, LANES)
    return pl.pallas_call(
        functools.partial(backward_kernel, count, heads),
        out_shape=(
            jax.ShapeDtypeStruct((groups, block, wide), bf16),
            jax.ShapeDtypeStruct(residual.shape, bf16),
            jax.ShapeDtypeStruct((count, by_row[0]) + by_row[3:], bf16),
        ),
        in_specs=in_place(1)
        + whole_vmem(5)
        + in_place(3)
        + whole_vmem(1)
        + in_place(4),
        out_specs=tuple(in_place(1) + whole_vmem(1) + in_place(1)),
        scratch_shapes=vmem_like(qkv, att, rden, carry, ga, residual, branch)
        + [
            pltpu.VMEM((groups, block, wide), bf16),
            pltpu.VMEM((groups, heads, block, 2 * HV), bf16),
            pltpu.VMEM(states, bf16),
            pltpu.VMEM(sums, f32),
            pltpu.VMEM(states, bf16),
            pltpu.VMEM(sums, f32),
            pltpu.VMEM((groups, block, heads * FDIM), f32),
            pltpu.VMEM((groups, heads, block, HV), f32),
            pltpu.VMEM((groups,) + residual.shape, bf16),
            pltpu.VMEM((6, block // 2, residual.shape[1]), bf16),
            pltpu.SemaphoreType.DMA((2, groups)),
            pltpu.SemaphoreType.DMA((2, groups)),
            pltpu.SemaphoreType.DMA((6,)),
            pltpu.SemaphoreType.DMA((6,)),
            pltpu.SemaphoreType.DMA((1,)),
            pltpu.SemaphoreType.DMA((7,)),
            pltpu.SemaphoreType.DMA((groups + 1,)),
        ]
        + sibling_scratch(by_row),
        compiler_params=pltpu.CompilerParams(
            collective_id=1, has_side_effects=True, vmem_limit_bytes=60 << 20
        ),
        cost_estimate=pl.CostEstimate(flops=0, bytes_accessed=1 << 20, transcendentals=0),
        name="attention_backward",
    )(qkv, segc, segr, *tables, att, rden, carry, csum, ga, down, residual, branch)


def peers(f):
    return 2 * (f // 2) + 1 - f % 2, (f + 2) % 4, 3 - f


def greet(targets):
    barrier = pltpu.get_barrier_semaphore()
    for target in targets:
        pl.semaphore_signal(barrier, inc=1, device_id=target, device_id_type=MESH)
    pl.semaphore_wait(barrier, len(targets))


def push(src, dst, send_sem, recv_sem, target):
    return pltpu.make_async_remote_copy(
        src_ref=src,
        dst_ref=dst,
        send_sem=send_sem,
        recv_sem=recv_sem,
        device_id=target,
        device_id_type=MESH,
    )


def square_targets(f):
    return [{"feat": p} for p in peers(f)]


class Loads:
    def __init__(self, pairs, sem):
        self.copies = [pltpu.make_async_copy(a, b, sem.at[i]) for i, (a, b) in enumerate(pairs)]

    def start(self):
        for c in self.copies:
            c.start()
        return self

    def wait(self):
        for c in self.copies:
            c.wait()


def vmem_like(*arrays):
    return [pltpu.VMEM(a.shape, a.dtype) for a in arrays]


class SquareGather:
    def __init__(self, slots, f, send_sem, recv_sem, own=None, base=0, rows=None):
        side, above, across = peers(f)
        half = (slots.shape[1] if rows is None else rows) // 2
        first, second = pl.ds(base, half), pl.ds(base + half, half)

        def copy(i, slot, rows, to):
            ref = slots.at[slot, rows]
            src = ref if own is None or i > 3 else own.at[rows]
            return push(src, ref, send_sem.at[i], recv_sem.at[i], {"feat": to})

        self.direct = [
            copy(0, f, first, side),
            copy(1, f, second, above),
            copy(2, f, second, side),
            copy(3, f, first, above),
        ]
        self.forward = [copy(4, side, first, above), copy(5, above, second, side)]

    def start(self):
        for c in self.direct:
            c.start()

    def relay(self):
        self.direct[0].wait_recv()
        self.forward[0].start()
        self.direct[1].wait_recv()
        self.forward[1].start()

    def near(self):
        self.direct[2].wait_recv()
        self.direct[3].wait_recv()

    def far(self):
        for c in self.forward:
            c.wait_recv()

    def sent(self):
        for c in self.direct + self.forward:
            c.wait_send()

    def finish(self):
        self.near()
        self.far()
        self.sent()


class SquareSum:
    def __init__(self, part, land, f, send_sem, recv_sem, base=0, rows=None):
        self.side, self.above, self.across = peers(f)
        self.f, self.part, self.land, self.base = f, part, land, base
        self.half = (part.shape[1] if rows is None else rows) // 2
        first, second = pl.ds(base, self.half), pl.ds(base + self.half, self.half)

        def copy(i, slot, rows, to):
            return push(
                part.at[slot, rows], land.at[i], send_sem.at[i], recv_sem.at[i], {"feat": to}
            )

        self.cross = [copy(0, self.across, first, self.side), copy(1, self.across, second, self.above)]
        self.near = [copy(2, self.side, first, self.side), copy(3, self.above, second, self.above)]
        self.late = [copy(4, self.above, first, self.above), copy(5, self.side, second, self.side)]

    def start_cross(self):
        for c in self.cross:
            c.start()

    def add_rows(self, slot, base, landed):
        step = 16

        def one(i, none):
            rows = pl.ds(pl.multiple_of(base + i * step, step), step)
            came = self.land[landed, pl.ds(pl.multiple_of(i * step, step), step), :]
            self.part[slot, rows, :] = (
                self.part[slot, rows, :].astype(f32) + came.astype(f32)
            ).astype(bf16)
            return none

        lax.fori_loop(0, self.half // step, one, 0)

    def start_near(self):
        for c in self.near:
            c.start()

    def relay(self):
        self.cross[0].wait_recv()
        self.add_rows(self.above, self.base, 0)
        self.late[0].start()
        self.cross[1].wait_recv()
        self.add_rows(self.side, self.base + self.half, 1)
        self.late[1].start()

    def arrive(self):
        for c in self.near + self.late:
            c.wait_recv()

    def total(self, half, rows):
        base = self.base + half * self.half
        own = self.part[self.f, pl.ds(pl.multiple_of(base + rows.start, 16), rows.size), :]
        near = self.land[2 + half, rows, :]
        late = self.land[4 + half, rows, :]
        return own.astype(f32) + near.astype(f32) + late.astype(f32)

    def finish(self):
        for c in self.cross + self.near + self.late:
            c.wait_send()


class SiblingSum:
    def __init__(self, term, acc, land, sems, d, dps):
        self.term, self.acc, self.land, self.d = term, acc, land, d
        others = [lax.rem(d + k, dps) for k in range(1, dps)]
        self.copies = [
            push(term.at[:, :, o], land.at[k], sems[0].at[k], sems[1].at[k], {"dp": o})
            for k, o in enumerate(others)
        ]

    def start(self):
        for c in self.copies:
            c.start()

    def add(self):
        for c in self.copies:
            c.wait_recv()
        seqs, parts = self.acc.shape[:2]

        def one(i, none):
            p, c = i // seqs, lax.rem(i, seqs)
            total = self.term[p, c, self.d].astype(f32)
            for k in range(len(self.copies)):
                total = total + self.land[k, p, c].astype(f32)
            self.acc[c, p] = total.astype(bf16)
            return none

        lax.fori_loop(0, parts * seqs, one, 0)

    def finish(self):
        for c in self.copies:
            c.wait_send()


class RowSum:
    def __init__(self, acc, shares, land, total, sems, f, s):
        self.acc, self.shares, self.land, self.total = acc, shares, land, total
        self.f, self.s = f, s
        seqs, self.parts = acc.shape[:2]
        columns = [lax.rem(s + k, seqs) for k in range(1, seqs)]
        z_send, z_recv, a_send, a_recv = sems
        self.two = [
            push(acc.at[c], land.at[k], z_send.at[k], z_recv.at[k], {"seq": c})
            for k, c in enumerate(columns)
        ]
        self.three = [
            push(total.at[p], shares.at[f], a_send.at[i], a_recv.at[i], {"feat": p})
            for i, p in enumerate(peers(f))
        ]

    def start(self):
        for c in self.two:
            c.start()

    def over_feat(self):
        for c in self.two:
            c.wait_recv()

        def one(p, none):
            total = self.acc[self.s, p].astype(f32)
            for k in range(len(self.two)):
                total = total + self.land[k, p].astype(f32)
            self.total[p] = total.astype(bf16)
            return none

        lax.fori_loop(0, self.parts, one, 0)
        self.shares[self.f] = self.total[self.f]
        for c in self.three:
            c.start()

    def arrive(self):
        for c in self.three:
            c.wait_recv()

    def finish(self):
        for c in self.two + self.three:
            c.wait_send()


def sibling_scratch(shape):
    parts, seqs, dps, rows, wide = shape
    others = max(dps - 1, 1)
    dma = pltpu.SemaphoreType.DMA
    return [
        pltpu.VMEM(shape, bf16),
        pltpu.VMEM((seqs, parts, rows, wide), bf16),
        pltpu.VMEM((others, parts, seqs, rows, wide), bf16),
        dma((others,)),
        dma((others,)),
    ]


def row_sum_scratch(shape):
    seqs, parts, rows, wide = shape
    dma = pltpu.SemaphoreType.DMA
    return [
        pltpu.VMEM((parts, rows, wide), bf16),
        pltpu.VMEM((seqs - 1, parts, rows, wide), bf16),
        pltpu.VMEM((parts, rows, wide), bf16),
        dma((seqs - 1,)),
        dma((seqs - 1,)),
        dma((3,)),
        dma((3,)),
    ]


def opening_kernel(
    seqs,
    dps,
    tok_ref,
    query_ref,
    key_ref,
    value_ref,
    out_ref,
    one_ref,
    two_ref,
    x_ref,
    w_ref,
    g_ref,
    o_ref,
    pack,
    opack,
    tile,
    x_send,
    x_recv,
    a_send,
    a_recv,
    z_send,
    z_recv,
    d_send,
    d_recv,
    local_sem,
):
    f, s, d = lax.axis_index("feat"), lax.axis_index("seq"), lax.axis_index("dp")
    parts, rows_each = pack.shape[0], pack.shape[1]
    near = peers(f)
    columns = [lax.rem(s + k, seqs) for k in range(1, seqs)]
    others = [lax.rem(d + k, dps) for k in range(1, dps)]
    stay = pltpu.make_async_copy(tok_ref, x_ref.at[f], local_sem.at[0])
    stay.start()
    first = 0
    for ref in (query_ref, key_ref, value_ref):
        each = ref.shape[1] // parts
        for p in range(parts):
            pack[p, :, first : first + each] = ref[:, p * each : (p + 1) * each]
        first += each
    tile[...] = jnp.zeros_like(tile)
    tile[0:1, :rows_each] = one_ref[...].astype(f32)
    tile[1:2, :rows_each] = two_ref[...].astype(f32)
    outs = (w_ref, g_ref)
    own = [
        pltpu.make_async_copy(pack.at[f], w_ref.at[f, s, d], local_sem.at[1]),
        pltpu.make_async_copy(tile, g_ref.at[f, s, d], local_sem.at[2]),
    ]
    for c in own:
        c.start()
    greet(
        square_targets(f) + [{"seq": c} for c in columns] + [{"dp": o} for o in others]
    )
    shares = [
        [
            push(pack.at[p], w_ref.at[f, s, d], a_send.at[0, i], a_recv.at[0, i], {"feat": p}),
            push(tile, g_ref.at[f, s, d], a_send.at[1, i], a_recv.at[1, i], {"feat": p}),
        ]
        for i, p in enumerate(near)
    ]
    for pair in shares:
        for c in pair:
            c.start()
    gather = SquareGather(x_ref, f, x_send, x_recv, tok_ref)
    gather.start()
    each = out_ref.shape[1] // parts
    for p in range(parts):
        opack[p] = out_ref[:, p * each : (p + 1) * each]
    own_out = pltpu.make_async_copy(opack.at[f], o_ref.at[f], local_sem.at[3])
    own_out.start()
    out_shares = [
        push(opack.at[p], o_ref.at[f], a_send.at[2, i], a_recv.at[2, i], {"feat": p})
        for i, p in enumerate(near)
    ]
    for c in out_shares:
        c.start()
    for c in own:
        c.wait()

    chunks = (f,) + near

    def to_column(n, k):
        return [
            push(
                ref.at[chunks[n], s, d],
                ref.at[chunks[n], s, d],
                z_send.at[j, k - 1, n],
                z_recv.at[j, k - 1, n],
                {"seq": columns[k - 1]},
            )
            for j, ref in enumerate(outs)
        ]

    def to_sibling(n, k):
        back = lax.rem(s + seqs - k, seqs)
        return [
            push(
                ref.at[chunks[n], back, d],
                ref.at[chunks[n], back, d],
                d_send.at[j, o, k, n],
                d_recv.at[j, o, k, n],
                {"dp": other},
            )
            for j, ref in enumerate(outs)
            for o, other in enumerate(others)
        ]

    def start_all(copies):
        for c in copies:
            c.start()

    for n in range(parts):
        if n:
            for c in shares[n - 1]:
                c.wait_recv()
        for k in range(1, seqs):
            start_all(to_column(n, k))
        start_all(to_sibling(n, 0))
    for n in range(parts):
        for k in range(1, seqs):
            for c in to_column(n, k):
                c.wait_recv()
            start_all(to_sibling(n, k))
    gather.relay()
    for n in range(parts):
        for k in range(seqs):
            for c in to_sibling(n, k):
                c.wait_recv()
    for n in range(parts):
        for k in range(seqs):
            for c in to_sibling(n, k):
                c.wait_send()
        for k in range(1, seqs):
            for c in to_column(n, k):
                c.wait_send()
    for pair in shares:
        for c in pair:
            c.wait_send()
    stay.wait()
    own_out.wait()
    for c in out_shares:
        c.wait_recv()
    for c in out_shares:
        c.wait_send()
    gather.finish()


def in_place(count):
    return [pl.BlockSpec(memory_space=pltpu.HBM)] * count


def opening(own, w_query, w_key, w_value, w_out, gain_one, gain_two):
    parts, seqs, dps = (lax.axis_size(a) for a in ALL)
    block, width = own.shape
    rows_each = w_query.shape[0]
    wide = (w_query.shape[1] + w_key.shape[1] + w_value.shape[1]) // parts
    others = max(dps - 1, 1)
    dma = pltpu.SemaphoreType.DMA
    out_wide = w_out.shape[1] // parts
    x_all, w_all, g_all, o_own = pl.pallas_call(
        functools.partial(opening_kernel, seqs, dps),
        out_shape=(
            jax.ShapeDtypeStruct((parts, block, width), bf16),
            jax.ShapeDtypeStruct((parts, seqs, dps, rows_each, wide), bf16),
            jax.ShapeDtypeStruct((parts, seqs, dps, 8, HV), f32),
            jax.ShapeDtypeStruct((parts, rows_each, out_wide), bf16),
        ),
        in_specs=in_place(1) + whole_vmem(6),
        out_specs=tuple(in_place(4)),
        scratch_shapes=[
            pltpu.VMEM((parts, rows_each, wide), bf16),
            pltpu.VMEM((parts, rows_each, out_wide), bf16),
            pltpu.VMEM((8, HV), f32),
            dma((6,)),
            dma((6,)),
            dma((3, 3)),
            dma((3, 3)),
            dma((2, seqs - 1, parts)),
            dma((2, seqs - 1, parts)),
            dma((2, others, seqs, parts)),
            dma((2, others, seqs, parts)),
            dma((4,)),
        ],
        compiler_params=pltpu.CompilerParams(collective_id=2, has_side_effects=True, vmem_limit_bytes=60 << 20),
        cost_estimate=pl.CostEstimate(flops=0, bytes_accessed=1 << 20, transcendentals=0),
        name="opening",
    )(own, w_query, w_key, w_value, w_out, gain_one, gain_two)
    gains = g_all[..., :2, :rows_each].transpose(3, 0, 1, 2, 4).reshape(2, width)
    return x_all, w_all.reshape(width, wide), gains, o_own


def inverse_rms(values):
    return lax.rsqrt(jnp.mean(values * values, axis=-1, keepdims=True) + epsilon)


def norm_back(grad, unit, inverse, gain):
    scaled = grad * gain
    return (scaled - unit * jnp.mean(scaled * unit, axis=-1, keepdims=True)) * inverse


class ByShare:
    def __init__(self, ref):
        self.ref = ref

    def tile(self, i, size):
        block = self.ref[:, i]
        return block.reshape(size, block.shape[2])


class ByTiles:
    def __init__(self, src, ref, sem, tile):
        self.ref = ref
        self.fills = [
            pltpu.make_async_copy(
                src.at[pl.ds(i * tile, tile)], ref.at[pl.ds(i * tile, tile)], sem.at[i]
            )
            for i in range(ref.shape[0] // tile)
        ]

    def tile(self, i, size):
        return self.ref[pl.ds(pl.multiple_of(i * size, size), size), :]


def product_tiles(part, slot, pairs, tile, first=False):
    def one(i, none):
        cols = pl.ds(pl.multiple_of(i * tile, tile), tile)
        total = None
        for rows, weights in pairs:
            if hasattr(weights, "tile"):
                block = weights.tile(i, tile)
            else:
                block = weights[cols, :]
            term = dot_nt(rows[slot], block)
            total = term if total is None else total + term
        part[slot, :, cols] = total.astype(bf16)
        return none

    if first:
        for i in range(part.shape[2] // tile):
            for _, weights in pairs:
                weights.fills[i].wait()
            one(i, 0)
    else:
        lax.fori_loop(0, part.shape[2] // tile, one, 0)


def summed_products(part, land, f, pairs, send_sem, recv_sem, chunks=1, beside=(), first=False):
    side, above, across = peers(f)
    rows = part.shape[1] // chunks
    rings = [
        SquareSum(
            part, land.at[c], f, send_sem.at[c], recv_sem.at[c], base=c * rows, rows=rows
        )
        for c in range(chunks)
    ]
    product_tiles(part, across, pairs, 512, first)
    for ring in rings:
        ring.start_cross()
    beside = iter(beside)
    next(beside, int)()
    product_tiles(part, side, pairs, 512)
    for ring in rings:
        ring.near[0].start()
    product_tiles(part, above, pairs, 512)
    for ring in rings:
        ring.near[1].start()
    next(beside, int)()
    rings[0].relay()
    product_tiles(part, f, pairs, 512)
    next(beside, int)()
    for ring in rings[1:]:
        ring.relay()
    return rings


def sum_then_gather(rings, finish_rows, slots, f, send_sem, recv_sem):
    gathers = []
    for c, ring in enumerate(rings):
        ring.arrive()
        by_rows(ring, finish_rows)
        gather = SquareGather(
            slots, f, send_sem.at[c], recv_sem.at[c], base=ring.base, rows=2 * ring.half
        )
        gather.start()
        gathers.append(gather)
    for ring in rings:
        ring.finish()
    return gathers


def by_rows(ring, body, step=16):
    for half in (0, 1):

        def one(i, none):
            start = pl.multiple_of(i * step, step)
            rows = pl.ds(
                pl.multiple_of(ring.base + half * ring.half + i * step, step), step
            )
            body(rows, ring.total(half, pl.ds(start, step)))
            return none

        lax.fori_loop(0, ring.half // step, one, 0)


def branch_kernel(
    att_hbm,
    w_hbm,
    tok_hbm,
    gain_ref,
    rows_hbm,
    res_hbm,
    rows_ref,
    res_ref,
    att_ref,
    w_ref,
    tok_ref,
    part,
    land,
    s_send,
    s_recv,
    g_send,
    g_recv,
    load_sem,
    store_sem,
):
    f = lax.axis_index("feat")
    loads = Loads(((att_hbm, att_ref), (w_hbm, w_ref), (tok_hbm, tok_ref)), load_sem).start()
    greet(square_targets(f))
    loads.wait()
    rings = summed_products(
        part, land, f, [(att_ref, ByShare(w_ref))], s_send, s_recv, land.shape[0]
    )

    def finish_rows(rows, total):
        residual = tok_ref[rows, :].astype(f32) + total
        res_ref[rows, :] = residual
        rows_ref[f, rows, :] = (residual * inverse_rms(residual) * gain_ref[...]).astype(bf16)

    gathers = sum_then_gather(rings, finish_rows, rows_ref, f, g_send, g_recv)
    stores = [pltpu.make_async_copy(res_ref, res_hbm, store_sem.at[0])]
    stores[0].start()

    def store(slot):
        c = pltpu.make_async_copy(rows_ref.at[slot], rows_hbm.at[slot], store_sem.at[len(stores)])
        c.start()
        stores.append(c)

    side, above, across = peers(f)
    store(f)
    for gather in gathers:
        gather.relay()
    for gather in gathers:
        gather.near()
    store(side)
    store(above)
    for gather in gathers:
        gather.far()
    store(across)
    for gather in gathers:
        gather.sent()
    for c in stores:
        c.wait()


CHUNKS = 2


def square_scratch(parts, block, width, chunks=CHUNKS):
    dma = pltpu.SemaphoreType.DMA
    return [
        pltpu.VMEM((parts, block, width), bf16),
        pltpu.VMEM((chunks, 6, block // 2 // chunks, width), bf16),
        dma((chunks, 6)),
        dma((chunks, 6)),
    ]


def branch_step(att, out_w, own, gain_two):
    parts, block, _ = att.shape
    width = own.shape[1]
    dma = pltpu.SemaphoreType.DMA
    return pl.pallas_call(
        branch_kernel,
        out_shape=(
            jax.ShapeDtypeStruct((parts, block, width), bf16),
            jax.ShapeDtypeStruct((block, width), f32),
        ),
        in_specs=in_place(3) + whole_vmem(1),
        out_specs=tuple(in_place(2)),
        scratch_shapes=[pltpu.VMEM((parts, block, width), bf16), pltpu.VMEM((block, width), f32)]
        + vmem_like(att, out_w, own)
        + square_scratch(parts, block, width)
        + [dma((CHUNKS, 6)), dma((CHUNKS, 6)), dma((3,)), dma((1 + parts,))],
        compiler_params=pltpu.CompilerParams(
            collective_id=3, has_side_effects=True, vmem_limit_bytes=60 << 20
        ),
        cost_estimate=pl.CostEstimate(flops=0, bytes_accessed=1 << 20, transcendentals=0),
        name="branch_step",
    )(att, out_w, own, gain_two)


def rows_back_kernel(
    grads_hbm,
    wg_hbm,
    wu_hbm,
    res_hbm,
    cot_hbm,
    gain_ref,
    mixed_hbm,
    wd_hbm,
    wo_hbm,
    all_hbm,
    gres_hbm,
    gsum_ref,
    down_hbm,
    ga_hbm,
    all_ref,
    gres_ref,
    down_ref,
    ga_ref,
    gg_ref,
    gu_ref,
    res_ref,
    cot_ref,
    part,
    land,
    wg,
    wu,
    mixed,
    wd,
    wo,
    s_send,
    s_recv,
    g_send,
    g_recv,
    local_sem,
    tile_sem,
    load_sem,
    store_sem,
):
    f = lax.axis_index("feat")
    rows_in = Loads(((grads_hbm.at[0], gg_ref), (grads_hbm.at[1], gu_ref)), load_sem).start()
    weights = [
        ByTiles(src, dst, tile_sem.at[i], 512)
        for i, (src, dst) in enumerate(((wg_hbm, wg), (wu_hbm, wu)))
    ]
    for pair in zip(*(w.fills for w in weights)):
        for c in pair:
            c.start()
    fills = [
        pltpu.make_async_copy(src, dst, local_sem.at[i])
        for i, (src, dst) in enumerate(((mixed_hbm, mixed), (wd_hbm, wd), (wo_hbm, wo)))
    ]
    late_in = Loads(((res_hbm, res_ref), (cot_hbm, cot_ref)), load_sem.at[pl.ds(2, 2)]).start()
    for c in fills:
        c.start()
    greet(square_targets(f))
    rows_in.wait()
    pairs = [(gg_ref, weights[0]), (gu_ref, weights[1])]

    def down_products(slots):
        for p in slots:
            product_tiles(down_ref, p, [(mixed, wd)], 512)

    rings = summed_products(part, land, f, pairs, s_send, s_recv, land.shape[0], first=True)
    gsum_ref[...] = jnp.zeros_like(gsum_ref)
    late_in.wait()

    def finish_rows(rows, grad):
        residual = res_ref[rows, :]
        inverse = inverse_rms(residual)
        unit = residual * inverse
        gsum_ref[...] += jnp.sum(grad * unit, axis=0, keepdims=True)
        grad_res = cot_ref[rows, :].astype(f32) + norm_back(grad, unit, inverse, gain_ref[...])
        gres_ref[rows, :] = grad_res
        all_ref[f, rows, :] = grad_res.astype(bf16)

    gathers = sum_then_gather(rings, finish_rows, all_ref, f, g_send, g_recv)
    side, above, across = peers(f)

    def attended_grad(slot):
        blocks = ByShare(wo)
        size = all_ref.shape[2] // wo.shape[1]
        total = None
        for i in range(wo.shape[1]):
            term = dot(all_ref[slot, :, i * size : (i + 1) * size], blocks.tile(i, size))
            total = term if total is None else total + term
        ga_ref[slot] = total
        store(ga_ref.at[slot], ga_hbm.at[slot])
        store(all_ref.at[slot], all_hbm.at[slot])

    stores = []

    def store(src, dst):
        c = pltpu.make_async_copy(src, dst, store_sem.at[len(stores)])
        c.start()
        stores.append(c)

    store(gres_ref, gres_hbm)
    for c in fills:
        c.wait()
    attended_grad(f)
    down_products(range(2))
    for gather in gathers:
        gather.relay()
    down_products(range(2, part.shape[0]))
    store(down_ref, down_hbm)
    for gather in gathers:
        gather.near()
    attended_grad(side)
    attended_grad(above)
    for gather in gathers:
        gather.far()
    attended_grad(across)
    for gather in gathers:
        gather.sent()
    for c in stores:
        c.wait()


def rows_back(
    grads, gate_w, up_w, residual, cot_own, gain_two, mixed, down_w, out_w
):
    _, parts, block, hidden = grads.shape
    width = residual.shape[1]
    dma = pltpu.SemaphoreType.DMA
    return pl.pallas_call(
        rows_back_kernel,
        out_shape=(
            jax.ShapeDtypeStruct((parts, block, width), bf16),
            jax.ShapeDtypeStruct((block, width), f32),
            jax.ShapeDtypeStruct((1, width), f32),
            jax.ShapeDtypeStruct((parts, block, width), bf16),
            jax.ShapeDtypeStruct((parts, block, out_w.shape[3]), f32),
        ),
        in_specs=in_place(5) + whole_vmem(1) + in_place(3),
        out_specs=tuple(in_place(2) + whole_vmem(1) + in_place(2)),
        scratch_shapes=[
            pltpu.VMEM((parts, block, width), bf16),
            pltpu.VMEM((block, width), f32),
            pltpu.VMEM((parts, block, width), bf16),
            pltpu.VMEM((parts, block, out_w.shape[3]), f32),
        ]
        + [pltpu.VMEM((parts, block, hidden), bf16)] * 2
        + vmem_like(residual, cot_own)
        + square_scratch(parts, block, width)[:2]
        + [
            pltpu.VMEM((width, hidden), bf16),
            pltpu.VMEM((width, hidden), bf16),
            pltpu.VMEM((parts, block, hidden), bf16),
            pltpu.VMEM((width, hidden), bf16),
            pltpu.VMEM(out_w.shape, bf16),
        ]
        + [dma((CHUNKS, 6))] * 4
        + [dma((3,)), dma((2, width // 512)), dma((4,)), dma((2 * parts + 2,))],
        compiler_params=pltpu.CompilerParams(
            collective_id=4, has_side_effects=True, vmem_limit_bytes=60 << 20
        ),
        cost_estimate=pl.CostEstimate(flops=0, bytes_accessed=1 << 20, transcendentals=0),
        name="rows_back",
    )(grads, gate_w, up_w, residual, cot_own, gain_two, mixed, down_w, out_w)


def closing_kernel(
    seqs,
    dps,
    dqkv_hbm,
    w_hbm,
    tok_hbm,
    gres_hbm,
    gain_ref,
    gsum_two_ref,
    normed_hbm,
    oacc_hbm,
    down_hbm,
    x_ref,
    tile_ref,
    query_ref,
    key_ref,
    value_ref,
    ograd_ref,
    part,
    land,
    s_send,
    s_recv,
    gsum,
    cut,
    came,
    mid,
    tail,
    c_send,
    c_recv,
    d_send,
    d_recv,
    dqkv_ref,
    w_ref,
    tok_ref,
    gres_ref,
    normed_ref,
    oacc_ref,
    load_sem,
    first_sem,
    term_ref,
    acc_ref,
    sib_land,
    sib_send,
    sib_recv,
    *sum_scratch,
):
    begin = Loads(((oacc_hbm, oacc_ref),), first_sem).start()
    loads = Loads(
        (
            (dqkv_hbm, dqkv_ref),
            (normed_hbm, normed_ref),
            (w_hbm, w_ref),
            (tok_hbm, tok_ref),
            (gres_hbm, gres_ref),
        ),
        load_sem,
    ).start()
    half = len(sum_scratch) // 2
    f, s, d = lax.axis_index("feat"), lax.axis_index("seq"), lax.axis_index("dp")
    parts = 4
    others = [lax.rem(d + k, dps) for k in range(1, dps)]
    circle = [
        (lax.rem(f + i, parts), lax.rem(s + j, seqs))
        for i in range(parts)
        for j in range(seqs)
        if i or j
    ]
    greet(
        [{"feat": a, "seq": b} for a, b in circle] + [{"dp": o} for o in others]
    )
    begin.wait()
    rows_sum = RowSum(acc_ref, *sum_scratch[:3], sum_scratch[3:half], f, s)
    out_sum = RowSum(oacc_ref, *sum_scratch[half : half + 3], sum_scratch[half + 3 :], f, s)
    out_sum.start()
    loads.wait()
    term_tiles(term_ref, normed_ref, dqkv_ref)
    sibling = SiblingSum(term_ref, acc_ref, sib_land, (sib_send, sib_recv), d, dps)
    sibling.start()

    def over_seq():
        sibling.add()
        rows_sum.start()

    rings = summed_products(
        part, land, f, [(dqkv_ref, w_ref)], s_send, s_recv, land.shape[0], (over_seq,)
    )
    gsum[...] = jnp.zeros_like(gsum)

    def finish_rows(rows, grad):
        values = tok_ref[rows, :].astype(f32)
        inverse = inverse_rms(values)
        unit = values * inverse
        gsum[...] += jnp.sum(grad * unit, axis=0, keepdims=True)
        x_ref[rows, :] = gres_ref[rows, :] + norm_back(grad, unit, inverse, gain_ref[...])

    for ring in rings:
        ring.arrive()
        by_rows(ring, finish_rows)
    for ring in rings:
        ring.finish()

    lanes = gsum.shape[1] // (parts * seqs)
    cut[...] = jnp.zeros_like(cut)
    for k in range(parts * seqs):
        cut[k, 0:1, :] = gsum[:, k * lanes : (k + 1) * lanes]
        cut[k, 1:2, :] = gsum_two_ref[:, k * lanes : (k + 1) * lanes]
    place = f * seqs + s
    sends = []
    for i, (a, b) in enumerate(circle):
        sends.append(
            push(
                cut.at[a * seqs + b],
                came.at[i],
                c_send.at[i],
                c_recv.at[i],
                {"feat": a, "seq": b},
            )
        )
    for c in sends:
        c.start()
    total = cut[place]
    for c in sends:
        c.wait_recv()
    for i in range(len(circle)):
        total = total + came[i]
    mid[...] = total
    last = [
        push(mid, tail.at[k], d_send.at[k], d_recv.at[k], {"dp": o})
        for k, o in enumerate(others)
    ]
    for c in last:
        c.start()
    for c in last:
        c.wait_recv()
    for k in range(len(others)):
        total = total + tail[k]
    tile_ref[...] = total
    out_sum.over_feat()
    rows_sum.over_feat()
    rows_sum.arrive()
    first = 0
    for ref in (query_ref, key_ref, value_ref):
        each = ref.shape[1] // parts
        for p in range(parts):
            piece = rows_sum.shares[p, :, first : first + each]
            ref[:, p * each : (p + 1) * each] = piece.astype(f32)
        first += each
    rows_sum.finish()
    sibling.finish()
    out_sum.arrive()
    each = ograd_ref.shape[1] // parts
    for p in range(parts):
        ograd_ref[:, p * each : (p + 1) * each] = out_sum.shares[p].astype(f32)
    out_sum.finish()
    for c in sends + last:
        c.wait_send()


def closing(dqkv, qkv_w, own, grad_residual, gain_one, gain_two_sum, normed, out_acc, down_grad):
    parts, seqs, dps = (lax.axis_size(a) for a in ALL)
    block, width = own.shape
    others = max(dps - 1, 1)
    lanes = width // (parts * seqs)
    circle = parts * seqs - 1
    rows_each = out_acc.shape[2]
    by_row = (parts, seqs, dps, rows_each, dqkv.shape[2])
    acc_shape = out_acc.shape[:3] + dqkv.shape[2:]
    dma = pltpu.SemaphoreType.DMA
    return pl.pallas_call(
        functools.partial(closing_kernel, seqs, dps),
        out_shape=(
            jax.ShapeDtypeStruct((block, width), f32),
            jax.ShapeDtypeStruct((8, lanes), f32),
            jax.ShapeDtypeStruct((rows_each, HEADS * FDIM), f32),
            jax.ShapeDtypeStruct((rows_each, HEADS * FDIM), f32),
            jax.ShapeDtypeStruct((rows_each, HEADS * HV), f32),
            jax.ShapeDtypeStruct((rows_each, HEADS * HV), f32),
        ),
        in_specs=in_place(4) + whole_vmem(2) + in_place(3),
        out_specs=tuple(whole_vmem(6)),
        scratch_shapes=square_scratch(parts, block, width)
        + [
            pltpu.VMEM((1, width), f32),
            pltpu.VMEM((parts * seqs, 8, lanes), f32),
            pltpu.VMEM((circle, 8, lanes), f32),
            pltpu.VMEM((8, lanes), f32),
            pltpu.VMEM((others, 8, lanes), f32),
            dma((circle,)),
            dma((circle,)),
            dma((others,)),
            dma((others,)),
        ]
        + vmem_like(dqkv, qkv_w, own, grad_residual, normed, out_acc)
        + [dma((5,)), dma((1,))]
        + sibling_scratch(by_row)
        + row_sum_scratch(acc_shape)
        + row_sum_scratch(out_acc.shape),
        compiler_params=pltpu.CompilerParams(
            collective_id=5, has_side_effects=True, vmem_limit_bytes=60 << 20
        ),
        cost_estimate=pl.CostEstimate(flops=0, bytes_accessed=1 << 20, transcendentals=0),
        name="closing",
    )(dqkv, qkv_w, own, grad_residual, gain_one, gain_two_sum, normed, out_acc, down_grad)


def local(
    tokens,
    segments,
    norm1_gain,
    norm2_gain,
    w_query,
    w_key,
    w_value,
    w_out,
    w_gate,
    w_up,
    w_down,
    cotangent,
):
    parts = lax.axis_size("feat")
    heads = HEADS // parts
    block, width = tokens.shape[2], tokens.shape[3]
    rows_total = parts * block
    rows_each = w_query.shape[0]
    own = tokens.reshape(block, width)
    cot_own = cotangent.reshape(block, width)

    x_all, qkv_w, gains, out_share = opening(
        own, w_query, w_key, w_value, w_out.T, norm1_gain[None], norm2_gain[None]
    )
    qkv_width = qkv_w.shape[1]
    gate_w = lax.all_gather(w_gate, ("seq", "dp"), axis=0, tiled=True)
    gain_one, gain_two = gains[0:1], gains[1:2]

    x_wide = x_all.astype(f32).reshape(rows_total, width)
    normed = (x_wide * inverse_rms(x_wide) * gain_one).astype(bf16)
    qkv = dot(normed, qkv_w).astype(bf16).reshape(parts, block, qkv_width)
    qkv, gate_w, out_share, w_up, w_down = lax.optimization_barrier(
        (qkv, gate_w, out_share, w_up, w_down)
    )
    out_w = lax.all_gather(out_share[None], ("seq", "dp"), axis=0, tiled=True)
    up_w = lax.all_gather(w_up, ("seq", "dp"), axis=0, tiled=True)
    down_w = lax.all_gather(w_down.T, ("seq", "dp"), axis=0, tiled=True)
    segment = segments.reshape(parts, block).astype(f32)
    segc, segr = segment[:, :, None], segment[:, None, :]
    tables = feature_tables(heads)
    att, rden, carry, csum, cot_all = attention_forward(qkv, segc, segr, tables, cot_own, heads)
    cot_all = cot_all.reshape(rows_total, width)
    rows_all, residual = branch_step(att, out_w, own, gain_two)
    rows_all = rows_all.reshape(rows_total, width)

    gate_out = dot(rows_all, gate_w)
    up_out = dot(rows_all, up_w)
    sig = jax.nn.sigmoid(gate_out)
    silu = gate_out * sig
    mixed = (silu * up_out).astype(bf16)
    down_term = dot_tn(cot_all, mixed).astype(bf16)
    mixed, cot_late, down_term = lax.optimization_barrier((mixed, cot_all, down_term))
    grad_mixed = dot(cot_late, down_w)
    grads = jnp.stack(
        [grad_mixed * up_out * sig * (1.0 + gate_out * (1.0 - sig)), grad_mixed * silu]
    ).astype(bf16)

    def summed(term, dim):
        return lax.psum_scatter(term, ("seq", "dp"), scatter_dimension=dim, tiled=True)

    both_term = jnp.einsum("xtf,td->xfd", grads, rows_all, preferred_element_type=f32).astype(bf16)
    grads, both_term = lax.optimization_barrier((grads, both_term))
    down_sum, both_sum = summed(down_term, 0), summed(both_term, 2)

    by_device = (parts, block, -1)
    branch_all, grad_residual, gain_two_sum, down, ga = rows_back(
        grads.reshape((2,) + by_device),
        gate_w,
        up_w,
        residual,
        cot_own,
        gain_two,
        mixed.reshape(by_device),
        down_w,
        out_w,
    )
    dqkv, output, out_acc = attention_backward(
        qkv,
        segc,
        segr,
        tables,
        att,
        rden,
        carry,
        csum,
        ga,
        down,
        residual,
        branch_all,
        heads,
    )
    down_grad = down_sum.T.astype(f32)
    x_grad, gain_grads, query_grad, key_grad, value_grad, out_grad = closing(
        dqkv,
        qkv_w,
        own,
        grad_residual,
        gain_one,
        gain_two_sum,
        normed.reshape(parts, block, width),
        out_acc,
        down_grad,
    )
    gain_each = gain_grads.shape[1] // lax.axis_size("dp")
    gain_grads = lax.dynamic_slice_in_dim(
        gain_grads, lax.axis_index("dp") * gain_each, gain_each, axis=1
    )
    return (
        output.reshape(tokens.shape),
        x_grad.reshape(tokens.shape),
        gain_grads[0],
        gain_grads[1],
        query_grad,
        key_grad,
        value_grad,
        out_grad.T,
        both_sum[0].T.astype(f32),
        both_sum[1].T.astype(f32),
        down_grad,
    )


def solution(mesh):
    placed = (
        P("feat", "dp", "seq", None),
        P(None, "dp", "seq"),
        P(ALL),
        P(ALL),
        P(ALL, None),
        P(ALL, None),
        P(ALL, None),
        P(None, ALL),
        P(("seq", "dp"), "feat"),
        P(("seq", "dp"), "feat"),
        P("feat", ("seq", "dp")),
        P("feat", "dp", "seq", None),
    )
    return jax.shard_map(
        local,
        mesh=mesh,
        in_specs=placed,
        out_specs=(
            P("feat", "dp", "seq", None),
            P("feat", "dp", "seq", None),
            P(ALL),
            P(ALL),
            P(ALL, None),
            P(ALL, None),
            P(ALL, None),
            P(None, ALL),
            P(("seq", "dp"), "feat"),
            P(("seq", "dp"), "feat"),
            P("feat", ("seq", "dp")),
        ),
        check_vma=False,
    )
```

```python
import functools

import jax
import jax.numpy as jnp
import numpy as np
from jax import lax
from jax.experimental import pallas as pl
from jax.experimental.pallas import tpu as pltpu
from jax.sharding import PartitionSpec as P

HEADS = 16
FDIM = 16
HV = 128
STATE = 160
LANES = 256
epsilon = 1e-05
MESH = pl.DeviceIdType.MESH
ALL = ("feat", "seq", "dp")
f32 = jnp.float32
bf16 = jnp.bfloat16


def dot(a, b):
    return lax.dot_general(a, b, (((1,), (0,)), ((), ())), preferred_element_type=f32)


def dot_nt(a, b):
    return lax.dot_general(a, b, (((1,), (1,)), ((), ())), preferred_element_type=f32)


def dot_tn(a, b):
    return lax.dot_general(a, b, (((0,), (0,)), ((), ())), preferred_element_type=f32)


def feature_tables(heads):
    pairs = [(i, j) for i in range(FDIM) for j in range(i, FDIM)]
    left = np.zeros((heads, heads * FDIM, LANES), np.float32)
    right = np.zeros((heads, heads * FDIM, LANES), np.float32)
    rows = np.zeros((8, LANES), np.float32)
    for h in range(heads):
        for p, (i, j) in enumerate(pairs):
            left[h, h * FDIM + i, p] = 1.0
            right[h, h * FDIM + j, p] = 1.0
            rows[2, p] = 0.25 / 2.0**0.5 if i == j else 0.25
        for i in range(FDIM):
            p = len(pairs) + i
            left[h, h * FDIM + i, p] = 1.0
            rows[1, p] = 1.0
            rows[2, p] = 0.5
        p = len(pairs) + FDIM
        rows[0, p] = rows[1, p] = rows[2, p] = 1.0
    return jnp.asarray(left, bf16), jnp.asarray(right, bf16), jnp.asarray(rows)


def both_sides(entries, h, left_ref, right_ref, rows_ref):
    one = dot(entries, left_ref[h]) + rows_ref[0:1, :]
    two = dot(entries, right_ref[h]) + rows_ref[1:2, :]
    return one, two * rows_ref[2:3, :]


def features(entries, h, left_ref, right_ref, rows_ref):
    one, two = both_sides(entries, h, left_ref, right_ref, rows_ref)
    return one * two


def pull_features(grad, entries, h, left_ref, right_ref, rows_ref):
    one, two = both_sides(entries, h, left_ref, right_ref, rows_ref)
    scaled = rows_ref[2:3, :]
    return dot_nt((grad * two).astype(bf16), left_ref[h]) + dot_nt(
        (grad * one * scaled).astype(bf16), right_ref[h]
    )


def only_head(entries, h):
    lane = lax.broadcasted_iota(jnp.int32, entries.shape, 1)
    keep = (lane >= h * FDIM) & (lane < (h + 1) * FDIM)
    return jnp.where(keep, entries, jnp.zeros_like(entries))


def padded_state(state):
    return jnp.concatenate([state, jnp.zeros((LANES - STATE, state.shape[1]), state.dtype)], 0)


def allowed_of(segc, segr):
    block = segc.shape[0]
    row = lax.broadcasted_iota(jnp.int32, (block, block), 0)
    col = lax.broadcasted_iota(jnp.int32, (block, block), 1)
    return (row >= col) & (segc == segr)


def forward_kernel(
    count,
    heads,
    qkv_ref,
    segc_ref,
    segr_ref,
    left_ref,
    right_ref,
    rows_ref,
    cot_ref,
    att_hbm,
    rden_hbm,
    carry_hbm,
    csum_hbm,
    cots_ref,
    att_ref,
    rden_ref,
    carry_ref,
    csum_ref,
    send_state,
    send_sum,
    part,
    send_sem,
    recv_sem,
    f_send,
    f_recv,
    local_sem,
    store_sem,
):
    place, f = lax.axis_index("seq"), lax.axis_index("feat")
    groups, block = qkv_ref.shape[0], qkv_ref.shape[1]
    width = heads * FDIM
    tables = (left_ref, right_ref, rows_ref)

    def stores(g):
        pairs = (
            (att_ref, att_hbm),
            (rden_ref, rden_hbm),
            (carry_ref, carry_hbm),
            (csum_ref, csum_hbm),
        )
        return Loads([(a.at[g], b.at[g]) for a, b in pairs], store_sem.at[g])

    def hop(g):
        target = {"seq": lax.rem(place + 1, count)}
        return [
            pltpu.make_async_remote_copy(
                src_ref=src.at[g],
                dst_ref=dst.at[g],
                send_sem=send_sem.at[i, g],
                recv_sem=recv_sem.at[i, g],
                device_id=target,
                device_id_type=MESH,
            )
            for i, (src, dst) in enumerate(((send_state, carry_ref), (send_sum, csum_ref)))
        ]

    def send(g):
        for copy in hop(g):
            copy.start()

    chain = [lax.rem(place + 1, count), lax.rem(place + count - 1, count)]
    stay = pltpu.make_async_copy(cot_ref, cots_ref.at[f], local_sem.at[0])
    stay.start()
    greet(square_targets(f) + [{"seq": c} for c in chain])
    gather = SquareGather(cots_ref, f, f_send, f_recv, cot_ref)
    gather.start()

    @pl.when(place == 0)
    def _():
        carry_ref[...] = jnp.zeros_like(carry_ref)
        csum_ref[...] = jnp.full_like(csum_ref, -1.0)

    def summarize(g, none):
        segc, segr = segc_ref[g], segr_ref[g]
        tail = segr[:, block - 1 : block]
        at_tail = (segc == tail).astype(f32)
        send_sum[g, heads : heads + 1, :] = jnp.broadcast_to(tail, (1, LANES))
        for h in range(heads):
            key = qkv_ref[g, :, width : 2 * width]
            value = qkv_ref[g, :, 2 * width + h * HV : 2 * width + (h + 1) * HV]
            phi = (features(key, h, *tables) * at_tail).astype(bf16)
            send_state[g, h] = dot_tn(phi, value)[:STATE].astype(bf16)
            ones = jnp.ones((8, block), bf16)
            send_sum[g, h : h + 1, :] = dot(ones, phi)[0:1]

        @pl.when(place == 0)
        def _():
            send(g)

        return none

    lax.fori_loop(0, groups, summarize, 0)
    def join(g, none):
        for copy in hop(g):
            copy.wait_recv()
        segr = segr_ref[g]
        mark = csum_ref[g, heads : heads + 1, 0:1]
        head, tail = segr[:, 0:1], segr[:, block - 1 : block]
        whole = ((head == tail) & (head == mark)).astype(f32)
        for h in range(heads):
            send_state[g, h] = (
                send_state[g, h].astype(f32) + whole * carry_ref[g, h].astype(f32)
            ).astype(bf16)
            send_sum[g, h : h + 1, :] = (
                send_sum[g, h : h + 1, :] + whole * csum_ref[g, h : h + 1, :]
            )
        send(g)
        return none

    def attend(g, none):
        segc, segr = segc_ref[g], segr_ref[g]
        allowed = allowed_of(segc, segr)
        for h in range(heads):
            query = only_head(qkv_ref[g, :, 0:width], h)
            key = qkv_ref[g, :, width : 2 * width]
            value = qkv_ref[g, :, 2 * width + h * HV : 2 * width + (h + 1) * HV]
            c = dot_nt(query, key)
            kernel = jnp.where(allowed, 1.0 + c * (0.25 + c * 0.03125), 0.0).astype(bf16)
            wide = jnp.concatenate([value, jnp.ones_like(value)], axis=1)
            part[g, h] = dot(kernel, wide)

        @pl.when((place > 0) & (place < count - 1) & (g == place - 1))
        def _():
            lax.fori_loop(0, groups, join, 0)

        return none

    lax.fori_loop(0, groups, attend, 0)
    gather.relay()

    def carry_on(g, none):
        segc = segc_ref[g]

        @pl.when(place == count - 1)
        def _():
            for copy in hop(g):
                copy.wait_recv()

        mark = csum_ref[g, heads : heads + 1, 0:1]
        carried = (segc == mark).astype(f32)
        for h in range(heads):
            phi = features(qkv_ref[g, :, 0:width], h, *tables) * carried
            state = padded_state(carry_ref[g, h])
            both = part[g, h]
            numer = both[:, :HV] + dot(phi.astype(bf16), state)
            denom = both[:, HV:] + jnp.sum(
                phi * csum_ref[g, h : h + 1, :], axis=1, keepdims=True
            )
            inverse = 1.0 / denom
            att_ref[g, :, h * HV : (h + 1) * HV] = (numer * inverse).astype(bf16)
            rden_ref[g, :, h * HV : (h + 1) * HV] = inverse
        stores(g).start()
        return none

    lax.fori_loop(0, groups, carry_on, 0)

    @pl.when(place < count - 1)
    def _():
        def finish(g, none):
            for copy in hop(g):
                copy.wait_send()
            return none

        lax.fori_loop(0, groups, finish, 0)

    stay.wait()
    gather.finish()

    def stored(g, none):
        stores(g).wait()
        return none

    lax.fori_loop(0, groups, stored, 0)


def backward_kernel(
    count,
    heads,
    qkv_hbm,
    segc_ref,
    segr_ref,
    left_ref,
    right_ref,
    rows_ref,
    att_hbm,
    rden_hbm,
    carry_hbm,
    csum_ref,
    ga_hbm,
    down_ref,
    res_hbm,
    branch_hbm,
    out_hbm,
    final_ref,
    acc_hbm,
    qkv_ref,
    att_ref,
    rden_ref,
    carry_ref,
    ga_ref,
    res_ref,
    branch_ref,
    out_ref,
    gn,
    send_state,
    send_sum,
    recv_state,
    recv_sum,
    dkey,
    dvalue,
    terms,
    land,
    send_sem,
    recv_sem,
    f_send,
    f_recv,
    local_sem,
    load_sem,
    store_sem,
    term_ref,
    acc_ref,
    sib_land,
    sib_send,
    sib_recv,
):
    place, f, d = lax.axis_index("seq"), lax.axis_index("feat"), lax.axis_index("dp")
    dps = term_ref.shape[2]
    loads = Loads(
        (
            (qkv_hbm, qkv_ref),
            (ga_hbm, ga_ref),
            (rden_hbm, rden_ref),
            (att_hbm, att_ref),
            (carry_hbm, carry_ref),
            (res_hbm, res_ref),
        ),
        load_sem,
    ).start()
    late = Loads(((branch_hbm, branch_ref),), load_sem.at[pl.ds(6, 1)]).start()
    groups, block = qkv_ref.shape[0], qkv_ref.shape[1]
    width = heads * FDIM
    tables = (left_ref, right_ref, rows_ref)

    def hop(g):
        target = {"seq": lax.rem(place + count - 1, count)}
        return [
            pltpu.make_async_remote_copy(
                src_ref=src.at[g],
                dst_ref=dst.at[g],
                send_sem=send_sem.at[i, g],
                recv_sem=recv_sem.at[i, g],
                device_id=target,
                device_id_type=MESH,
            )
            for i, (src, dst) in enumerate(((send_state, recv_state), (send_sum, recv_sum)))
        ]

    def send(g):
        for copy in hop(g):
            copy.start()

    chain = [lax.rem(place + 1, count), lax.rem(place + count - 1, count)]
    greet(
        square_targets(f)
        + [{"seq": c} for c in chain]
        + [{"dp": lax.rem(d + o, dps)} for o in range(1, dps)]
    )
    fill = pltpu.make_async_copy(down_ref, terms, local_sem.at[0])
    fill.start()
    ring = SquareSum(terms, land, f, f_send, f_recv)
    loads.wait()

    def store(g):
        return pltpu.make_async_copy(out_ref.at[g], out_hbm.at[g], store_sem.at[g])


    @pl.when(place == count - 1)
    def _():
        recv_state[...] = jnp.zeros_like(recv_state)
        recv_sum[...] = jnp.full_like(recv_sum, -1.0)

    def summarize(g, none):
        segc, segr = segc_ref[g], segr_ref[g]
        head = segr[:, 0:1]
        at_head = (segc == head).astype(f32)
        send_sum[g, heads : heads + 1, :] = jnp.broadcast_to(head, (1, LANES))
        for h in range(heads):
            lanes = slice(h * HV, (h + 1) * HV)
            ga = ga_ref[g, :, lanes]
            inverse = rden_ref[g, :, lanes]
            numer = (ga * inverse).astype(bf16)
            dots = jnp.sum(ga * att_ref[g, :, lanes].astype(f32), axis=1, keepdims=True)
            lane = lax.broadcasted_iota(jnp.int32, (block, HV), 1)
            denom = jnp.where(lane == 0, -dots * inverse, 0.0).astype(bf16)
            gn[g, h, :, :HV] = numer
            gn[g, h, :, HV:] = denom
            phi = (features(qkv_ref[g, :, 0:width], h, *tables) * at_head).astype(bf16)
            send_state[g, h] = dot_tn(phi, numer)[:STATE].astype(bf16)
            send_sum[g, h : h + 1, :] = dot_tn(denom, phi)[0:1]

        @pl.when(place == count - 1)
        def _():
            send(g)

        return none

    lax.fori_loop(0, groups, summarize, 0)
    fill.wait()
    ring.start_cross()
    ring.start_near()

    def join(g, none):
        for copy in hop(g):
            copy.wait_recv()
        segr = segr_ref[g]
        mark = recv_sum[g, heads : heads + 1, 0:1]
        head, tail = segr[:, 0:1], segr[:, block - 1 : block]
        whole = ((head == tail) & (head == mark)).astype(f32)
        for h in range(heads):
            send_state[g, h] = (
                send_state[g, h].astype(f32) + whole * recv_state[g, h].astype(f32)
            ).astype(bf16)
            send_sum[g, h : h + 1, :] = (
                send_sum[g, h : h + 1, :] + whole * recv_sum[g, h : h + 1, :]
            )
        send(g)
        return none

    def pull(g, none):
        segc, segr = segc_ref[g], segr_ref[g]
        allowed = allowed_of(segc, segr)
        query_all = qkv_ref[g, :, 0:width]
        key_all = qkv_ref[g, :, width : 2 * width]
        carried = (segc == csum_ref[g, heads : heads + 1, 0:1]).astype(f32)
        dquery = jnp.zeros((block, width), f32)
        dkey_sum = jnp.zeros((block, width), f32)
        for h in range(heads):
            query, key = only_head(query_all, h), only_head(key_all, h)
            value = qkv_ref[g, :, 2 * width + h * HV : 2 * width + (h + 1) * HV]
            wide = jnp.concatenate([value, jnp.ones_like(value)], axis=1)
            both = gn[g, h]
            c = dot_nt(query, key_all)
            kernel = jnp.where(allowed, 1.0 + c * (0.25 + c * 0.03125), 0.0).astype(bf16)
            grad = jnp.where(allowed, dot_nt(both, wide), 0.0)
            grad_c = (grad * (0.25 + c * 0.0625)).astype(bf16)
            dvalue[g, h] = dot_tn(kernel, both[:, :HV])
            dkey_sum = dkey_sum + dot_tn(grad_c, query)
            dquery = dquery + dot(grad_c, key)
            state = padded_state(carry_ref[g, h])
            gphi = dot_nt(both[:, :HV], state) + both[:, HV : HV + 1].astype(f32) * csum_ref[
                g, h : h + 1, :
            ]
            dquery = dquery + pull_features(gphi * carried, query_all, h, *tables)
        out_ref[g, :, 0:width] = dquery.astype(bf16)
        dkey[g] = dkey_sum

        @pl.when((place > 0) & (place < count - 1) & (g == count - 2 - place))
        def _():
            lax.fori_loop(0, groups, join, 0)

        return none

    lax.fori_loop(0, groups, pull, 0)
    ring.relay()
    late.wait()
    term_tiles(term_ref, branch_ref, att_ref)
    sibling = SiblingSum(term_ref, acc_ref, sib_land, (sib_send, sib_recv), d, dps)
    sibling.start()

    def carry_back(g, none):
        segc = segc_ref[g]
        key_all = qkv_ref[g, :, width : 2 * width]

        @pl.when(place == 0)
        def _():
            for copy in hop(g):
                copy.wait_recv()

        mark = recv_sum[g, heads : heads + 1, 0:1]
        later = (segc == mark).astype(f32)
        total = dkey[g]
        for h in range(heads):
            value = qkv_ref[g, :, 2 * width + h * HV : 2 * width + (h + 1) * HV]
            state = padded_state(recv_state[g, h])
            phi = (features(key_all, h, *tables) * later).astype(bf16)
            dv = dvalue[g, h] + dot(phi, state)
            out_ref[g, :, 2 * width + h * HV : 2 * width + (h + 1) * HV] = dv.astype(bf16)
            gphi = (dot_nt(value, state) + recv_sum[g, h : h + 1, :]) * later
            total = total + pull_features(gphi, key_all, h, *tables)
        out_ref[g, :, width : 2 * width] = total.astype(bf16)
        store(g).start()
        return none

    lax.fori_loop(0, groups, carry_back, 0)

    @pl.when(place > 0)
    def _():
        def finish(g, none):
            for copy in hop(g):
                copy.wait_send()
            return none

        lax.fori_loop(0, groups, finish, 0)

    ring.arrive()

    def add_up(rows, total):
        final_ref[rows, :] = (res_ref[rows, :] + total).astype(bf16)

    by_rows(ring, add_up)
    ring.finish()
    sibling.add()
    keep = pltpu.make_async_copy(acc_ref, acc_hbm, store_sem.at[groups])
    keep.start()

    def stored(g, none):
        store(g).wait()
        return none

    lax.fori_loop(0, groups, stored, 0)
    sibling.finish()
    keep.wait()


def term_tiles(term, left, right):
    parts, *shape = term.shape
    tile = left.shape[2] // parts

    def one(i, none):
        cols = pl.ds(pl.multiple_of(i * tile, tile), tile)
        total = dot_tn(left[0, :, cols], right[0])
        for g in range(1, left.shape[0]):
            total = total + dot_tn(left[g, :, cols], right[g])
        term[i] = total.astype(bf16).reshape(shape)
        return none

    lax.fori_loop(0, parts, one, 0)


def whole_vmem(count):
    return [pl.BlockSpec(memory_space=pltpu.VMEM)] * count


def attention_forward(qkv, segc, segr, tables, cot_own, heads):
    groups, block, _ = qkv.shape
    count = lax.axis_size("seq")
    dma = pltpu.SemaphoreType.DMA
    states = (groups, heads, STATE, HV)
    sums = (groups, 8, LANES)
    return pl.pallas_call(
        functools.partial(forward_kernel, count, heads),
        out_shape=(
            jax.ShapeDtypeStruct((groups, block, heads * HV), bf16),
            jax.ShapeDtypeStruct((groups, block, heads * HV), f32),
            jax.ShapeDtypeStruct(states, bf16),
            jax.ShapeDtypeStruct(sums, f32),
            jax.ShapeDtypeStruct((groups,) + cot_own.shape, bf16),
        ),
        in_specs=whole_vmem(6) + in_place(1),
        out_specs=tuple(in_place(5)),
        scratch_shapes=[
            pltpu.VMEM((groups, block, heads * HV), bf16),
            pltpu.VMEM((groups, block, heads * HV), f32),
            pltpu.VMEM(states, bf16),
            pltpu.VMEM(sums, f32),
            pltpu.VMEM(states, bf16),
            pltpu.VMEM(sums, f32),
            pltpu.VMEM((groups, heads, block, 2 * HV), f32),
            dma((2, groups)),
            dma((2, groups)),
            dma((6,)),
            dma((6,)),
            dma((1,)),
            dma((groups, 4)),
        ],
        compiler_params=pltpu.CompilerParams(
            collective_id=0, has_side_effects=True, vmem_limit_bytes=60 << 20
        ),
        cost_estimate=pl.CostEstimate(flops=0, bytes_accessed=1 << 20, transcendentals=0),
        name="attention_forward",
    )(qkv, segc, segr, *tables, cot_own)


def attention_backward(
    qkv, segc, segr, tables, att, rden, carry, csum, ga, down, residual, branch, heads
):
    groups, block, wide = qkv.shape
    count = lax.axis_size("seq")
    parts, dps = lax.axis_size("feat"), lax.axis_size("dp")
    rows_each = branch.shape[2] // (parts * count * dps)
    by_row = (parts, count, dps, rows_each, heads * HV)
    states = (groups, heads, STATE, HV)
    sums = (groups, 8, LANES)
    return pl.pallas_call(
        functools.partial(backward_kernel, count, heads),
        out_shape=(
            jax.ShapeDtypeStruct((groups, block, wide), bf16),
            jax.ShapeDtypeStruct(residual.shape, bf16),
            jax.ShapeDtypeStruct((count, by_row[0]) + by_row[3:], bf16),
        ),
        in_specs=in_place(1)
        + whole_vmem(5)
        + in_place(3)
        + whole_vmem(1)
        + in_place(4),
        out_specs=tuple(in_place(1) + whole_vmem(1) + in_place(1)),
        scratch_shapes=vmem_like(qkv, att, rden, carry, ga, residual, branch)
        + [
            pltpu.VMEM((groups, block, wide), bf16),
            pltpu.VMEM((groups, heads, block, 2 * HV), bf16),
            pltpu.VMEM(states, bf16),
            pltpu.VMEM(sums, f32),
            pltpu.VMEM(states, bf16),
            pltpu.VMEM(sums, f32),
            pltpu.VMEM((groups, block, heads * FDIM), f32),
            pltpu.VMEM((groups, heads, block, HV), f32),
            pltpu.VMEM((groups,) + residual.shape, bf16),
            pltpu.VMEM((6, block // 2, residual.shape[1]), bf16),
            pltpu.SemaphoreType.DMA((2, groups)),
            pltpu.SemaphoreType.DMA((2, groups)),
            pltpu.SemaphoreType.DMA((6,)),
            pltpu.SemaphoreType.DMA((6,)),
            pltpu.SemaphoreType.DMA((1,)),
            pltpu.SemaphoreType.DMA((7,)),
            pltpu.SemaphoreType.DMA((groups + 1,)),
        ]
        + sibling_scratch(by_row),
        compiler_params=pltpu.CompilerParams(
            collective_id=1, has_side_effects=True, vmem_limit_bytes=60 << 20
        ),
        cost_estimate=pl.CostEstimate(flops=0, bytes_accessed=1 << 20, transcendentals=0),
        name="attention_backward",
    )(qkv, segc, segr, *tables, att, rden, carry, csum, ga, down, residual, branch)


def peers(f):
    return 2 * (f // 2) + 1 - f % 2, (f + 2) % 4, 3 - f


def greet(targets):
    barrier = pltpu.get_barrier_semaphore()
    for target in targets:
        pl.semaphore_signal(barrier, inc=1, device_id=target, device_id_type=MESH)
    pl.semaphore_wait(barrier, len(targets))


def push(src, dst, send_sem, recv_sem, target):
    return pltpu.make_async_remote_copy(
        src_ref=src,
        dst_ref=dst,
        send_sem=send_sem,
        recv_sem=recv_sem,
        device_id=target,
        device_id_type=MESH,
    )


def square_targets(f):
    return [{"feat": p} for p in peers(f)]


class Loads:
    def __init__(self, pairs, sem):
        self.copies = [pltpu.make_async_copy(a, b, sem.at[i]) for i, (a, b) in enumerate(pairs)]

    def start(self):
        for c in self.copies:
            c.start()
        return self

    def wait(self):
        for c in self.copies:
            c.wait()


def vmem_like(*arrays):
    return [pltpu.VMEM(a.shape, a.dtype) for a in arrays]


class SquareGather:
    def __init__(self, slots, f, send_sem, recv_sem, own=None, base=0, rows=None):
        side, above, across = peers(f)
        half = (slots.shape[1] if rows is None else rows) // 2
        first, second = pl.ds(base, half), pl.ds(base + half, half)

        def copy(i, slot, rows, to):
            ref = slots.at[slot, rows]
            src = ref if own is None or i > 3 else own.at[rows]
            return push(src, ref, send_sem.at[i], recv_sem.at[i], {"feat": to})

        self.direct = [
            copy(0, f, first, side),
            copy(1, f, second, above),
            copy(2, f, second, side),
            copy(3, f, first, above),
        ]
        self.forward = [copy(4, side, first, above), copy(5, above, second, side)]

    def start(self):
        for c in self.direct:
            c.start()

    def relay(self):
        self.direct[0].wait_recv()
        self.forward[0].start()
        self.direct[1].wait_recv()
        self.forward[1].start()

    def near(self):
        self.direct[2].wait_recv()
        self.direct[3].wait_recv()

    def far(self):
        for c in self.forward:
            c.wait_recv()

    def sent(self):
        for c in self.direct + self.forward:
            c.wait_send()

    def finish(self):
        self.near()
        self.far()
        self.sent()


class SquareSum:
    def __init__(self, part, land, f, send_sem, recv_sem, base=0, rows=None):
        self.side, self.above, self.across = peers(f)
        self.f, self.part, self.land, self.base = f, part, land, base
        self.half = (part.shape[1] if rows is None else rows) // 2
        first, second = pl.ds(base, self.half), pl.ds(base + self.half, self.half)

        def copy(i, slot, rows, to):
            return push(
                part.at[slot, rows], land.at[i], send_sem.at[i], recv_sem.at[i], {"feat": to}
            )

        self.cross = [copy(0, self.across, first, self.side), copy(1, self.across, second, self.above)]
        self.near = [copy(2, self.side, first, self.side), copy(3, self.above, second, self.above)]
        self.late = [copy(4, self.above, first, self.above), copy(5, self.side, second, self.side)]

    def start_cross(self):
        for c in self.cross:
            c.start()

    def add_rows(self, slot, base, landed):
        step = 16

        def one(i, none):
            rows = pl.ds(pl.multiple_of(base + i * step, step), step)
            came = self.land[landed, pl.ds(pl.multiple_of(i * step, step), step), :]
            self.part[slot, rows, :] = (
                self.part[slot, rows, :].astype(f32) + came.astype(f32)
            ).astype(bf16)
            return none

        lax.fori_loop(0, self.half // step, one, 0)

    def start_near(self):
        for c in self.near:
            c.start()

    def relay(self):
        self.cross[0].wait_recv()
        self.add_rows(self.above, self.base, 0)
        self.late[0].start()
        self.cross[1].wait_recv()
        self.add_rows(self.side, self.base + self.half, 1)
        self.late[1].start()

    def arrive(self):
        for c in self.near + self.late:
            c.wait_recv()

    def total(self, half, rows):
        base = self.base + half * self.half
        own = self.part[self.f, pl.ds(pl.multiple_of(base + rows.start, 16), rows.size), :]
        near = self.land[2 + half, rows, :]
        late = self.land[4 + half, rows, :]
        return own.astype(f32) + near.astype(f32) + late.astype(f32)

    def finish(self):
        for c in self.cross + self.near + self.late:
            c.wait_send()


class SiblingSum:
    def __init__(self, term, acc, land, sems, d, dps):
        self.term, self.acc, self.land, self.d = term, acc, land, d
        others = [lax.rem(d + k, dps) for k in range(1, dps)]
        self.copies = [
            push(term.at[:, :, o], land.at[k], sems[0].at[k], sems[1].at[k], {"dp": o})
            for k, o in enumerate(others)
        ]

    def start(self):
        for c in self.copies:
            c.start()

    def add(self):
        for c in self.copies:
            c.wait_recv()
        seqs, parts = self.acc.shape[:2]

        def one(i, none):
            p, c = i // seqs, lax.rem(i, seqs)
            total = self.term[p, c, self.d].astype(f32)
            for k in range(len(self.copies)):
                total = total + self.land[k, p, c].astype(f32)
            self.acc[c, p] = total.astype(bf16)
            return none

        lax.fori_loop(0, parts * seqs, one, 0)

    def finish(self):
        for c in self.copies:
            c.wait_send()


class RowSum:
    def __init__(self, acc, shares, land, total, sems, f, s):
        self.acc, self.shares, self.land, self.total = acc, shares, land, total
        self.f, self.s = f, s
        self.seqs, self.parts = seqs, parts = acc.shape[:2]
        to = (lax.rem(s + 1, seqs), lax.rem(s + seqs - 1, seqs))
        z_send, z_recv, a_send, a_recv = sems
        self.blocks, self.sends, self.comes, self.two = [], [], [], []
        for t in range(1, seqs):
            blocks = (lax.rem(s + seqs - t, seqs), lax.rem(s + t, seqs))
            self.blocks.append(blocks)
            self.sends.append((s < t, s > seqs - 1 - t))
            self.comes.append(((s > 0) & (s - 1 < t), (s < seqs - 1) & (s + 1 > seqs - 1 - t)))
            self.two.append(
                [
                    push(
                        acc.at[blocks[i]],
                        land.at[t - 1, i],
                        z_send.at[t - 1, i],
                        z_recv.at[t - 1, i],
                        {"seq": to[i]},
                    )
                    for i in range(2)
                ]
            )
        self.three = [
            push(total.at[p], shares.at[f], a_send.at[i], a_recv.at[i], {"feat": p})
            for i, p in enumerate(peers(f))
        ]

    def add(self, into, t, i):
        @pl.when(self.comes[t - 1][i])
        def _():
            self.two[t - 1][i].wait_recv()

            def one(p, none):
                into[p] = (
                    into[p].astype(f32) + self.land[t - 1, i, p].astype(f32)
                ).astype(bf16)
                return none

            lax.fori_loop(0, self.parts, one, 0)

    def step(self, t):
        for i in range(2):
            if t > 1:
                self.add(self.acc.at[self.blocks[t - 1][i]], t - 1, i)
            pl.when(self.sends[t - 1][i])(self.two[t - 1][i].start)

    def over_feat(self):
        self.total[...] = self.acc[self.s]
        for i in range(2):
            self.add(self.total, self.seqs - 1, i)
        self.shares[self.f] = self.total[self.f]
        for c in self.three:
            c.start()

    def arrive(self):
        for c in self.three:
            c.wait_recv()

    def finish(self):
        for sends, copies in zip(self.sends, self.two):
            for i in range(2):
                pl.when(sends[i])(copies[i].wait_send)
        for c in self.three:
            c.wait_send()


def sibling_scratch(shape):
    parts, seqs, dps, rows, wide = shape
    others = max(dps - 1, 1)
    dma = pltpu.SemaphoreType.DMA
    return [
        pltpu.VMEM(shape, bf16),
        pltpu.VMEM((seqs, parts, rows, wide), bf16),
        pltpu.VMEM((others, parts, seqs, rows, wide), bf16),
        dma((others,)),
        dma((others,)),
    ]


def row_sum_scratch(shape):
    seqs, parts, rows, wide = shape
    dma = pltpu.SemaphoreType.DMA
    return [
        pltpu.VMEM((parts, rows, wide), bf16),
        pltpu.VMEM((seqs - 1, 2, parts, rows, wide), bf16),
        pltpu.VMEM((parts, rows, wide), bf16),
        dma((seqs - 1, 2)),
        dma((seqs - 1, 2)),
        dma((3,)),
        dma((3,)),
    ]


def opening_kernel(
    seqs,
    dps,
    tok_ref,
    query_ref,
    key_ref,
    value_ref,
    out_ref,
    one_ref,
    two_ref,
    x_ref,
    w_ref,
    g_ref,
    o_ref,
    pack,
    opack,
    tile,
    x_send,
    x_recv,
    a_send,
    a_recv,
    z_send,
    z_recv,
    d_send,
    d_recv,
    local_sem,
):
    f, s, d = lax.axis_index("feat"), lax.axis_index("seq"), lax.axis_index("dp")
    parts, rows_each = pack.shape[0], pack.shape[1]
    near = peers(f)
    columns = [lax.rem(s + k, seqs) for k in range(1, seqs)]
    others = [lax.rem(d + k, dps) for k in range(1, dps)]
    stay = pltpu.make_async_copy(tok_ref, x_ref.at[f], local_sem.at[0])
    stay.start()
    first = 0
    for ref in (query_ref, key_ref, value_ref):
        each = ref.shape[1] // parts
        for p in range(parts):
            pack[p, :, first : first + each] = ref[:, p * each : (p + 1) * each]
        first += each
    tile[...] = jnp.zeros_like(tile)
    tile[0:1, :rows_each] = one_ref[...].astype(f32)
    tile[1:2, :rows_each] = two_ref[...].astype(f32)
    outs = (w_ref, g_ref)
    own = [
        pltpu.make_async_copy(pack.at[f], w_ref.at[f, s, d], local_sem.at[1]),
        pltpu.make_async_copy(tile, g_ref.at[f, s, d], local_sem.at[2]),
    ]
    for c in own:
        c.start()
    greet(
        square_targets(f) + [{"seq": c} for c in columns] + [{"dp": o} for o in others]
    )
    shares = [
        [
            push(pack.at[p], w_ref.at[f, s, d], a_send.at[0, i], a_recv.at[0, i], {"feat": p}),
            push(tile, g_ref.at[f, s, d], a_send.at[1, i], a_recv.at[1, i], {"feat": p}),
        ]
        for i, p in enumerate(near)
    ]
    for pair in shares:
        for c in pair:
            c.start()
    gather = SquareGather(x_ref, f, x_send, x_recv, tok_ref)
    gather.start()
    each = out_ref.shape[1] // parts
    for p in range(parts):
        opack[p] = out_ref[:, p * each : (p + 1) * each]
    own_out = pltpu.make_async_copy(opack.at[f], o_ref.at[f], local_sem.at[3])
    own_out.start()
    out_shares = [
        push(opack.at[p], o_ref.at[f], a_send.at[2, i], a_recv.at[2, i], {"feat": p})
        for i, p in enumerate(near)
    ]
    for c in out_shares:
        c.start()
    for c in own:
        c.wait()

    chunks = (f,) + near

    def to_column(n, k):
        return [
            push(
                ref.at[chunks[n], s, d],
                ref.at[chunks[n], s, d],
                z_send.at[j, k - 1, n],
                z_recv.at[j, k - 1, n],
                {"seq": columns[k - 1]},
            )
            for j, ref in enumerate(outs)
        ]

    def to_sibling(n, k):
        back = lax.rem(s + seqs - k, seqs)
        return [
            push(
                ref.at[chunks[n], back, d],
                ref.at[chunks[n], back, d],
                d_send.at[j, o, k, n],
                d_recv.at[j, o, k, n],
                {"dp": other},
            )
            for j, ref in enumerate(outs)
            for o, other in enumerate(others)
        ]

    def start_all(copies):
        for c in copies:
            c.start()

    for n in range(parts):
        if n:
            for c in shares[n - 1]:
                c.wait_recv()
        for k in range(1, seqs):
            start_all(to_column(n, k))
        start_all(to_sibling(n, 0))
    for n in range(parts):
        for k in range(1, seqs):
            for c in to_column(n, k):
                c.wait_recv()
            start_all(to_sibling(n, k))
    gather.relay()
    for n in range(parts):
        for k in range(seqs):
            for c in to_sibling(n, k):
                c.wait_recv()
    for n in range(parts):
        for k in range(seqs):
            for c in to_sibling(n, k):
                c.wait_send()
        for k in range(1, seqs):
            for c in to_column(n, k):
                c.wait_send()
    for pair in shares:
        for c in pair:
            c.wait_send()
    stay.wait()
    own_out.wait()
    for c in out_shares:
        c.wait_recv()
    for c in out_shares:
        c.wait_send()
    gather.finish()


def in_place(count):
    return [pl.BlockSpec(memory_space=pltpu.HBM)] * count


def opening(own, w_query, w_key, w_value, w_out, gain_one, gain_two):
    parts, seqs, dps = (lax.axis_size(a) for a in ALL)
    block, width = own.shape
    rows_each = w_query.shape[0]
    wide = (w_query.shape[1] + w_key.shape[1] + w_value.shape[1]) // parts
    others = max(dps - 1, 1)
    dma = pltpu.SemaphoreType.DMA
    out_wide = w_out.shape[1] // parts
    x_all, w_all, g_all, o_own = pl.pallas_call(
        functools.partial(opening_kernel, seqs, dps),
        out_shape=(
            jax.ShapeDtypeStruct((parts, block, width), bf16),
            jax.ShapeDtypeStruct((parts, seqs, dps, rows_each, wide), bf16),
            jax.ShapeDtypeStruct((parts, seqs, dps, 8, HV), f32),
            jax.ShapeDtypeStruct((parts, rows_each, out_wide), bf16),
        ),
        in_specs=in_place(1) + whole_vmem(6),
        out_specs=tuple(in_place(4)),
        scratch_shapes=[
            pltpu.VMEM((parts, rows_each, wide), bf16),
            pltpu.VMEM((parts, rows_each, out_wide), bf16),
            pltpu.VMEM((8, HV), f32),
            dma((6,)),
            dma((6,)),
            dma((3, 3)),
            dma((3, 3)),
            dma((2, seqs - 1, parts)),
            dma((2, seqs - 1, parts)),
            dma((2, others, seqs, parts)),
            dma((2, others, seqs, parts)),
            dma((4,)),
        ],
        compiler_params=pltpu.CompilerParams(collective_id=2, has_side_effects=True, vmem_limit_bytes=60 << 20),
        cost_estimate=pl.CostEstimate(flops=0, bytes_accessed=1 << 20, transcendentals=0),
        name="opening",
    )(own, w_query, w_key, w_value, w_out, gain_one, gain_two)
    gains = g_all[..., :2, :rows_each].transpose(3, 0, 1, 2, 4).reshape(2, width)
    return x_all, w_all.reshape(width, wide), gains, o_own


def inverse_rms(values):
    return lax.rsqrt(jnp.mean(values * values, axis=-1, keepdims=True) + epsilon)


def norm_back(grad, unit, inverse, gain):
    scaled = grad * gain
    return (scaled - unit * jnp.mean(scaled * unit, axis=-1, keepdims=True)) * inverse


class ByShare:
    def __init__(self, ref):
        self.ref = ref

    def tile(self, i, size):
        block = self.ref[:, i]
        return block.reshape(size, block.shape[2])


class ByTiles:
    def __init__(self, src, ref, sem, tile):
        self.ref = ref
        self.fills = [
            pltpu.make_async_copy(
                src.at[pl.ds(i * tile, tile)], ref.at[pl.ds(i * tile, tile)], sem.at[i]
            )
            for i in range(ref.shape[0] // tile)
        ]

    def tile(self, i, size):
        return self.ref[pl.ds(pl.multiple_of(i * size, size), size), :]


def product_tiles(part, slot, pairs, tile, first=False):
    def one(i, none):
        cols = pl.ds(pl.multiple_of(i * tile, tile), tile)
        total = None
        for rows, weights in pairs:
            if hasattr(weights, "tile"):
                block = weights.tile(i, tile)
            else:
                block = weights[cols, :]
            term = dot_nt(rows[slot], block)
            total = term if total is None else total + term
        part[slot, :, cols] = total.astype(bf16)
        return none

    if first:
        for i in range(part.shape[2] // tile):
            for _, weights in pairs:
                weights.fills[i].wait()
            one(i, 0)
    else:
        lax.fori_loop(0, part.shape[2] // tile, one, 0)


def summed_products(part, land, f, pairs, send_sem, recv_sem, chunks=1, beside=(), first=False):
    side, above, across = peers(f)
    rows = part.shape[1] // chunks
    rings = [
        SquareSum(
            part, land.at[c], f, send_sem.at[c], recv_sem.at[c], base=c * rows, rows=rows
        )
        for c in range(chunks)
    ]
    product_tiles(part, across, pairs, 512, first)
    for ring in rings:
        ring.start_cross()
    beside = iter(beside)
    next(beside, int)()
    product_tiles(part, side, pairs, 512)
    for ring in rings:
        ring.near[0].start()
    product_tiles(part, above, pairs, 512)
    for ring in rings:
        ring.near[1].start()
    next(beside, int)()
    rings[0].relay()
    product_tiles(part, f, pairs, 512)
    next(beside, int)()
    for ring in rings[1:]:
        ring.relay()
    return rings


def sum_then_gather(rings, finish_rows, slots, f, send_sem, recv_sem):
    gathers = []
    for c, ring in enumerate(rings):
        ring.arrive()
        by_rows(ring, finish_rows)
        gather = SquareGather(
            slots, f, send_sem.at[c], recv_sem.at[c], base=ring.base, rows=2 * ring.half
        )
        gather.start()
        gathers.append(gather)
    for ring in rings:
        ring.finish()
    return gathers


def by_rows(ring, body, step=16):
    for half in (0, 1):

        def one(i, none):
            start = pl.multiple_of(i * step, step)
            rows = pl.ds(
                pl.multiple_of(ring.base + half * ring.half + i * step, step), step
            )
            body(rows, ring.total(half, pl.ds(start, step)))
            return none

        lax.fori_loop(0, ring.half // step, one, 0)


def branch_kernel(
    att_hbm,
    w_hbm,
    tok_hbm,
    gain_ref,
    rows_hbm,
    res_hbm,
    rows_ref,
    res_ref,
    att_ref,
    w_ref,
    tok_ref,
    part,
    land,
    s_send,
    s_recv,
    g_send,
    g_recv,
    load_sem,
    store_sem,
):
    f = lax.axis_index("feat")
    loads = Loads(((att_hbm, att_ref), (w_hbm, w_ref), (tok_hbm, tok_ref)), load_sem).start()
    greet(square_targets(f))
    loads.wait()
    rings = summed_products(
        part, land, f, [(att_ref, ByShare(w_ref))], s_send, s_recv, land.shape[0]
    )

    def finish_rows(rows, total):
        residual = tok_ref[rows, :].astype(f32) + total
        res_ref[rows, :] = residual
        rows_ref[f, rows, :] = (residual * inverse_rms(residual) * gain_ref[...]).astype(bf16)

    gathers = sum_then_gather(rings, finish_rows, rows_ref, f, g_send, g_recv)
    stores = [pltpu.make_async_copy(res_ref, res_hbm, store_sem.at[0])]
    stores[0].start()

    def store(slot):
        c = pltpu.make_async_copy(rows_ref.at[slot], rows_hbm.at[slot], store_sem.at[len(stores)])
        c.start()
        stores.append(c)

    side, above, across = peers(f)
    store(f)
    for gather in gathers:
        gather.relay()
    for gather in gathers:
        gather.near()
    store(side)
    store(above)
    for gather in gathers:
        gather.far()
    store(across)
    for gather in gathers:
        gather.sent()
    for c in stores:
        c.wait()


CHUNKS = 2


def square_scratch(parts, block, width, chunks=CHUNKS):
    dma = pltpu.SemaphoreType.DMA
    return [
        pltpu.VMEM((parts, block, width), bf16),
        pltpu.VMEM((chunks, 6, block // 2 // chunks, width), bf16),
        dma((chunks, 6)),
        dma((chunks, 6)),
    ]


def branch_step(att, out_w, own, gain_two):
    parts, block, _ = att.shape
    width = own.shape[1]
    dma = pltpu.SemaphoreType.DMA
    return pl.pallas_call(
        branch_kernel,
        out_shape=(
            jax.ShapeDtypeStruct((parts, block, width), bf16),
            jax.ShapeDtypeStruct((block, width), f32),
        ),
        in_specs=in_place(3) + whole_vmem(1),
        out_specs=tuple(in_place(2)),
        scratch_shapes=[pltpu.VMEM((parts, block, width), bf16), pltpu.VMEM((block, width), f32)]
        + vmem_like(att, out_w, own)
        + square_scratch(parts, block, width)
        + [dma((CHUNKS, 6)), dma((CHUNKS, 6)), dma((3,)), dma((1 + parts,))],
        compiler_params=pltpu.CompilerParams(
            collective_id=3, has_side_effects=True, vmem_limit_bytes=60 << 20
        ),
        cost_estimate=pl.CostEstimate(flops=0, bytes_accessed=1 << 20, transcendentals=0),
        name="branch_step",
    )(att, out_w, own, gain_two)


def rows_back_kernel(
    grads_hbm,
    wg_hbm,
    wu_hbm,
    res_hbm,
    cot_hbm,
    gain_ref,
    mixed_hbm,
    wd_hbm,
    wo_hbm,
    all_hbm,
    gres_hbm,
    gsum_ref,
    down_hbm,
    ga_hbm,
    all_ref,
    gres_ref,
    down_ref,
    ga_ref,
    gg_ref,
    gu_ref,
    res_ref,
    cot_ref,
    part,
    land,
    wg,
    wu,
    mixed,
    wd,
    wo,
    s_send,
    s_recv,
    g_send,
    g_recv,
    local_sem,
    tile_sem,
    load_sem,
    store_sem,
):
    f = lax.axis_index("feat")
    rows_in = Loads(((grads_hbm.at[0], gg_ref), (grads_hbm.at[1], gu_ref)), load_sem).start()
    weights = [
        ByTiles(src, dst, tile_sem.at[i], 512)
        for i, (src, dst) in enumerate(((wg_hbm, wg), (wu_hbm, wu)))
    ]
    for pair in zip(*(w.fills for w in weights)):
        for c in pair:
            c.start()
    fills = [
        pltpu.make_async_copy(src, dst, local_sem.at[i])
        for i, (src, dst) in enumerate(((mixed_hbm, mixed), (wd_hbm, wd), (wo_hbm, wo)))
    ]
    late_in = Loads(((res_hbm, res_ref), (cot_hbm, cot_ref)), load_sem.at[pl.ds(2, 2)]).start()
    for c in fills:
        c.start()
    greet(square_targets(f))
    rows_in.wait()
    pairs = [(gg_ref, weights[0]), (gu_ref, weights[1])]

    def down_products(slots):
        for p in slots:
            product_tiles(down_ref, p, [(mixed, wd)], 512)

    rings = summed_products(part, land, f, pairs, s_send, s_recv, land.shape[0], first=True)
    gsum_ref[...] = jnp.zeros_like(gsum_ref)
    late_in.wait()

    def finish_rows(rows, grad):
        residual = res_ref[rows, :]
        inverse = inverse_rms(residual)
        unit = residual * inverse
        gsum_ref[...] += jnp.sum(grad * unit, axis=0, keepdims=True)
        grad_res = cot_ref[rows, :].astype(f32) + norm_back(grad, unit, inverse, gain_ref[...])
        gres_ref[rows, :] = grad_res
        all_ref[f, rows, :] = grad_res.astype(bf16)

    gathers = sum_then_gather(rings, finish_rows, all_ref, f, g_send, g_recv)
    side, above, across = peers(f)

    def attended_grad(slot):
        blocks = ByShare(wo)
        size = all_ref.shape[2] // wo.shape[1]
        total = None
        for i in range(wo.shape[1]):
            term = dot(all_ref[slot, :, i * size : (i + 1) * size], blocks.tile(i, size))
            total = term if total is None else total + term
        ga_ref[slot] = total
        store(ga_ref.at[slot], ga_hbm.at[slot])
        store(all_ref.at[slot], all_hbm.at[slot])

    stores = []

    def store(src, dst):
        c = pltpu.make_async_copy(src, dst, store_sem.at[len(stores)])
        c.start()
        stores.append(c)

    store(gres_ref, gres_hbm)
    for c in fills:
        c.wait()
    attended_grad(f)
    down_products(range(2))
    for gather in gathers:
        gather.relay()
    down_products(range(2, part.shape[0]))
    store(down_ref, down_hbm)
    for gather in gathers:
        gather.near()
    attended_grad(side)
    attended_grad(above)
    for gather in gathers:
        gather.far()
    attended_grad(across)
    for gather in gathers:
        gather.sent()
    for c in stores:
        c.wait()


def rows_back(
    grads, gate_w, up_w, residual, cot_own, gain_two, mixed, down_w, out_w
):
    _, parts, block, hidden = grads.shape
    width = residual.shape[1]
    dma = pltpu.SemaphoreType.DMA
    return pl.pallas_call(
        rows_back_kernel,
        out_shape=(
            jax.ShapeDtypeStruct((parts, block, width), bf16),
            jax.ShapeDtypeStruct((block, width), f32),
            jax.ShapeDtypeStruct((1, width), f32),
            jax.ShapeDtypeStruct((parts, block, width), bf16),
            jax.ShapeDtypeStruct((parts, block, out_w.shape[3]), f32),
        ),
        in_specs=in_place(5) + whole_vmem(1) + in_place(3),
        out_specs=tuple(in_place(2) + whole_vmem(1) + in_place(2)),
        scratch_shapes=[
            pltpu.VMEM((parts, block, width), bf16),
            pltpu.VMEM((block, width), f32),
            pltpu.VMEM((parts, block, width), bf16),
            pltpu.VMEM((parts, block, out_w.shape[3]), f32),
        ]
        + [pltpu.VMEM((parts, block, hidden), bf16)] * 2
        + vmem_like(residual, cot_own)
        + square_scratch(parts, block, width)[:2]
        + [
            pltpu.VMEM((width, hidden), bf16),
            pltpu.VMEM((width, hidden), bf16),
            pltpu.VMEM((parts, block, hidden), bf16),
            pltpu.VMEM((width, hidden), bf16),
            pltpu.VMEM(out_w.shape, bf16),
        ]
        + [dma((CHUNKS, 6))] * 4
        + [dma((3,)), dma((2, width // 512)), dma((4,)), dma((2 * parts + 2,))],
        compiler_params=pltpu.CompilerParams(
            collective_id=4, has_side_effects=True, vmem_limit_bytes=60 << 20
        ),
        cost_estimate=pl.CostEstimate(flops=0, bytes_accessed=1 << 20, transcendentals=0),
        name="rows_back",
    )(grads, gate_w, up_w, residual, cot_own, gain_two, mixed, down_w, out_w)


def closing_kernel(
    seqs,
    dps,
    dqkv_hbm,
    w_hbm,
    tok_hbm,
    gres_hbm,
    gain_ref,
    gsum_two_ref,
    normed_hbm,
    oacc_hbm,
    down_hbm,
    x_ref,
    tile_ref,
    query_ref,
    key_ref,
    value_ref,
    ograd_ref,
    part,
    land,
    s_send,
    s_recv,
    gsum,
    cut,
    came,
    mid,
    tail,
    c_send,
    c_recv,
    d_send,
    d_recv,
    dqkv_ref,
    w_ref,
    tok_ref,
    gres_ref,
    normed_ref,
    oacc_ref,
    load_sem,
    first_sem,
    term_ref,
    acc_ref,
    sib_land,
    sib_send,
    sib_recv,
    *sum_scratch,
):
    begin = Loads(((oacc_hbm, oacc_ref),), first_sem).start()
    loads = Loads(
        (
            (dqkv_hbm, dqkv_ref),
            (normed_hbm, normed_ref),
            (w_hbm, w_ref),
            (tok_hbm, tok_ref),
            (gres_hbm, gres_ref),
        ),
        load_sem,
    ).start()
    half = len(sum_scratch) // 2
    f, s, d = lax.axis_index("feat"), lax.axis_index("seq"), lax.axis_index("dp")
    parts = 4
    others = [lax.rem(d + k, dps) for k in range(1, dps)]
    circle = [
        (lax.rem(f + i, parts), lax.rem(s + j, seqs))
        for i in range(parts)
        for j in range(seqs)
        if i or j
    ]
    greet(
        [{"feat": a, "seq": b} for a, b in circle] + [{"dp": o} for o in others]
    )
    begin.wait()
    rows_sum = RowSum(acc_ref, *sum_scratch[:3], sum_scratch[3:half], f, s)
    out_sum = RowSum(oacc_ref, *sum_scratch[half : half + 3], sum_scratch[half + 3 :], f, s)
    out_sum.step(1)
    loads.wait()
    term_tiles(term_ref, normed_ref, dqkv_ref)
    sibling = SiblingSum(term_ref, acc_ref, sib_land, (sib_send, sib_recv), d, dps)
    sibling.start()
    out_sum.step(2)

    def over_seq():
        sibling.add()
        rows_sum.step(1)
        for t in range(3, seqs):
            out_sum.step(t)

    rings = summed_products(
        part, land, f, [(dqkv_ref, w_ref)], s_send, s_recv, land.shape[0], (over_seq,)
    )
    for t in range(2, seqs):
        rows_sum.step(t)
    gsum[...] = jnp.zeros_like(gsum)

    def finish_rows(rows, grad):
        values = tok_ref[rows, :].astype(f32)
        inverse = inverse_rms(values)
        unit = values * inverse
        gsum[...] += jnp.sum(grad * unit, axis=0, keepdims=True)
        x_ref[rows, :] = gres_ref[rows, :] + norm_back(grad, unit, inverse, gain_ref[...])

    for ring in rings:
        ring.arrive()
        by_rows(ring, finish_rows)
    for ring in rings:
        ring.finish()

    lanes = gsum.shape[1] // (parts * seqs)
    cut[...] = jnp.zeros_like(cut)
    for k in range(parts * seqs):
        cut[k, 0:1, :] = gsum[:, k * lanes : (k + 1) * lanes]
        cut[k, 1:2, :] = gsum_two_ref[:, k * lanes : (k + 1) * lanes]
    place = f * seqs + s
    sends = []
    for i, (a, b) in enumerate(circle):
        sends.append(
            push(
                cut.at[a * seqs + b],
                came.at[i],
                c_send.at[i],
                c_recv.at[i],
                {"feat": a, "seq": b},
            )
        )
    for c in sends:
        c.start()
    total = cut[place]
    for c in sends:
        c.wait_recv()
    for i in range(len(circle)):
        total = total + came[i]
    mid[...] = total
    last = [
        push(mid, tail.at[k], d_send.at[k], d_recv.at[k], {"dp": o})
        for k, o in enumerate(others)
    ]
    for c in last:
        c.start()
    for c in last:
        c.wait_recv()
    for k in range(len(others)):
        total = total + tail[k]
    tile_ref[...] = total
    out_sum.over_feat()
    rows_sum.over_feat()
    rows_sum.arrive()
    first = 0
    for ref in (query_ref, key_ref, value_ref):
        each = ref.shape[1] // parts
        for p in range(parts):
            piece = rows_sum.shares[p, :, first : first + each]
            ref[:, p * each : (p + 1) * each] = piece.astype(f32)
        first += each
    rows_sum.finish()
    sibling.finish()
    out_sum.arrive()
    each = ograd_ref.shape[1] // parts
    for p in range(parts):
        ograd_ref[:, p * each : (p + 1) * each] = out_sum.shares[p].astype(f32)
    out_sum.finish()
    for c in sends + last:
        c.wait_send()


def closing(dqkv, qkv_w, own, grad_residual, gain_one, gain_two_sum, normed, out_acc, down_grad):
    parts, seqs, dps = (lax.axis_size(a) for a in ALL)
    block, width = own.shape
    others = max(dps - 1, 1)
    lanes = width // (parts * seqs)
    circle = parts * seqs - 1
    rows_each = out_acc.shape[2]
    by_row = (parts, seqs, dps, rows_each, dqkv.shape[2])
    acc_shape = out_acc.shape[:3] + dqkv.shape[2:]
    dma = pltpu.SemaphoreType.DMA
    return pl.pallas_call(
        functools.partial(closing_kernel, seqs, dps),
        out_shape=(
            jax.ShapeDtypeStruct((block, width), f32),
            jax.ShapeDtypeStruct((8, lanes), f32),
            jax.ShapeDtypeStruct((rows_each, HEADS * FDIM), f32),
            jax.ShapeDtypeStruct((rows_each, HEADS * FDIM), f32),
            jax.ShapeDtypeStruct((rows_each, HEADS * HV), f32),
            jax.ShapeDtypeStruct((rows_each, HEADS * HV), f32),
        ),
        in_specs=in_place(4) + whole_vmem(2) + in_place(3),
        out_specs=tuple(whole_vmem(6)),
        scratch_shapes=square_scratch(parts, block, width)
        + [
            pltpu.VMEM((1, width), f32),
            pltpu.VMEM((parts * seqs, 8, lanes), f32),
            pltpu.VMEM((circle, 8, lanes), f32),
            pltpu.VMEM((8, lanes), f32),
            pltpu.VMEM((others, 8, lanes), f32),
            dma((circle,)),
            dma((circle,)),
            dma((others,)),
            dma((others,)),
        ]
        + vmem_like(dqkv, qkv_w, own, grad_residual, normed, out_acc)
        + [dma((5,)), dma((1,))]
        + sibling_scratch(by_row)
        + row_sum_scratch(acc_shape)
        + row_sum_scratch(out_acc.shape),
        compiler_params=pltpu.CompilerParams(
            collective_id=5, has_side_effects=True, vmem_limit_bytes=60 << 20
        ),
        cost_estimate=pl.CostEstimate(flops=0, bytes_accessed=1 << 20, transcendentals=0),
        name="closing",
    )(dqkv, qkv_w, own, grad_residual, gain_one, gain_two_sum, normed, out_acc, down_grad)


def local(
    tokens,
    segments,
    norm1_gain,
    norm2_gain,
    w_query,
    w_key,
    w_value,
    w_out,
    w_gate,
    w_up,
    w_down,
    cotangent,
):
    parts = lax.axis_size("feat")
    heads = HEADS // parts
    block, width = tokens.shape[2], tokens.shape[3]
    rows_total = parts * block
    rows_each = w_query.shape[0]
    own = tokens.reshape(block, width)
    cot_own = cotangent.reshape(block, width)

    x_all, qkv_w, gains, out_share = opening(
        own, w_query, w_key, w_value, w_out.T, norm1_gain[None], norm2_gain[None]
    )
    qkv_width = qkv_w.shape[1]
    gate_w = lax.all_gather(w_gate, ("seq", "dp"), axis=0, tiled=True)
    gain_one, gain_two = gains[0:1], gains[1:2]

    x_wide = x_all.astype(f32).reshape(rows_total, width)
    normed = (x_wide * inverse_rms(x_wide) * gain_one).astype(bf16)
    qkv = dot(normed, qkv_w).astype(bf16).reshape(parts, block, qkv_width)
    qkv, gate_w, out_share, w_up, w_down = lax.optimization_barrier(
        (qkv, gate_w, out_share, w_up, w_down)
    )
    out_w = lax.all_gather(out_share[None], ("seq", "dp"), axis=0, tiled=True)
    up_w = lax.all_gather(w_up, ("seq", "dp"), axis=0, tiled=True)
    down_w = lax.all_gather(w_down.T, ("seq", "dp"), axis=0, tiled=True)
    segment = segments.reshape(parts, block).astype(f32)
    segc, segr = segment[:, :, None], segment[:, None, :]
    tables = feature_tables(heads)
    att, rden, carry, csum, cot_all = attention_forward(qkv, segc, segr, tables, cot_own, heads)
    cot_all = cot_all.reshape(rows_total, width)
    rows_all, residual = branch_step(att, out_w, own, gain_two)
    rows_all = rows_all.reshape(rows_total, width)

    gate_out = dot(rows_all, gate_w)
    up_out = dot(rows_all, up_w)
    sig = jax.nn.sigmoid(gate_out)
    silu = gate_out * sig
    mixed = (silu * up_out).astype(bf16)
    down_term = dot_tn(cot_all, mixed).astype(bf16)
    mixed, cot_late, down_term = lax.optimization_barrier((mixed, cot_all, down_term))
    grad_mixed = dot(cot_late, down_w)
    grads = jnp.stack(
        [grad_mixed * up_out * sig * (1.0 + gate_out * (1.0 - sig)), grad_mixed * silu]
    ).astype(bf16)

    def summed(term, dim):
        return lax.psum_scatter(term, ("seq", "dp"), scatter_dimension=dim, tiled=True)

    both_term = jnp.einsum("xtf,td->xfd", grads, rows_all, preferred_element_type=f32).astype(bf16)
    grads, both_term = lax.optimization_barrier((grads, both_term))
    down_sum, both_sum = summed(down_term, 0), summed(both_term, 2)

    by_device = (parts, block, -1)
    branch_all, grad_residual, gain_two_sum, down, ga = rows_back(
        grads.reshape((2,) + by_device),
        gate_w,
        up_w,
        residual,
        cot_own,
        gain_two,
        mixed.reshape(by_device),
        down_w,
        out_w,
    )
    dqkv, output, out_acc = attention_backward(
        qkv,
        segc,
        segr,
        tables,
        att,
        rden,
        carry,
        csum,
        ga,
        down,
        residual,
        branch_all,
        heads,
    )
    down_grad = down_sum.T.astype(f32)
    x_grad, gain_grads, query_grad, key_grad, value_grad, out_grad = closing(
        dqkv,
        qkv_w,
        own,
        grad_residual,
        gain_one,
        gain_two_sum,
        normed.reshape(parts, block, width),
        out_acc,
        down_grad,
    )
    gain_each = gain_grads.shape[1] // lax.axis_size("dp")
    gain_grads = lax.dynamic_slice_in_dim(
        gain_grads, lax.axis_index("dp") * gain_each, gain_each, axis=1
    )
    return (
        output.reshape(tokens.shape),
        x_grad.reshape(tokens.shape),
        gain_grads[0],
        gain_grads[1],
        query_grad,
        key_grad,
        value_grad,
        out_grad.T,
        both_sum[0].T.astype(f32),
        both_sum[1].T.astype(f32),
        down_grad,
    )


def solution(mesh):
    placed = (
        P("feat", "dp", "seq", None),
        P(None, "dp", "seq"),
        P(ALL),
        P(ALL),
        P(ALL, None),
        P(ALL, None),
        P(ALL, None),
        P(None, ALL),
        P(("seq", "dp"), "feat"),
        P(("seq", "dp"), "feat"),
        P("feat", ("seq", "dp")),
        P("feat", "dp", "seq", None),
    )
    return jax.shard_map(
        local,
        mesh=mesh,
        in_specs=placed,
        out_specs=(
            P("feat", "dp", "seq", None),
            P("feat", "dp", "seq", None),
            P(ALL),
            P(ALL),
            P(ALL, None),
            P(ALL, None),
            P(ALL, None),
            P(None, ALL),
            P(("seq", "dp"), "feat"),
            P(("seq", "dp"), "feat"),
            P("feat", ("seq", "dp")),
        ),
        check_vma=False,
    )
```

```python
import functools

import jax
import jax.numpy as jnp
import numpy as np
from jax import lax
from jax.experimental import pallas as pl
from jax.experimental.pallas import tpu as pltpu
from jax.sharding import PartitionSpec as P

HEADS = 16
FDIM = 16
HV = 128
STATE = 160
LANES = 256
epsilon = 1e-05
MESH = pl.DeviceIdType.MESH
ALL = ("feat", "seq", "dp")
f32 = jnp.float32
bf16 = jnp.bfloat16


def dot(a, b):
    return lax.dot_general(a, b, (((1,), (0,)), ((), ())), preferred_element_type=f32)


def dot_nt(a, b):
    return lax.dot_general(a, b, (((1,), (1,)), ((), ())), preferred_element_type=f32)


def dot_tn(a, b):
    return lax.dot_general(a, b, (((0,), (0,)), ((), ())), preferred_element_type=f32)


def feature_tables(heads):
    pairs = [(i, j) for i in range(FDIM) for j in range(i, FDIM)]
    left = np.zeros((heads, heads * FDIM, LANES), np.float32)
    right = np.zeros((heads, heads * FDIM, LANES), np.float32)
    rows = np.zeros((8, LANES), np.float32)
    for h in range(heads):
        for p, (i, j) in enumerate(pairs):
            left[h, h * FDIM + i, p] = 1.0
            right[h, h * FDIM + j, p] = 1.0
            rows[2, p] = 0.25 / 2.0**0.5 if i == j else 0.25
        for i in range(FDIM):
            p = len(pairs) + i
            left[h, h * FDIM + i, p] = 1.0
            rows[1, p] = 1.0
            rows[2, p] = 0.5
        p = len(pairs) + FDIM
        rows[0, p] = rows[1, p] = rows[2, p] = 1.0
    return jnp.asarray(left, bf16), jnp.asarray(right, bf16), jnp.asarray(rows)


def both_sides(entries, h, left_ref, right_ref, rows_ref):
    one = dot(entries, left_ref[h]) + rows_ref[0:1, :]
    two = dot(entries, right_ref[h]) + rows_ref[1:2, :]
    return one, two * rows_ref[2:3, :]


def features(entries, h, left_ref, right_ref, rows_ref):
    one, two = both_sides(entries, h, left_ref, right_ref, rows_ref)
    return one * two


def pull_features(grad, entries, h, left_ref, right_ref, rows_ref):
    one, two = both_sides(entries, h, left_ref, right_ref, rows_ref)
    scaled = rows_ref[2:3, :]
    return dot_nt((grad * two).astype(bf16), left_ref[h]) + dot_nt(
        (grad * one * scaled).astype(bf16), right_ref[h]
    )


def only_head(entries, h):
    lane = lax.broadcasted_iota(jnp.int32, entries.shape, 1)
    keep = (lane >= h * FDIM) & (lane < (h + 1) * FDIM)
    return jnp.where(keep, entries, jnp.zeros_like(entries))


def padded_state(state):
    return jnp.concatenate([state, jnp.zeros((LANES - STATE, state.shape[1]), state.dtype)], 0)


def allowed_of(segc, segr):
    block = segc.shape[0]
    row = lax.broadcasted_iota(jnp.int32, (block, block), 0)
    col = lax.broadcasted_iota(jnp.int32, (block, block), 1)
    return (row >= col) & (segc == segr)


def forward_kernel(
    count,
    heads,
    qkv_ref,
    segc_ref,
    segr_ref,
    left_ref,
    right_ref,
    rows_ref,
    cot_ref,
    att_hbm,
    rden_hbm,
    carry_hbm,
    csum_hbm,
    cots_ref,
    att_ref,
    rden_ref,
    carry_ref,
    csum_ref,
    send_state,
    send_sum,
    part,
    send_sem,
    recv_sem,
    f_send,
    f_recv,
    local_sem,
    store_sem,
):
    place, f = lax.axis_index("seq"), lax.axis_index("feat")
    groups, block = qkv_ref.shape[0], qkv_ref.shape[1]
    width = heads * FDIM
    tables = (left_ref, right_ref, rows_ref)

    def stores(g):
        pairs = (
            (att_ref, att_hbm),
            (rden_ref, rden_hbm),
            (carry_ref, carry_hbm),
            (csum_ref, csum_hbm),
        )
        return Loads([(a.at[g], b.at[g]) for a, b in pairs], store_sem.at[g])

    def hop(g):
        target = {"seq": lax.rem(place + 1, count)}
        return [
            pltpu.make_async_remote_copy(
                src_ref=src.at[g],
                dst_ref=dst.at[g],
                send_sem=send_sem.at[i, g],
                recv_sem=recv_sem.at[i, g],
                device_id=target,
                device_id_type=MESH,
            )
            for i, (src, dst) in enumerate(((send_state, carry_ref), (send_sum, csum_ref)))
        ]

    def send(g):
        for copy in hop(g):
            copy.start()

    chain = [lax.rem(place + 1, count), lax.rem(place + count - 1, count)]
    stay = pltpu.make_async_copy(cot_ref, cots_ref.at[f], local_sem.at[0])
    stay.start()
    greet(square_targets(f) + [{"seq": c} for c in chain])
    gather = SquareGather(cots_ref, f, f_send, f_recv, cot_ref)
    gather.start()

    @pl.when(place == 0)
    def _():
        carry_ref[...] = jnp.zeros_like(carry_ref)
        csum_ref[...] = jnp.full_like(csum_ref, -1.0)

    def summarize(g, none):
        segc, segr = segc_ref[g], segr_ref[g]
        tail = segr[:, block - 1 : block]
        at_tail = (segc == tail).astype(f32)
        send_sum[g, heads : heads + 1, :] = jnp.broadcast_to(tail, (1, LANES))
        for h in range(heads):
            key = qkv_ref[g, :, width : 2 * width]
            value = qkv_ref[g, :, 2 * width + h * HV : 2 * width + (h + 1) * HV]
            phi = (features(key, h, *tables) * at_tail).astype(bf16)
            send_state[g, h] = dot_tn(phi, value)[:STATE].astype(bf16)
            ones = jnp.ones((8, block), bf16)
            send_sum[g, h : h + 1, :] = dot(ones, phi)[0:1]

        @pl.when(place == 0)
        def _():
            send(g)

        return none

    lax.fori_loop(0, groups, summarize, 0)
    def join(g, none):
        for copy in hop(g):
            copy.wait_recv()
        segr = segr_ref[g]
        mark = csum_ref[g, heads : heads + 1, 0:1]
        head, tail = segr[:, 0:1], segr[:, block - 1 : block]
        whole = ((head == tail) & (head == mark)).astype(f32)
        for h in range(heads):
            send_state[g, h] = (
                send_state[g, h].astype(f32) + whole * carry_ref[g, h].astype(f32)
            ).astype(bf16)
            send_sum[g, h : h + 1, :] = (
                send_sum[g, h : h + 1, :] + whole * csum_ref[g, h : h + 1, :]
            )
        send(g)
        return none

    def attend(g, none):
        segc, segr = segc_ref[g], segr_ref[g]
        allowed = allowed_of(segc, segr)
        for h in range(heads):
            query = only_head(qkv_ref[g, :, 0:width], h)
            key = qkv_ref[g, :, width : 2 * width]
            value = qkv_ref[g, :, 2 * width + h * HV : 2 * width + (h + 1) * HV]
            c = dot_nt(query, key)
            kernel = jnp.where(allowed, 1.0 + c * (0.25 + c * 0.03125), 0.0).astype(bf16)
            wide = jnp.concatenate([value, jnp.ones_like(value)], axis=1)
            part[g, h] = dot(kernel, wide)

        @pl.when((place > 0) & (place < count - 1) & (g == place - 1))
        def _():
            lax.fori_loop(0, groups, join, 0)

        return none

    lax.fori_loop(0, groups, attend, 0)
    gather.relay()

    def carry_on(g, none):
        segc = segc_ref[g]

        @pl.when(place == count - 1)
        def _():
            for copy in hop(g):
                copy.wait_recv()

        mark = csum_ref[g, heads : heads + 1, 0:1]
        carried = (segc == mark).astype(f32)
        for h in range(heads):
            phi = features(qkv_ref[g, :, 0:width], h, *tables) * carried
            state = padded_state(carry_ref[g, h])
            both = part[g, h]
            numer = both[:, :HV] + dot(phi.astype(bf16), state)
            denom = both[:, HV:] + jnp.sum(
                phi * csum_ref[g, h : h + 1, :], axis=1, keepdims=True
            )
            inverse = 1.0 / denom
            att_ref[g, :, h * HV : (h + 1) * HV] = (numer * inverse).astype(bf16)
            rden_ref[g, :, h * HV : (h + 1) * HV] = inverse
        stores(g).start()
        return none

    lax.fori_loop(0, groups, carry_on, 0)

    @pl.when(place < count - 1)
    def _():
        def finish(g, none):
            for copy in hop(g):
                copy.wait_send()
            return none

        lax.fori_loop(0, groups, finish, 0)

    stay.wait()
    gather.finish()

    def stored(g, none):
        stores(g).wait()
        return none

    lax.fori_loop(0, groups, stored, 0)


def backward_kernel(
    count,
    heads,
    qkv_hbm,
    segc_ref,
    segr_ref,
    left_ref,
    right_ref,
    rows_ref,
    att_hbm,
    rden_hbm,
    carry_hbm,
    csum_ref,
    ga_hbm,
    down_ref,
    res_hbm,
    branch_hbm,
    out_hbm,
    final_ref,
    acc_hbm,
    qkv_ref,
    att_ref,
    rden_ref,
    carry_ref,
    ga_ref,
    res_ref,
    branch_ref,
    out_ref,
    gn,
    send_state,
    send_sum,
    recv_state,
    recv_sum,
    dkey,
    dvalue,
    terms,
    land,
    send_sem,
    recv_sem,
    f_send,
    f_recv,
    local_sem,
    load_sem,
    store_sem,
    term_ref,
    acc_ref,
    sib_land,
    sib_send,
    sib_recv,
):
    place, f, d = lax.axis_index("seq"), lax.axis_index("feat"), lax.axis_index("dp")
    dps = term_ref.shape[2]
    loads = Loads(
        (
            (qkv_hbm, qkv_ref),
            (ga_hbm, ga_ref),
            (rden_hbm, rden_ref),
            (att_hbm, att_ref),
            (carry_hbm, carry_ref),
            (res_hbm, res_ref),
        ),
        load_sem,
    ).start()
    late = Loads(((branch_hbm, branch_ref),), load_sem.at[pl.ds(6, 1)]).start()
    groups, block = qkv_ref.shape[0], qkv_ref.shape[1]
    width = heads * FDIM
    tables = (left_ref, right_ref, rows_ref)

    def hop(g):
        target = {"seq": lax.rem(place + count - 1, count)}
        return [
            pltpu.make_async_remote_copy(
                src_ref=src.at[g],
                dst_ref=dst.at[g],
                send_sem=send_sem.at[i, g],
                recv_sem=recv_sem.at[i, g],
                device_id=target,
                device_id_type=MESH,
            )
            for i, (src, dst) in enumerate(((send_state, recv_state), (send_sum, recv_sum)))
        ]

    def send(g):
        for copy in hop(g):
            copy.start()

    chain = [lax.rem(place + 1, count), lax.rem(place + count - 1, count)]
    greet(
        square_targets(f)
        + [{"seq": c} for c in chain]
        + [{"dp": lax.rem(d + o, dps)} for o in range(1, dps)]
    )
    fill = pltpu.make_async_copy(down_ref, terms, local_sem.at[0])
    fill.start()
    ring = SquareSum(terms, land, f, f_send, f_recv)
    loads.wait()

    def store(g):
        return pltpu.make_async_copy(out_ref.at[g], out_hbm.at[g], store_sem.at[g])


    @pl.when(place == count - 1)
    def _():
        recv_state[...] = jnp.zeros_like(recv_state)
        recv_sum[...] = jnp.full_like(recv_sum, -1.0)

    def summarize(g, none):
        segc, segr = segc_ref[g], segr_ref[g]
        head = segr[:, 0:1]
        at_head = (segc == head).astype(f32)
        send_sum[g, heads : heads + 1, :] = jnp.broadcast_to(head, (1, LANES))
        for h in range(heads):
            lanes = slice(h * HV, (h + 1) * HV)
            ga = ga_ref[g, :, lanes]
            inverse = rden_ref[g, :, lanes]
            numer = (ga * inverse).astype(bf16)
            dots = jnp.sum(ga * att_ref[g, :, lanes].astype(f32), axis=1, keepdims=True)
            lane = lax.broadcasted_iota(jnp.int32, (block, HV), 1)
            denom = jnp.where(lane == 0, -dots * inverse, 0.0).astype(bf16)
            gn[g, h, :, :HV] = numer
            gn[g, h, :, HV:] = denom
            phi = (features(qkv_ref[g, :, 0:width], h, *tables) * at_head).astype(bf16)
            send_state[g, h] = dot_tn(phi, numer)[:STATE].astype(bf16)
            send_sum[g, h : h + 1, :] = dot_tn(denom, phi)[0:1]

        @pl.when(place == count - 1)
        def _():
            send(g)

        return none

    lax.fori_loop(0, groups, summarize, 0)
    fill.wait()
    ring.start_cross()
    ring.start_near()

    def join(g, none):
        for copy in hop(g):
            copy.wait_recv()
        segr = segr_ref[g]
        mark = recv_sum[g, heads : heads + 1, 0:1]
        head, tail = segr[:, 0:1], segr[:, block - 1 : block]
        whole = ((head == tail) & (head == mark)).astype(f32)
        for h in range(heads):
            send_state[g, h] = (
                send_state[g, h].astype(f32) + whole * recv_state[g, h].astype(f32)
            ).astype(bf16)
            send_sum[g, h : h + 1, :] = (
                send_sum[g, h : h + 1, :] + whole * recv_sum[g, h : h + 1, :]
            )
        send(g)
        return none

    def pull(g, none):
        segc, segr = segc_ref[g], segr_ref[g]
        allowed = allowed_of(segc, segr)
        query_all = qkv_ref[g, :, 0:width]
        key_all = qkv_ref[g, :, width : 2 * width]
        carried = (segc == csum_ref[g, heads : heads + 1, 0:1]).astype(f32)
        dquery = jnp.zeros((block, width), f32)
        dkey_sum = jnp.zeros((block, width), f32)
        for h in range(heads):
            query, key = only_head(query_all, h), only_head(key_all, h)
            value = qkv_ref[g, :, 2 * width + h * HV : 2 * width + (h + 1) * HV]
            wide = jnp.concatenate([value, jnp.ones_like(value)], axis=1)
            both = gn[g, h]
            c = dot_nt(query, key_all)
            kernel = jnp.where(allowed, 1.0 + c * (0.25 + c * 0.03125), 0.0).astype(bf16)
            grad = jnp.where(allowed, dot_nt(both, wide), 0.0)
            grad_c = (grad * (0.25 + c * 0.0625)).astype(bf16)
            dvalue[g, h] = dot_tn(kernel, both[:, :HV])
            dkey_sum = dkey_sum + dot_tn(grad_c, query)
            dquery = dquery + dot(grad_c, key)
            state = padded_state(carry_ref[g, h])
            gphi = dot_nt(both[:, :HV], state) + both[:, HV : HV + 1].astype(f32) * csum_ref[
                g, h : h + 1, :
            ]
            dquery = dquery + pull_features(gphi * carried, query_all, h, *tables)
        out_ref[g, :, 0:width] = dquery.astype(bf16)
        dkey[g] = dkey_sum

        @pl.when((place > 0) & (place < count - 1) & (g == count - 2 - place))
        def _():
            lax.fori_loop(0, groups, join, 0)

        return none

    lax.fori_loop(0, groups, pull, 0)
    ring.relay()
    late.wait()
    term_tiles(term_ref, branch_ref, att_ref)
    sibling = SiblingSum(term_ref, acc_ref, sib_land, (sib_send, sib_recv), d, dps)
    sibling.start()

    def carry_back(g, none):
        segc = segc_ref[g]
        key_all = qkv_ref[g, :, width : 2 * width]

        @pl.when(place == 0)
        def _():
            for copy in hop(g):
                copy.wait_recv()

        mark = recv_sum[g, heads : heads + 1, 0:1]
        later = (segc == mark).astype(f32)
        total = dkey[g]
        for h in range(heads):
            value = qkv_ref[g, :, 2 * width + h * HV : 2 * width + (h + 1) * HV]
            state = padded_state(recv_state[g, h])
            phi = (features(key_all, h, *tables) * later).astype(bf16)
            dv = dvalue[g, h] + dot(phi, state)
            out_ref[g, :, 2 * width + h * HV : 2 * width + (h + 1) * HV] = dv.astype(bf16)
            gphi = (dot_nt(value, state) + recv_sum[g, h : h + 1, :]) * later
            total = total + pull_features(gphi, key_all, h, *tables)
        out_ref[g, :, width : 2 * width] = total.astype(bf16)
        store(g).start()
        return none

    lax.fori_loop(0, groups, carry_back, 0)

    @pl.when(place > 0)
    def _():
        def finish(g, none):
            for copy in hop(g):
                copy.wait_send()
            return none

        lax.fori_loop(0, groups, finish, 0)

    ring.arrive()

    def add_up(rows, total):
        final_ref[rows, :] = res_ref[rows, :] + total

    by_rows(ring, add_up)
    ring.finish()
    sibling.add()
    keep = pltpu.make_async_copy(acc_ref, acc_hbm, store_sem.at[groups])
    keep.start()

    def stored(g, none):
        store(g).wait()
        return none

    lax.fori_loop(0, groups, stored, 0)
    sibling.finish()
    keep.wait()


def term_tiles(term, left, right):
    parts, *shape = term.shape
    tile = left.shape[2] // parts

    def one(i, none):
        cols = pl.ds(pl.multiple_of(i * tile, tile), tile)
        total = dot_tn(left[0, :, cols], right[0])
        for g in range(1, left.shape[0]):
            total = total + dot_tn(left[g, :, cols], right[g])
        term[i] = total.astype(bf16).reshape(shape)
        return none

    lax.fori_loop(0, parts, one, 0)


def whole_vmem(count):
    return [pl.BlockSpec(memory_space=pltpu.VMEM)] * count


def attention_forward(qkv, segc, segr, tables, cot_own, heads):
    groups, block, _ = qkv.shape
    count = lax.axis_size("seq")
    dma = pltpu.SemaphoreType.DMA
    states = (groups, heads, STATE, HV)
    sums = (groups, 8, LANES)
    return pl.pallas_call(
        functools.partial(forward_kernel, count, heads),
        out_shape=(
            jax.ShapeDtypeStruct((groups, block, heads * HV), bf16),
            jax.ShapeDtypeStruct((groups, block, heads * HV), f32),
            jax.ShapeDtypeStruct(states, bf16),
            jax.ShapeDtypeStruct(sums, f32),
            jax.ShapeDtypeStruct((groups,) + cot_own.shape, bf16),
        ),
        in_specs=whole_vmem(6) + in_place(1),
        out_specs=tuple(in_place(5)),
        scratch_shapes=[
            pltpu.VMEM((groups, block, heads * HV), bf16),
            pltpu.VMEM((groups, block, heads * HV), f32),
            pltpu.VMEM(states, bf16),
            pltpu.VMEM(sums, f32),
            pltpu.VMEM(states, bf16),
            pltpu.VMEM(sums, f32),
            pltpu.VMEM((groups, heads, block, 2 * HV), f32),
            dma((2, groups)),
            dma((2, groups)),
            dma((6,)),
            dma((6,)),
            dma((1,)),
            dma((groups, 4)),
        ],
        compiler_params=pltpu.CompilerParams(
            collective_id=0, has_side_effects=True, vmem_limit_bytes=60 << 20
        ),
        cost_estimate=pl.CostEstimate(flops=0, bytes_accessed=1 << 20, transcendentals=0),
        name="attention_forward",
    )(qkv, segc, segr, *tables, cot_own)


def attention_backward(
    qkv, segc, segr, tables, att, rden, carry, csum, ga, down, residual, branch, heads
):
    groups, block, wide = qkv.shape
    count = lax.axis_size("seq")
    parts, dps = lax.axis_size("feat"), lax.axis_size("dp")
    rows_each = branch.shape[2] // (parts * count * dps)
    by_row = (parts, count, dps, rows_each, heads * HV)
    states = (groups, heads, STATE, HV)
    sums = (groups, 8, LANES)
    return pl.pallas_call(
        functools.partial(backward_kernel, count, heads),
        out_shape=(
            jax.ShapeDtypeStruct((groups, block, wide), bf16),
            jax.ShapeDtypeStruct(residual.shape, f32),
            jax.ShapeDtypeStruct((count, by_row[0]) + by_row[3:], bf16),
        ),
        in_specs=in_place(1)
        + whole_vmem(5)
        + in_place(3)
        + whole_vmem(1)
        + in_place(4),
        out_specs=tuple(in_place(1) + whole_vmem(1) + in_place(1)),
        scratch_shapes=vmem_like(qkv, att, rden, carry, ga, residual, branch)
        + [
            pltpu.VMEM((groups, block, wide), bf16),
            pltpu.VMEM((groups, heads, block, 2 * HV), bf16),
            pltpu.VMEM(states, bf16),
            pltpu.VMEM(sums, f32),
            pltpu.VMEM(states, bf16),
            pltpu.VMEM(sums, f32),
            pltpu.VMEM((groups, block, heads * FDIM), f32),
            pltpu.VMEM((groups, heads, block, HV), f32),
            pltpu.VMEM((groups,) + residual.shape, bf16),
            pltpu.VMEM((6, block // 2, residual.shape[1]), bf16),
            pltpu.SemaphoreType.DMA((2, groups)),
            pltpu.SemaphoreType.DMA((2, groups)),
            pltpu.SemaphoreType.DMA((6,)),
            pltpu.SemaphoreType.DMA((6,)),
            pltpu.SemaphoreType.DMA((1,)),
            pltpu.SemaphoreType.DMA((7,)),
            pltpu.SemaphoreType.DMA((groups + 1,)),
        ]
        + sibling_scratch(by_row),
        compiler_params=pltpu.CompilerParams(
            collective_id=1, has_side_effects=True, vmem_limit_bytes=60 << 20
        ),
        cost_estimate=pl.CostEstimate(flops=0, bytes_accessed=1 << 20, transcendentals=0),
        name="attention_backward",
    )(qkv, segc, segr, *tables, att, rden, carry, csum, ga, down, residual, branch)


def peers(f):
    return 2 * (f // 2) + 1 - f % 2, (f + 2) % 4, 3 - f


def greet(targets):
    barrier = pltpu.get_barrier_semaphore()
    for target in targets:
        pl.semaphore_signal(barrier, inc=1, device_id=target, device_id_type=MESH)
    pl.semaphore_wait(barrier, len(targets))


def push(src, dst, send_sem, recv_sem, target):
    return pltpu.make_async_remote_copy(
        src_ref=src,
        dst_ref=dst,
        send_sem=send_sem,
        recv_sem=recv_sem,
        device_id=target,
        device_id_type=MESH,
    )


def square_targets(f):
    return [{"feat": p} for p in peers(f)]


class Loads:
    def __init__(self, pairs, sem):
        self.copies = [pltpu.make_async_copy(a, b, sem.at[i]) for i, (a, b) in enumerate(pairs)]

    def start(self):
        for c in self.copies:
            c.start()
        return self

    def wait(self):
        for c in self.copies:
            c.wait()


def vmem_like(*arrays):
    return [pltpu.VMEM(a.shape, a.dtype) for a in arrays]


class SquareGather:
    def __init__(self, slots, f, send_sem, recv_sem, own=None, base=0, rows=None):
        side, above, across = peers(f)
        half = (slots.shape[1] if rows is None else rows) // 2
        first, second = pl.ds(base, half), pl.ds(base + half, half)

        def copy(i, slot, rows, to):
            ref = slots.at[slot, rows]
            src = ref if own is None or i > 3 else own.at[rows]
            return push(src, ref, send_sem.at[i], recv_sem.at[i], {"feat": to})

        self.direct = [
            copy(0, f, first, side),
            copy(1, f, second, above),
            copy(2, f, second, side),
            copy(3, f, first, above),
        ]
        self.forward = [copy(4, side, first, above), copy(5, above, second, side)]

    def start(self):
        for c in self.direct:
            c.start()

    def relay(self):
        self.direct[0].wait_recv()
        self.forward[0].start()
        self.direct[1].wait_recv()
        self.forward[1].start()

    def near(self):
        self.direct[2].wait_recv()
        self.direct[3].wait_recv()

    def far(self):
        for c in self.forward:
            c.wait_recv()

    def sent(self):
        for c in self.direct + self.forward:
            c.wait_send()

    def finish(self):
        self.near()
        self.far()
        self.sent()


class SquareSum:
    def __init__(self, part, land, f, send_sem, recv_sem, base=0, rows=None):
        self.side, self.above, self.across = peers(f)
        self.f, self.part, self.land, self.base = f, part, land, base
        self.half = (part.shape[1] if rows is None else rows) // 2
        first, second = pl.ds(base, self.half), pl.ds(base + self.half, self.half)

        def copy(i, slot, rows, to):
            return push(
                part.at[slot, rows], land.at[i], send_sem.at[i], recv_sem.at[i], {"feat": to}
            )

        self.cross = [copy(0, self.across, first, self.side), copy(1, self.across, second, self.above)]
        self.near = [copy(2, self.side, first, self.side), copy(3, self.above, second, self.above)]
        self.late = [copy(4, self.above, first, self.above), copy(5, self.side, second, self.side)]

    def start_cross(self):
        for c in self.cross:
            c.start()

    def add_rows(self, slot, base, landed):
        step = 16

        def one(i, none):
            rows = pl.ds(pl.multiple_of(base + i * step, step), step)
            came = self.land[landed, pl.ds(pl.multiple_of(i * step, step), step), :]
            self.part[slot, rows, :] = (
                self.part[slot, rows, :].astype(f32) + came.astype(f32)
            ).astype(bf16)
            return none

        lax.fori_loop(0, self.half // step, one, 0)

    def start_near(self):
        for c in self.near:
            c.start()

    def relay(self):
        self.cross[0].wait_recv()
        self.add_rows(self.above, self.base, 0)
        self.late[0].start()
        self.cross[1].wait_recv()
        self.add_rows(self.side, self.base + self.half, 1)
        self.late[1].start()

    def arrive(self):
        for c in self.near + self.late:
            c.wait_recv()

    def total(self, half, rows):
        base = self.base + half * self.half
        own = self.part[self.f, pl.ds(pl.multiple_of(base + rows.start, 16), rows.size), :]
        near = self.land[2 + half, rows, :]
        late = self.land[4 + half, rows, :]
        return own.astype(f32) + near.astype(f32) + late.astype(f32)

    def finish(self):
        for c in self.cross + self.near + self.late:
            c.wait_send()


class SiblingSum:
    def __init__(self, term, acc, land, sems, d, dps):
        self.term, self.acc, self.land, self.d = term, acc, land, d
        others = [lax.rem(d + k, dps) for k in range(1, dps)]
        self.copies = [
            push(term.at[:, :, o], land.at[k], sems[0].at[k], sems[1].at[k], {"dp": o})
            for k, o in enumerate(others)
        ]

    def start(self):
        for c in self.copies:
            c.start()

    def add(self):
        for c in self.copies:
            c.wait_recv()
        seqs, parts = self.acc.shape[:2]

        def one(i, none):
            p, c = i // seqs, lax.rem(i, seqs)
            total = self.term[p, c, self.d].astype(f32)
            for k in range(len(self.copies)):
                total = total + self.land[k, p, c].astype(f32)
            self.acc[c, p] = total.astype(bf16)
            return none

        lax.fori_loop(0, parts * seqs, one, 0)

    def finish(self):
        for c in self.copies:
            c.wait_send()


class RowSum:
    def __init__(self, acc, shares, land, total, sems, f, s):
        self.acc, self.shares, self.land, self.total = acc, shares, land, total
        self.f, self.s = f, s
        self.seqs, self.parts = seqs, parts = acc.shape[:2]
        to = (lax.rem(s + 1, seqs), lax.rem(s + seqs - 1, seqs))
        z_send, z_recv, a_send, a_recv = sems
        self.blocks, self.sends, self.comes, self.two = [], [], [], []
        for t in range(1, seqs):
            blocks = (lax.rem(s + seqs - t, seqs), lax.rem(s + t, seqs))
            self.blocks.append(blocks)
            self.sends.append((s < t, s > seqs - 1 - t))
            self.comes.append(((s > 0) & (s - 1 < t), (s < seqs - 1) & (s + 1 > seqs - 1 - t)))
            self.two.append(
                [
                    push(
                        acc.at[blocks[i]],
                        land.at[t - 1, i],
                        z_send.at[t - 1, i],
                        z_recv.at[t - 1, i],
                        {"seq": to[i]},
                    )
                    for i in range(2)
                ]
            )
        self.three = [
            push(total.at[p], shares.at[f], a_send.at[i], a_recv.at[i], {"feat": p})
            for i, p in enumerate(peers(f))
        ]

    def add(self, into, t, i):
        @pl.when(self.comes[t - 1][i])
        def _():
            self.two[t - 1][i].wait_recv()

            def one(p, none):
                into[p] = (
                    into[p].astype(f32) + self.land[t - 1, i, p].astype(f32)
                ).astype(bf16)
                return none

            lax.fori_loop(0, self.parts, one, 0)

    def step(self, t):
        for i in range(2):
            if t > 1:
                self.add(self.acc.at[self.blocks[t - 1][i]], t - 1, i)
            pl.when(self.sends[t - 1][i])(self.two[t - 1][i].start)

    def over_feat(self):
        self.total[...] = self.acc[self.s]
        for i in range(2):
            self.add(self.total, self.seqs - 1, i)
        self.shares[self.f] = self.total[self.f]
        for c in self.three:
            c.start()

    def arrive(self):
        for c in self.three:
            c.wait_recv()

    def finish(self):
        for sends, copies in zip(self.sends, self.two):
            for i in range(2):
                pl.when(sends[i])(copies[i].wait_send)
        for c in self.three:
            c.wait_send()


def sibling_scratch(shape):
    parts, seqs, dps, rows, wide = shape
    others = max(dps - 1, 1)
    dma = pltpu.SemaphoreType.DMA
    return [
        pltpu.VMEM(shape, bf16),
        pltpu.VMEM((seqs, parts, rows, wide), bf16),
        pltpu.VMEM((others, parts, seqs, rows, wide), bf16),
        dma((others,)),
        dma((others,)),
    ]


def row_sum_scratch(shape):
    seqs, parts, rows, wide = shape
    dma = pltpu.SemaphoreType.DMA
    return [
        pltpu.VMEM((parts, rows, wide), bf16),
        pltpu.VMEM((seqs - 1, 2, parts, rows, wide), bf16),
        pltpu.VMEM((parts, rows, wide), bf16),
        dma((seqs - 1, 2)),
        dma((seqs - 1, 2)),
        dma((3,)),
        dma((3,)),
    ]


def opening_kernel(
    seqs,
    dps,
    tok_ref,
    query_ref,
    key_ref,
    value_ref,
    out_ref,
    one_ref,
    two_ref,
    x_ref,
    w_ref,
    g_ref,
    o_ref,
    pack,
    opack,
    tile,
    x_send,
    x_recv,
    a_send,
    a_recv,
    z_send,
    z_recv,
    d_send,
    d_recv,
    local_sem,
):
    f, s, d = lax.axis_index("feat"), lax.axis_index("seq"), lax.axis_index("dp")
    parts, rows_each = pack.shape[0], pack.shape[1]
    near = peers(f)
    columns = [lax.rem(s + k, seqs) for k in range(1, seqs)]
    others = [lax.rem(d + k, dps) for k in range(1, dps)]
    stay = pltpu.make_async_copy(tok_ref, x_ref.at[f], local_sem.at[0])
    stay.start()
    first = 0
    for ref in (query_ref, key_ref, value_ref):
        each = ref.shape[1] // parts
        for p in range(parts):
            pack[p, :, first : first + each] = ref[:, p * each : (p + 1) * each]
        first += each
    tile[...] = jnp.zeros_like(tile)
    tile[0:1, :rows_each] = one_ref[...].astype(f32)
    tile[1:2, :rows_each] = two_ref[...].astype(f32)
    outs = (w_ref, g_ref)
    own = [
        pltpu.make_async_copy(pack.at[f], w_ref.at[f, s, d], local_sem.at[1]),
        pltpu.make_async_copy(tile, g_ref.at[f, s, d], local_sem.at[2]),
    ]
    for c in own:
        c.start()
    greet(
        square_targets(f) + [{"seq": c} for c in columns] + [{"dp": o} for o in others]
    )
    shares = [
        [
            push(pack.at[p], w_ref.at[f, s, d], a_send.at[0, i], a_recv.at[0, i], {"feat": p}),
            push(tile, g_ref.at[f, s, d], a_send.at[1, i], a_recv.at[1, i], {"feat": p}),
        ]
        for i, p in enumerate(near)
    ]
    for pair in shares:
        for c in pair:
            c.start()
    gather = SquareGather(x_ref, f, x_send, x_recv, tok_ref)
    gather.start()
    each = out_ref.shape[1] // parts
    for p in range(parts):
        opack[p] = out_ref[:, p * each : (p + 1) * each]
    own_out = pltpu.make_async_copy(opack.at[f], o_ref.at[f], local_sem.at[3])
    own_out.start()
    out_shares = [
        push(opack.at[p], o_ref.at[f], a_send.at[2, i], a_recv.at[2, i], {"feat": p})
        for i, p in enumerate(near)
    ]
    for c in out_shares:
        c.start()
    for c in own:
        c.wait()

    chunks = (f,) + near

    def to_column(n, k):
        return [
            push(
                ref.at[chunks[n], s, d],
                ref.at[chunks[n], s, d],
                z_send.at[j, k - 1, n],
                z_recv.at[j, k - 1, n],
                {"seq": columns[k - 1]},
            )
            for j, ref in enumerate(outs)
        ]

    def to_sibling(n, k):
        back = lax.rem(s + seqs - k, seqs)
        return [
            push(
                ref.at[chunks[n], back, d],
                ref.at[chunks[n], back, d],
                d_send.at[j, o, k, n],
                d_recv.at[j, o, k, n],
                {"dp": other},
            )
            for j, ref in enumerate(outs)
            for o, other in enumerate(others)
        ]

    def start_all(copies):
        for c in copies:
            c.start()

    for n in range(parts):
        if n:
            for c in shares[n - 1]:
                c.wait_recv()
        for k in range(1, seqs):
            start_all(to_column(n, k))
        start_all(to_sibling(n, 0))
    for n in range(parts):
        for k in range(1, seqs):
            for c in to_column(n, k):
                c.wait_recv()
            start_all(to_sibling(n, k))
    gather.relay()
    for n in range(parts):
        for k in range(seqs):
            for c in to_sibling(n, k):
                c.wait_recv()
    for n in range(parts):
        for k in range(seqs):
            for c in to_sibling(n, k):
                c.wait_send()
        for k in range(1, seqs):
            for c in to_column(n, k):
                c.wait_send()
    for pair in shares:
        for c in pair:
            c.wait_send()
    stay.wait()
    own_out.wait()
    for c in out_shares:
        c.wait_recv()
    for c in out_shares:
        c.wait_send()
    gather.finish()


def in_place(count):
    return [pl.BlockSpec(memory_space=pltpu.HBM)] * count


def opening(own, w_query, w_key, w_value, w_out, gain_one, gain_two):
    parts, seqs, dps = (lax.axis_size(a) for a in ALL)
    block, width = own.shape
    rows_each = w_query.shape[0]
    wide = (w_query.shape[1] + w_key.shape[1] + w_value.shape[1]) // parts
    others = max(dps - 1, 1)
    dma = pltpu.SemaphoreType.DMA
    out_wide = w_out.shape[1] // parts
    x_all, w_all, g_all, o_own = pl.pallas_call(
        functools.partial(opening_kernel, seqs, dps),
        out_shape=(
            jax.ShapeDtypeStruct((parts, block, width), bf16),
            jax.ShapeDtypeStruct((parts, seqs, dps, rows_each, wide), bf16),
            jax.ShapeDtypeStruct((parts, seqs, dps, 8, HV), f32),
            jax.ShapeDtypeStruct((parts, rows_each, out_wide), bf16),
        ),
        in_specs=in_place(1) + whole_vmem(6),
        out_specs=tuple(in_place(4)),
        scratch_shapes=[
            pltpu.VMEM((parts, rows_each, wide), bf16),
            pltpu.VMEM((parts, rows_each, out_wide), bf16),
            pltpu.VMEM((8, HV), f32),
            dma((6,)),
            dma((6,)),
            dma((3, 3)),
            dma((3, 3)),
            dma((2, seqs - 1, parts)),
            dma((2, seqs - 1, parts)),
            dma((2, others, seqs, parts)),
            dma((2, others, seqs, parts)),
            dma((4,)),
        ],
        compiler_params=pltpu.CompilerParams(collective_id=2, has_side_effects=True, vmem_limit_bytes=60 << 20),
        cost_estimate=pl.CostEstimate(flops=0, bytes_accessed=1 << 20, transcendentals=0),
        name="opening",
    )(own, w_query, w_key, w_value, w_out, gain_one, gain_two)
    gains = g_all[..., :2, :rows_each].transpose(3, 0, 1, 2, 4).reshape(2, width)
    return x_all, w_all.reshape(width, wide), gains, o_own


def inverse_rms(values):
    return lax.rsqrt(jnp.mean(values * values, axis=-1, keepdims=True) + epsilon)


def norm_back(grad, unit, inverse, gain):
    scaled = grad * gain
    return (scaled - unit * jnp.mean(scaled * unit, axis=-1, keepdims=True)) * inverse


class ByShare:
    def __init__(self, ref):
        self.ref = ref

    def tile(self, i, size):
        block = self.ref[:, i]
        return block.reshape(size, block.shape[2])


class ByTiles:
    def __init__(self, src, ref, sem, tile):
        self.ref = ref
        self.fills = [
            pltpu.make_async_copy(
                src.at[pl.ds(i * tile, tile)], ref.at[pl.ds(i * tile, tile)], sem.at[i]
            )
            for i in range(ref.shape[0] // tile)
        ]

    def tile(self, i, size):
        return self.ref[pl.ds(pl.multiple_of(i * size, size), size), :]


def product_tiles(part, slot, pairs, tile, first=False):
    def one(i, none):
        cols = pl.ds(pl.multiple_of(i * tile, tile), tile)
        total = None
        for rows, weights in pairs:
            if hasattr(weights, "tile"):
                block = weights.tile(i, tile)
            else:
                block = weights[cols, :]
            term = dot_nt(rows[slot], block)
            total = term if total is None else total + term
        part[slot, :, cols] = total.astype(bf16)
        return none

    if first:
        for i in range(part.shape[2] // tile):
            for _, weights in pairs:
                weights.fills[i].wait()
            one(i, 0)
    else:
        lax.fori_loop(0, part.shape[2] // tile, one, 0)


def summed_products(part, land, f, pairs, send_sem, recv_sem, chunks=1, beside=(), first=False):
    side, above, across = peers(f)
    rows = part.shape[1] // chunks
    rings = [
        SquareSum(
            part, land.at[c], f, send_sem.at[c], recv_sem.at[c], base=c * rows, rows=rows
        )
        for c in range(chunks)
    ]
    product_tiles(part, across, pairs, 512, first)
    for ring in rings:
        ring.start_cross()
    beside = iter(beside)
    next(beside, int)()
    product_tiles(part, side, pairs, 512)
    for ring in rings:
        ring.near[0].start()
    product_tiles(part, above, pairs, 512)
    for ring in rings:
        ring.near[1].start()
    next(beside, int)()
    rings[0].relay()
    product_tiles(part, f, pairs, 512)
    next(beside, int)()
    for ring in rings[1:]:
        ring.relay()
    return rings


def sum_then_gather(rings, finish_rows, slots, f, send_sem, recv_sem):
    gathers = []
    for c, ring in enumerate(rings):
        ring.arrive()
        by_rows(ring, finish_rows)
        gather = SquareGather(
            slots, f, send_sem.at[c], recv_sem.at[c], base=ring.base, rows=2 * ring.half
        )
        gather.start()
        gathers.append(gather)
    for ring in rings:
        ring.finish()
    return gathers


def by_rows(ring, body, step=16):
    for half in (0, 1):

        def one(i, none):
            start = pl.multiple_of(i * step, step)
            rows = pl.ds(
                pl.multiple_of(ring.base + half * ring.half + i * step, step), step
            )
            body(rows, ring.total(half, pl.ds(start, step)))
            return none

        lax.fori_loop(0, ring.half // step, one, 0)


def branch_kernel(
    att_hbm,
    w_hbm,
    tok_hbm,
    gain_ref,
    rows_hbm,
    res_hbm,
    rows_ref,
    res_ref,
    att_ref,
    w_ref,
    tok_ref,
    part,
    land,
    s_send,
    s_recv,
    g_send,
    g_recv,
    load_sem,
    store_sem,
):
    f = lax.axis_index("feat")
    loads = Loads(((att_hbm, att_ref), (w_hbm, w_ref), (tok_hbm, tok_ref)), load_sem).start()
    greet(square_targets(f))
    loads.wait()
    rings = summed_products(
        part, land, f, [(att_ref, ByShare(w_ref))], s_send, s_recv, land.shape[0]
    )

    def finish_rows(rows, total):
        residual = tok_ref[rows, :].astype(f32) + total
        res_ref[rows, :] = residual
        rows_ref[f, rows, :] = (residual * inverse_rms(residual) * gain_ref[...]).astype(bf16)

    gathers = sum_then_gather(rings, finish_rows, rows_ref, f, g_send, g_recv)
    stores = [pltpu.make_async_copy(res_ref, res_hbm, store_sem.at[0])]
    stores[0].start()

    def store(slot):
        c = pltpu.make_async_copy(rows_ref.at[slot], rows_hbm.at[slot], store_sem.at[len(stores)])
        c.start()
        stores.append(c)

    side, above, across = peers(f)
    store(f)
    for gather in gathers:
        gather.relay()
    for gather in gathers:
        gather.near()
    store(side)
    store(above)
    for gather in gathers:
        gather.far()
    store(across)
    for gather in gathers:
        gather.sent()
    for c in stores:
        c.wait()


CHUNKS = 2


def square_scratch(parts, block, width, chunks=CHUNKS):
    dma = pltpu.SemaphoreType.DMA
    return [
        pltpu.VMEM((parts, block, width), bf16),
        pltpu.VMEM((chunks, 6, block // 2 // chunks, width), bf16),
        dma((chunks, 6)),
        dma((chunks, 6)),
    ]


def branch_step(att, out_w, own, gain_two):
    parts, block, _ = att.shape
    width = own.shape[1]
    dma = pltpu.SemaphoreType.DMA
    return pl.pallas_call(
        branch_kernel,
        out_shape=(
            jax.ShapeDtypeStruct((parts, block, width), bf16),
            jax.ShapeDtypeStruct((block, width), f32),
        ),
        in_specs=in_place(3) + whole_vmem(1),
        out_specs=tuple(in_place(2)),
        scratch_shapes=[pltpu.VMEM((parts, block, width), bf16), pltpu.VMEM((block, width), f32)]
        + vmem_like(att, out_w, own)
        + square_scratch(parts, block, width)
        + [dma((CHUNKS, 6)), dma((CHUNKS, 6)), dma((3,)), dma((1 + parts,))],
        compiler_params=pltpu.CompilerParams(
            collective_id=3, has_side_effects=True, vmem_limit_bytes=60 << 20
        ),
        cost_estimate=pl.CostEstimate(flops=0, bytes_accessed=1 << 20, transcendentals=0),
        name="branch_step",
    )(att, out_w, own, gain_two)


def rows_back_kernel(
    grads_hbm,
    wg_hbm,
    wu_hbm,
    res_hbm,
    cot_hbm,
    gain_ref,
    mixed_hbm,
    wd_hbm,
    wo_hbm,
    all_hbm,
    gres_hbm,
    gsum_ref,
    down_hbm,
    ga_hbm,
    all_ref,
    gres_ref,
    down_ref,
    ga_ref,
    gg_ref,
    gu_ref,
    res_ref,
    cot_ref,
    part,
    land,
    wg,
    wu,
    mixed,
    wd,
    wo,
    s_send,
    s_recv,
    g_send,
    g_recv,
    local_sem,
    tile_sem,
    load_sem,
    store_sem,
):
    f = lax.axis_index("feat")
    rows_in = Loads(((grads_hbm.at[0], gg_ref), (grads_hbm.at[1], gu_ref)), load_sem).start()
    weights = [
        ByTiles(src, dst, tile_sem.at[i], 512)
        for i, (src, dst) in enumerate(((wg_hbm, wg), (wu_hbm, wu)))
    ]
    for pair in zip(*(w.fills for w in weights)):
        for c in pair:
            c.start()
    fills = [
        pltpu.make_async_copy(src, dst, local_sem.at[i])
        for i, (src, dst) in enumerate(((mixed_hbm, mixed), (wd_hbm, wd), (wo_hbm, wo)))
    ]
    late_in = Loads(((res_hbm, res_ref), (cot_hbm, cot_ref)), load_sem.at[pl.ds(2, 2)]).start()
    for c in fills:
        c.start()
    greet(square_targets(f))
    rows_in.wait()
    pairs = [(gg_ref, weights[0]), (gu_ref, weights[1])]

    def down_products(slots):
        for p in slots:
            product_tiles(down_ref, p, [(mixed, wd)], 512)

    rings = summed_products(part, land, f, pairs, s_send, s_recv, land.shape[0], first=True)
    gsum_ref[...] = jnp.zeros_like(gsum_ref)
    late_in.wait()

    def finish_rows(rows, grad):
        residual = res_ref[rows, :]
        inverse = inverse_rms(residual)
        unit = residual * inverse
        gsum_ref[...] += jnp.sum(grad * unit, axis=0, keepdims=True)
        grad_res = cot_ref[rows, :].astype(f32) + norm_back(grad, unit, inverse, gain_ref[...])
        gres_ref[rows, :] = grad_res
        all_ref[f, rows, :] = grad_res.astype(bf16)

    gathers = sum_then_gather(rings, finish_rows, all_ref, f, g_send, g_recv)
    side, above, across = peers(f)

    def attended_grad(slot):
        blocks = ByShare(wo)
        size = all_ref.shape[2] // wo.shape[1]
        total = None
        for i in range(wo.shape[1]):
            term = dot(all_ref[slot, :, i * size : (i + 1) * size], blocks.tile(i, size))
            total = term if total is None else total + term
        ga_ref[slot] = total
        store(ga_ref.at[slot], ga_hbm.at[slot])
        store(all_ref.at[slot], all_hbm.at[slot])

    stores = []

    def store(src, dst):
        c = pltpu.make_async_copy(src, dst, store_sem.at[len(stores)])
        c.start()
        stores.append(c)

    store(gres_ref, gres_hbm)
    for c in fills:
        c.wait()
    attended_grad(f)
    down_products(range(2))
    for gather in gathers:
        gather.relay()
    down_products(range(2, part.shape[0]))
    store(down_ref, down_hbm)
    for gather in gathers:
        gather.near()
    attended_grad(side)
    attended_grad(above)
    for gather in gathers:
        gather.far()
    attended_grad(across)
    for gather in gathers:
        gather.sent()
    for c in stores:
        c.wait()


def rows_back(
    grads, gate_w, up_w, residual, cot_own, gain_two, mixed, down_w, out_w
):
    _, parts, block, hidden = grads.shape
    width = residual.shape[1]
    dma = pltpu.SemaphoreType.DMA
    return pl.pallas_call(
        rows_back_kernel,
        out_shape=(
            jax.ShapeDtypeStruct((parts, block, width), bf16),
            jax.ShapeDtypeStruct((block, width), f32),
            jax.ShapeDtypeStruct((1, width), f32),
            jax.ShapeDtypeStruct((parts, block, width), bf16),
            jax.ShapeDtypeStruct((parts, block, out_w.shape[3]), f32),
        ),
        in_specs=in_place(5) + whole_vmem(1) + in_place(3),
        out_specs=tuple(in_place(2) + whole_vmem(1) + in_place(2)),
        scratch_shapes=[
            pltpu.VMEM((parts, block, width), bf16),
            pltpu.VMEM((block, width), f32),
            pltpu.VMEM((parts, block, width), bf16),
            pltpu.VMEM((parts, block, out_w.shape[3]), f32),
        ]
        + [pltpu.VMEM((parts, block, hidden), bf16)] * 2
        + vmem_like(residual, cot_own)
        + square_scratch(parts, block, width)[:2]
        + [
            pltpu.VMEM((width, hidden), bf16),
            pltpu.VMEM((width, hidden), bf16),
            pltpu.VMEM((parts, block, hidden), bf16),
            pltpu.VMEM((width, hidden), bf16),
            pltpu.VMEM(out_w.shape, bf16),
        ]
        + [dma((CHUNKS, 6))] * 4
        + [dma((3,)), dma((2, width // 512)), dma((4,)), dma((2 * parts + 2,))],
        compiler_params=pltpu.CompilerParams(
            collective_id=4, has_side_effects=True, vmem_limit_bytes=60 << 20
        ),
        cost_estimate=pl.CostEstimate(flops=0, bytes_accessed=1 << 20, transcendentals=0),
        name="rows_back",
    )(grads, gate_w, up_w, residual, cot_own, gain_two, mixed, down_w, out_w)


def closing_kernel(
    seqs,
    dps,
    dqkv_hbm,
    w_hbm,
    tok_hbm,
    gres_hbm,
    gain_ref,
    gsum_two_ref,
    normed_hbm,
    oacc_hbm,
    down_hbm,
    output_hbm,
    x_ref,
    tile_ref,
    query_ref,
    key_ref,
    value_ref,
    ograd_ref,
    part,
    land,
    s_send,
    s_recv,
    gsum,
    cut,
    came,
    mid,
    tail,
    c_send,
    c_recv,
    d_send,
    d_recv,
    dqkv_ref,
    w_ref,
    tok_ref,
    gres_ref,
    normed_ref,
    oacc_ref,
    load_sem,
    first_sem,
    term_ref,
    acc_ref,
    sib_land,
    sib_send,
    sib_recv,
    *sum_scratch,
):
    begin = Loads(((oacc_hbm, oacc_ref),), first_sem).start()
    loads = Loads(
        (
            (dqkv_hbm, dqkv_ref),
            (normed_hbm, normed_ref),
            (w_hbm, w_ref),
            (tok_hbm, tok_ref),
            (gres_hbm, gres_ref),
        ),
        load_sem,
    ).start()
    half = len(sum_scratch) // 2
    f, s, d = lax.axis_index("feat"), lax.axis_index("seq"), lax.axis_index("dp")
    parts = 4
    others = [lax.rem(d + k, dps) for k in range(1, dps)]
    circle = [
        (lax.rem(f + i, parts), lax.rem(s + j, seqs))
        for i in range(parts)
        for j in range(seqs)
        if i or j
    ]
    greet(
        [{"feat": a, "seq": b} for a, b in circle] + [{"dp": o} for o in others]
    )
    begin.wait()
    rows_sum = RowSum(acc_ref, *sum_scratch[:3], sum_scratch[3:half], f, s)
    out_sum = RowSum(oacc_ref, *sum_scratch[half : half + 3], sum_scratch[half + 3 :], f, s)
    out_sum.step(1)
    loads.wait()
    term_tiles(term_ref, normed_ref, dqkv_ref)
    sibling = SiblingSum(term_ref, acc_ref, sib_land, (sib_send, sib_recv), d, dps)
    sibling.start()
    out_sum.step(2)

    def over_seq():
        sibling.add()
        rows_sum.step(1)
        for t in range(3, seqs):
            out_sum.step(t)

    rings = summed_products(
        part, land, f, [(dqkv_ref, w_ref)], s_send, s_recv, land.shape[0], (over_seq,)
    )
    for t in range(2, seqs):
        rows_sum.step(t)
    gsum[...] = jnp.zeros_like(gsum)

    def finish_rows(rows, grad):
        values = tok_ref[rows, :].astype(f32)
        inverse = inverse_rms(values)
        unit = values * inverse
        gsum[...] += jnp.sum(grad * unit, axis=0, keepdims=True)
        x_ref[rows, :] = gres_ref[rows, :] + norm_back(grad, unit, inverse, gain_ref[...])

    for ring in rings:
        ring.arrive()
        by_rows(ring, finish_rows)
    for ring in rings:
        ring.finish()

    lanes = gsum.shape[1] // (parts * seqs)
    cut[...] = jnp.zeros_like(cut)
    for k in range(parts * seqs):
        cut[k, 0:1, :] = gsum[:, k * lanes : (k + 1) * lanes]
        cut[k, 1:2, :] = gsum_two_ref[:, k * lanes : (k + 1) * lanes]
    place = f * seqs + s
    sends = []
    for i, (a, b) in enumerate(circle):
        sends.append(
            push(
                cut.at[a * seqs + b],
                came.at[i],
                c_send.at[i],
                c_recv.at[i],
                {"feat": a, "seq": b},
            )
        )
    for c in sends:
        c.start()
    total = cut[place]
    for c in sends:
        c.wait_recv()
    for i in range(len(circle)):
        total = total + came[i]
    mid[...] = total
    last = [
        push(mid, tail.at[k], d_send.at[k], d_recv.at[k], {"dp": o})
        for k, o in enumerate(others)
    ]
    for c in last:
        c.start()
    for c in last:
        c.wait_recv()
    for k in range(len(others)):
        total = total + tail[k]
    tile_ref[...] = total
    out_sum.over_feat()
    rows_sum.over_feat()
    rows_sum.arrive()
    first = 0
    for ref in (query_ref, key_ref, value_ref):
        each = ref.shape[1] // parts
        for p in range(parts):
            piece = rows_sum.shares[p, :, first : first + each]
            ref[:, p * each : (p + 1) * each] = piece.astype(f32)
        first += each
    rows_sum.finish()
    sibling.finish()
    out_sum.arrive()
    each = ograd_ref.shape[1] // parts
    for p in range(parts):
        ograd_ref[:, p * each : (p + 1) * each] = out_sum.shares[p].astype(f32)
    out_sum.finish()
    for c in sends + last:
        c.wait_send()


def closing(dqkv, qkv_w, own, grad_residual, gain_one, gain_two_sum, normed, out_acc, down_grad, output):
    parts, seqs, dps = (lax.axis_size(a) for a in ALL)
    block, width = own.shape
    others = max(dps - 1, 1)
    lanes = width // (parts * seqs)
    circle = parts * seqs - 1
    rows_each = out_acc.shape[2]
    by_row = (parts, seqs, dps, rows_each, dqkv.shape[2])
    acc_shape = out_acc.shape[:3] + dqkv.shape[2:]
    dma = pltpu.SemaphoreType.DMA
    return pl.pallas_call(
        functools.partial(closing_kernel, seqs, dps),
        out_shape=(
            jax.ShapeDtypeStruct((block, width), f32),
            jax.ShapeDtypeStruct((8, lanes), f32),
            jax.ShapeDtypeStruct((rows_each, HEADS * FDIM), f32),
            jax.ShapeDtypeStruct((rows_each, HEADS * FDIM), f32),
            jax.ShapeDtypeStruct((rows_each, HEADS * HV), f32),
            jax.ShapeDtypeStruct((rows_each, HEADS * HV), f32),
        ),
        in_specs=in_place(4) + whole_vmem(2) + in_place(4),
        out_specs=tuple(whole_vmem(6)),
        scratch_shapes=square_scratch(parts, block, width)
        + [
            pltpu.VMEM((1, width), f32),
            pltpu.VMEM((parts * seqs, 8, lanes), f32),
            pltpu.VMEM((circle, 8, lanes), f32),
            pltpu.VMEM((8, lanes), f32),
            pltpu.VMEM((others, 8, lanes), f32),
            dma((circle,)),
            dma((circle,)),
            dma((others,)),
            dma((others,)),
        ]
        + vmem_like(dqkv, qkv_w, own, grad_residual, normed, out_acc)
        + [dma((5,)), dma((1,))]
        + sibling_scratch(by_row)
        + row_sum_scratch(acc_shape)
        + row_sum_scratch(out_acc.shape),
        compiler_params=pltpu.CompilerParams(
            collective_id=5, has_side_effects=True, vmem_limit_bytes=60 << 20
        ),
        cost_estimate=pl.CostEstimate(flops=0, bytes_accessed=1 << 20, transcendentals=0),
        name="closing",
    )(dqkv, qkv_w, own, grad_residual, gain_one, gain_two_sum, normed, out_acc, down_grad, output)


def local(
    tokens,
    segments,
    norm1_gain,
    norm2_gain,
    w_query,
    w_key,
    w_value,
    w_out,
    w_gate,
    w_up,
    w_down,
    cotangent,
):
    parts = lax.axis_size("feat")
    heads = HEADS // parts
    block, width = tokens.shape[2], tokens.shape[3]
    rows_total = parts * block
    rows_each = w_query.shape[0]
    own = tokens.reshape(block, width)
    cot_own = cotangent.reshape(block, width)

    x_all, qkv_w, gains, out_share = opening(
        own, w_query, w_key, w_value, w_out.T, norm1_gain[None], norm2_gain[None]
    )
    qkv_width = qkv_w.shape[1]
    gate_w = lax.all_gather(w_gate, ("seq", "dp"), axis=0, tiled=True)
    gain_one, gain_two = gains[0:1], gains[1:2]

    x_wide = x_all.astype(f32).reshape(rows_total, width)
    normed = (x_wide * inverse_rms(x_wide) * gain_one).astype(bf16)
    qkv = dot(normed, qkv_w).astype(bf16).reshape(parts, block, qkv_width)
    qkv, gate_w, out_share, w_up, w_down = lax.optimization_barrier(
        (qkv, gate_w, out_share, w_up, w_down)
    )
    out_w = lax.all_gather(out_share[None], ("seq", "dp"), axis=0, tiled=True)
    up_w = lax.all_gather(w_up, ("seq", "dp"), axis=0, tiled=True)
    down_w = lax.all_gather(w_down.T, ("seq", "dp"), axis=0, tiled=True)
    segment = segments.reshape(parts, block).astype(f32)
    segc, segr = segment[:, :, None], segment[:, None, :]
    tables = feature_tables(heads)
    att, rden, carry, csum, cot_all = attention_forward(qkv, segc, segr, tables, cot_own, heads)
    cot_all = cot_all.reshape(rows_total, width)
    rows_all, residual = branch_step(att, out_w, own, gain_two)
    rows_all = rows_all.reshape(rows_total, width)

    gate_out = dot(rows_all, gate_w)
    up_out = dot(rows_all, up_w)
    sig = jax.nn.sigmoid(gate_out)
    silu = gate_out * sig
    mixed = (silu * up_out).astype(bf16)
    down_term = dot_tn(cot_all, mixed).astype(bf16)
    mixed, cot_late, down_term = lax.optimization_barrier((mixed, cot_all, down_term))
    grad_mixed = dot(cot_late, down_w)
    grads = jnp.stack(
        [grad_mixed * up_out * sig * (1.0 + gate_out * (1.0 - sig)), grad_mixed * silu]
    ).astype(bf16)

    def summed(term, dim):
        return lax.psum_scatter(term, ("seq", "dp"), scatter_dimension=dim, tiled=True)

    both_term = jnp.einsum("xtf,td->xfd", grads, rows_all, preferred_element_type=f32).astype(bf16)
    grads, both_term = lax.optimization_barrier((grads, both_term))
    down_sum, both_sum = summed(down_term, 0), summed(both_term, 2)

    by_device = (parts, block, -1)
    branch_all, grad_residual, gain_two_sum, down, ga = rows_back(
        grads.reshape((2,) + by_device),
        gate_w,
        up_w,
        residual,
        cot_own,
        gain_two,
        mixed.reshape(by_device),
        down_w,
        out_w,
    )
    dqkv, output, out_acc = attention_backward(
        qkv,
        segc,
        segr,
        tables,
        att,
        rden,
        carry,
        csum,
        ga,
        down,
        residual,
        branch_all,
        heads,
    )
    output = output.astype(bf16)
    down_grad = down_sum.T.astype(f32)
    x_grad, gain_grads, query_grad, key_grad, value_grad, out_grad = closing(
        dqkv,
        qkv_w,
        own,
        grad_residual,
        gain_one,
        gain_two_sum,
        normed.reshape(parts, block, width),
        out_acc,
        down_grad,
        output,
    )
    gain_each = gain_grads.shape[1] // lax.axis_size("dp")
    gain_grads = lax.dynamic_slice_in_dim(
        gain_grads, lax.axis_index("dp") * gain_each, gain_each, axis=1
    )
    return (
        output.reshape(tokens.shape),
        x_grad.reshape(tokens.shape),
        gain_grads[0],
        gain_grads[1],
        query_grad,
        key_grad,
        value_grad,
        out_grad.T,
        both_sum[0].T.astype(f32),
        both_sum[1].T.astype(f32),
        down_grad,
    )


def solution(mesh):
    placed = (
        P("feat", "dp", "seq", None),
        P(None, "dp", "seq"),
        P(ALL),
        P(ALL),
        P(ALL, None),
        P(ALL, None),
        P(ALL, None),
        P(None, ALL),
        P(("seq", "dp"), "feat"),
        P(("seq", "dp"), "feat"),
        P("feat", ("seq", "dp")),
        P("feat", "dp", "seq", None),
    )
    return jax.shard_map(
        local,
        mesh=mesh,
        in_specs=placed,
        out_specs=(
            P("feat", "dp", "seq", None),
            P("feat", "dp", "seq", None),
            P(ALL),
            P(ALL),
            P(ALL, None),
            P(ALL, None),
            P(ALL, None),
            P(None, ALL),
            P(("seq", "dp"), "feat"),
            P(("seq", "dp"), "feat"),
            P("feat", ("seq", "dp")),
        ),
        check_vma=False,
    )
```

```python
import functools

import jax
import jax.numpy as jnp
import numpy as np
from jax import lax
from jax.experimental import pallas as pl
from jax.experimental.pallas import tpu as pltpu
from jax.sharding import PartitionSpec as P

HEADS = 16
FDIM = 16
HV = 128
STATE = 160
LANES = 256
epsilon = 1e-05
MESH = pl.DeviceIdType.MESH
ALL = ("feat", "seq", "dp")
f32 = jnp.float32
bf16 = jnp.bfloat16


def dot(a, b):
    return lax.dot_general(a, b, (((1,), (0,)), ((), ())), preferred_element_type=f32)


def dot_nt(a, b):
    return lax.dot_general(a, b, (((1,), (1,)), ((), ())), preferred_element_type=f32)


def dot_tn(a, b):
    return lax.dot_general(a, b, (((0,), (0,)), ((), ())), preferred_element_type=f32)


def feature_tables(heads):
    pairs = [(i, j) for i in range(FDIM) for j in range(i, FDIM)]
    left = np.zeros((heads, heads * FDIM, LANES), np.float32)
    right = np.zeros((heads, heads * FDIM, LANES), np.float32)
    rows = np.zeros((8, LANES), np.float32)
    for h in range(heads):
        for p, (i, j) in enumerate(pairs):
            left[h, h * FDIM + i, p] = 1.0
            right[h, h * FDIM + j, p] = 1.0
            rows[2, p] = 0.25 / 2.0**0.5 if i == j else 0.25
        for i in range(FDIM):
            p = len(pairs) + i
            left[h, h * FDIM + i, p] = 1.0
            rows[1, p] = 1.0
            rows[2, p] = 0.5
        p = len(pairs) + FDIM
        rows[0, p] = rows[1, p] = rows[2, p] = 1.0
    return jnp.asarray(left, bf16), jnp.asarray(right, bf16), jnp.asarray(rows)


def both_sides(entries, h, left_ref, right_ref, rows_ref):
    one = dot(entries, left_ref[h]) + rows_ref[0:1, :]
    two = dot(entries, right_ref[h]) + rows_ref[1:2, :]
    return one, two * rows_ref[2:3, :]


def features(entries, h, left_ref, right_ref, rows_ref):
    one, two = both_sides(entries, h, left_ref, right_ref, rows_ref)
    return one * two


def pull_features(grad, entries, h, left_ref, right_ref, rows_ref):
    one, two = both_sides(entries, h, left_ref, right_ref, rows_ref)
    scaled = rows_ref[2:3, :]
    return dot_nt((grad * two).astype(bf16), left_ref[h]) + dot_nt(
        (grad * one * scaled).astype(bf16), right_ref[h]
    )


def only_head(entries, h):
    lane = lax.broadcasted_iota(jnp.int32, entries.shape, 1)
    keep = (lane >= h * FDIM) & (lane < (h + 1) * FDIM)
    return jnp.where(keep, entries, jnp.zeros_like(entries))


def padded_state(state):
    return jnp.concatenate([state, jnp.zeros((LANES - STATE, state.shape[1]), state.dtype)], 0)


def allowed_of(segc, segr):
    block = segc.shape[0]
    row = lax.broadcasted_iota(jnp.int32, (block, block), 0)
    col = lax.broadcasted_iota(jnp.int32, (block, block), 1)
    return (row >= col) & (segc == segr)


def forward_kernel(
    count,
    heads,
    qkv_ref,
    segc_ref,
    segr_ref,
    left_ref,
    right_ref,
    rows_ref,
    cot_ref,
    att_hbm,
    rden_hbm,
    carry_hbm,
    csum_hbm,
    cots_ref,
    att_ref,
    rden_ref,
    carry_ref,
    csum_ref,
    send_state,
    send_sum,
    part,
    send_sem,
    recv_sem,
    f_send,
    f_recv,
    local_sem,
    store_sem,
):
    place, f = lax.axis_index("seq"), lax.axis_index("feat")
    groups, block = qkv_ref.shape[0], qkv_ref.shape[1]
    width = heads * FDIM
    tables = (left_ref, right_ref, rows_ref)

    def stores(g):
        pairs = (
            (att_ref, att_hbm),
            (rden_ref, rden_hbm),
            (carry_ref, carry_hbm),
            (csum_ref, csum_hbm),
        )
        return Loads([(a.at[g], b.at[g]) for a, b in pairs], store_sem.at[g])

    def hop(g):
        target = {"seq": lax.rem(place + 1, count)}
        return [
            pltpu.make_async_remote_copy(
                src_ref=src.at[g],
                dst_ref=dst.at[g],
                send_sem=send_sem.at[i, g],
                recv_sem=recv_sem.at[i, g],
                device_id=target,
                device_id_type=MESH,
            )
            for i, (src, dst) in enumerate(((send_state, carry_ref), (send_sum, csum_ref)))
        ]

    def send(g):
        for copy in hop(g):
            copy.start()

    chain = [lax.rem(place + 1, count), lax.rem(place + count - 1, count)]
    stay = pltpu.make_async_copy(cot_ref, cots_ref.at[f], local_sem.at[0])
    stay.start()
    greet(square_targets(f) + [{"seq": c} for c in chain])
    gather = SquareGather(cots_ref, f, f_send, f_recv, cot_ref)
    gather.start()

    @pl.when(place == 0)
    def _():
        carry_ref[...] = jnp.zeros_like(carry_ref)
        csum_ref[...] = jnp.full_like(csum_ref, -1.0)

    def summarize(g, none):
        segc, segr = segc_ref[g], segr_ref[g]
        tail = segr[:, block - 1 : block]
        at_tail = (segc == tail).astype(f32)
        send_sum[g, heads : heads + 1, :] = jnp.broadcast_to(tail, (1, LANES))
        for h in range(heads):
            key = qkv_ref[g, :, width : 2 * width]
            value = qkv_ref[g, :, 2 * width + h * HV : 2 * width + (h + 1) * HV]
            phi = (features(key, h, *tables) * at_tail).astype(bf16)
            send_state[g, h] = dot_tn(phi, value)[:STATE].astype(bf16)
            ones = jnp.ones((8, block), bf16)
            send_sum[g, h : h + 1, :] = dot(ones, phi)[0:1]

        @pl.when(place == 0)
        def _():
            send(g)

        return none

    lax.fori_loop(0, groups, summarize, 0)
    def join(g, none):
        for copy in hop(g):
            copy.wait_recv()
        segr = segr_ref[g]
        mark = csum_ref[g, heads : heads + 1, 0:1]
        head, tail = segr[:, 0:1], segr[:, block - 1 : block]
        whole = ((head == tail) & (head == mark)).astype(f32)
        for h in range(heads):
            send_state[g, h] = (
                send_state[g, h].astype(f32) + whole * carry_ref[g, h].astype(f32)
            ).astype(bf16)
            send_sum[g, h : h + 1, :] = (
                send_sum[g, h : h + 1, :] + whole * csum_ref[g, h : h + 1, :]
            )
        send(g)
        return none

    def attend(g, none):
        segc, segr = segc_ref[g], segr_ref[g]
        allowed = allowed_of(segc, segr)
        for h in range(heads):
            query = only_head(qkv_ref[g, :, 0:width], h)
            key = qkv_ref[g, :, width : 2 * width]
            value = qkv_ref[g, :, 2 * width + h * HV : 2 * width + (h + 1) * HV]
            c = dot_nt(query, key)
            kernel = jnp.where(allowed, 1.0 + c * (0.25 + c * 0.03125), 0.0).astype(bf16)
            wide = jnp.concatenate([value, jnp.ones_like(value)], axis=1)
            part[g, h] = dot(kernel, wide)

        @pl.when((place > 0) & (place < count - 1) & (g == place - 1))
        def _():
            lax.fori_loop(0, groups, join, 0)

        return none

    lax.fori_loop(0, groups, attend, 0)
    gather.relay()

    def carry_on(g, none):
        segc = segc_ref[g]

        @pl.when(place == count - 1)
        def _():
            for copy in hop(g):
                copy.wait_recv()

        mark = csum_ref[g, heads : heads + 1, 0:1]
        carried = (segc == mark).astype(f32)
        for h in range(heads):
            phi = features(qkv_ref[g, :, 0:width], h, *tables) * carried
            state = padded_state(carry_ref[g, h])
            both = part[g, h]
            numer = both[:, :HV] + dot(phi.astype(bf16), state)
            denom = both[:, HV:] + jnp.sum(
                phi * csum_ref[g, h : h + 1, :], axis=1, keepdims=True
            )
            inverse = 1.0 / denom
            att_ref[g, :, h * HV : (h + 1) * HV] = (numer * inverse).astype(bf16)
            rden_ref[g, :, h * HV : (h + 1) * HV] = inverse
        stores(g).start()
        return none

    lax.fori_loop(0, groups, carry_on, 0)

    @pl.when(place < count - 1)
    def _():
        def finish(g, none):
            for copy in hop(g):
                copy.wait_send()
            return none

        lax.fori_loop(0, groups, finish, 0)

    stay.wait()
    gather.finish()

    def stored(g, none):
        stores(g).wait()
        return none

    lax.fori_loop(0, groups, stored, 0)


def backward_kernel(
    count,
    heads,
    qkv_hbm,
    segc_ref,
    segr_ref,
    left_ref,
    right_ref,
    rows_ref,
    att_hbm,
    rden_hbm,
    carry_hbm,
    csum_ref,
    ga_hbm,
    down_ref,
    res_hbm,
    branch_hbm,
    out_hbm,
    final_ref,
    acc_hbm,
    qkv_ref,
    att_ref,
    rden_ref,
    carry_ref,
    ga_ref,
    res_ref,
    branch_ref,
    out_ref,
    gn,
    send_state,
    send_sum,
    recv_state,
    recv_sum,
    dkey,
    dvalue,
    terms,
    land,
    send_sem,
    recv_sem,
    f_send,
    f_recv,
    local_sem,
    load_sem,
    store_sem,
    term_ref,
    acc_ref,
    sib_land,
    sib_send,
    sib_recv,
):
    place, f, d = lax.axis_index("seq"), lax.axis_index("feat"), lax.axis_index("dp")
    dps = term_ref.shape[2]
    loads = Loads(
        (
            (qkv_hbm, qkv_ref),
            (ga_hbm, ga_ref),
            (rden_hbm, rden_ref),
            (att_hbm, att_ref),
            (carry_hbm, carry_ref),
            (res_hbm, res_ref),
        ),
        load_sem,
    ).start()
    late = Loads(((branch_hbm, branch_ref),), load_sem.at[pl.ds(6, 1)]).start()
    groups, block = qkv_ref.shape[0], qkv_ref.shape[1]
    width = heads * FDIM
    tables = (left_ref, right_ref, rows_ref)

    def hop(g):
        target = {"seq": lax.rem(place + count - 1, count)}
        return [
            pltpu.make_async_remote_copy(
                src_ref=src.at[g],
                dst_ref=dst.at[g],
                send_sem=send_sem.at[i, g],
                recv_sem=recv_sem.at[i, g],
                device_id=target,
                device_id_type=MESH,
            )
            for i, (src, dst) in enumerate(((send_state, recv_state), (send_sum, recv_sum)))
        ]

    def send(g):
        for copy in hop(g):
            copy.start()

    chain = [lax.rem(place + 1, count), lax.rem(place + count - 1, count)]
    greet(
        square_targets(f)
        + [{"seq": c} for c in chain]
        + [{"dp": lax.rem(d + o, dps)} for o in range(1, dps)]
    )
    fill = pltpu.make_async_copy(down_ref, terms, local_sem.at[0])
    fill.start()
    ring = SquareSum(terms, land, f, f_send, f_recv)
    loads.wait()

    def store(g):
        return pltpu.make_async_copy(out_ref.at[g], out_hbm.at[g], store_sem.at[g])


    @pl.when(place == count - 1)
    def _():
        recv_state[...] = jnp.zeros_like(recv_state)
        recv_sum[...] = jnp.full_like(recv_sum, -1.0)

    def summarize(g, none):
        segc, segr = segc_ref[g], segr_ref[g]
        head = segr[:, 0:1]
        at_head = (segc == head).astype(f32)
        send_sum[g, heads : heads + 1, :] = jnp.broadcast_to(head, (1, LANES))
        for h in range(heads):
            lanes = slice(h * HV, (h + 1) * HV)
            ga = ga_ref[g, :, lanes]
            inverse = rden_ref[g, :, lanes]
            numer = (ga * inverse).astype(bf16)
            dots = jnp.sum(ga * att_ref[g, :, lanes].astype(f32), axis=1, keepdims=True)
            lane = lax.broadcasted_iota(jnp.int32, (block, HV), 1)
            denom = jnp.where(lane == 0, -dots * inverse, 0.0).astype(bf16)
            gn[g, h, :, :HV] = numer
            gn[g, h, :, HV:] = denom
            phi = (features(qkv_ref[g, :, 0:width], h, *tables) * at_head).astype(bf16)
            send_state[g, h] = dot_tn(phi, numer)[:STATE].astype(bf16)
            send_sum[g, h : h + 1, :] = dot_tn(denom, phi)[0:1]

        @pl.when(place == count - 1)
        def _():
            send(g)

        return none

    lax.fori_loop(0, groups, summarize, 0)
    fill.wait()
    ring.start_cross()
    ring.start_near()

    def join(g, none):
        for copy in hop(g):
            copy.wait_recv()
        segr = segr_ref[g]
        mark = recv_sum[g, heads : heads + 1, 0:1]
        head, tail = segr[:, 0:1], segr[:, block - 1 : block]
        whole = ((head == tail) & (head == mark)).astype(f32)
        for h in range(heads):
            send_state[g, h] = (
                send_state[g, h].astype(f32) + whole * recv_state[g, h].astype(f32)
            ).astype(bf16)
            send_sum[g, h : h + 1, :] = (
                send_sum[g, h : h + 1, :] + whole * recv_sum[g, h : h + 1, :]
            )
        send(g)
        return none

    def pull(g, none):
        segc, segr = segc_ref[g], segr_ref[g]
        allowed = allowed_of(segc, segr)
        query_all = qkv_ref[g, :, 0:width]
        key_all = qkv_ref[g, :, width : 2 * width]
        carried = (segc == csum_ref[g, heads : heads + 1, 0:1]).astype(f32)
        dquery = jnp.zeros((block, width), f32)
        dkey_sum = jnp.zeros((block, width), f32)
        for h in range(heads):
            query, key = only_head(query_all, h), only_head(key_all, h)
            value = qkv_ref[g, :, 2 * width + h * HV : 2 * width + (h + 1) * HV]
            wide = jnp.concatenate([value, jnp.ones_like(value)], axis=1)
            both = gn[g, h]
            c = dot_nt(query, key_all)
            kernel = jnp.where(allowed, 1.0 + c * (0.25 + c * 0.03125), 0.0).astype(bf16)
            grad = jnp.where(allowed, dot_nt(both, wide), 0.0)
            grad_c = (grad * (0.25 + c * 0.0625)).astype(bf16)
            dvalue[g, h] = dot_tn(kernel, both[:, :HV])
            dkey_sum = dkey_sum + dot_tn(grad_c, query)
            dquery = dquery + dot(grad_c, key)
            state = padded_state(carry_ref[g, h])
            gphi = dot_nt(both[:, :HV], state) + both[:, HV : HV + 1].astype(f32) * csum_ref[
                g, h : h + 1, :
            ]
            dquery = dquery + pull_features(gphi * carried, query_all, h, *tables)
        out_ref[g, :, 0:width] = dquery.astype(bf16)
        dkey[g] = dkey_sum

        @pl.when((place > 0) & (place < count - 1) & (g == count - 2 - place))
        def _():
            lax.fori_loop(0, groups, join, 0)

        return none

    lax.fori_loop(0, groups, pull, 0)
    ring.relay()
    late.wait()
    term_tiles(term_ref, branch_ref, att_ref)
    sibling = SiblingSum(term_ref, acc_ref, sib_land, (sib_send, sib_recv), d, dps)
    sibling.start()

    def carry_back(g, none):
        segc = segc_ref[g]
        key_all = qkv_ref[g, :, width : 2 * width]

        @pl.when(place == 0)
        def _():
            for copy in hop(g):
                copy.wait_recv()

        mark = recv_sum[g, heads : heads + 1, 0:1]
        later = (segc == mark).astype(f32)
        total = dkey[g]
        for h in range(heads):
            value = qkv_ref[g, :, 2 * width + h * HV : 2 * width + (h + 1) * HV]
            state = padded_state(recv_state[g, h])
            phi = (features(key_all, h, *tables) * later).astype(bf16)
            dv = dvalue[g, h] + dot(phi, state)
            out_ref[g, :, 2 * width + h * HV : 2 * width + (h + 1) * HV] = dv.astype(bf16)
            gphi = (dot_nt(value, state) + recv_sum[g, h : h + 1, :]) * later
            total = total + pull_features(gphi, key_all, h, *tables)
        out_ref[g, :, width : 2 * width] = total.astype(bf16)
        store(g).start()
        return none

    lax.fori_loop(0, groups, carry_back, 0)

    @pl.when(place > 0)
    def _():
        def finish(g, none):
            for copy in hop(g):
                copy.wait_send()
            return none

        lax.fori_loop(0, groups, finish, 0)

    ring.arrive()

    def add_up(rows, total):
        final_ref[rows, :] = res_ref[rows, :] + total

    by_rows(ring, add_up)
    ring.finish()
    sibling.add()
    keep = pltpu.make_async_copy(acc_ref, acc_hbm, store_sem.at[groups])
    keep.start()

    def stored(g, none):
        store(g).wait()
        return none

    lax.fori_loop(0, groups, stored, 0)
    sibling.finish()
    keep.wait()


def term_tiles(term, left, right):
    parts, *shape = term.shape
    tile = left.shape[2] // parts

    def one(i, none):
        cols = pl.ds(pl.multiple_of(i * tile, tile), tile)
        total = dot_tn(left[0, :, cols], right[0])
        for g in range(1, left.shape[0]):
            total = total + dot_tn(left[g, :, cols], right[g])
        term[i] = total.astype(bf16).reshape(shape)
        return none

    lax.fori_loop(0, parts, one, 0)


def whole_vmem(count):
    return [pl.BlockSpec(memory_space=pltpu.VMEM)] * count


def attention_forward(qkv, segc, segr, tables, cot_own, heads):
    groups, block, _ = qkv.shape
    count = lax.axis_size("seq")
    dma = pltpu.SemaphoreType.DMA
    states = (groups, heads, STATE, HV)
    sums = (groups, 8, LANES)
    return pl.pallas_call(
        functools.partial(forward_kernel, count, heads),
        out_shape=(
            jax.ShapeDtypeStruct((groups, block, heads * HV), bf16),
            jax.ShapeDtypeStruct((groups, block, heads * HV), f32),
            jax.ShapeDtypeStruct(states, bf16),
            jax.ShapeDtypeStruct(sums, f32),
            jax.ShapeDtypeStruct((groups,) + cot_own.shape, bf16),
        ),
        in_specs=whole_vmem(6) + in_place(1),
        out_specs=tuple(in_place(5)),
        scratch_shapes=[
            pltpu.VMEM((groups, block, heads * HV), bf16),
            pltpu.VMEM((groups, block, heads * HV), f32),
            pltpu.VMEM(states, bf16),
            pltpu.VMEM(sums, f32),
            pltpu.VMEM(states, bf16),
            pltpu.VMEM(sums, f32),
            pltpu.VMEM((groups, heads, block, 2 * HV), f32),
            dma((2, groups)),
            dma((2, groups)),
            dma((6,)),
            dma((6,)),
            dma((1,)),
            dma((groups, 4)),
        ],
        compiler_params=pltpu.CompilerParams(
            collective_id=0, has_side_effects=True, vmem_limit_bytes=60 << 20
        ),
        cost_estimate=pl.CostEstimate(flops=0, bytes_accessed=1 << 20, transcendentals=0),
        name="attention_forward",
    )(qkv, segc, segr, *tables, cot_own)


def attention_backward(
    qkv, segc, segr, tables, att, rden, carry, csum, ga, down, residual, branch, heads
):
    groups, block, wide = qkv.shape
    count = lax.axis_size("seq")
    parts, dps = lax.axis_size("feat"), lax.axis_size("dp")
    rows_each = branch.shape[2] // (parts * count * dps)
    by_row = (parts, count, dps, rows_each, heads * HV)
    states = (groups, heads, STATE, HV)
    sums = (groups, 8, LANES)
    return pl.pallas_call(
        functools.partial(backward_kernel, count, heads),
        out_shape=(
            jax.ShapeDtypeStruct((groups, block, wide), bf16),
            jax.ShapeDtypeStruct(residual.shape, f32),
            jax.ShapeDtypeStruct((count, by_row[0]) + by_row[3:], bf16),
        ),
        in_specs=in_place(1)
        + whole_vmem(5)
        + in_place(3)
        + whole_vmem(1)
        + in_place(4),
        out_specs=tuple(in_place(1) + whole_vmem(1) + in_place(1)),
        scratch_shapes=vmem_like(qkv, att, rden, carry, ga, residual, branch)
        + [
            pltpu.VMEM((groups, block, wide), bf16),
            pltpu.VMEM((groups, heads, block, 2 * HV), bf16),
            pltpu.VMEM(states, bf16),
            pltpu.VMEM(sums, f32),
            pltpu.VMEM(states, bf16),
            pltpu.VMEM(sums, f32),
            pltpu.VMEM((groups, block, heads * FDIM), f32),
            pltpu.VMEM((groups, heads, block, HV), f32),
            pltpu.VMEM((groups,) + residual.shape, bf16),
            pltpu.VMEM((6, block // 2, residual.shape[1]), bf16),
            pltpu.SemaphoreType.DMA((2, groups)),
            pltpu.SemaphoreType.DMA((2, groups)),
            pltpu.SemaphoreType.DMA((6,)),
            pltpu.SemaphoreType.DMA((6,)),
            pltpu.SemaphoreType.DMA((1,)),
            pltpu.SemaphoreType.DMA((7,)),
            pltpu.SemaphoreType.DMA((groups + 1,)),
        ]
        + sibling_scratch(by_row),
        compiler_params=pltpu.CompilerParams(
            collective_id=1, has_side_effects=True, vmem_limit_bytes=60 << 20
        ),
        cost_estimate=pl.CostEstimate(flops=0, bytes_accessed=1 << 20, transcendentals=0),
        name="attention_backward",
    )(qkv, segc, segr, *tables, att, rden, carry, csum, ga, down, residual, branch)


def peers(f):
    return 2 * (f // 2) + 1 - f % 2, (f + 2) % 4, 3 - f


def greet(targets):
    barrier = pltpu.get_barrier_semaphore()
    for target in targets:
        pl.semaphore_signal(barrier, inc=1, device_id=target, device_id_type=MESH)
    pl.semaphore_wait(barrier, len(targets))


def push(src, dst, send_sem, recv_sem, target):
    return pltpu.make_async_remote_copy(
        src_ref=src,
        dst_ref=dst,
        send_sem=send_sem,
        recv_sem=recv_sem,
        device_id=target,
        device_id_type=MESH,
    )


def square_targets(f):
    return [{"feat": p} for p in peers(f)]


class Loads:
    def __init__(self, pairs, sem):
        self.copies = [pltpu.make_async_copy(a, b, sem.at[i]) for i, (a, b) in enumerate(pairs)]

    def start(self):
        for c in self.copies:
            c.start()
        return self

    def wait(self):
        for c in self.copies:
            c.wait()


def vmem_like(*arrays):
    return [pltpu.VMEM(a.shape, a.dtype) for a in arrays]


class SquareGather:
    def __init__(self, slots, f, send_sem, recv_sem, own=None, base=0, rows=None):
        side, above, across = peers(f)
        half = (slots.shape[1] if rows is None else rows) // 2
        first, second = pl.ds(base, half), pl.ds(base + half, half)

        def copy(i, slot, rows, to):
            ref = slots.at[slot, rows]
            src = ref if own is None or i > 3 else own.at[rows]
            return push(src, ref, send_sem.at[i], recv_sem.at[i], {"feat": to})

        self.direct = [
            copy(0, f, first, side),
            copy(1, f, second, above),
            copy(2, f, second, side),
            copy(3, f, first, above),
        ]
        self.forward = [copy(4, side, first, above), copy(5, above, second, side)]

    def start(self):
        for c in self.direct:
            c.start()

    def relay(self):
        self.direct[0].wait_recv()
        self.forward[0].start()
        self.direct[1].wait_recv()
        self.forward[1].start()

    def near(self):
        self.direct[2].wait_recv()
        self.direct[3].wait_recv()

    def far(self):
        for c in self.forward:
            c.wait_recv()

    def sent(self):
        for c in self.direct + self.forward:
            c.wait_send()

    def finish(self):
        self.near()
        self.far()
        self.sent()


class SquareSum:
    def __init__(self, part, land, f, send_sem, recv_sem, base=0, rows=None):
        self.side, self.above, self.across = peers(f)
        self.f, self.part, self.land, self.base = f, part, land, base
        self.half = (part.shape[1] if rows is None else rows) // 2
        first, second = pl.ds(base, self.half), pl.ds(base + self.half, self.half)

        def copy(i, slot, rows, to):
            return push(
                part.at[slot, rows], land.at[i], send_sem.at[i], recv_sem.at[i], {"feat": to}
            )

        self.cross = [copy(0, self.across, first, self.side), copy(1, self.across, second, self.above)]
        self.near = [copy(2, self.side, first, self.side), copy(3, self.above, second, self.above)]
        self.late = [copy(4, self.above, first, self.above), copy(5, self.side, second, self.side)]

    def start_cross(self):
        for c in self.cross:
            c.start()

    def add_rows(self, slot, base, landed):
        step = 16

        def one(i, none):
            rows = pl.ds(pl.multiple_of(base + i * step, step), step)
            came = self.land[landed, pl.ds(pl.multiple_of(i * step, step), step), :]
            self.part[slot, rows, :] = (
                self.part[slot, rows, :].astype(f32) + came.astype(f32)
            ).astype(bf16)
            return none

        lax.fori_loop(0, self.half // step, one, 0)

    def start_near(self):
        for c in self.near:
            c.start()

    def relay(self):
        self.cross[0].wait_recv()
        self.add_rows(self.above, self.base, 0)
        self.late[0].start()
        self.cross[1].wait_recv()
        self.add_rows(self.side, self.base + self.half, 1)
        self.late[1].start()

    def arrive(self):
        for c in self.near + self.late:
            c.wait_recv()

    def total(self, half, rows):
        base = self.base + half * self.half
        own = self.part[self.f, pl.ds(pl.multiple_of(base + rows.start, 16), rows.size), :]
        near = self.land[2 + half, rows, :]
        late = self.land[4 + half, rows, :]
        return own.astype(f32) + near.astype(f32) + late.astype(f32)

    def finish(self):
        for c in self.cross + self.near + self.late:
            c.wait_send()


class SiblingSum:
    def __init__(self, term, acc, land, sems, d, dps):
        self.term, self.acc, self.land, self.d = term, acc, land, d
        others = [lax.rem(d + k, dps) for k in range(1, dps)]
        self.copies = [
            push(term.at[:, :, o], land.at[k], sems[0].at[k], sems[1].at[k], {"dp": o})
            for k, o in enumerate(others)
        ]

    def start(self):
        for c in self.copies:
            c.start()

    def add(self):
        for c in self.copies:
            c.wait_recv()
        seqs, parts = self.acc.shape[:2]

        def one(i, none):
            p, c = i // seqs, lax.rem(i, seqs)
            total = self.term[p, c, self.d].astype(f32)
            for k in range(len(self.copies)):
                total = total + self.land[k, p, c].astype(f32)
            self.acc[c, p] = total.astype(bf16)
            return none

        lax.fori_loop(0, parts * seqs, one, 0)

    def finish(self):
        for c in self.copies:
            c.wait_send()


class RowSum:
    def __init__(self, acc, shares, land, total, sems, f, s):
        self.acc, self.shares, self.land, self.total = acc, shares, land, total
        self.f, self.s = f, s
        self.seqs, self.parts = seqs, parts = acc.shape[:2]
        to = (lax.rem(s + 1, seqs), lax.rem(s + seqs - 1, seqs))
        z_send, z_recv, a_send, a_recv = sems
        self.blocks, self.sends, self.comes, self.two = [], [], [], []
        for t in range(1, seqs):
            blocks = (lax.rem(s + seqs - t, seqs), lax.rem(s + t, seqs))
            self.blocks.append(blocks)
            self.sends.append((s < t, s > seqs - 1 - t))
            self.comes.append(((s > 0) & (s - 1 < t), (s < seqs - 1) & (s + 1 > seqs - 1 - t)))
            self.two.append(
                [
                    push(
                        acc.at[blocks[i]],
                        land.at[t - 1, i],
                        z_send.at[t - 1, i],
                        z_recv.at[t - 1, i],
                        {"seq": to[i]},
                    )
                    for i in range(2)
                ]
            )
        self.three = [
            push(total.at[p], shares.at[f], a_send.at[i], a_recv.at[i], {"feat": p})
            for i, p in enumerate(peers(f))
        ]

    def add(self, into, t, i):
        @pl.when(self.comes[t - 1][i])
        def _():
            self.two[t - 1][i].wait_recv()

            def one(p, none):
                into[p] = (
                    into[p].astype(f32) + self.land[t - 1, i, p].astype(f32)
                ).astype(bf16)
                return none

            lax.fori_loop(0, self.parts, one, 0)

    def step(self, t):
        for i in range(2):
            if t > 1:
                self.add(self.acc.at[self.blocks[t - 1][i]], t - 1, i)
            pl.when(self.sends[t - 1][i])(self.two[t - 1][i].start)

    def over_feat(self):
        self.total[...] = self.acc[self.s]
        for i in range(2):
            self.add(self.total, self.seqs - 1, i)
        self.shares[self.f] = self.total[self.f]
        for c in self.three:
            c.start()

    def arrive(self):
        for c in self.three:
            c.wait_recv()

    def finish(self):
        for sends, copies in zip(self.sends, self.two):
            for i in range(2):
                pl.when(sends[i])(copies[i].wait_send)
        for c in self.three:
            c.wait_send()


def sibling_scratch(shape):
    parts, seqs, dps, rows, wide = shape
    others = max(dps - 1, 1)
    dma = pltpu.SemaphoreType.DMA
    return [
        pltpu.VMEM(shape, bf16),
        pltpu.VMEM((seqs, parts, rows, wide), bf16),
        pltpu.VMEM((others, parts, seqs, rows, wide), bf16),
        dma((others,)),
        dma((others,)),
    ]


def row_sum_scratch(shape):
    seqs, parts, rows, wide = shape
    dma = pltpu.SemaphoreType.DMA
    return [
        pltpu.VMEM((parts, rows, wide), bf16),
        pltpu.VMEM((seqs - 1, 2, parts, rows, wide), bf16),
        pltpu.VMEM((parts, rows, wide), bf16),
        dma((seqs - 1, 2)),
        dma((seqs - 1, 2)),
        dma((3,)),
        dma((3,)),
    ]


def opening_kernel(
    seqs,
    dps,
    tok_ref,
    query_ref,
    key_ref,
    value_ref,
    out_ref,
    one_ref,
    two_ref,
    x_ref,
    w_ref,
    g_ref,
    o_ref,
    pack,
    opack,
    tile,
    x_send,
    x_recv,
    a_send,
    a_recv,
    z_send,
    z_recv,
    d_send,
    d_recv,
    local_sem,
):
    f, s, d = lax.axis_index("feat"), lax.axis_index("seq"), lax.axis_index("dp")
    parts, rows_each = pack.shape[0], pack.shape[1]
    near = peers(f)
    columns = [lax.rem(s + k, seqs) for k in range(1, seqs)]
    others = [lax.rem(d + k, dps) for k in range(1, dps)]
    stay = pltpu.make_async_copy(tok_ref, x_ref.at[f], local_sem.at[0])
    stay.start()
    first = 0
    for ref in (query_ref, key_ref, value_ref):
        each = ref.shape[1] // parts
        for p in range(parts):
            pack[p, :, first : first + each] = ref[:, p * each : (p + 1) * each]
        first += each
    tile[...] = jnp.zeros_like(tile)
    tile[0:1, :rows_each] = one_ref[...].astype(f32)
    tile[1:2, :rows_each] = two_ref[...].astype(f32)
    outs = (w_ref, g_ref)
    own = [
        pltpu.make_async_copy(pack.at[f], w_ref.at[f, s, d], local_sem.at[1]),
        pltpu.make_async_copy(tile, g_ref.at[f, s, d], local_sem.at[2]),
    ]
    for c in own:
        c.start()
    greet(
        square_targets(f) + [{"seq": c} for c in columns] + [{"dp": o} for o in others]
    )
    shares = [
        [
            push(pack.at[p], w_ref.at[f, s, d], a_send.at[0, i], a_recv.at[0, i], {"feat": p}),
            push(tile, g_ref.at[f, s, d], a_send.at[1, i], a_recv.at[1, i], {"feat": p}),
        ]
        for i, p in enumerate(near)
    ]
    for pair in shares:
        for c in pair:
            c.start()
    gather = SquareGather(x_ref, f, x_send, x_recv, tok_ref)
    gather.start()
    each = out_ref.shape[1] // parts
    for p in range(parts):
        opack[p] = out_ref[:, p * each : (p + 1) * each]
    own_out = pltpu.make_async_copy(opack.at[f], o_ref.at[f], local_sem.at[3])
    own_out.start()
    out_shares = [
        push(opack.at[p], o_ref.at[f], a_send.at[2, i], a_recv.at[2, i], {"feat": p})
        for i, p in enumerate(near)
    ]
    for c in out_shares:
        c.start()
    for c in own:
        c.wait()

    chunks = (f,) + near

    def to_column(n, k):
        return [
            push(
                ref.at[chunks[n], s, d],
                ref.at[chunks[n], s, d],
                z_send.at[j, k - 1, n],
                z_recv.at[j, k - 1, n],
                {"seq": columns[k - 1]},
            )
            for j, ref in enumerate(outs)
        ]

    def to_sibling(n, k):
        back = lax.rem(s + seqs - k, seqs)
        return [
            push(
                ref.at[chunks[n], back, d],
                ref.at[chunks[n], back, d],
                d_send.at[j, o, k, n],
                d_recv.at[j, o, k, n],
                {"dp": other},
            )
            for j, ref in enumerate(outs)
            for o, other in enumerate(others)
        ]

    def start_all(copies):
        for c in copies:
            c.start()

    for n in range(parts):
        if n:
            for c in shares[n - 1]:
                c.wait_recv()
        for k in range(1, seqs):
            start_all(to_column(n, k))
        start_all(to_sibling(n, 0))
    for n in range(parts):
        for k in range(1, seqs):
            for c in to_column(n, k):
                c.wait_recv()
            start_all(to_sibling(n, k))
    gather.relay()
    for n in range(parts):
        for k in range(seqs):
            for c in to_sibling(n, k):
                c.wait_recv()
    for n in range(parts):
        for k in range(seqs):
            for c in to_sibling(n, k):
                c.wait_send()
        for k in range(1, seqs):
            for c in to_column(n, k):
                c.wait_send()
    for pair in shares:
        for c in pair:
            c.wait_send()
    stay.wait()
    own_out.wait()
    for c in out_shares:
        c.wait_recv()
    for c in out_shares:
        c.wait_send()
    gather.finish()


def in_place(count):
    return [pl.BlockSpec(memory_space=pltpu.HBM)] * count


def opening(own, w_query, w_key, w_value, w_out, gain_one, gain_two):
    parts, seqs, dps = (lax.axis_size(a) for a in ALL)
    block, width = own.shape
    rows_each = w_query.shape[0]
    wide = (w_query.shape[1] + w_key.shape[1] + w_value.shape[1]) // parts
    others = max(dps - 1, 1)
    dma = pltpu.SemaphoreType.DMA
    out_wide = w_out.shape[1] // parts
    x_all, w_all, g_all, o_own = pl.pallas_call(
        functools.partial(opening_kernel, seqs, dps),
        out_shape=(
            jax.ShapeDtypeStruct((parts, block, width), bf16),
            jax.ShapeDtypeStruct((parts, seqs, dps, rows_each, wide), bf16),
            jax.ShapeDtypeStruct((parts, seqs, dps, 8, HV), f32),
            jax.ShapeDtypeStruct((parts, rows_each, out_wide), bf16),
        ),
        in_specs=in_place(1) + whole_vmem(6),
        out_specs=tuple(in_place(4)),
        scratch_shapes=[
            pltpu.VMEM((parts, rows_each, wide), bf16),
            pltpu.VMEM((parts, rows_each, out_wide), bf16),
            pltpu.VMEM((8, HV), f32),
            dma((6,)),
            dma((6,)),
            dma((3, 3)),
            dma((3, 3)),
            dma((2, seqs - 1, parts)),
            dma((2, seqs - 1, parts)),
            dma((2, others, seqs, parts)),
            dma((2, others, seqs, parts)),
            dma((4,)),
        ],
        compiler_params=pltpu.CompilerParams(collective_id=2, has_side_effects=True, vmem_limit_bytes=60 << 20),
        cost_estimate=pl.CostEstimate(flops=0, bytes_accessed=1 << 20, transcendentals=0),
        name="opening",
    )(own, w_query, w_key, w_value, w_out, gain_one, gain_two)
    gains = g_all[..., :2, :rows_each].transpose(3, 0, 1, 2, 4).reshape(2, width)
    return x_all, w_all.reshape(width, wide), gains, o_own


def inverse_rms(values):
    return lax.rsqrt(jnp.mean(values * values, axis=-1, keepdims=True) + epsilon)


def norm_back(grad, unit, inverse, gain):
    scaled = grad * gain
    return (scaled - unit * jnp.mean(scaled * unit, axis=-1, keepdims=True)) * inverse


class ByShare:
    def __init__(self, ref):
        self.ref = ref

    def tile(self, i, size):
        block = self.ref[:, i]
        return block.reshape(size, block.shape[2])


class ByTiles:
    def __init__(self, src, ref, sem, tile):
        self.ref = ref
        self.fills = [
            pltpu.make_async_copy(
                src.at[pl.ds(i * tile, tile)], ref.at[pl.ds(i * tile, tile)], sem.at[i]
            )
            for i in range(ref.shape[0] // tile)
        ]

    def tile(self, i, size):
        return self.ref[pl.ds(pl.multiple_of(i * size, size), size), :]


def product_tiles(part, slot, pairs, tile, first=False):
    def one(i, none):
        cols = pl.ds(pl.multiple_of(i * tile, tile), tile)
        total = None
        for rows, weights in pairs:
            if hasattr(weights, "tile"):
                block = weights.tile(i, tile)
            else:
                block = weights[cols, :]
            term = dot_nt(rows[slot], block)
            total = term if total is None else total + term
        part[slot, :, cols] = total.astype(bf16)
        return none

    if first:
        for i in range(part.shape[2] // tile):
            for _, weights in pairs:
                weights.fills[i].wait()
            one(i, 0)
    else:
        lax.fori_loop(0, part.shape[2] // tile, one, 0)


def summed_products(part, land, f, pairs, send_sem, recv_sem, chunks=1, beside=(), first=False):
    side, above, across = peers(f)
    rows = part.shape[1] // chunks
    rings = [
        SquareSum(
            part, land.at[c], f, send_sem.at[c], recv_sem.at[c], base=c * rows, rows=rows
        )
        for c in range(chunks)
    ]
    product_tiles(part, across, pairs, 512, first)
    for ring in rings:
        ring.start_cross()
    beside = iter(beside)
    next(beside, int)()
    product_tiles(part, side, pairs, 512)
    for ring in rings:
        ring.near[0].start()
    product_tiles(part, above, pairs, 512)
    for ring in rings:
        ring.near[1].start()
    next(beside, int)()
    rings[0].relay()
    product_tiles(part, f, pairs, 512)
    next(beside, int)()
    for ring in rings[1:]:
        ring.relay()
    return rings


def sum_then_gather(rings, finish_rows, slots, f, send_sem, recv_sem):
    gathers = []
    for c, ring in enumerate(rings):
        ring.arrive()
        by_rows(ring, finish_rows)
        gather = SquareGather(
            slots, f, send_sem.at[c], recv_sem.at[c], base=ring.base, rows=2 * ring.half
        )
        gather.start()
        gathers.append(gather)
    for ring in rings:
        ring.finish()
    return gathers


def by_rows(ring, body, step=16):
    for half in (0, 1):

        def one(i, none):
            start = pl.multiple_of(i * step, step)
            rows = pl.ds(
                pl.multiple_of(ring.base + half * ring.half + i * step, step), step
            )
            body(rows, ring.total(half, pl.ds(start, step)))
            return none

        lax.fori_loop(0, ring.half // step, one, 0)


def branch_kernel(
    att_hbm,
    w_hbm,
    tok_hbm,
    gain_ref,
    rows_hbm,
    res_hbm,
    rows_ref,
    res_ref,
    att_ref,
    w_ref,
    tok_ref,
    part,
    land,
    s_send,
    s_recv,
    g_send,
    g_recv,
    load_sem,
    store_sem,
):
    f = lax.axis_index("feat")
    loads = Loads(((att_hbm, att_ref), (w_hbm, w_ref), (tok_hbm, tok_ref)), load_sem).start()
    greet(square_targets(f))
    loads.wait()
    rings = summed_products(
        part, land, f, [(att_ref, ByShare(w_ref))], s_send, s_recv, land.shape[0]
    )

    def finish_rows(rows, total):
        residual = tok_ref[rows, :].astype(f32) + total
        res_ref[rows, :] = residual
        rows_ref[f, rows, :] = (residual * inverse_rms(residual) * gain_ref[...]).astype(bf16)

    gathers = sum_then_gather(rings, finish_rows, rows_ref, f, g_send, g_recv)
    stores = [pltpu.make_async_copy(res_ref, res_hbm, store_sem.at[0])]
    stores[0].start()

    def store(slot):
        c = pltpu.make_async_copy(rows_ref.at[slot], rows_hbm.at[slot], store_sem.at[len(stores)])
        c.start()
        stores.append(c)

    side, above, across = peers(f)
    store(f)
    for gather in gathers:
        gather.relay()
    for gather in gathers:
        gather.near()
    store(side)
    store(above)
    for gather in gathers:
        gather.far()
    store(across)
    for gather in gathers:
        gather.sent()
    for c in stores:
        c.wait()


CHUNKS = 4


def square_scratch(parts, block, width, chunks=CHUNKS):
    dma = pltpu.SemaphoreType.DMA
    return [
        pltpu.VMEM((parts, block, width), bf16),
        pltpu.VMEM((chunks, 6, block // 2 // chunks, width), bf16),
        dma((chunks, 6)),
        dma((chunks, 6)),
    ]


def branch_step(att, out_w, own, gain_two):
    parts, block, _ = att.shape
    width = own.shape[1]
    dma = pltpu.SemaphoreType.DMA
    return pl.pallas_call(
        branch_kernel,
        out_shape=(
            jax.ShapeDtypeStruct((parts, block, width), bf16),
            jax.ShapeDtypeStruct((block, width), f32),
        ),
        in_specs=in_place(3) + whole_vmem(1),
        out_specs=tuple(in_place(2)),
        scratch_shapes=[pltpu.VMEM((parts, block, width), bf16), pltpu.VMEM((block, width), f32)]
        + vmem_like(att, out_w, own)
        + square_scratch(parts, block, width)
        + [dma((CHUNKS, 6)), dma((CHUNKS, 6)), dma((3,)), dma((1 + parts,))],
        compiler_params=pltpu.CompilerParams(
            collective_id=3, has_side_effects=True, vmem_limit_bytes=60 << 20
        ),
        cost_estimate=pl.CostEstimate(flops=0, bytes_accessed=1 << 20, transcendentals=0),
        name="branch_step",
    )(att, out_w, own, gain_two)


def rows_back_kernel(
    grads_hbm,
    wg_hbm,
    wu_hbm,
    res_hbm,
    cot_hbm,
    gain_ref,
    mixed_hbm,
    wd_hbm,
    wo_hbm,
    all_hbm,
    gres_hbm,
    gsum_ref,
    down_hbm,
    ga_hbm,
    all_ref,
    gres_ref,
    down_ref,
    ga_ref,
    gg_ref,
    gu_ref,
    res_ref,
    cot_ref,
    part,
    land,
    wg,
    wu,
    mixed,
    wd,
    wo,
    s_send,
    s_recv,
    g_send,
    g_recv,
    local_sem,
    tile_sem,
    load_sem,
    store_sem,
):
    f = lax.axis_index("feat")
    rows_in = Loads(((grads_hbm.at[0], gg_ref), (grads_hbm.at[1], gu_ref)), load_sem).start()
    weights = [
        ByTiles(src, dst, tile_sem.at[i], 512)
        for i, (src, dst) in enumerate(((wg_hbm, wg), (wu_hbm, wu)))
    ]
    for pair in zip(*(w.fills for w in weights)):
        for c in pair:
            c.start()
    fills = [
        pltpu.make_async_copy(src, dst, local_sem.at[i])
        for i, (src, dst) in enumerate(((mixed_hbm, mixed), (wd_hbm, wd), (wo_hbm, wo)))
    ]
    late_in = Loads(((res_hbm, res_ref), (cot_hbm, cot_ref)), load_sem.at[pl.ds(2, 2)]).start()
    for c in fills:
        c.start()
    greet(square_targets(f))
    rows_in.wait()
    pairs = [(gg_ref, weights[0]), (gu_ref, weights[1])]

    def down_products(slots):
        for p in slots:
            product_tiles(down_ref, p, [(mixed, wd)], 512)

    rings = summed_products(part, land, f, pairs, s_send, s_recv, land.shape[0], first=True)
    gsum_ref[...] = jnp.zeros_like(gsum_ref)
    late_in.wait()

    def finish_rows(rows, grad):
        residual = res_ref[rows, :]
        inverse = inverse_rms(residual)
        unit = residual * inverse
        gsum_ref[...] += jnp.sum(grad * unit, axis=0, keepdims=True)
        grad_res = cot_ref[rows, :].astype(f32) + norm_back(grad, unit, inverse, gain_ref[...])
        gres_ref[rows, :] = grad_res
        all_ref[f, rows, :] = grad_res.astype(bf16)

    gathers = sum_then_gather(rings, finish_rows, all_ref, f, g_send, g_recv)
    side, above, across = peers(f)

    def attended_grad(slot):
        blocks = ByShare(wo)
        size = all_ref.shape[2] // wo.shape[1]
        total = None
        for i in range(wo.shape[1]):
            term = dot(all_ref[slot, :, i * size : (i + 1) * size], blocks.tile(i, size))
            total = term if total is None else total + term
        ga_ref[slot] = total
        store(ga_ref.at[slot], ga_hbm.at[slot])
        store(all_ref.at[slot], all_hbm.at[slot])

    stores = []

    def store(src, dst):
        c = pltpu.make_async_copy(src, dst, store_sem.at[len(stores)])
        c.start()
        stores.append(c)

    store(gres_ref, gres_hbm)
    for c in fills:
        c.wait()
    attended_grad(f)
    down_products(range(2))
    for gather in gathers:
        gather.relay()
    down_products(range(2, part.shape[0]))
    store(down_ref, down_hbm)
    for gather in gathers:
        gather.near()
    attended_grad(side)
    attended_grad(above)
    for gather in gathers:
        gather.far()
    attended_grad(across)
    for gather in gathers:
        gather.sent()
    for c in stores:
        c.wait()


def rows_back(
    grads, gate_w, up_w, residual, cot_own, gain_two, mixed, down_w, out_w
):
    _, parts, block, hidden = grads.shape
    width = residual.shape[1]
    dma = pltpu.SemaphoreType.DMA
    return pl.pallas_call(
        rows_back_kernel,
        out_shape=(
            jax.ShapeDtypeStruct((parts, block, width), bf16),
            jax.ShapeDtypeStruct((block, width), f32),
            jax.ShapeDtypeStruct((1, width), f32),
            jax.ShapeDtypeStruct((parts, block, width), bf16),
            jax.ShapeDtypeStruct((parts, block, out_w.shape[3]), f32),
        ),
        in_specs=in_place(5) + whole_vmem(1) + in_place(3),
        out_specs=tuple(in_place(2) + whole_vmem(1) + in_place(2)),
        scratch_shapes=[
            pltpu.VMEM((parts, block, width), bf16),
            pltpu.VMEM((block, width), f32),
            pltpu.VMEM((parts, block, width), bf16),
            pltpu.VMEM((parts, block, out_w.shape[3]), f32),
        ]
        + [pltpu.VMEM((parts, block, hidden), bf16)] * 2
        + vmem_like(residual, cot_own)
        + square_scratch(parts, block, width)[:2]
        + [
            pltpu.VMEM((width, hidden), bf16),
            pltpu.VMEM((width, hidden), bf16),
            pltpu.VMEM((parts, block, hidden), bf16),
            pltpu.VMEM((width, hidden), bf16),
            pltpu.VMEM(out_w.shape, bf16),
        ]
        + [dma((CHUNKS, 6))] * 4
        + [dma((3,)), dma((2, width // 512)), dma((4,)), dma((2 * parts + 2,))],
        compiler_params=pltpu.CompilerParams(
            collective_id=4, has_side_effects=True, vmem_limit_bytes=60 << 20
        ),
        cost_estimate=pl.CostEstimate(flops=0, bytes_accessed=1 << 20, transcendentals=0),
        name="rows_back",
    )(grads, gate_w, up_w, residual, cot_own, gain_two, mixed, down_w, out_w)


def closing_kernel(
    seqs,
    dps,
    dqkv_hbm,
    w_hbm,
    tok_hbm,
    gres_hbm,
    gain_ref,
    gsum_two_ref,
    normed_hbm,
    oacc_hbm,
    down_hbm,
    output_hbm,
    x_ref,
    tile_ref,
    query_ref,
    key_ref,
    value_ref,
    ograd_ref,
    part,
    land,
    s_send,
    s_recv,
    gsum,
    cut,
    came,
    mid,
    tail,
    c_send,
    c_recv,
    d_send,
    d_recv,
    dqkv_ref,
    w_ref,
    tok_ref,
    gres_ref,
    normed_ref,
    oacc_ref,
    load_sem,
    first_sem,
    term_ref,
    acc_ref,
    sib_land,
    sib_send,
    sib_recv,
    *sum_scratch,
):
    begin = Loads(((oacc_hbm, oacc_ref),), first_sem).start()
    loads = Loads(
        (
            (dqkv_hbm, dqkv_ref),
            (normed_hbm, normed_ref),
            (w_hbm, w_ref),
            (tok_hbm, tok_ref),
            (gres_hbm, gres_ref),
        ),
        load_sem,
    ).start()
    half = len(sum_scratch) // 2
    f, s, d = lax.axis_index("feat"), lax.axis_index("seq"), lax.axis_index("dp")
    parts = 4
    others = [lax.rem(d + k, dps) for k in range(1, dps)]
    circle = [
        (lax.rem(f + i, parts), lax.rem(s + j, seqs))
        for i in range(parts)
        for j in range(seqs)
        if i or j
    ]
    greet(
        [{"feat": a, "seq": b} for a, b in circle] + [{"dp": o} for o in others]
    )
    begin.wait()
    rows_sum = RowSum(acc_ref, *sum_scratch[:3], sum_scratch[3:half], f, s)
    out_sum = RowSum(oacc_ref, *sum_scratch[half : half + 3], sum_scratch[half + 3 :], f, s)
    out_sum.step(1)
    loads.wait()
    term_tiles(term_ref, normed_ref, dqkv_ref)
    sibling = SiblingSum(term_ref, acc_ref, sib_land, (sib_send, sib_recv), d, dps)
    sibling.start()
    out_sum.step(2)

    def over_seq():
        sibling.add()
        rows_sum.step(1)
        for t in range(3, seqs):
            out_sum.step(t)

    rings = summed_products(
        part, land, f, [(dqkv_ref, w_ref)], s_send, s_recv, land.shape[0], (over_seq,)
    )
    for t in range(2, seqs):
        rows_sum.step(t)
    gsum[...] = jnp.zeros_like(gsum)

    def finish_rows(rows, grad):
        values = tok_ref[rows, :].astype(f32)
        inverse = inverse_rms(values)
        unit = values * inverse
        gsum[...] += jnp.sum(grad * unit, axis=0, keepdims=True)
        x_ref[rows, :] = gres_ref[rows, :] + norm_back(grad, unit, inverse, gain_ref[...])

    for ring in rings:
        ring.arrive()
        by_rows(ring, finish_rows)
    for ring in rings:
        ring.finish()

    lanes = gsum.shape[1] // (parts * seqs)
    cut[...] = jnp.zeros_like(cut)
    for k in range(parts * seqs):
        cut[k, 0:1, :] = gsum[:, k * lanes : (k + 1) * lanes]
        cut[k, 1:2, :] = gsum_two_ref[:, k * lanes : (k + 1) * lanes]
    place = f * seqs + s
    sends = []
    for i, (a, b) in enumerate(circle):
        sends.append(
            push(
                cut.at[a * seqs + b],
                came.at[i],
                c_send.at[i],
                c_recv.at[i],
                {"feat": a, "seq": b},
            )
        )
    for c in sends:
        c.start()
    total = cut[place]
    for c in sends:
        c.wait_recv()
    for i in range(len(circle)):
        total = total + came[i]
    mid[...] = total
    last = [
        push(mid, tail.at[k], d_send.at[k], d_recv.at[k], {"dp": o})
        for k, o in enumerate(others)
    ]
    for c in last:
        c.start()
    for c in last:
        c.wait_recv()
    for k in range(len(others)):
        total = total + tail[k]
    tile_ref[...] = total
    out_sum.over_feat()
    rows_sum.over_feat()
    rows_sum.arrive()
    first = 0
    for ref in (query_ref, key_ref, value_ref):
        each = ref.shape[1] // parts
        for p in range(parts):
            piece = rows_sum.shares[p, :, first : first + each]
            ref[:, p * each : (p + 1) * each] = piece.astype(f32)
        first += each
    rows_sum.finish()
    sibling.finish()
    out_sum.arrive()
    each = ograd_ref.shape[1] // parts
    for p in range(parts):
        ograd_ref[:, p * each : (p + 1) * each] = out_sum.shares[p].astype(f32)
    out_sum.finish()
    for c in sends + last:
        c.wait_send()


def closing(dqkv, qkv_w, own, grad_residual, gain_one, gain_two_sum, normed, out_acc, down_grad, output):
    parts, seqs, dps = (lax.axis_size(a) for a in ALL)
    block, width = own.shape
    others = max(dps - 1, 1)
    lanes = width // (parts * seqs)
    circle = parts * seqs - 1
    rows_each = out_acc.shape[2]
    by_row = (parts, seqs, dps, rows_each, dqkv.shape[2])
    acc_shape = out_acc.shape[:3] + dqkv.shape[2:]
    dma = pltpu.SemaphoreType.DMA
    return pl.pallas_call(
        functools.partial(closing_kernel, seqs, dps),
        out_shape=(
            jax.ShapeDtypeStruct((block, width), f32),
            jax.ShapeDtypeStruct((8, lanes), f32),
            jax.ShapeDtypeStruct((rows_each, HEADS * FDIM), f32),
            jax.ShapeDtypeStruct((rows_each, HEADS * FDIM), f32),
            jax.ShapeDtypeStruct((rows_each, HEADS * HV), f32),
            jax.ShapeDtypeStruct((rows_each, HEADS * HV), f32),
        ),
        in_specs=in_place(4) + whole_vmem(2) + in_place(4),
        out_specs=tuple(whole_vmem(6)),
        scratch_shapes=square_scratch(parts, block, width)
        + [
            pltpu.VMEM((1, width), f32),
            pltpu.VMEM((parts * seqs, 8, lanes), f32),
            pltpu.VMEM((circle, 8, lanes), f32),
            pltpu.VMEM((8, lanes), f32),
            pltpu.VMEM((others, 8, lanes), f32),
            dma((circle,)),
            dma((circle,)),
            dma((others,)),
            dma((others,)),
        ]
        + vmem_like(dqkv, qkv_w, own, grad_residual, normed, out_acc)
        + [dma((5,)), dma((1,))]
        + sibling_scratch(by_row)
        + row_sum_scratch(acc_shape)
        + row_sum_scratch(out_acc.shape),
        compiler_params=pltpu.CompilerParams(
            collective_id=5, has_side_effects=True, vmem_limit_bytes=60 << 20
        ),
        cost_estimate=pl.CostEstimate(flops=0, bytes_accessed=1 << 20, transcendentals=0),
        name="closing",
    )(dqkv, qkv_w, own, grad_residual, gain_one, gain_two_sum, normed, out_acc, down_grad, output)


def local(
    tokens,
    segments,
    norm1_gain,
    norm2_gain,
    w_query,
    w_key,
    w_value,
    w_out,
    w_gate,
    w_up,
    w_down,
    cotangent,
):
    parts = lax.axis_size("feat")
    heads = HEADS // parts
    block, width = tokens.shape[2], tokens.shape[3]
    rows_total = parts * block
    rows_each = w_query.shape[0]
    own = tokens.reshape(block, width)
    cot_own = cotangent.reshape(block, width)

    x_all, qkv_w, gains, out_share = opening(
        own, w_query, w_key, w_value, w_out.T, norm1_gain[None], norm2_gain[None]
    )
    qkv_width = qkv_w.shape[1]
    gate_w = lax.all_gather(w_gate, ("seq", "dp"), axis=0, tiled=True)
    gain_one, gain_two = gains[0:1], gains[1:2]

    x_wide = x_all.astype(f32).reshape(rows_total, width)
    normed = (x_wide * inverse_rms(x_wide) * gain_one).astype(bf16)
    qkv = dot(normed, qkv_w).astype(bf16).reshape(parts, block, qkv_width)
    qkv, gate_w, out_share, w_up, w_down = lax.optimization_barrier(
        (qkv, gate_w, out_share, w_up, w_down)
    )
    out_w = lax.all_gather(out_share[None], ("seq", "dp"), axis=0, tiled=True)
    up_w = lax.all_gather(w_up, ("seq", "dp"), axis=0, tiled=True)
    down_w = lax.all_gather(w_down.T, ("seq", "dp"), axis=0, tiled=True)
    segment = segments.reshape(parts, block).astype(f32)
    segc, segr = segment[:, :, None], segment[:, None, :]
    tables = feature_tables(heads)
    att, rden, carry, csum, cot_all = attention_forward(qkv, segc, segr, tables, cot_own, heads)
    cot_all = cot_all.reshape(rows_total, width)
    rows_all, residual = branch_step(att, out_w, own, gain_two)
    rows_all = rows_all.reshape(rows_total, width)

    gate_out = dot(rows_all, gate_w)
    up_out = dot(rows_all, up_w)
    sig = jax.nn.sigmoid(gate_out)
    silu = gate_out * sig
    mixed = (silu * up_out).astype(bf16)
    down_term = dot_tn(cot_all, mixed).astype(bf16)
    mixed, cot_late, down_term = lax.optimization_barrier((mixed, cot_all, down_term))
    grad_mixed = dot(cot_late, down_w)
    grads = jnp.stack(
        [grad_mixed * up_out * sig * (1.0 + gate_out * (1.0 - sig)), grad_mixed * silu]
    ).astype(bf16)

    def summed(term, dim):
        return lax.psum_scatter(term, ("seq", "dp"), scatter_dimension=dim, tiled=True)

    both_term = jnp.einsum("xtf,td->xfd", grads, rows_all, preferred_element_type=f32).astype(bf16)
    grads, both_term = lax.optimization_barrier((grads, both_term))
    down_sum, both_sum = summed(down_term, 0), summed(both_term, 2)

    by_device = (parts, block, -1)
    branch_all, grad_residual, gain_two_sum, down, ga = rows_back(
        grads.reshape((2,) + by_device),
        gate_w,
        up_w,
        residual,
        cot_own,
        gain_two,
        mixed.reshape(by_device),
        down_w,
        out_w,
    )
    dqkv, output, out_acc = attention_backward(
        qkv,
        segc,
        segr,
        tables,
        att,
        rden,
        carry,
        csum,
        ga,
        down,
        residual,
        branch_all,
        heads,
    )
    output = output.astype(bf16)
    down_grad = down_sum.T.astype(f32)
    x_grad, gain_grads, query_grad, key_grad, value_grad, out_grad = closing(
        dqkv,
        qkv_w,
        own,
        grad_residual,
        gain_one,
        gain_two_sum,
        normed.reshape(parts, block, width),
        out_acc,
        down_grad,
        output,
    )
    gain_each = gain_grads.shape[1] // lax.axis_size("dp")
    gain_grads = lax.dynamic_slice_in_dim(
        gain_grads, lax.axis_index("dp") * gain_each, gain_each, axis=1
    )
    return (
        output.reshape(tokens.shape),
        x_grad.reshape(tokens.shape),
        gain_grads[0],
        gain_grads[1],
        query_grad,
        key_grad,
        value_grad,
        out_grad.T,
        both_sum[0].T.astype(f32),
        both_sum[1].T.astype(f32),
        down_grad,
    )


def solution(mesh):
    placed = (
        P("feat", "dp", "seq", None),
        P(None, "dp", "seq"),
        P(ALL),
        P(ALL),
        P(ALL, None),
        P(ALL, None),
        P(ALL, None),
        P(None, ALL),
        P(("seq", "dp"), "feat"),
        P(("seq", "dp"), "feat"),
        P("feat", ("seq", "dp")),
        P("feat", "dp", "seq", None),
    )
    return jax.shard_map(
        local,
        mesh=mesh,
        in_specs=placed,
        out_specs=(
            P("feat", "dp", "seq", None),
            P("feat", "dp", "seq", None),
            P(ALL),
            P(ALL),
            P(ALL, None),
            P(ALL, None),
            P(ALL, None),
            P(None, ALL),
            P(("seq", "dp"), "feat"),
            P(("seq", "dp"), "feat"),
            P("feat", ("seq", "dp")),
        ),
        check_vma=False,
    )
```
